128 devices in a mesh: freq: 8 (over y, core), sky: 16 (over z, x).
Axes of the slice: x: 4, y: 4, z: 4, core: 2. Of those that a mesh axis runs over, the one named last changes fastest.
Arguments:
- sky_cube: bfloat16 [256, 512, 1024], P(None, 'sky', 'freq'), may hold values from -6 to 6
- weight_first: bfloat16 [3, 3, 1024, 256], P(None, None, 'freq'), may hold values from -0.0625 to 0.0625
- weight_second: bfloat16 [3, 3, 256, 256], replicated, may hold values from -0.125 to 0.125
- cotangent: bfloat16 [256, 512, 256], P('freq', 'sky'), may hold values from -0.016479492 to 0.016479492
Outputs:
- features: bfloat16 [256, 512, 256], P('freq', 'sky')
- grad_first: float32 [3, 3, 1024, 256], P(None, None, 'freq')
- grad_second: float32 [3, 3, 256, 256], replicated
The draws below stay inside these ranges and needn't reach their ends.
All inputs are finite; a program needn't handle non-finite values.
Results may differ from the reference program's by a relative error of at most 0.024.
Values may be sent and summed in bfloat16 or wider, within the bound.
No kernel may reach another device: no remote copies, remote signals or barrier semaphores. Data moves between devices by JAX's collectives and lax.ppermute only.
A program may use at most 128 MiB of HBM per device.

```python
import jax
import jax.numpy as jnp

CIN = 1024
CH = 256
NCOL = 256
NROW = 512


def block_levels(rng, dims, pieces, smallest, top_value):
    def one(dim, parts):
        steps = jax.random.uniform(jax.random.fold_in(jax.random.fold_in(rng, 6), dim), (parts,), jnp.float32, smallest / len(pieces), top_value / len(pieces))
        return jnp.repeat(jnp.exp(steps), dims[dim] // parts).reshape((-1,) + (1,) * (len(dims) - dim - 1))

    factor_of = one(*pieces[0])
    for cut in pieces[1:]:
        factor_of = factor_of * one(*cut)
    return factor_of


def bell_draw(rng, dims, deviation, reach, shards=(), held_as=jnp.bfloat16):
    loudness = block_levels(rng, dims, shards, -0.22, 0.18) if shards else 1.0
    result = jax.random.normal(rng, dims, jnp.float32) * deviation * loudness
    return jnp.minimum(jnp.maximum(result, -reach), reach).astype(held_as)


def setup_inputs(seed: int = 0) -> dict:
    keys = jax.random.split(jax.random.key(seed), 5)
    return {
        "sky_cube": bell_draw(keys[0], (NCOL, NROW, CIN), 1.0, 6.0, ((1, 16), (2, 8))),
        "weight_first": bell_draw(keys[1], (3, 3, CIN, CH), (9 * CIN) ** -0.5, 0.0625, ((2, 8),)),
        "weight_second": bell_draw(keys[2], (3, 3, CH, CH), (9 * CH) ** -0.5, 0.125),
        "cotangent": bell_draw(keys[3], (NCOL, NROW, CH), (1.0 / (NCOL * NROW) ** 0.5), 0.016479492, ((0, 8), (1, 16))),
    }


def conv_taps(padded, kernel, col_count, row_count):
    total = jnp.zeros((col_count * row_count, kernel.shape[3]), jnp.float32)
    for tap_col in range(3):
        for tap_row in range(3):
            piece = padded[tap_col:tap_col + col_count, tap_row:tap_row + row_count].reshape(col_count * row_count, -1)
            total = total + jnp.dot(piece, kernel[tap_col, tap_row], preferred_element_type=jnp.float32)
    return total.reshape(col_count, row_count, kernel.shape[3])

def conv_back(padded, kernel, col_count, row_count):
    total = jnp.zeros((col_count * row_count, kernel.shape[2]), jnp.float32)
    for tap_col in range(3):
        for tap_row in range(3):
            piece = padded[2 - tap_col:2 - tap_col + col_count, 2 - tap_row:2 - tap_row + row_count].reshape(col_count * row_count, -1)
            total = total + jnp.dot(piece, kernel[tap_col, tap_row].T, preferred_element_type=jnp.float32)
    return total.reshape(col_count, row_count, kernel.shape[2])

def kernel_grad(padded, grads, col_count, row_count):
    flat = grads.reshape(col_count * row_count, -1)
    rows_out = []
    for tap_col in range(3):
        line = []
        for tap_row in range(3):
            piece = padded[tap_col:tap_col + col_count, tap_row:tap_row + row_count].reshape(col_count * row_count, -1)
            line.append(jnp.dot(piece.T, flat, preferred_element_type=jnp.float32))
        rows_out.append(jnp.stack(line))
    return jnp.stack(rows_out)

def pad_sky(field):
    return jnp.pad(field, ((1, 1), (1, 1), (0, 0)))

def reference(sky_cube, weight_first, weight_second, cotangent):
    cube_pad = pad_sky(sky_cube)
    pre = conv_taps(cube_pad, weight_first, NCOL, NROW)
    hidden = jax.nn.silu(pre).astype(jnp.bfloat16)
    hidden_pad = pad_sky(hidden)
    features = conv_taps(hidden_pad, weight_second, NCOL, NROW).astype(jnp.bfloat16)
    back = conv_back(pad_sky(cotangent), weight_second, NCOL, NROW)
    sigma = jax.nn.sigmoid(pre)
    delta = (back * sigma * (1.0 + pre * (1.0 - sigma))).astype(jnp.bfloat16)
    grad_first = kernel_grad(cube_pad, delta, NCOL, NROW)
    grad_second = kernel_grad(hidden_pad, cotangent, NCOL, NROW)
    return (features, grad_first, grad_second)
```

```python
import jax
import jax.numpy as jnp
from jax import lax
from jax.experimental import pallas as pl
from jax.experimental.pallas import tpu as pltpu
from jax.sharding import Mesh, PartitionSpec as P

FREQ = ("y", "c")
SKY = ("z", "x")
F32 = jnp.float32
BF16 = jnp.bfloat16
VMEM_LIMIT = 48 * 2**20


def shift(x, axis, step):
    count = lax.axis_size(axis)
    return lax.ppermute(x, axis, [(i, (i + step) % count) for i in range(count)])


def halo(x, axes, dim):
    count, length = lax.axis_size(axes), x.shape[dim]
    up = [(i, i + 1) for i in range(count - 1)]
    down = [(j, i) for i, j in up]
    last = lax.slice_in_dim(x, length - 1, length, axis=dim)
    first = lax.slice_in_dim(x, 0, 1, axis=dim)
    return lax.ppermute(last, axes, up), lax.ppermute(first, axes, down)


def with_halo(x):
    for axes, dim in ((FREQ, 0), (SKY, 1)):
        before, after = halo(x, axes, dim)
        x = jnp.concatenate([before, x, after], axis=dim)
    return x


def spread_kernel(cube_ref, before_ref, after_ref, out_ref):
    cols, rows, chans = cube_ref.shape
    zero = jnp.zeros((1, rows, 3 * chans), BF16)
    out_ref[0:1] = zero
    for tail in range(cols + 1, out_ref.shape[0]):
        out_ref[tail : tail + 1] = zero
    step = 8

    def block(i, _):
        at = pl.multiple_of(i * step, step)
        mid = cube_ref[pl.ds(at, step)]
        wide = mid.astype(F32).reshape(step * rows, chans)
        row = lax.broadcasted_iota(jnp.int32, (step, rows, chans), 1)
        ahead = pltpu.roll(wide, 1, 0).reshape(step, rows, chans)
        behind = pltpu.roll(wide, step * rows - 1, 0).reshape(step, rows, chans)
        before = before_ref[pl.ds(at, step), :].astype(F32)[:, None, :]
        after = after_ref[pl.ds(at, step), :].astype(F32)[:, None, :]
        ahead = jnp.where(row == 0, before, ahead)
        behind = jnp.where(row == rows - 1, after, behind)
        out_ref[pl.ds(at + 1, step), :, 0:chans] = ahead.astype(BF16)
        out_ref[pl.ds(at + 1, step), :, chans : 2 * chans] = mid
        out_ref[pl.ds(at + 1, step), :, 2 * chans : 3 * chans] = behind.astype(BF16)
        return 0

    lax.fori_loop(0, cols // step, block, 0)


def spread(cube, before, after):
    cols, rows, chans = cube.shape
    return pl.pallas_call(
        spread_kernel,
        out_shape=jax.ShapeDtypeStruct((cols + 8, rows, 3 * chans), BF16),
        in_specs=[pl.BlockSpec(memory_space=pltpu.VMEM)] * 3,
        out_specs=pl.BlockSpec(memory_space=pltpu.VMEM),
        compiler_params=pltpu.CompilerParams(vmem_limit_bytes=VMEM_LIMIT),
        name="spread",
    )(cube, before, after)


def conv_kernel(group_ref, wide_ref, kernel_ref, near_ref, far_ref):
    del group_ref
    strip, rows, outs = near_ref.shape
    step = 8
    core = lax.axis_index("c")

    def block(i, ref, base):
        at = base + i * step
        pieces = [wide_ref[pl.ds(at + tap, step)] for tap in range(3)]
        lhs = jnp.concatenate(pieces, axis=-1).reshape(step * rows, -1)
        total = jnp.dot(lhs, kernel_ref[...], preferred_element_type=F32)
        ref[pl.ds(i * step, step)] = total.reshape(step, rows, outs).astype(ref.dtype)
        return 0

    count = strip // step
    lax.fori_loop(0, count, lambda i, _: block(i, far_ref, (1 - core) * strip), 0)
    lax.fori_loop(0, count, lambda i, _: block(i, near_ref, core * strip), 0)


def conv_group(group, wide, kernel, strip):
    rows, depth, outs = wide.shape[1], wide.shape[2], kernel.shape[1]
    window = (pl.Element(2 * strip + 2), pl.Element(rows), pl.Element(depth))
    shape = (strip, rows, outs)
    return pl.pallas_call(
        conv_kernel,
        out_shape=(jax.ShapeDtypeStruct(shape, F32), jax.ShapeDtypeStruct(shape, BF16)),
        grid_spec=pltpu.PrefetchScalarGridSpec(
            num_scalar_prefetch=1,
            grid=(1,),
            in_specs=[
                pl.BlockSpec(window, lambda i, g: (g[0] * 2 * strip, 0, 0)),
                pl.BlockSpec(kernel.shape, lambda i, g: (0, 0)),
            ],
            out_specs=[pl.BlockSpec(shape, lambda i, g: (0, 0, 0))] * 2,
        ),
        compiler_params=pltpu.CompilerParams(vmem_limit_bytes=VMEM_LIMIT),
        cost_estimate=pl.CostEstimate(
            flops=4 * strip * rows * 3 * depth * outs, bytes_accessed=4 * 2**20, transcendentals=0
        ),
        name="conv_first",
    )(group.reshape(1), wide, kernel)


def grad_kernel(strips_ref, wide_a, wide_b, delta_a, delta_b, old_ref, new_ref, pad_ref):
    del strips_ref
    strip, rows, outs = delta_a.shape
    zero = jnp.zeros((2, rows, outs), BF16)
    total = old_ref[...]
    for wide_ref, delta_ref in ((wide_a, delta_a), (wide_b, delta_b)):
        cols = wide_ref.shape[0]
        pad_ref[0:2] = zero
        pad_ref[2 : 2 + strip] = delta_ref[...]
        pad_ref[2 + strip :] = jnp.zeros((pad_ref.shape[0] - 2 - strip, rows, outs), BF16)
        lhs = wide_ref[...].reshape(cols * rows, -1)
        rhs = jnp.concatenate(
            [pad_ref[2 - tap : 2 - tap + cols].reshape(cols * rows, outs) for tap in range(3)],
            axis=-1,
        )
        total = total + lax.dot_general(
            lhs, rhs, (((0,), (0,)), ((), ())), preferred_element_type=F32
        )
    new_ref[...] = total


def grad_strips(wide, deltas, strips, old):
    strip, rows, outs = deltas[0].shape
    depth = wide.shape[2]
    cols = strip + 8
    window = (pl.Element(cols), pl.Element(rows), pl.Element(depth))
    dspec = pl.BlockSpec((strip, rows, outs), lambda i, s: (0, 0, 0))
    tspec = pl.BlockSpec(old.shape, lambda i, s: (0, 0))
    return pl.pallas_call(
        grad_kernel,
        out_shape=jax.ShapeDtypeStruct(old.shape, F32),
        grid_spec=pltpu.PrefetchScalarGridSpec(
            num_scalar_prefetch=1,
            grid=(1,),
            in_specs=[
                pl.BlockSpec(window, lambda i, s: (s[0] * strip, 0, 0)),
                pl.BlockSpec(window, lambda i, s: (s[1] * strip, 0, 0)),
                dspec,
                dspec,
                tspec,
            ],
            out_specs=tspec,
            scratch_shapes=[pltpu.VMEM((cols + 2, rows, outs), BF16)],
        ),
        compiler_params=pltpu.CompilerParams(vmem_limit_bytes=VMEM_LIMIT),
        cost_estimate=pl.CostEstimate(
            flops=4 * cols * rows * depth * 3 * outs, bytes_accessed=6 * 2**20, transcendentals=0
        ),
        input_output_aliases={5: 0},
        name="grad_first",
    )(jnp.stack(strips), wide, wide, deltas[0], deltas[1], old)


def conv_taps(padded, kernel, col_count, row_count):
    total = jnp.zeros((col_count * row_count, kernel.shape[3]), F32)
    for tap_col in range(3):
        for tap_row in range(3):
            piece = padded[tap_col : tap_col + col_count, tap_row : tap_row + row_count].reshape(
                col_count * row_count, -1
            )
            total = total + jnp.dot(piece, kernel[tap_col, tap_row], preferred_element_type=F32)
    return total.reshape(col_count, row_count, kernel.shape[3])


def conv_back(padded, kernel, col_count, row_count):
    total = jnp.zeros((col_count * row_count, kernel.shape[2]), F32)
    for tap_col in range(3):
        for tap_row in range(3):
            piece = padded[
                2 - tap_col : 2 - tap_col + col_count, 2 - tap_row : 2 - tap_row + row_count
            ].reshape(col_count * row_count, -1)
            total = total + lax.dot_general(
                piece,
                kernel[tap_col, tap_row],
                (((1,), (1,)), ((), ())),
                preferred_element_type=F32,
            )
    return total.reshape(col_count, row_count, kernel.shape[2])


def kernel_grad(padded, grads, col_count, row_count):
    flat = grads.reshape(col_count * row_count, -1)
    lines = []
    for tap_col in range(3):
        for tap_row in range(3):
            piece = padded[tap_col : tap_col + col_count, tap_row : tap_row + row_count].reshape(
                col_count * row_count, -1
            )
            lines.append(
                lax.dot_general(piece, flat, (((0,), (0,)), ((), ())), preferred_element_type=F32)
            )
    return jnp.concatenate(lines, axis=0)


def reduce_pieces(parts, axis):
    count = lax.axis_size(axis)
    me = lax.axis_index(axis)

    def pick(at):
        return lax.dynamic_index_in_dim(parts, at, 0, keepdims=False)

    total = pick(me)
    for step in (1, count - 1, 2) if count == 4 else range(1, count):
        total = total + shift(pick((me + step) % count).astype(BF16), axis, step).astype(F32)
    return total


def gather_pieces(piece, axis):
    count = lax.axis_size(axis)
    me = lax.axis_index(axis)
    got = {0: piece}
    for step in (1, count - 1, 2) if count == 4 else range(1, count):
        got[step] = shift(piece, axis, step)
    turned = jnp.stack([got[(-j) % count] for j in range(count)] * 2)
    return lax.dynamic_slice_in_dim(turned, count - me, count, 0)


def body(sky_cube, weight_first, weight_second, cotangent):
    cols, rows, chans = sky_cube.shape
    strip, _, outs = cotangent.shape
    here, core = lax.axis_index("y"), lax.axis_index("c")
    chips = lax.axis_size("y")

    before, after = halo(sky_cube, SKY, 1)
    wide = spread(sky_cube, before.reshape(cols, chans), after.reshape(cols, chans))
    kernel = weight_first.reshape(9 * chans, outs)

    pre = None
    sent = []
    for step in (2, 1, chips - 1, 0):
        near, far = conv_group((here + step) % chips, wide, kernel, strip)
        both = near + shift(far, "c", 1).astype(F32)
        sent.append(shift(both.astype(BF16), "y", step).astype(F32) if step else both)
    pre = sent[3] + sent[0] + sent[1] + sent[2]

    back = conv_back(with_halo(cotangent), weight_second, strip, rows)
    sigma = jax.nn.sigmoid(pre)
    delta = (back * (sigma * (1.0 + pre * (1.0 - sigma)))).astype(BF16)
    hidden = (pre * sigma).astype(BF16)

    total = jnp.zeros((3 * chans, 3 * outs), F32)
    for step in (0, 1, chips - 1, 2):
        mine = shift(delta, "y", step) if step else delta
        other = shift(mine, "c", 1)
        chip = (here - step) % chips
        strips = [2 * chip + core, 2 * chip + 1 - core]
        total = grad_strips(wide, [mine, other], strips, total)

    hidden_pad = with_halo(hidden)
    features = conv_taps(hidden_pad, weight_second, strip, rows).astype(BF16)
    second = kernel_grad(hidden_pad, cotangent, strip, rows)
    depth = second.shape[0]
    second = reduce_pieces(second.reshape(2, depth // 2, outs), "c")
    second = reduce_pieces(second.reshape(chips, depth // (2 * chips), outs), "y")

    sx, sz = lax.axis_size("x"), lax.axis_size("z")
    width = 3 * outs
    first_parts = total.reshape(sx, -1, width)
    second_parts = second.reshape(sx, -1, width)
    split = first_parts.shape[1] // sz
    joined = jnp.concatenate(
        [first_parts.reshape(sx, sz, -1, width), second_parts.reshape(sx, sz, -1, width)], axis=2
    )
    summed = reduce_pieces(joined, "x")
    summed = reduce_pieces(summed, "z").astype(BF16)
    summed = gather_pieces(gather_pieces(summed, "z"), "x")
    first = summed[:, :, :split].reshape(3, chans, 3, outs)
    grad_first = jnp.transpose(first, (2, 0, 1, 3)).astype(F32)
    share = summed[:, :, split:].reshape(depth // (2 * chips), outs)
    share = gather_pieces(gather_pieces(share, "y"), "c")
    grad_second = share.reshape(3, 3, outs, outs).astype(F32)
    return features, grad_first, grad_second


def solution(mesh):
    sizes = (mesh.devices.shape[0] // 2, 2, 4, mesh.devices.shape[1] // 4)
    fine = Mesh(mesh.devices.reshape(sizes), FREQ + SKY)
    return jax.shard_map(
        body,
        mesh=fine,
        in_specs=(P(None, SKY, FREQ), P(None, None, FREQ, None), P(), P(FREQ, SKY, None)),
        out_specs=(P(FREQ, SKY, None), P(None, None, FREQ, None), P()),
        check_vma=False,
    )
```

```python
import functools

import jax
import jax.numpy as jnp
from jax import lax
from jax.experimental import pallas as pl
from jax.experimental.pallas import tpu as pltpu
from jax.sharding import Mesh, PartitionSpec as P

FREQ = ("y", "c")
SKY = ("z", "x")
F32 = jnp.float32
BF16 = jnp.bfloat16


def shift(x, axis, step):
    count = lax.axis_size(axis)
    return lax.ppermute(x, axis, [(i, (i + step) % count) for i in range(count)])


def halo(x, axes, dim):
    count, length = lax.axis_size(axes), x.shape[dim]
    up = [(i, i + 1) for i in range(count - 1)]
    down = [(j, i) for i, j in up]
    last = lax.slice_in_dim(x, length - 1, length, axis=dim)
    first = lax.slice_in_dim(x, 0, 1, axis=dim)
    return lax.ppermute(last, axes, up), lax.ppermute(first, axes, down)


def with_halo(x):
    for axes, dim in ((FREQ, 0), (SKY, 1)):
        before, after = halo(x, axes, dim)
        x = jnp.concatenate([before, x, after], axis=dim)
    return x


def spread_kernel(own_ref, far_ref, own_halo_ref, far_halo_ref, out_ref):
    chips, width, rows, depth = out_ref.shape
    cols, _, chans = own_ref.shape
    strip = cols // (2 * chips)
    core = lax.axis_index("c")
    step = 8
    row = lax.broadcasted_iota(jnp.int32, (step, rows, chans), 1)

    def block(i, base, chip):
        for side, (cube_ref, halo_ref) in enumerate(
            ((own_ref, own_halo_ref), (far_ref, far_halo_ref))
        ):
            at = pl.multiple_of(base + i * step, step)
            mid = cube_ref[pl.ds(at, step)]
            wide = mid.astype(F32).reshape(step * rows, chans)
            ahead = pltpu.roll(wide, 1, 0).reshape(step, rows, chans)
            behind = pltpu.roll(wide, step * rows - 1, 0).reshape(step, rows, chans)
            before = halo_ref[0, pl.ds(at, step), :].astype(F32)[:, None, :]
            after = halo_ref[1, pl.ds(at, step), :].astype(F32)[:, None, :]
            ahead = jnp.where(row == 0, before, ahead)
            behind = jnp.where(row == rows - 1, after, behind)
            to = pl.ds(1 + i * step, step)
            for tap, value in enumerate((ahead.astype(BF16), mid, behind.astype(BF16))):
                lane = (2 * tap + side) * chans
                out_ref[chip, to, :, lane : lane + chans] = value

    def edge(at, chip, slot):
        for side, (cube_ref, halo_ref) in enumerate(
            ((own_ref, own_halo_ref), (far_ref, far_halo_ref))
        ):
            first = pl.multiple_of((at // step) * step, step)
            mid = cube_ref[at]
            wide = mid.astype(F32)
            line = lax.broadcasted_iota(jnp.int32, (step, chans), 0) == at - first
            pick = lambda k: jnp.sum(
                jnp.where(line, halo_ref[k, pl.ds(first, step), :].astype(F32), 0.0),
                axis=0,
                keepdims=True,
            )
            place = lax.broadcasted_iota(jnp.int32, (rows, chans), 0)
            ahead = jnp.where(place == 0, pick(0), pltpu.roll(wide, 1, 0))
            behind = jnp.where(place == rows - 1, pick(1), pltpu.roll(wide, rows - 1, 0))
            for tap, value in enumerate((ahead.astype(BF16), mid, behind.astype(BF16))):
                lane = (2 * tap + side) * chans
                out_ref[chip, slot, :, lane : lane + chans] = value

    blank = jnp.zeros((rows, depth), BF16)
    for chip in range(chips):
        base = (2 * chip + core) * strip
        lax.fori_loop(0, strip // step, lambda i, _: block(i, base, chip), None)
        edge(jnp.maximum(base - 1, 0), chip, 0)
        edge(jnp.minimum(base + strip, cols - 1), chip, strip + 1)
        for slot in range(strip + 2, width):
            out_ref[chip, slot] = blank

    @pl.when(core == 0)
    def _():
        out_ref[0, 0] = blank

    @pl.when(core == 1)
    def _():
        out_ref[chips - 1, strip + 1] = blank


VMEM_SPEC = pl.BlockSpec(memory_space=pltpu.VMEM)
SMEM_SPEC = pl.BlockSpec(memory_space=pltpu.SMEM)


def spread(own, far, own_halo, far_halo, chips):
    cols, rows, chans = own.shape
    return pl.pallas_call(
        spread_kernel,
        out_shape=jax.ShapeDtypeStruct((chips, cols // (2 * chips) + 8, rows, 6 * chans), BF16),
        in_specs=[VMEM_SPEC] * 4,
        out_specs=VMEM_SPEC,
        compiler_params=pltpu.CompilerParams(vmem_limit_bytes=16 * 2**20),
        cost_estimate=pl.CostEstimate(flops=2**20, bytes_accessed=12 * 2**20, transcendentals=0),
        name="spread",
    )(own, far, own_halo, far_halo)


def conv_kernel(chip_ref, wide_ref, kernel_ref, out_ref):
    strip, rows, outs = out_ref.shape
    chip = chip_ref[0]
    pieces = [wide_ref[chip, tap : tap + strip] for tap in range(3)]
    lhs = jnp.concatenate(pieces, axis=-1).reshape(strip * rows, -1)
    total = jnp.dot(lhs, kernel_ref[...], preferred_element_type=F32)
    out_ref[...] = total.reshape(strip, rows, outs).astype(out_ref.dtype)


def conv_strip(chip, wide, kernel, strip, dtype):
    rows, depth, outs = wide.shape[2], kernel.shape[0], kernel.shape[1]
    return pl.pallas_call(
        conv_kernel,
        out_shape=jax.ShapeDtypeStruct((strip, rows, outs), dtype),
        in_specs=[SMEM_SPEC, VMEM_SPEC, VMEM_SPEC],
        out_specs=VMEM_SPEC,
        compiler_params=pltpu.CompilerParams(vmem_limit_bytes=16 * 2**20),
        cost_estimate=pl.CostEstimate(
            flops=2 * strip * rows * depth * outs, bytes_accessed=4 * 2**20, transcendentals=0
        ),
        name="conv_first",
    )(chip.reshape(1), wide, kernel)


def grad_kernel(has_old, last, chip_ref, wide_ref, delta_ref, *refs):
    old_ref = refs[0] if has_old else None
    outs_refs, pad_ref = refs[1 if has_old else 0 : -1], refs[-1]
    strip, rows, outs = delta_ref.shape
    cols, depth = wide_ref.shape[1], wide_ref.shape[3]
    pad_ref[0:2] = jnp.zeros((2, rows, outs), BF16)
    pad_ref[2 : 2 + strip] = delta_ref[...]
    pad_ref[2 + strip :] = jnp.zeros((cols - strip, rows, outs), BF16)
    lhs = wide_ref[chip_ref[0]].reshape(cols * rows, depth)
    rhs = jnp.concatenate(
        [pad_ref[2 - tap : 2 - tap + cols].reshape(cols * rows, outs) for tap in range(3)], axis=-1
    )
    total = lax.dot_general(lhs, rhs, (((0,), (0,)), ((), ())), preferred_element_type=F32)
    if has_old:
        total = total + old_ref[...]
    if not last:
        outs_refs[0][...] = total
    else:
        chans = depth // 6
        for tap in range(3):
            at = 2 * tap * chans
            outs_refs[0][tap * chans : (tap + 1) * chans] = total[at : at + chans]
            outs_refs[1][tap * chans : (tap + 1) * chans] = total[
                at + chans : at + 2 * chans
            ].astype(BF16)


def grad_strip(chip, wide, delta, old, last):
    strip, rows, outs = delta.shape
    depth, cols = wide.shape[3], wide.shape[1]
    shape = (depth, 3 * outs)
    half = (depth // 2, 3 * outs)
    if last:
        out_shape = (jax.ShapeDtypeStruct(half, F32), jax.ShapeDtypeStruct(half, BF16))
    else:
        out_shape = (jax.ShapeDtypeStruct(shape, F32),)
    args = [chip.reshape(1), wide, delta] + ([old] if old is not None else [])
    out = pl.pallas_call(
        functools.partial(grad_kernel, old is not None, last),
        out_shape=out_shape,
        in_specs=[SMEM_SPEC] + [VMEM_SPEC] * (len(args) - 1),
        out_specs=tuple([VMEM_SPEC] * len(out_shape)),
        scratch_shapes=[pltpu.VMEM((cols + 2, rows, outs), BF16)],
        compiler_params=pltpu.CompilerParams(vmem_limit_bytes=20 * 2**20),
        cost_estimate=pl.CostEstimate(
            flops=2 * cols * rows * depth * 3 * outs, bytes_accessed=6 * 2**20, transcendentals=0
        ),
        name="grad_first",
    )(*args)
    return out if last else out[0]


def conv_taps(padded, kernel, col_count, row_count):
    total = jnp.zeros((col_count * row_count, kernel.shape[3]), F32)
    for tap_col in range(3):
        for tap_row in range(3):
            piece = padded[tap_col : tap_col + col_count, tap_row : tap_row + row_count].reshape(
                col_count * row_count, -1
            )
            total = total + jnp.dot(piece, kernel[tap_col, tap_row], preferred_element_type=F32)
    return total.reshape(col_count, row_count, kernel.shape[3])


def conv_back(padded, kernel, col_count, row_count):
    total = jnp.zeros((col_count * row_count, kernel.shape[2]), F32)
    for tap_col in range(3):
        for tap_row in range(3):
            piece = padded[
                2 - tap_col : 2 - tap_col + col_count, 2 - tap_row : 2 - tap_row + row_count
            ].reshape(col_count * row_count, -1)
            total = total + lax.dot_general(
                piece,
                kernel[tap_col, tap_row],
                (((1,), (1,)), ((), ())),
                preferred_element_type=F32,
            )
    return total.reshape(col_count, row_count, kernel.shape[2])


def kernel_grad(padded, grads, col_count, row_count):
    flat = grads.reshape(col_count * row_count, -1)
    lines = []
    for tap_col in range(3):
        for tap_row in range(3):
            piece = padded[tap_col : tap_col + col_count, tap_row : tap_row + row_count].reshape(
                col_count * row_count, -1
            )
            lines.append(
                lax.dot_general(piece, flat, (((0,), (0,)), ((), ())), preferred_element_type=F32)
            )
    return jnp.concatenate(lines, axis=0)


def reduce_pieces(parts, axis):
    count = lax.axis_size(axis)
    me = lax.axis_index(axis)

    def pick(at):
        return lax.dynamic_index_in_dim(parts, at, 0, keepdims=False)

    total = pick(me)
    for step in (1, count - 1, 2) if count == 4 else range(1, count):
        total = total + shift(pick((me + step) % count).astype(BF16), axis, step).astype(F32)
    return total


def gather_pieces(piece, axis):
    count = lax.axis_size(axis)
    me = lax.axis_index(axis)
    got = {0: piece}
    for step in (1, count - 1, 2) if count == 4 else range(1, count):
        got[step] = shift(piece, axis, step)
    turned = jnp.stack([got[(-j) % count] for j in range(count)] * 2)
    return lax.dynamic_slice_in_dim(turned, count - me, count, 0)


def body(sky_cube, weight_first, weight_second, cotangent):
    cols, rows, chans = sky_cube.shape
    strip, _, outs = cotangent.shape
    here, core = lax.axis_index("y"), lax.axis_index("c")
    chips = lax.axis_size("y")

    edges = jnp.concatenate(halo(sky_cube, SKY, 1), axis=1)
    far_cube = shift(sky_cube, "c", 1)
    far_weight = shift(weight_first, "c", 1)
    edges = jnp.transpose(edges, (1, 0, 2))
    far_edges = shift(edges, "c", 1)
    wide = spread(sky_cube, far_cube, edges, far_edges, chips)
    kernel = jnp.concatenate([weight_first, far_weight], axis=2).reshape(18 * chans, outs)

    order = (2, 1, chips - 1)
    near = []
    hold = wide
    for step in order:
        part = conv_strip((here + step) % chips, hold, kernel, strip, BF16)
        near.append(part)
        hold, _ = lax.optimization_barrier((wide, part))
    own = conv_strip(here, hold, kernel, strip, F32)
    pre = own
    for step, part in zip(order, near):
        pre = pre + shift(part, "y", step).astype(F32)

    late_cotangent, _ = lax.optimization_barrier((cotangent, own))
    back = conv_back(with_halo(late_cotangent), weight_second, strip, rows)
    sigma = jax.nn.sigmoid(pre)
    delta = (back * (sigma * (1.0 + pre * (1.0 - sigma)))).astype(BF16)
    hidden = (pre * sigma).astype(BF16)

    total = grad_strip(here, wide, delta, None, False)
    for step in (1, chips - 1, 2):
        piece = shift(delta, "y", step)
        total = grad_strip((here - step) % chips, wide, piece, total, step == 2)
    first_own, first_far = total
    first = first_own + shift(first_far, "c", 1).astype(F32)

    hidden_pad = with_halo(hidden)
    features = conv_taps(hidden_pad, weight_second, strip, rows).astype(BF16)
    second = kernel_grad(hidden_pad, cotangent, strip, rows)
    depth = second.shape[0]
    second = reduce_pieces(second.reshape(2, depth // 2, outs), "c")
    second = reduce_pieces(second.reshape(chips, depth // (2 * chips), outs), "y")

    sx, sz = lax.axis_size("x"), lax.axis_size("z")
    width = 3 * outs
    first_parts = first.reshape(sx, -1, width)
    second_parts = second.reshape(sx, -1, width)
    split = first_parts.shape[1] // sz
    joined = jnp.concatenate(
        [first_parts.reshape(sx, sz, -1, width), second_parts.reshape(sx, sz, -1, width)], axis=2
    )
    summed = reduce_pieces(joined, "x")
    summed = reduce_pieces(summed, "z").astype(BF16)
    summed = gather_pieces(gather_pieces(summed, "z"), "x")
    first = summed[:, :, :split].reshape(3, chans, 3, outs)
    grad_first = jnp.transpose(first, (2, 0, 1, 3)).astype(F32)
    share = summed[:, :, split:].reshape(depth // (2 * chips), outs)
    share = gather_pieces(gather_pieces(share, "y"), "c")
    grad_second = share.reshape(3, 3, outs, outs).astype(F32)
    return features, grad_first, grad_second


def solution(mesh):
    sizes = (mesh.devices.shape[0] // 2, 2, 4, mesh.devices.shape[1] // 4)
    fine = Mesh(mesh.devices.reshape(sizes), FREQ + SKY)
    return jax.shard_map(
        body,
        mesh=fine,
        in_specs=(P(None, SKY, FREQ), P(None, None, FREQ, None), P(), P(FREQ, SKY, None)),
        out_specs=(P(FREQ, SKY, None), P(None, None, FREQ, None), P()),
        check_vma=False,
    )
```

```python
import functools

import jax
import jax.numpy as jnp
from jax import lax
from jax.experimental import pallas as pl
from jax.experimental.pallas import tpu as pltpu
from jax.sharding import Mesh, PartitionSpec as P

FREQ = ("y", "c")
SKY = ("z", "x")
F32 = jnp.float32
BF16 = jnp.bfloat16
QUICK = pl.CostEstimate(flops=1, bytes_accessed=1, transcendentals=0)


def shift(x, axis, step):
    count = lax.axis_size(axis)
    return lax.ppermute(x, axis, [(i, (i + step) % count) for i in range(count)])


def halo(x, axes, dim):
    count, length = lax.axis_size(axes), x.shape[dim]
    up = [(i, i + 1) for i in range(count - 1)]
    down = [(j, i) for i, j in up]
    last = lax.slice_in_dim(x, length - 1, length, axis=dim)
    first = lax.slice_in_dim(x, 0, 1, axis=dim)
    return lax.ppermute(last, axes, up), lax.ppermute(first, axes, down)


def spread_kernel(own_ref, far_ref, own_halo_ref, far_halo_ref, out_ref):
    chips, width, rows, depth = out_ref.shape
    cols, _, chans = own_ref.shape
    strip = cols // (2 * chips)
    core = lax.axis_index("c")
    step = 8
    row = lax.broadcasted_iota(jnp.int32, (step, rows, chans), 1)

    def block(i, base, chip):
        for side, (cube_ref, halo_ref) in enumerate(
            ((own_ref, own_halo_ref), (far_ref, far_halo_ref))
        ):
            at = pl.multiple_of(base + i * step, step)
            mid = cube_ref[pl.ds(at, step)]
            wide = mid.astype(F32).reshape(step * rows, chans)
            ahead = pltpu.roll(wide, 1, 0).reshape(step, rows, chans)
            behind = pltpu.roll(wide, step * rows - 1, 0).reshape(step, rows, chans)
            before = halo_ref[0, pl.ds(at, step), :].astype(F32)[:, None, :]
            after = halo_ref[1, pl.ds(at, step), :].astype(F32)[:, None, :]
            ahead = jnp.where(row == 0, before, ahead)
            behind = jnp.where(row == rows - 1, after, behind)
            to = pl.ds(1 + i * step, step)
            for tap, value in enumerate((ahead.astype(BF16), mid, behind.astype(BF16))):
                lane = (2 * tap + side) * chans
                out_ref[chip, to, :, lane : lane + chans] = value

    def edge(at, chip, slot):
        for side, (cube_ref, halo_ref) in enumerate(
            ((own_ref, own_halo_ref), (far_ref, far_halo_ref))
        ):
            first = pl.multiple_of((at // step) * step, step)
            mid = cube_ref[at]
            wide = mid.astype(F32)
            line = lax.broadcasted_iota(jnp.int32, (step, chans), 0) == at - first
            pick = lambda k: jnp.sum(
                jnp.where(line, halo_ref[k, pl.ds(first, step), :].astype(F32), 0.0),
                axis=0,
                keepdims=True,
            )
            place = lax.broadcasted_iota(jnp.int32, (rows, chans), 0)
            ahead = jnp.where(place == 0, pick(0), pltpu.roll(wide, 1, 0))
            behind = jnp.where(place == rows - 1, pick(1), pltpu.roll(wide, rows - 1, 0))
            for tap, value in enumerate((ahead.astype(BF16), mid, behind.astype(BF16))):
                lane = (2 * tap + side) * chans
                out_ref[chip, slot, :, lane : lane + chans] = value

    blank = jnp.zeros((rows, depth), BF16)
    for chip in range(chips):
        base = (2 * chip + core) * strip
        lax.fori_loop(0, strip // step, lambda i, _: block(i, base, chip), None)
        edge(jnp.maximum(base - 1, 0), chip, 0)
        edge(jnp.minimum(base + strip, cols - 1), chip, strip + 1)
        for slot in range(strip + 2, width):
            out_ref[chip, slot] = blank

    @pl.when(core == 0)
    def _():
        out_ref[0, 0] = blank

    @pl.when(core == 1)
    def _():
        out_ref[chips - 1, strip + 1] = blank


VMEM_SPEC = pl.BlockSpec(memory_space=pltpu.VMEM)
SMEM_SPEC = pl.BlockSpec(memory_space=pltpu.SMEM)


def spread(own, far, own_halo, far_halo, chips):
    cols, rows, chans = own.shape
    return pl.pallas_call(
        spread_kernel,
        out_shape=jax.ShapeDtypeStruct((chips, cols // (2 * chips) + 8, rows, 6 * chans), BF16),
        in_specs=[VMEM_SPEC] * 4,
        out_specs=VMEM_SPEC,
        compiler_params=pltpu.CompilerParams(vmem_limit_bytes=16 * 2**20),
        cost_estimate=QUICK,
        name="spread",
    )(own, far, own_halo, far_halo)


def conv_kernel(chip_ref, wide_ref, kernel_ref, out_ref):
    strip, rows, outs = out_ref.shape
    chip = chip_ref[0]
    pieces = [wide_ref[chip, tap : tap + strip] for tap in range(3)]
    lhs = jnp.concatenate(pieces, axis=-1).reshape(strip * rows, -1)
    total = jnp.dot(lhs, kernel_ref[...], preferred_element_type=F32)
    out_ref[...] = total.reshape(strip, rows, outs).astype(out_ref.dtype)


def conv_strip(chip, wide, kernel, strip, dtype):
    rows, depth, outs = wide.shape[2], kernel.shape[0], kernel.shape[1]
    return pl.pallas_call(
        conv_kernel,
        out_shape=jax.ShapeDtypeStruct((strip, rows, outs), dtype),
        in_specs=[SMEM_SPEC, VMEM_SPEC, VMEM_SPEC],
        out_specs=VMEM_SPEC,
        compiler_params=pltpu.CompilerParams(vmem_limit_bytes=16 * 2**20),
        cost_estimate=QUICK,
        name="conv_first",
    )(chip.reshape(1), wide, kernel)


def grad_kernel(has_old, last, chip_ref, wide_ref, delta_ref, *refs):
    old_ref = refs[0] if has_old else None
    outs_refs, pad_ref = refs[1 if has_old else 0 : -1], refs[-1]
    strip, rows, outs = delta_ref.shape
    cols, depth = wide_ref.shape[1], wide_ref.shape[3]
    pad_ref[0:2] = jnp.zeros((2, rows, outs), BF16)
    pad_ref[2 : 2 + strip] = delta_ref[...]
    pad_ref[2 + strip :] = jnp.zeros((cols - strip, rows, outs), BF16)
    lhs = wide_ref[chip_ref[0]].reshape(cols * rows, depth)
    rhs = jnp.concatenate(
        [pad_ref[2 - tap : 2 - tap + cols].reshape(cols * rows, outs) for tap in range(3)], axis=-1
    )
    total = lax.dot_general(lhs, rhs, (((0,), (0,)), ((), ())), preferred_element_type=F32)
    if has_old:
        total = total + old_ref[...]
    if not last:
        outs_refs[0][...] = total
    else:
        chans = depth // 6
        for tap in range(3):
            at = 2 * tap * chans
            outs_refs[0][tap * chans : (tap + 1) * chans] = total[at : at + chans]
            outs_refs[1][tap * chans : (tap + 1) * chans] = total[
                at + chans : at + 2 * chans
            ].astype(BF16)


def grad_strip(chip, wide, delta, old, last):
    strip, rows, outs = delta.shape
    depth, cols = wide.shape[3], wide.shape[1]
    shape = (depth, 3 * outs)
    half = (depth // 2, 3 * outs)
    if last:
        out_shape = (jax.ShapeDtypeStruct(half, F32), jax.ShapeDtypeStruct(half, BF16))
    else:
        out_shape = (jax.ShapeDtypeStruct(shape, F32),)
    args = [chip.reshape(1), wide, delta] + ([old] if old is not None else [])
    out = pl.pallas_call(
        functools.partial(grad_kernel, old is not None, last),
        out_shape=out_shape,
        in_specs=[SMEM_SPEC] + [VMEM_SPEC] * (len(args) - 1),
        out_specs=tuple([VMEM_SPEC] * len(out_shape)),
        scratch_shapes=[pltpu.VMEM((cols + 2, rows, outs), BF16)],
        compiler_params=pltpu.CompilerParams(vmem_limit_bytes=20 * 2**20),
        cost_estimate=QUICK,
        name="grad_first",
    )(*args)
    return out if last else out[0]


def spread_tile(ref, left_ref, right_ref, edge_ref, wide_ref):
    cols, rows, chans = ref.shape
    place = lax.broadcasted_iota(jnp.int32, (rows, chans), 0)

    def put(mid, j):
        wide = mid.astype(F32)
        before = edge_ref[0, j : j + 1, :].astype(F32)
        after = edge_ref[1, j : j + 1, :].astype(F32)
        ahead = jnp.where(place == 0, before, pltpu.roll(wide, 1, 0))
        behind = jnp.where(place == rows - 1, after, pltpu.roll(wide, rows - 1, 0))
        wide_ref[j, :, 0:chans] = ahead.astype(BF16)
        wide_ref[j, :, chans : 2 * chans] = mid
        wide_ref[j, :, 2 * chans :] = behind.astype(BF16)

    put(left_ref[0], 0)
    for j in range(cols):
        put(ref[j], j + 1)
    put(right_ref[0], cols + 1)


def back_kernel(cot_ref, left_ref, right_ref, edge_ref, kernel_ref, out_ref, wide_ref):
    cols, rows, chans = cot_ref.shape
    spread_tile(cot_ref, left_ref, right_ref, edge_ref, wide_ref)
    total = None
    for tap_col in range(3):
        lhs = wide_ref[tap_col : tap_col + cols].reshape(cols * rows, 3 * chans)
        for tap_row in range(3):
            part = lax.dot_general(
                lhs[:, tap_row * chans : (tap_row + 1) * chans],
                kernel_ref[2 - tap_col, 2 - tap_row],
                (((1,), (1,)), ((), ())),
                preferred_element_type=F32,
            )
            total = part if total is None else total + part
    out_ref[...] = total.reshape(cols, rows, -1)


def back_tile(tile, left, right, edges, kernel):
    cols, rows, chans = tile.shape
    return pl.pallas_call(
        back_kernel,
        out_shape=jax.ShapeDtypeStruct((cols, rows, kernel.shape[2]), F32),
        in_specs=[VMEM_SPEC] * 5,
        out_specs=VMEM_SPEC,
        scratch_shapes=[pltpu.VMEM((cols + 2, rows, 3 * chans), BF16)],
        compiler_params=pltpu.CompilerParams(vmem_limit_bytes=20 * 2**20),
        cost_estimate=QUICK,
        name="back",
    )(tile, left, right, edges, kernel)


def second_kernel(
    chips, hid_ref, left_ref, right_ref, edge_ref, kernel_ref, cot_ref,
    out_ref, near_ref, far_ref, wide_ref, pad_ref, sum_ref,
):
    cols, rows, chans = hid_ref.shape
    outs = cot_ref.shape[2]
    width = wide_ref.shape[0]
    core = lax.axis_index("c")
    spread_tile(hid_ref, left_ref, right_ref, edge_ref, wide_ref)
    wide_ref[cols + 2 :] = jnp.zeros((width - cols - 2, rows, 3 * chans), BF16)
    pieces = [wide_ref[tap : tap + cols] for tap in range(3)]
    lhs = jnp.concatenate(pieces, axis=-1).reshape(cols * rows, 9 * chans)
    total = jnp.dot(lhs, kernel_ref[...], preferred_element_type=F32)
    out_ref[...] = total.reshape(cols, rows, outs).astype(BF16)

    pad_ref[0:2] = jnp.zeros((2, rows, outs), BF16)
    pad_ref[2 : 2 + cols] = cot_ref[...]
    pad_ref[2 + cols :] = jnp.zeros((width - cols, rows, outs), BF16)
    rhs = jnp.concatenate(
        [pad_ref[2 - tap : 2 - tap + width].reshape(width * rows, outs) for tap in range(3)],
        axis=-1,
    )
    sum_ref[...] = lax.dot_general(
        wide_ref[...].reshape(width * rows, 3 * chans),
        rhs,
        (((0,), (0,)), ((), ())),
        preferred_element_type=F32,
    )
    size = sum_ref.shape[0] // (2 * chips)
    for half, ref in ((core, near_ref), (1 - core, far_ref)):
        for chip in range(chips):
            at = pl.multiple_of((half * chips + chip) * size, size)
            for tap in range(3):
                ref[chip, tap * size : (tap + 1) * size, :] = sum_ref[
                    pl.ds(at, size), tap * outs : (tap + 1) * outs
                ].astype(ref.dtype)


def second_tile(tile, left, right, edges, kernel, cotangent, chips):
    cols, rows, chans = tile.shape
    outs = cotangent.shape[2]
    width = cols + 8
    cut = (chips, 9 * chans // (2 * chips), outs)
    return pl.pallas_call(
        functools.partial(second_kernel, chips),
        out_shape=(
            jax.ShapeDtypeStruct((cols, rows, outs), BF16),
            jax.ShapeDtypeStruct(cut, F32),
            jax.ShapeDtypeStruct(cut, BF16),
        ),
        in_specs=[VMEM_SPEC] * 6,
        out_specs=(VMEM_SPEC,) * 3,
        scratch_shapes=[
            pltpu.VMEM((width, rows, 3 * chans), BF16),
            pltpu.VMEM((width + 2, rows, outs), BF16),
            pltpu.VMEM((3 * chans, 3 * outs), F32),
        ],
        compiler_params=pltpu.CompilerParams(vmem_limit_bytes=28 * 2**20),
        cost_estimate=QUICK,
        name="second",
    )(tile, left, right, edges, kernel.reshape(9 * chans, outs), cotangent)


def fold_kernel(near_ref, got_ref, keep_ref, *send_refs):
    chips = near_ref.shape[0]
    here = lax.axis_index("y")
    keep_ref[...] = near_ref[here] + got_ref[here].astype(F32)
    for step, ref in zip(STEPS[1:], send_refs):
        to = lax.rem(here + step, chips)
        ref[...] = (near_ref[to] + got_ref[to].astype(F32)).astype(BF16)


def fold(near, got):
    shape = near.shape[1:]
    return pl.pallas_call(
        fold_kernel,
        out_shape=(jax.ShapeDtypeStruct(shape, F32),) + (jax.ShapeDtypeStruct(shape, BF16),) * 3,
        in_specs=[VMEM_SPEC] * 2,
        out_specs=(VMEM_SPEC,) * 4,
        compiler_params=pltpu.CompilerParams(vmem_limit_bytes=12 * 2**20),
        cost_estimate=QUICK,
        name="fold",
    )(near, got)


def tile_halo(x):
    left, right = halo(x, FREQ, 0)
    last = x.shape[1] - 1
    ends = [
        jnp.concatenate([left[:, r], x[:, r], right[:, r]], axis=0) for r in (last, 0)
    ]
    count = lax.axis_size(SKY)
    up = [(i, i + 1) for i in range(count - 1)]
    down = [(j, i) for i, j in up]
    edges = jnp.stack([lax.ppermute(ends[0], SKY, up), lax.ppermute(ends[1], SKY, down)])
    return left, right, edges


def join_kernel(own_ref, far_ref, second_ref, out_ref):
    pieces, extra, outs = second_ref.shape
    chans = own_ref.shape[0] // 3
    size = chans // pieces
    for tap_col in range(3):
        for tap_row in range(3):
            rows = slice(tap_row * chans, (tap_row + 1) * chans)
            lanes = slice(tap_col * outs, (tap_col + 1) * outs)
            value = own_ref[rows, lanes] + far_ref[rows, lanes].astype(F32)
            at = (3 * tap_col + tap_row) * size
            out_ref[:, at : at + size, :] = value.reshape(pieces, size, outs).astype(BF16)
    out_ref[:, 9 * size :, :] = second_ref[...]


def join(own, far, second):
    pieces, extra, outs = second.shape
    rows = 9 * (own.shape[0] // 3 // pieces) + extra
    return pl.pallas_call(
        join_kernel,
        out_shape=jax.ShapeDtypeStruct((pieces, rows, outs), BF16),
        in_specs=[VMEM_SPEC] * 3,
        out_specs=VMEM_SPEC,
        compiler_params=pltpu.CompilerParams(vmem_limit_bytes=16 * 2**20),
        cost_estimate=QUICK,
        name="join",
    )(own, far, second)


STEPS = (0, 1, 3, 2)


def first_kernel(sz, a_ref, b_ref, c_ref, d_ref, out_ref):
    sx = lax.axis_size("x")
    size = out_ref.shape[2] // (sx * sz)
    me = lax.axis_index("x")
    for step, ref in zip(STEPS, (a_ref, b_ref, c_ref, d_ref)):
        x = lax.rem(me + sx - step, sx)
        value = ref[...].astype(F32)
        for z in range(sz):
            at = pl.multiple_of((z * sx + x) * size, size)
            for tap in range(9):
                rows = (z * 9 + tap) * size
                out_ref[tap // 3, tap % 3, pl.ds(at, size), :] = value[rows : rows + size]


def lay_first(parts, sz, chans):
    outs = parts[0].shape[1]
    return pl.pallas_call(
        functools.partial(first_kernel, sz),
        out_shape=jax.ShapeDtypeStruct((3, 3, chans, outs), F32),
        in_specs=[VMEM_SPEC] * 4,
        out_specs=VMEM_SPEC,
        compiler_params=pltpu.CompilerParams(vmem_limit_bytes=16 * 2**20),
        cost_estimate=QUICK,
        name="lay_first",
    )(*parts)


def lay_second_kernel(near_ref, far_ref, out_ref):
    sy, sx, rows, _ = near_ref.shape
    size = rows // 3
    third = out_ref.shape[0] // 3
    core, y, x = lax.axis_index("c"), lax.axis_index("y"), lax.axis_index("x")
    for half, ref in ((core, near_ref), (1 - core, far_ref)):
        for i in range(sy):
            for j in range(sx):
                place = (half * sy + lax.rem(y + sy - STEPS[i], sy)) * sx
                place = place + lax.rem(x + sx - STEPS[j], sx)
                value = ref[i, j].astype(F32)
                for tap in range(3):
                    at = pl.multiple_of(tap * third + place * size, 8)
                    out_ref[pl.ds(at, size), :] = value[tap * size : (tap + 1) * size]


def lay_second(near, far):
    sy, sx, rows, outs = near.shape
    return pl.pallas_call(
        lay_second_kernel,
        out_shape=jax.ShapeDtypeStruct((2 * sy * sx * rows, outs), F32),
        in_specs=[VMEM_SPEC] * 2,
        out_specs=VMEM_SPEC,
        compiler_params=pltpu.CompilerParams(vmem_limit_bytes=16 * 2**20),
        cost_estimate=QUICK,
        name="lay_second",
    )(near, far)


def gather_steps(piece, axis):
    return [piece] + [shift(piece, axis, step) for step in STEPS[1:]]


def body(sky_cube, weight_first, weight_second, cotangent):
    cols, rows, chans = sky_cube.shape
    strip, _, outs = cotangent.shape
    here, core = lax.axis_index("y"), lax.axis_index("c")
    chips = lax.axis_size("y")

    edges = jnp.concatenate(halo(sky_cube, SKY, 1), axis=1)
    far_cube = shift(sky_cube, "c", 1)
    far_weight = shift(weight_first, "c", 1)
    edges = jnp.transpose(edges, (1, 0, 2))
    far_edges = shift(edges, "c", 1)
    wide = spread(sky_cube, far_cube, edges, far_edges, chips)
    kernel = jnp.concatenate([weight_first, far_weight], axis=2).reshape(18 * chans, outs)

    order = (2, 1, chips - 1)
    near = []
    hold = wide
    for step in order:
        part = conv_strip((here + step) % chips, hold, kernel, strip, BF16)
        near.append(part)
        hold, _ = lax.optimization_barrier((wide, part))
    own = conv_strip(here, wide, kernel, strip, F32)
    pre = own
    for step, part in zip(order, near):
        pre = pre + shift(part, "y", step).astype(F32)

    late_cotangent, _ = lax.optimization_barrier((cotangent, near[-1]))
    back = back_tile(late_cotangent, *tile_halo(late_cotangent), weight_second)
    sigma = jax.nn.sigmoid(pre)
    delta = (back * (sigma * (1.0 + pre * (1.0 - sigma)))).astype(BF16)
    hidden = (pre * sigma).astype(BF16)

    pieces = [(step, shift(delta, "y", step)) for step in (1, chips - 1, 2)]
    total = grad_strip(here, wide, delta, None, False)
    late_hidden, _ = lax.optimization_barrier((hidden, total))

    edges = tile_halo(late_hidden)
    for step, piece in pieces[:2]:
        total = grad_strip((here - step) % chips, wide, piece, total, False)
    late_hidden, _ = lax.optimization_barrier((late_hidden, total))
    features, near, far = second_tile(late_hidden, *edges, weight_second, cotangent, chips)
    keep, *sends = fold(near, shift(far, "c", 1))
    for step, send in zip(STEPS[1:], sends):
        keep = keep + shift(send, "y", step).astype(F32)
    sx, sz = lax.axis_size("x"), lax.axis_size("z")
    second = keep.astype(BF16).reshape(3, sx, -1, outs)
    second = jnp.transpose(second, (1, 0, 2, 3)).reshape(sx, sz, -1, outs)
    second = jnp.transpose(second, (1, 0, 2, 3)).reshape(sx * sz, -1, outs)
    extra = second.shape[1]

    step, piece = pieces[2]
    total = grad_strip((here - step) % chips, wide, piece, total, True)
    first_own, first_far = total

    joined = join(first_own, shift(first_far, "c", 1), second)
    summed = lax.all_to_all(joined, SKY, 0, 0, tiled=True)
    summed = jnp.sum(summed.astype(F32), axis=0).astype(BF16)
    rows_z = jnp.stack(gather_steps(summed, "z"))
    me_z = lax.axis_index("z")
    back_to = jnp.stack([(me_z - k) % sz for k in range(sz)])
    slot_of = jnp.asarray([STEPS.index(k) for k in range(sz)])[back_to]
    rows_z = jnp.concatenate([lax.dynamic_index_in_dim(rows_z, slot_of[k], 0) for k in range(sz)])
    main = rows_z[:, :-extra].reshape(-1, outs)
    rest = rows_z[:, -extra:].reshape(-1, outs)
    parts = gather_steps(jnp.concatenate([main, rest]), "x")
    grad_first = lay_first([part[: main.shape[0]] for part in parts], sz, chans)
    share = jnp.stack([part[main.shape[0] :] for part in parts])
    share = jnp.stack(gather_steps(share, "y"))
    grad_second = lay_second(share, shift(share, "c", 1)).reshape(3, 3, outs, outs)
    return features, grad_first, grad_second


def solution(mesh):
    sizes = (mesh.devices.shape[0] // 2, 2, 4, mesh.devices.shape[1] // 4)
    fine = Mesh(mesh.devices.reshape(sizes), FREQ + SKY)
    return jax.shard_map(
        body,
        mesh=fine,
        in_specs=(P(None, SKY, FREQ), P(None, None, FREQ, None), P(), P(FREQ, SKY, None)),
        out_specs=(P(FREQ, SKY, None), P(None, None, FREQ, None), P()),
        check_vma=False,
    )
```

```python
import functools

import jax
import jax.numpy as jnp
from jax import lax
from jax.experimental import pallas as pl
from jax.experimental.pallas import tpu as pltpu
from jax.sharding import Mesh, PartitionSpec as P

FREQ = ("y", "c")
SKY = ("z", "x")
F32 = jnp.float32
BF16 = jnp.bfloat16
QUICK = pl.CostEstimate(flops=1, bytes_accessed=8 * 2**20, transcendentals=0)


def shift(x, axis, step):
    count = lax.axis_size(axis)
    return lax.ppermute(x, axis, [(i, (i + step) % count) for i in range(count)])


def halo(x, axes, dim):
    count, length = lax.axis_size(axes), x.shape[dim]
    up = [(i, i + 1) for i in range(count - 1)]
    down = [(j, i) for i, j in up]
    last = lax.slice_in_dim(x, length - 1, length, axis=dim)
    first = lax.slice_in_dim(x, 0, 1, axis=dim)
    return lax.ppermute(last, axes, up), lax.ppermute(first, axes, down)


def spread_kernel(own_ref, far_ref, own_halo_ref, far_halo_ref, out_ref):
    chips, width, rows, depth = out_ref.shape
    cols, _, chans = own_ref.shape
    strip = cols // (2 * chips)
    core = lax.axis_index("c")
    step = 8
    row = lax.broadcasted_iota(jnp.int32, (step, rows, chans), 1)

    def block(i, base, chip):
        for side, (cube_ref, halo_ref) in enumerate(
            ((own_ref, own_halo_ref), (far_ref, far_halo_ref))
        ):
            at = pl.multiple_of(base + i * step, step)
            mid = cube_ref[pl.ds(at, step)]
            wide = mid.astype(F32).reshape(step * rows, chans)
            ahead = pltpu.roll(wide, 1, 0).reshape(step, rows, chans)
            behind = pltpu.roll(wide, step * rows - 1, 0).reshape(step, rows, chans)
            before = halo_ref[0, pl.ds(at, step), :].astype(F32)[:, None, :]
            after = halo_ref[1, pl.ds(at, step), :].astype(F32)[:, None, :]
            ahead = jnp.where(row == 0, before, ahead)
            behind = jnp.where(row == rows - 1, after, behind)
            to = pl.ds(2 + i * step, step)
            for tap, value in enumerate((ahead.astype(BF16), mid, behind.astype(BF16))):
                lane = (2 * tap + side) * chans
                out_ref[chip, to, :, lane : lane + chans] = value

    def edge(at, chip, slot):
        for side, (cube_ref, halo_ref) in enumerate(
            ((own_ref, own_halo_ref), (far_ref, far_halo_ref))
        ):
            first = pl.multiple_of((at // step) * step, step)
            mid = cube_ref[at]
            wide = mid.astype(F32)
            line = lax.broadcasted_iota(jnp.int32, (step, chans), 0) == at - first
            pick = lambda k: jnp.sum(
                jnp.where(line, halo_ref[k, pl.ds(first, step), :].astype(F32), 0.0),
                axis=0,
                keepdims=True,
            )
            place = lax.broadcasted_iota(jnp.int32, (rows, chans), 0)
            ahead = jnp.where(place == 0, pick(0), pltpu.roll(wide, 1, 0))
            behind = jnp.where(place == rows - 1, pick(1), pltpu.roll(wide, rows - 1, 0))
            for tap, value in enumerate((ahead.astype(BF16), mid, behind.astype(BF16))):
                lane = (2 * tap + side) * chans
                out_ref[chip, slot, :, lane : lane + chans] = value

    blank = jnp.zeros((rows, depth), BF16)
    for chip in range(chips):
        base = (2 * chip + core) * strip
        lax.fori_loop(0, strip // step, lambda i, _: block(i, base, chip), None)
        for slot in (0, 1):
            edge(jnp.maximum(base - 2 + slot, 0), chip, slot)
            edge(jnp.minimum(base + strip + slot, cols - 1), chip, strip + 2 + slot)
        for slot in range(strip + 4, width):
            out_ref[chip, slot] = blank

    @pl.when(core == 0)
    def _():
        out_ref[0, 0] = blank
        out_ref[0, 1] = blank

    @pl.when(core == 1)
    def _():
        out_ref[chips - 1, strip + 2] = blank
        out_ref[chips - 1, strip + 3] = blank


VMEM_SPEC = pl.BlockSpec(memory_space=pltpu.VMEM)


def spread(own, far, own_halo, far_halo, chips):
    cols, rows, chans = own.shape
    return pl.pallas_call(
        spread_kernel,
        out_shape=jax.ShapeDtypeStruct((chips, cols // (2 * chips) + 8, rows, 6 * chans), BF16),
        in_specs=[VMEM_SPEC] * 4,
        out_specs=VMEM_SPEC,
        compiler_params=pltpu.CompilerParams(vmem_limit_bytes=2 * 2**20),
        cost_estimate=QUICK,
        name="spread",
    )(own, far, own_halo, far_halo)


def chip_at(step):
    return lax.rem(lax.axis_index("y") + step, lax.axis_size("y"))


def conv_kernel(step, wide_ref, kernel_ref, out_ref):
    strip, rows, outs = out_ref.shape
    chip = chip_at(step)
    pieces = [wide_ref[chip, tap : tap + strip] for tap in range(3)]
    lhs = jnp.concatenate(pieces, axis=-1).reshape(strip * rows, -1)
    total = jnp.dot(lhs, kernel_ref[...], preferred_element_type=F32)
    out_ref[...] = total.reshape(strip, rows, outs).astype(out_ref.dtype)


def conv_strip(step, wide, kernel, strip, dtype):
    rows, depth, outs = wide.shape[2], kernel.shape[0], kernel.shape[1]
    return pl.pallas_call(
        functools.partial(conv_kernel, step),
        out_shape=jax.ShapeDtypeStruct((strip, rows, outs), dtype),
        in_specs=[VMEM_SPEC, VMEM_SPEC],
        out_specs=VMEM_SPEC,
        compiler_params=pltpu.CompilerParams(vmem_limit_bytes=3 * 2**20),
        cost_estimate=QUICK,
        name="conv_first",
    )(wide, kernel)


def grad_kernel(step, has_old, last, wide_ref, delta_ref, *refs):
    old_ref = refs[0] if has_old else None
    outs_refs, pad_ref = refs[1 if has_old else 0 : -1], refs[-1]
    strip, rows, outs = delta_ref.shape
    cols, depth = wide_ref.shape[1], wide_ref.shape[3]
    pad_ref[0:3] = jnp.zeros((3, rows, outs), BF16)
    pad_ref[3 : 3 + strip] = delta_ref[...]
    pad_ref[3 + strip :] = jnp.zeros((cols - strip - 1, rows, outs), BF16)
    lhs = wide_ref[chip_at(step)].reshape(cols * rows, depth)
    rhs = jnp.concatenate(
        [pad_ref[2 - tap : 2 - tap + cols].reshape(cols * rows, outs) for tap in range(3)], axis=-1
    )
    total = lax.dot_general(lhs, rhs, (((0,), (0,)), ((), ())), preferred_element_type=F32)
    if has_old:
        total = total + old_ref[...]
    if not last:
        outs_refs[0][...] = total
    else:
        chans = depth // 6
        for tap in range(3):
            at = 2 * tap * chans
            outs_refs[0][tap * chans : (tap + 1) * chans] = total[at : at + chans]
            outs_refs[1][tap * chans : (tap + 1) * chans] = total[
                at + chans : at + 2 * chans
            ].astype(BF16)


def grad_strip(step, wide, delta, old, last):
    strip, rows, outs = delta.shape
    depth, cols = wide.shape[3], wide.shape[1]
    shape = (depth, 3 * outs)
    half = (depth // 2, 3 * outs)
    if last:
        out_shape = (jax.ShapeDtypeStruct(half, F32), jax.ShapeDtypeStruct(half, BF16))
    else:
        out_shape = (jax.ShapeDtypeStruct(shape, F32),)
    args = [wide, delta] + ([old] if old is not None else [])
    out = pl.pallas_call(
        functools.partial(grad_kernel, step, old is not None, last),
        out_shape=out_shape,
        in_specs=[VMEM_SPEC] * len(args),
        out_specs=tuple([VMEM_SPEC] * len(out_shape)),
        scratch_shapes=[pltpu.VMEM((cols + 2, rows, outs), BF16)],
        compiler_params=pltpu.CompilerParams(vmem_limit_bytes=5 * 2**20),
        cost_estimate=QUICK,
        name="grad_first",
    )(*args)
    return out if last else out[0]


def spread_tile(columns, edge_ref, wide_ref):
    rows, chans = wide_ref.shape[1], wide_ref.shape[2] // 3
    place = lax.broadcasted_iota(jnp.int32, (rows, chans), 0)

    def put(mid, j):
        wide = mid.astype(F32)
        before = edge_ref[0, j : j + 1, :].astype(F32)
        after = edge_ref[1, j : j + 1, :].astype(F32)
        ahead = jnp.where(place == 0, before, pltpu.roll(wide, 1, 0))
        behind = jnp.where(place == rows - 1, after, pltpu.roll(wide, rows - 1, 0))
        wide_ref[j, :, 0:chans] = ahead.astype(BF16)
        wide_ref[j, :, chans : 2 * chans] = mid
        wide_ref[j, :, 2 * chans :] = behind.astype(BF16)

    for j, (ref, at) in enumerate(columns):
        put(ref[at], j)


def back_kernel(cot_ref, left_ref, right_ref, edge_ref, kernel_ref, out_ref, wide_ref):
    cols, rows, chans = cot_ref.shape
    columns = [(left_ref, 0)] + [(cot_ref, j) for j in range(cols)] + [(right_ref, 0)]
    spread_tile(columns, edge_ref, wide_ref)
    total = None
    for tap_col in range(3):
        lhs = wide_ref[tap_col : tap_col + cols].reshape(cols * rows, 3 * chans)
        for tap_row in range(3):
            part = lax.dot_general(
                lhs[:, tap_row * chans : (tap_row + 1) * chans],
                kernel_ref[2 - tap_col, 2 - tap_row],
                (((1,), (1,)), ((), ())),
                preferred_element_type=F32,
            )
            total = part if total is None else total + part
    out_ref[...] = total.reshape(cols, rows, -1)


def back_tile(tile, left, right, edges, kernel):
    cols, rows, chans = tile.shape
    return pl.pallas_call(
        back_kernel,
        out_shape=jax.ShapeDtypeStruct((cols, rows, kernel.shape[2]), F32),
        in_specs=[VMEM_SPEC] * 5,
        out_specs=VMEM_SPEC,
        scratch_shapes=[pltpu.VMEM((cols + 2, rows, 3 * chans), BF16)],
        compiler_params=pltpu.CompilerParams(vmem_limit_bytes=4 * 2**20),
        cost_estimate=QUICK,
        name="back",
    )(tile, left, right, edges, kernel)


def second_kernel(
    chips, hid_ref, edge_ref, kernel_ref, cot_ref,
    out_ref, near_ref, far_ref, wide_ref, pad_ref, sum_ref,
):
    chans = hid_ref.shape[2]
    cols, rows, outs = cot_ref.shape
    width = wide_ref.shape[0]
    core = lax.axis_index("c")
    spread_tile([(hid_ref, j) for j in range(cols + 2)], edge_ref, wide_ref)
    wide_ref[cols + 2 :] = jnp.zeros((width - cols - 2, rows, 3 * chans), BF16)
    pieces = [wide_ref[tap : tap + cols] for tap in range(3)]
    lhs = jnp.concatenate(pieces, axis=-1).reshape(cols * rows, 9 * chans)
    total = jnp.dot(lhs, kernel_ref[...], preferred_element_type=F32)
    out_ref[...] = total.reshape(cols, rows, outs).astype(BF16)

    pad_ref[0:2] = jnp.zeros((2, rows, outs), BF16)
    pad_ref[2 : 2 + cols] = cot_ref[...]
    pad_ref[2 + cols :] = jnp.zeros((width - cols, rows, outs), BF16)
    rhs = jnp.concatenate(
        [pad_ref[2 - tap : 2 - tap + width].reshape(width * rows, outs) for tap in range(3)],
        axis=-1,
    )
    sum_ref[...] = lax.dot_general(
        wide_ref[...].reshape(width * rows, 3 * chans),
        rhs,
        (((0,), (0,)), ((), ())),
        preferred_element_type=F32,
    )
    size = sum_ref.shape[0] // (2 * chips)
    for half, ref in ((core, near_ref), (1 - core, far_ref)):
        for chip in range(chips):
            at = pl.multiple_of((half * chips + chip) * size, size)
            for tap in range(3):
                ref[chip, tap * size : (tap + 1) * size, :] = sum_ref[
                    pl.ds(at, size), tap * outs : (tap + 1) * outs
                ].astype(ref.dtype)


def second_tile(tile, edges, kernel, cotangent, chips):
    chans = tile.shape[2]
    cols, rows, outs = cotangent.shape
    width = cols + 8
    cut = (chips, 9 * chans // (2 * chips), outs)
    return pl.pallas_call(
        functools.partial(second_kernel, chips),
        out_shape=(
            jax.ShapeDtypeStruct((cols, rows, outs), BF16),
            jax.ShapeDtypeStruct(cut, F32),
            jax.ShapeDtypeStruct(cut, BF16),
        ),
        in_specs=[VMEM_SPEC] * 4,
        out_specs=(VMEM_SPEC,) * 3,
        scratch_shapes=[
            pltpu.VMEM((width, rows, 3 * chans), BF16),
            pltpu.VMEM((width + 2, rows, outs), BF16),
            pltpu.VMEM((3 * chans, 3 * outs), F32),
        ],
        compiler_params=pltpu.CompilerParams(vmem_limit_bytes=9 * 2**20),
        cost_estimate=QUICK,
        name="second",
    )(tile, edges, kernel.reshape(9 * chans, outs), cotangent)


def point_kernel(own_ref, a_ref, b_ref, c_ref, back_ref, delta_ref, hidden_ref):
    cols = own_ref.shape[0]
    strip = 2 * lax.axis_index("y") + lax.axis_index("c")
    strips = 2 * lax.axis_size("y")

    def column(j, sees_delta, keep):
        pre = own_ref[j] + a_ref[j].astype(F32) + b_ref[j].astype(F32) + c_ref[j].astype(F32)
        sigma = jax.nn.sigmoid(pre)
        hidden = pre * sigma
        if keep is not None:
            hidden = jnp.where(keep, hidden, 0.0)
        hidden_ref[j] = hidden.astype(BF16)
        if sees_delta:
            slope = sigma * (1.0 + pre * (1.0 - sigma))
            delta_ref[j - 1] = (back_ref[j - 1] * slope).astype(BF16)

    column(0, False, strip > 0)
    column(cols - 1, False, strip < strips - 1)

    def each(j, _):
        column(j, True, None)

    lax.fori_loop(1, cols - 1, each, None)


def point(own, parts, back):
    return pl.pallas_call(
        point_kernel,
        out_shape=(
            jax.ShapeDtypeStruct(back.shape, BF16),
            jax.ShapeDtypeStruct(own.shape, BF16),
        ),
        in_specs=[VMEM_SPEC] * 5,
        out_specs=(VMEM_SPEC,) * 2,
        compiler_params=pltpu.CompilerParams(vmem_limit_bytes=2 * 2**20),
        cost_estimate=QUICK,
        name="point",
    )(own, *parts, back)


def fold_kernel(near_ref, got_ref, keep_ref, *send_refs):
    chips = near_ref.shape[0]
    here = lax.axis_index("y")
    keep_ref[...] = near_ref[here] + got_ref[here].astype(F32)
    for step, ref in zip(STEPS[1:], send_refs):
        to = lax.rem(here + step, chips)
        ref[...] = (near_ref[to] + got_ref[to].astype(F32)).astype(BF16)


def fold(near, got):
    shape = near.shape[1:]
    return pl.pallas_call(
        fold_kernel,
        out_shape=(jax.ShapeDtypeStruct(shape, F32),) + (jax.ShapeDtypeStruct(shape, BF16),) * 3,
        in_specs=[VMEM_SPEC] * 2,
        out_specs=(VMEM_SPEC,) * 4,
        compiler_params=pltpu.CompilerParams(vmem_limit_bytes=2 * 2**20),
        cost_estimate=QUICK,
        name="fold",
    )(near, got)


def row_halo(pieces):
    last = pieces[0].shape[1] - 1
    ends = [jnp.concatenate([piece[:, r] for piece in pieces], axis=0) for r in (last, 0)]
    count = lax.axis_size(SKY)
    up = [(i, i + 1) for i in range(count - 1)]
    down = [(j, i) for i, j in up]
    return jnp.stack([lax.ppermute(ends[0], SKY, up), lax.ppermute(ends[1], SKY, down)])


def join_kernel(own_ref, far_ref, second_ref, out_ref):
    pieces, extra, outs = second_ref.shape
    chans = own_ref.shape[0] // 3
    size = chans // pieces
    for tap_col in range(3):
        for tap_row in range(3):
            rows = slice(tap_row * chans, (tap_row + 1) * chans)
            lanes = slice(tap_col * outs, (tap_col + 1) * outs)
            value = own_ref[rows, lanes] + far_ref[rows, lanes].astype(F32)
            at = (3 * tap_col + tap_row) * size
            out_ref[:, at : at + size, :] = value.reshape(pieces, size, outs).astype(BF16)
    out_ref[:, 9 * size :, :] = second_ref[...]


def join(own, far, second):
    pieces, extra, outs = second.shape
    rows = 9 * (own.shape[0] // 3 // pieces) + extra
    return pl.pallas_call(
        join_kernel,
        out_shape=jax.ShapeDtypeStruct((pieces, rows, outs), BF16),
        in_specs=[VMEM_SPEC] * 3,
        out_specs=VMEM_SPEC,
        compiler_params=pltpu.CompilerParams(vmem_limit_bytes=2 * 2**20),
        cost_estimate=QUICK,
        name="join",
    )(own, far, second)


STEPS = (0, 1, 3, 2)


def order_kernel(extra, a_ref, b_ref, c_ref, d_ref, out_ref):
    rows = a_ref.shape[0] - extra
    sz = lax.axis_size("z")
    me = lax.axis_index("z")
    values = [ref[...].astype(F32) for ref in (a_ref, b_ref, c_ref, d_ref)]
    rest = []
    for z in range(len(STEPS)):
        value = values[0]
        for step, other in zip(STEPS[1:], values[1:]):
            value = jnp.where(lax.rem(me + sz - step, sz) == z, other, value)
        out_ref[z * rows : (z + 1) * rows, :] = value[:rows].astype(BF16)
        rest.append(value[rows:])
    out_ref[len(STEPS) * rows :, :] = jnp.concatenate(rest, axis=0).astype(BF16)


def order_pieces(parts, extra):
    rows, outs = parts[0].shape
    return pl.pallas_call(
        functools.partial(order_kernel, extra),
        out_shape=jax.ShapeDtypeStruct((4 * rows, outs), BF16),
        in_specs=[VMEM_SPEC] * 4,
        out_specs=VMEM_SPEC,
        compiler_params=pltpu.CompilerParams(vmem_limit_bytes=4 * 2**20),
        cost_estimate=QUICK,
        name="order_pieces",
    )(*parts)


def first_kernel(sz, a_ref, b_ref, c_ref, d_ref, out_ref):
    sx = lax.axis_size("x")
    size = out_ref.shape[2] // (sx * sz)
    me = lax.axis_index("x")
    for step, ref in zip(STEPS, (a_ref, b_ref, c_ref, d_ref)):
        x = lax.rem(me + sx - step, sx)
        value = ref[...].astype(F32)
        for z in range(sz):
            at = pl.multiple_of((z * sx + x) * size, size)
            for tap in range(9):
                rows = (z * 9 + tap) * size
                out_ref[tap // 3, tap % 3, pl.ds(at, size), :] = value[rows : rows + size]


def lay_first(parts, sz, chans):
    outs = parts[0].shape[1]
    return pl.pallas_call(
        functools.partial(first_kernel, sz),
        out_shape=jax.ShapeDtypeStruct((3, 3, chans, outs), F32),
        in_specs=[VMEM_SPEC] * 4,
        out_specs=VMEM_SPEC,
        compiler_params=pltpu.CompilerParams(vmem_limit_bytes=4 * 2**20),
        cost_estimate=QUICK,
        name="lay_first",
    )(*parts)


def lay_second_kernel(near_ref, far_ref, out_ref):
    sy, sx, rows, _ = near_ref.shape
    size = rows // 3
    third = out_ref.shape[0] // 3
    core, y, x = lax.axis_index("c"), lax.axis_index("y"), lax.axis_index("x")
    for half, ref in ((core, near_ref), (1 - core, far_ref)):
        for i in range(sy):
            for j in range(sx):
                place = (half * sy + lax.rem(y + sy - STEPS[i], sy)) * sx
                place = place + lax.rem(x + sx - STEPS[j], sx)
                value = ref[i, j].astype(F32)
                for tap in range(3):
                    at = pl.multiple_of(tap * third + place * size, 8)
                    out_ref[pl.ds(at, size), :] = value[tap * size : (tap + 1) * size]


def lay_second(near, far):
    sy, sx, rows, outs = near.shape
    return pl.pallas_call(
        lay_second_kernel,
        out_shape=jax.ShapeDtypeStruct((2 * sy * sx * rows, outs), F32),
        in_specs=[VMEM_SPEC] * 2,
        out_specs=VMEM_SPEC,
        compiler_params=pltpu.CompilerParams(vmem_limit_bytes=4 * 2**20),
        cost_estimate=QUICK,
        name="lay_second",
    )(near, far)


def gather_steps(piece, axis):
    return [piece] + [shift(piece, axis, step) for step in STEPS[1:]]


def body(sky_cube, weight_first, weight_second, cotangent):
    cols, rows, chans = sky_cube.shape
    strip, _, outs = cotangent.shape
    chips = lax.axis_size("y")

    edges = jnp.concatenate(halo(sky_cube, SKY, 1), axis=1)
    far_cube = shift(sky_cube, "c", 1)
    far_weight = shift(weight_first, "c", 1)
    edges = jnp.transpose(edges, (1, 0, 2))
    far_edges = shift(edges, "c", 1)
    left, right = halo(cotangent, FREQ, 0)
    own_cube, left, right = lax.optimization_barrier((sky_cube, left, right))
    wide = spread(own_cube, far_cube, edges, far_edges, chips)
    kernel = jnp.concatenate([weight_first, far_weight], axis=2).reshape(18 * chans, outs)

    order = (2, 1, chips - 1)
    near = []
    hold = wide
    for step in order:
        part = conv_strip(step, hold, kernel, strip + 2, BF16)
        near.append(part)
        hold, _ = lax.optimization_barrier((wide, part))
    own = conv_strip(0, wide, kernel, strip + 2, F32)
    got = [shift(part, "y", step) for step, part in zip(order, near)]

    late, left, right, _ = lax.optimization_barrier((cotangent, left, right, near[-1]))
    back = back_tile(late, left, right, row_halo([left, late, right]), weight_second)
    delta, hidden = point(own, got, back)

    pieces = [(step, shift(delta, "y", step)) for step in (1, chips - 1, 2)]
    total = grad_strip(0, wide, delta, None, False)
    late_hidden, _ = lax.optimization_barrier((hidden, total))

    edges = row_halo([late_hidden])
    for step, piece in pieces[:2]:
        total = grad_strip(chips - step, wide, piece, total, False)
    late_hidden, _ = lax.optimization_barrier((late_hidden, total))
    features, near, far = second_tile(late_hidden, edges, weight_second, cotangent, chips)
    keep, *sends = fold(near, shift(far, "c", 1))
    for step, send in zip(STEPS[1:], sends):
        keep = keep + shift(send, "y", step).astype(F32)
    sx, sz = lax.axis_size("x"), lax.axis_size("z")
    second = keep.astype(BF16).reshape(3, sx, -1, outs)
    second = jnp.transpose(second, (1, 0, 2, 3)).reshape(sx, sz, -1, outs)
    second = jnp.transpose(second, (1, 0, 2, 3)).reshape(sx * sz, -1, outs)
    extra = second.shape[1]

    step, piece = pieces[2]
    total = grad_strip(chips - step, wide, piece, total, True)
    first_own, first_far = total

    joined = join(first_own, shift(first_far, "c", 1), second)
    summed = lax.all_to_all(joined, SKY, 0, 0, tiled=True)
    summed = jnp.sum(summed.astype(F32), axis=0).astype(BF16)
    parts = gather_steps(order_pieces(gather_steps(summed, "z"), extra), "x")
    main = parts[0].shape[0] - sz * extra
    grad_first = lay_first(parts, sz, chans)
    share = jnp.stack([part[main:] for part in parts])
    share = jnp.stack(gather_steps(share, "y"))
    grad_second = lay_second(share, shift(share, "c", 1)).reshape(3, 3, outs, outs)
    return features, grad_first, grad_second


def solution(mesh):
    sizes = (mesh.devices.shape[0] // 2, 2, 4, mesh.devices.shape[1] // 4)
    fine = Mesh(mesh.devices.reshape(sizes), FREQ + SKY)
    return jax.shard_map(
        body,
        mesh=fine,
        in_specs=(P(None, SKY, FREQ), P(None, None, FREQ, None), P(), P(FREQ, SKY, None)),
        out_specs=(P(FREQ, SKY, None), P(None, None, FREQ, None), P()),
        check_vma=False,
    )
```

```python
import functools

import jax
import jax.numpy as jnp
from jax import lax
from jax.experimental import pallas as pl
from jax.experimental.pallas import tpu as pltpu
from jax.sharding import Mesh, PartitionSpec as P

FREQ = ("y", "c")
SKY = ("z", "x")
F32 = jnp.float32
BF16 = jnp.bfloat16
QUICK = pl.CostEstimate(flops=1, bytes_accessed=1, transcendentals=0)


def shift(x, axis, step):
    count = lax.axis_size(axis)
    return lax.ppermute(x, axis, [(i, (i + step) % count) for i in range(count)])


def halo(x, axes, dim):
    count, length = lax.axis_size(axes), x.shape[dim]
    up = [(i, i + 1) for i in range(count - 1)]
    down = [(j, i) for i, j in up]
    last = lax.slice_in_dim(x, length - 1, length, axis=dim)
    first = lax.slice_in_dim(x, 0, 1, axis=dim)
    return lax.ppermute(last, axes, up), lax.ppermute(first, axes, down)


def spread_kernel(own_ref, far_ref, own_halo_ref, far_halo_ref, out_ref):
    chips, width, rows, depth = out_ref.shape
    cols, _, chans = own_ref.shape
    strip = cols // (2 * chips)
    core = lax.axis_index("c")
    step = 8
    row = lax.broadcasted_iota(jnp.int32, (step, rows, chans), 1)

    def block(i, base, chip):
        for side, (cube_ref, halo_ref) in enumerate(
            ((own_ref, own_halo_ref), (far_ref, far_halo_ref))
        ):
            at = pl.multiple_of(base + i * step, step)
            mid = cube_ref[pl.ds(at, step)]
            wide = mid.astype(F32).reshape(step * rows, chans)
            ahead = pltpu.roll(wide, 1, 0).reshape(step, rows, chans)
            behind = pltpu.roll(wide, step * rows - 1, 0).reshape(step, rows, chans)
            before = halo_ref[0, pl.ds(at, step), :].astype(F32)[:, None, :]
            after = halo_ref[1, pl.ds(at, step), :].astype(F32)[:, None, :]
            ahead = jnp.where(row == 0, before, ahead)
            behind = jnp.where(row == rows - 1, after, behind)
            to = pl.ds(2 + i * step, step)
            for tap, value in enumerate((ahead.astype(BF16), mid, behind.astype(BF16))):
                lane = (2 * tap + side) * chans
                out_ref[chip, to, :, lane : lane + chans] = value

    def edge(at, chip, slot):
        for side, (cube_ref, halo_ref) in enumerate(
            ((own_ref, own_halo_ref), (far_ref, far_halo_ref))
        ):
            first = pl.multiple_of((at // step) * step, step)
            mid = cube_ref[at]
            wide = mid.astype(F32)
            line = lax.broadcasted_iota(jnp.int32, (step, chans), 0) == at - first
            pick = lambda k: jnp.sum(
                jnp.where(line, halo_ref[k, pl.ds(first, step), :].astype(F32), 0.0),
                axis=0,
                keepdims=True,
            )
            place = lax.broadcasted_iota(jnp.int32, (rows, chans), 0)
            ahead = jnp.where(place == 0, pick(0), pltpu.roll(wide, 1, 0))
            behind = jnp.where(place == rows - 1, pick(1), pltpu.roll(wide, rows - 1, 0))
            for tap, value in enumerate((ahead.astype(BF16), mid, behind.astype(BF16))):
                lane = (2 * tap + side) * chans
                out_ref[chip, slot, :, lane : lane + chans] = value

    blank = jnp.zeros((rows, depth), BF16)
    for chip in range(chips):
        base = (2 * chip + core) * strip
        lax.fori_loop(0, strip // step, lambda i, _: block(i, base, chip), None)
        for slot in (0, 1):
            edge(jnp.maximum(base - 2 + slot, 0), chip, slot)
            edge(jnp.minimum(base + strip + slot, cols - 1), chip, strip + 2 + slot)
        for slot in range(strip + 4, width):
            out_ref[chip, slot] = blank

    @pl.when(core == 0)
    def _():
        out_ref[0, 0] = blank
        out_ref[0, 1] = blank

    @pl.when(core == 1)
    def _():
        out_ref[chips - 1, strip + 2] = blank
        out_ref[chips - 1, strip + 3] = blank


VMEM_SPEC = pl.BlockSpec(memory_space=pltpu.VMEM)


def spread(own, far, own_halo, far_halo, chips):
    cols, rows, chans = own.shape
    return pl.pallas_call(
        spread_kernel,
        out_shape=jax.ShapeDtypeStruct((chips, cols // (2 * chips) + 8, rows, 6 * chans), BF16),
        in_specs=[VMEM_SPEC] * 4,
        out_specs=VMEM_SPEC,
        compiler_params=pltpu.CompilerParams(vmem_limit_bytes=2 * 2**20),
        cost_estimate=QUICK,
        name="spread",
    )(own, far, own_halo, far_halo)


def chip_at(step):
    return lax.rem(lax.axis_index("y") + step, lax.axis_size("y"))


def conv_kernel(parts, adds, wide_ref, kernel_ref, *refs):
    rows = wide_ref.shape[2]
    for (step, first), add_ref, out_ref in zip(parts, refs[:adds] or [None] * len(parts), refs[adds:]):
        count, _, outs = out_ref.shape
        chip = chip_at(step)
        pieces = [wide_ref[chip, first + tap : first + tap + count] for tap in range(3)]
        lhs = jnp.concatenate(pieces, axis=-1).reshape(count * rows, -1)
        total = jnp.dot(lhs, kernel_ref[...], preferred_element_type=F32)
        total = total.reshape(count, rows, outs)
        if add_ref is not None:
            total = total + add_ref[...].astype(F32)
        out_ref[...] = total.astype(out_ref.dtype)


def conv_parts(parts, wide, kernel, count, dtype, adds=()):
    rows, outs = wide.shape[2], kernel.shape[1]
    return pl.pallas_call(
        functools.partial(conv_kernel, parts, len(adds)),
        out_shape=(jax.ShapeDtypeStruct((count, rows, outs), dtype),) * len(parts),
        in_specs=[VMEM_SPEC] * (2 + len(adds)),
        out_specs=(VMEM_SPEC,) * len(parts),
        compiler_params=pltpu.CompilerParams(vmem_limit_bytes=4 * 2**20),
        cost_estimate=QUICK,
        name="conv_first",
    )(wide, kernel, *adds)


def grad_kernel(step, has_old, last, wide_ref, a_ref, b_ref, *refs):
    old_ref = refs[0] if has_old else None
    outs_refs, pad_ref = refs[1 if has_old else 0 : -1], refs[-1]
    half, rows, outs = a_ref.shape
    strip = 2 * half
    cols, depth = wide_ref.shape[1], wide_ref.shape[3]
    pad_ref[0:3] = jnp.zeros((3, rows, outs), BF16)
    pad_ref[3 : 3 + half] = a_ref[...]
    pad_ref[3 + half : 3 + strip] = b_ref[...]
    pad_ref[3 + strip :] = jnp.zeros((cols - strip - 1, rows, outs), BF16)
    lhs = wide_ref[chip_at(step)].reshape(cols * rows, depth)
    rhs = jnp.concatenate(
        [pad_ref[2 - tap : 2 - tap + cols].reshape(cols * rows, outs) for tap in range(3)], axis=-1
    )
    total = lax.dot_general(lhs, rhs, (((0,), (0,)), ((), ())), preferred_element_type=F32)
    if has_old:
        total = total + old_ref[...]
    if not last:
        outs_refs[0][...] = total
    else:
        chans = depth // 6
        for tap in range(3):
            at = 2 * tap * chans
            outs_refs[0][tap * chans : (tap + 1) * chans] = total[at : at + chans]
            outs_refs[1][tap * chans : (tap + 1) * chans] = total[
                at + chans : at + 2 * chans
            ].astype(BF16)


def grad_strip(step, wide, halves, old, last):
    _, rows, outs = halves[0].shape
    depth, cols = wide.shape[3], wide.shape[1]
    shape = (depth, 3 * outs)
    half = (depth // 2, 3 * outs)
    if last:
        out_shape = (jax.ShapeDtypeStruct(half, F32), jax.ShapeDtypeStruct(half, BF16))
    else:
        out_shape = (jax.ShapeDtypeStruct(shape, F32),)
    args = [wide, *halves] + ([old] if old is not None else [])
    out = pl.pallas_call(
        functools.partial(grad_kernel, step, old is not None, last),
        out_shape=out_shape,
        in_specs=[VMEM_SPEC] * len(args),
        out_specs=tuple([VMEM_SPEC] * len(out_shape)),
        scratch_shapes=[pltpu.VMEM((cols + 2, rows, outs), BF16)],
        compiler_params=pltpu.CompilerParams(vmem_limit_bytes=5 * 2**20),
        cost_estimate=QUICK,
        name="grad_first",
    )(*args)
    return out if last else out[0]


def spread_tile(columns, edge_ref, wide_ref):
    rows, chans = wide_ref.shape[1], wide_ref.shape[2] // 3
    place = lax.broadcasted_iota(jnp.int32, (rows, chans), 0)

    def put(mid, j):
        wide = mid.astype(F32)
        before = edge_ref[0, j : j + 1, :].astype(F32)
        after = edge_ref[1, j : j + 1, :].astype(F32)
        ahead = jnp.where(place == 0, before, pltpu.roll(wide, 1, 0))
        behind = jnp.where(place == rows - 1, after, pltpu.roll(wide, rows - 1, 0))
        wide_ref[j, :, 0:chans] = ahead.astype(BF16)
        wide_ref[j, :, chans : 2 * chans] = mid
        wide_ref[j, :, 2 * chans :] = behind.astype(BF16)

    for j, (ref, at) in enumerate(columns):
        put(ref[at], j)


def back_kernel(cot_ref, left_ref, right_ref, edge_ref, kernel_ref, out_ref, wide_ref):
    cols, rows, chans = cot_ref.shape
    columns = [(left_ref, 0)] + [(cot_ref, j) for j in range(cols)] + [(right_ref, 0)]
    spread_tile(columns, edge_ref, wide_ref)
    total = None
    for tap_col in range(3):
        lhs = wide_ref[tap_col : tap_col + cols].reshape(cols * rows, 3 * chans)
        for tap_row in range(3):
            part = lax.dot_general(
                lhs[:, tap_row * chans : (tap_row + 1) * chans],
                kernel_ref[2 - tap_col, 2 - tap_row],
                (((1,), (1,)), ((), ())),
                preferred_element_type=F32,
            )
            total = part if total is None else total + part
    out_ref[...] = total.reshape(cols, rows, -1)


def back_tile(tile, left, right, edges, kernel):
    cols, rows, chans = tile.shape
    return pl.pallas_call(
        back_kernel,
        out_shape=jax.ShapeDtypeStruct((cols, rows, kernel.shape[2]), F32),
        in_specs=[VMEM_SPEC] * 5,
        out_specs=VMEM_SPEC,
        scratch_shapes=[pltpu.VMEM((cols + 2, rows, 3 * chans), BF16)],
        compiler_params=pltpu.CompilerParams(vmem_limit_bytes=4 * 2**20),
        cost_estimate=QUICK,
        name="back",
    )(tile, left, right, edges, kernel)


def second_kernel(
    chips, hid_ref, edge_ref, kernel_ref, cot_ref,
    out_ref, near_ref, far_ref, wide_ref, pad_ref, sum_ref,
):
    chans = hid_ref.shape[2]
    cols, rows, outs = cot_ref.shape
    width = wide_ref.shape[0]
    core = lax.axis_index("c")
    spread_tile([(hid_ref, j) for j in range(cols + 2)], edge_ref, wide_ref)
    wide_ref[cols + 2 :] = jnp.zeros((width - cols - 2, rows, 3 * chans), BF16)
    pieces = [wide_ref[tap : tap + cols] for tap in range(3)]
    lhs = jnp.concatenate(pieces, axis=-1).reshape(cols * rows, 9 * chans)
    total = jnp.dot(lhs, kernel_ref[...], preferred_element_type=F32)
    out_ref[...] = total.reshape(cols, rows, outs).astype(BF16)

    pad_ref[0:2] = jnp.zeros((2, rows, outs), BF16)
    pad_ref[2 : 2 + cols] = cot_ref[...]
    pad_ref[2 + cols :] = jnp.zeros((width - cols, rows, outs), BF16)
    rhs = jnp.concatenate(
        [pad_ref[2 - tap : 2 - tap + width].reshape(width * rows, outs) for tap in range(3)],
        axis=-1,
    )
    sum_ref[...] = lax.dot_general(
        wide_ref[...].reshape(width * rows, 3 * chans),
        rhs,
        (((0,), (0,)), ((), ())),
        preferred_element_type=F32,
    )
    size = sum_ref.shape[0] // (2 * chips)
    for half, ref in ((core, near_ref), (1 - core, far_ref)):
        for chip in range(chips):
            at = pl.multiple_of((half * chips + chip) * size, size)
            for tap in range(3):
                ref[chip, tap * size : (tap + 1) * size, :] = sum_ref[
                    pl.ds(at, size), tap * outs : (tap + 1) * outs
                ].astype(ref.dtype)


def second_tile(tile, edges, kernel, cotangent, chips):
    chans = tile.shape[2]
    cols, rows, outs = cotangent.shape
    width = cols + 8
    cut = (chips, 9 * chans // (2 * chips), outs)
    return pl.pallas_call(
        functools.partial(second_kernel, chips),
        out_shape=(
            jax.ShapeDtypeStruct((cols, rows, outs), BF16),
            jax.ShapeDtypeStruct(cut, F32),
            jax.ShapeDtypeStruct(cut, BF16),
        ),
        in_specs=[VMEM_SPEC] * 4,
        out_specs=(VMEM_SPEC,) * 3,
        scratch_shapes=[
            pltpu.VMEM((width, rows, 3 * chans), BF16),
            pltpu.VMEM((width + 2, rows, outs), BF16),
            pltpu.VMEM((3 * chans, 3 * outs), F32),
        ],
        compiler_params=pltpu.CompilerParams(vmem_limit_bytes=9 * 2**20),
        cost_estimate=QUICK,
        name="second",
    )(tile, edges, kernel.reshape(9 * chans, outs), cotangent)


def point_kernel(own_ref, a0_ref, a1_ref, b0_ref, b1_ref, back_ref, da_ref, db_ref, hidden_ref):
    cols = own_ref.shape[0]
    half = da_ref.shape[0]
    strip = 2 * lax.axis_index("y") + lax.axis_index("c")
    strips = 2 * lax.axis_size("y")

    def column(j, i, refs, delta_ref, keep):
        pre = own_ref[j] + refs[0][i].astype(F32) + refs[1][i].astype(F32)
        sigma = jax.nn.sigmoid(pre)
        hidden = pre * sigma
        if keep is not None:
            hidden = jnp.where(keep, hidden, 0.0)
        hidden_ref[j] = hidden.astype(BF16)
        if keep is None:
            slope = sigma * (1.0 + pre * (1.0 - sigma))
            at = j - 1 if delta_ref is da_ref else j - 1 - half
            delta_ref[at] = (back_ref[j - 1] * slope).astype(BF16)

    left, right = (a0_ref, a1_ref), (b0_ref, b1_ref)
    column(0, 0, left, None, strip > 0)
    column(cols - 1, half, right, None, strip < strips - 1)

    def each(i, _):
        column(i, i, left, da_ref, None)
        column(half + i, i - 1, right, db_ref, None)

    lax.fori_loop(1, half + 1, each, None)


def point(own, left, right, back):
    strip, rows, outs = back.shape
    cut = jax.ShapeDtypeStruct((strip // 2, rows, outs), BF16)
    return pl.pallas_call(
        point_kernel,
        out_shape=(cut, cut, jax.ShapeDtypeStruct(own.shape, BF16)),
        in_specs=[VMEM_SPEC] * 6,
        out_specs=(VMEM_SPEC,) * 3,
        compiler_params=pltpu.CompilerParams(vmem_limit_bytes=2 * 2**20),
        cost_estimate=QUICK,
        name="point",
    )(own, *left, *right, back)


def fold_kernel(near_ref, got_ref, keep_ref, *send_refs):
    chips = near_ref.shape[0]
    here = lax.axis_index("y")
    keep_ref[...] = near_ref[here] + got_ref[here].astype(F32)
    for step, ref in zip(STEPS[1:], send_refs):
        to = lax.rem(here + step, chips)
        ref[...] = (near_ref[to] + got_ref[to].astype(F32)).astype(BF16)


def fold(near, got):
    shape = near.shape[1:]
    return pl.pallas_call(
        fold_kernel,
        out_shape=(jax.ShapeDtypeStruct(shape, F32),) + (jax.ShapeDtypeStruct(shape, BF16),) * 3,
        in_specs=[VMEM_SPEC] * 2,
        out_specs=(VMEM_SPEC,) * 4,
        compiler_params=pltpu.CompilerParams(vmem_limit_bytes=2 * 2**20),
        cost_estimate=QUICK,
        name="fold",
    )(near, got)


def row_halo(pieces):
    last = pieces[0].shape[1] - 1
    ends = [jnp.concatenate([piece[:, r] for piece in pieces], axis=0) for r in (last, 0)]
    count = lax.axis_size(SKY)
    up = [(i, i + 1) for i in range(count - 1)]
    down = [(j, i) for i, j in up]
    return jnp.stack([lax.ppermute(ends[0], SKY, up), lax.ppermute(ends[1], SKY, down)])


def join_kernel(own_ref, far_ref, second_ref, out_ref):
    pieces, extra, outs = second_ref.shape
    chans = own_ref.shape[0] // 3
    size = chans // pieces
    for tap_col in range(3):
        for tap_row in range(3):
            rows = slice(tap_row * chans, (tap_row + 1) * chans)
            lanes = slice(tap_col * outs, (tap_col + 1) * outs)
            value = own_ref[rows, lanes] + far_ref[rows, lanes].astype(F32)
            at = (3 * tap_col + tap_row) * size
            out_ref[:, at : at + size, :] = value.reshape(pieces, size, outs).astype(BF16)
    out_ref[:, 9 * size :, :] = second_ref[...]


def join(own, far, second):
    pieces, extra, outs = second.shape
    rows = 9 * (own.shape[0] // 3 // pieces) + extra
    return pl.pallas_call(
        join_kernel,
        out_shape=jax.ShapeDtypeStruct((pieces, rows, outs), BF16),
        in_specs=[VMEM_SPEC] * 3,
        out_specs=VMEM_SPEC,
        compiler_params=pltpu.CompilerParams(vmem_limit_bytes=2 * 2**20),
        cost_estimate=QUICK,
        name="join",
    )(own, far, second)


STEPS = (0, 1, 3, 2)


def order_kernel(extra, a_ref, b_ref, c_ref, d_ref, out_ref):
    rows = a_ref.shape[0] - extra
    sz = lax.axis_size("z")
    me = lax.axis_index("z")
    values = [ref[...].astype(F32) for ref in (a_ref, b_ref, c_ref, d_ref)]
    rest = []
    for z in range(len(STEPS)):
        value = values[0]
        for step, other in zip(STEPS[1:], values[1:]):
            value = jnp.where(lax.rem(me + sz - step, sz) == z, other, value)
        out_ref[z * rows : (z + 1) * rows, :] = value[:rows].astype(BF16)
        rest.append(value[rows:])
    out_ref[len(STEPS) * rows :, :] = jnp.concatenate(rest, axis=0).astype(BF16)


def order_pieces(parts, extra):
    rows, outs = parts[0].shape
    return pl.pallas_call(
        functools.partial(order_kernel, extra),
        out_shape=jax.ShapeDtypeStruct((4 * rows, outs), BF16),
        in_specs=[VMEM_SPEC] * 4,
        out_specs=VMEM_SPEC,
        compiler_params=pltpu.CompilerParams(vmem_limit_bytes=4 * 2**20),
        cost_estimate=QUICK,
        name="order_pieces",
    )(*parts)


def first_kernel(sz, a_ref, b_ref, c_ref, d_ref, out_ref):
    sx = lax.axis_size("x")
    size = out_ref.shape[2] // (sx * sz)
    me = lax.axis_index("x")
    for step, ref in zip(STEPS, (a_ref, b_ref, c_ref, d_ref)):
        x = lax.rem(me + sx - step, sx)
        value = ref[...].astype(F32)
        for z in range(sz):
            at = pl.multiple_of((z * sx + x) * size, size)
            for tap in range(9):
                rows = (z * 9 + tap) * size
                out_ref[tap // 3, tap % 3, pl.ds(at, size), :] = value[rows : rows + size]


def lay_first(parts, sz, chans):
    outs = parts[0].shape[1]
    return pl.pallas_call(
        functools.partial(first_kernel, sz),
        out_shape=jax.ShapeDtypeStruct((3, 3, chans, outs), F32),
        in_specs=[VMEM_SPEC] * 4,
        out_specs=VMEM_SPEC,
        compiler_params=pltpu.CompilerParams(vmem_limit_bytes=4 * 2**20),
        cost_estimate=QUICK,
        name="lay_first",
    )(*parts)


def lay_second_kernel(near_ref, far_ref, out_ref):
    sy, sx, rows, _ = near_ref.shape
    size = rows // 3
    third = out_ref.shape[0] // 3
    core, y, x = lax.axis_index("c"), lax.axis_index("y"), lax.axis_index("x")
    for half, ref in ((core, near_ref), (1 - core, far_ref)):
        for i in range(sy):
            for j in range(sx):
                place = (half * sy + lax.rem(y + sy - STEPS[i], sy)) * sx
                place = place + lax.rem(x + sx - STEPS[j], sx)
                value = ref[i, j].astype(F32)
                for tap in range(3):
                    at = pl.multiple_of(tap * third + place * size, 8)
                    out_ref[pl.ds(at, size), :] = value[tap * size : (tap + 1) * size]


def lay_second(near, far):
    sy, sx, rows, outs = near.shape
    return pl.pallas_call(
        lay_second_kernel,
        out_shape=jax.ShapeDtypeStruct((2 * sy * sx * rows, outs), F32),
        in_specs=[VMEM_SPEC] * 2,
        out_specs=VMEM_SPEC,
        compiler_params=pltpu.CompilerParams(vmem_limit_bytes=4 * 2**20),
        cost_estimate=QUICK,
        name="lay_second",
    )(near, far)


def gather_steps(piece, axis):
    return [piece] + [shift(piece, axis, step) for step in STEPS[1:]]


def body(sky_cube, weight_first, weight_second, cotangent):
    cols, rows, chans = sky_cube.shape
    strip, _, outs = cotangent.shape
    chips = lax.axis_size("y")

    edges = jnp.concatenate(halo(sky_cube, SKY, 1), axis=1)
    far_cube = shift(sky_cube, "c", 1)
    far_weight = shift(weight_first, "c", 1)
    edges = jnp.transpose(edges, (1, 0, 2))
    far_edges = shift(edges, "c", 1)
    left, right = halo(cotangent, FREQ, 0)
    wide = spread(sky_cube, far_cube, edges, far_edges, chips)
    kernel = jnp.concatenate([weight_first, far_weight], axis=2).reshape(18 * chans, outs)

    on, off = 1, chips - 1
    cut = strip // 2 + 1
    far_a, far_b = conv_parts(((2, 0), (2, cut)), wide, kernel, cut, BF16)
    hold, left, right, _ = lax.optimization_barrier((wide, left, right, far_a))
    near_b, near_a = conv_parts(((on, cut), (off, 0)), hold, kernel, cut, BF16)
    got_a, got_b = shift(far_a, "y", on), shift(far_b, "y", off)
    late, left, right, _ = lax.optimization_barrier((cotangent, left, right, near_b))
    edges = row_halo([left, late, right])
    got_a, edges = lax.optimization_barrier((got_a, edges))
    both_a, both_b = conv_parts(((on, 0), (off, cut)), wide, kernel, cut, BF16, (got_a, got_b))
    own = conv_parts(((0, 0),), wide, kernel, strip + 2, F32)[0]
    from_a = shift(both_a, "y", on), shift(near_a, "y", off)
    from_b = shift(near_b, "y", on), shift(both_b, "y", off)

    back = back_tile(late, left, right, edges, weight_second)
    delta_a, delta_b, hidden = point(own, from_a, from_b, back)

    on_a, off_b = shift(delta_a, "y", on), shift(delta_b, "y", off)
    on_b, off_a = shift(delta_b, "y", on), shift(delta_a, "y", off)
    on_a, off_b, edges = lax.optimization_barrier((on_a, off_b, row_halo([hidden])))
    fwd_a, fwd_b = shift(on_a, "y", on), shift(off_b, "y", off)
    total = grad_strip(0, wide, (delta_a, delta_b), None, False)
    total = grad_strip(off, wide, (on_a, on_b), total, False)
    total = grad_strip(on, wide, (off_a, off_b), total, False)
    features, near, far = second_tile(hidden, edges, weight_second, cotangent, chips)
    far, fwd_a, fwd_b, total = lax.optimization_barrier((far, fwd_a, fwd_b, total))
    keep, *sends = fold(near, shift(far, "c", 1))
    for step, send in zip(STEPS[1:], sends):
        keep = keep + shift(send, "y", step).astype(F32)
    sx, sz = lax.axis_size("x"), lax.axis_size("z")
    second = keep.astype(BF16).reshape(3, sx, -1, outs)
    second = jnp.transpose(second, (1, 0, 2, 3)).reshape(sx, sz, -1, outs)
    second = jnp.transpose(second, (1, 0, 2, 3)).reshape(sx * sz, -1, outs)
    extra = second.shape[1]
    first_own, first_far = grad_strip(2, wide, (fwd_a, fwd_b), total, True)

    joined = join(first_own, shift(first_far, "c", 1), second)
    summed = lax.all_to_all(joined, SKY, 0, 0, tiled=True)
    summed = jnp.sum(summed.astype(F32), axis=0).astype(BF16)
    parts = gather_steps(order_pieces(gather_steps(summed, "z"), extra), "x")
    main = parts[0].shape[0] - sz * extra
    grad_first = lay_first(parts, sz, chans)
    share = jnp.stack([part[main:] for part in parts])
    share = jnp.stack(gather_steps(share, "y"))
    grad_second = lay_second(share, shift(share, "c", 1)).reshape(3, 3, outs, outs)
    return features, grad_first, grad_second


def solution(mesh):
    sizes = (mesh.devices.shape[0] // 2, 2, 4, mesh.devices.shape[1] // 4)
    fine = Mesh(mesh.devices.reshape(sizes), FREQ + SKY)
    return jax.shard_map(
        body,
        mesh=fine,
        in_specs=(P(None, SKY, FREQ), P(None, None, FREQ, None), P(), P(FREQ, SKY, None)),
        out_specs=(P(FREQ, SKY, None), P(None, None, FREQ, None), P()),
        check_vma=False,
    )
```

```python
import functools

import jax
import jax.numpy as jnp
from jax import lax
from jax.experimental import pallas as pl
from jax.experimental.pallas import tpu as pltpu
from jax.sharding import Mesh, PartitionSpec as P

FREQ = ("y", "c")
SKY = ("z", "x")
F32 = jnp.float32
BF16 = jnp.bfloat16
QUICK = pl.CostEstimate(flops=1, bytes_accessed=1, transcendentals=0)


def shift(x, axis, step):
    count = lax.axis_size(axis)
    return lax.ppermute(x, axis, [(i, (i + step) % count) for i in range(count)])


def spread_kernel(own_ref, far_ref, own_halo_ref, far_halo_ref, out_ref):
    chips, width, rows, depth = out_ref.shape
    cols, _, chans = own_ref.shape
    strip = cols // (2 * chips)
    core = lax.axis_index("c")
    step = 8
    row = lax.broadcasted_iota(jnp.int32, (step, rows, chans), 1)

    def block(i, base, chip):
        for side, (cube_ref, halo_ref) in enumerate(
            ((own_ref, own_halo_ref), (far_ref, far_halo_ref))
        ):
            at = pl.multiple_of(base + i * step, step)
            mid = cube_ref[pl.ds(at, step)]
            wide = mid.astype(F32).reshape(step * rows, chans)
            ahead = pltpu.roll(wide, 1, 0).reshape(step, rows, chans)
            behind = pltpu.roll(wide, step * rows - 1, 0).reshape(step, rows, chans)
            before = halo_ref[0, pl.ds(at, step), :].astype(F32)[:, None, :]
            after = halo_ref[1, pl.ds(at, step), :].astype(F32)[:, None, :]
            ahead = jnp.where(row == 0, before, ahead)
            behind = jnp.where(row == rows - 1, after, behind)
            to = pl.ds(2 + i * step, step)
            for tap, value in enumerate((ahead.astype(BF16), mid, behind.astype(BF16))):
                lane = (2 * tap + side) * chans
                out_ref[chip, to, :, lane : lane + chans] = value

    def edge(at, chip, slot):
        for side, (cube_ref, halo_ref) in enumerate(
            ((own_ref, own_halo_ref), (far_ref, far_halo_ref))
        ):
            first = pl.multiple_of((at // step) * step, step)
            mid = cube_ref[at]
            wide = mid.astype(F32)
            line = lax.broadcasted_iota(jnp.int32, (step, chans), 0) == at - first
            pick = lambda k: jnp.sum(
                jnp.where(line, halo_ref[k, pl.ds(first, step), :].astype(F32), 0.0),
                axis=0,
                keepdims=True,
            )
            place = lax.broadcasted_iota(jnp.int32, (rows, chans), 0)
            ahead = jnp.where(place == 0, pick(0), pltpu.roll(wide, 1, 0))
            behind = jnp.where(place == rows - 1, pick(1), pltpu.roll(wide, rows - 1, 0))
            for tap, value in enumerate((ahead.astype(BF16), mid, behind.astype(BF16))):
                lane = (2 * tap + side) * chans
                out_ref[chip, slot, :, lane : lane + chans] = value

    blank = jnp.zeros((rows, depth), BF16)
    for chip in range(chips):
        base = (2 * chip + core) * strip
        lax.fori_loop(0, strip // step, lambda i, _: block(i, base, chip), None)
        for slot in (0, 1):
            edge(jnp.maximum(base - 2 + slot, 0), chip, slot)
            edge(jnp.minimum(base + strip + slot, cols - 1), chip, strip + 2 + slot)
        for slot in range(strip + 4, width):
            out_ref[chip, slot] = blank

    @pl.when(core == 0)
    def _():
        out_ref[0, 0] = blank
        out_ref[0, 1] = blank

    @pl.when(core == 1)
    def _():
        out_ref[chips - 1, strip + 2] = blank
        out_ref[chips - 1, strip + 3] = blank


VMEM_SPEC = pl.BlockSpec(memory_space=pltpu.VMEM)


def spread(own, far, own_halo, far_halo, chips):
    cols, rows, chans = own.shape
    return pl.pallas_call(
        spread_kernel,
        out_shape=jax.ShapeDtypeStruct((chips, cols // (2 * chips) + 8, rows, 6 * chans), BF16),
        in_specs=[VMEM_SPEC] * 4,
        out_specs=VMEM_SPEC,
        compiler_params=pltpu.CompilerParams(vmem_limit_bytes=2 * 2**20),
        cost_estimate=QUICK,
        name="spread",
    )(own, far, own_halo, far_halo)


def chip_at(step):
    return lax.rem(lax.axis_index("y") + step, lax.axis_size("y"))


def conv_kernel(parts, adds, wide_ref, kernel_ref, *refs):
    rows = wide_ref.shape[2]
    for (step, first), add_ref, out_ref in zip(parts, refs[:adds] or [None] * len(parts), refs[adds:]):
        count, _, outs = out_ref.shape
        chip = chip_at(step)
        pieces = [wide_ref[chip, first + tap : first + tap + count] for tap in range(3)]
        lhs = jnp.concatenate(pieces, axis=-1).reshape(count * rows, -1)
        total = jnp.dot(lhs, kernel_ref[...], preferred_element_type=F32)
        total = total.reshape(count, rows, outs)
        if add_ref is not None:
            total = total + add_ref[...].astype(F32)
        out_ref[...] = total.astype(out_ref.dtype)


def conv_parts(parts, wide, kernel, count, dtype, adds=()):
    rows, outs = wide.shape[2], kernel.shape[1]
    return pl.pallas_call(
        functools.partial(conv_kernel, parts, len(adds)),
        out_shape=(jax.ShapeDtypeStruct((count, rows, outs), dtype),) * len(parts),
        in_specs=[VMEM_SPEC] * (2 + len(adds)),
        out_specs=(VMEM_SPEC,) * len(parts),
        compiler_params=pltpu.CompilerParams(vmem_limit_bytes=4 * 2**20),
        cost_estimate=QUICK,
        name="conv_first",
    )(wide, kernel, *adds)


def grad_kernel(step, has_old, last, wide_ref, a_ref, b_ref, *refs):
    old_ref = refs[0] if has_old else None
    outs_refs, pad_ref = refs[1 if has_old else 0 : -1], refs[-1]
    half, rows, outs = a_ref.shape
    strip = 2 * half
    cols, depth = wide_ref.shape[1], wide_ref.shape[3]
    pad_ref[0:3] = jnp.zeros((3, rows, outs), BF16)
    pad_ref[3 : 3 + half] = a_ref[...]
    pad_ref[3 + half : 3 + strip] = b_ref[...]
    pad_ref[3 + strip :] = jnp.zeros((cols - strip - 1, rows, outs), BF16)
    lhs = wide_ref[chip_at(step)].reshape(cols * rows, depth)
    rhs = jnp.concatenate(
        [pad_ref[2 - tap : 2 - tap + cols].reshape(cols * rows, outs) for tap in range(3)], axis=-1
    )
    total = lax.dot_general(lhs, rhs, (((0,), (0,)), ((), ())), preferred_element_type=F32)
    if has_old:
        total = total + old_ref[...]
    if not last:
        outs_refs[0][...] = total
    else:
        chans = depth // 6
        for tap in range(3):
            at = 2 * tap * chans
            outs_refs[0][tap * chans : (tap + 1) * chans] = total[at : at + chans]
            outs_refs[1][tap * chans : (tap + 1) * chans] = total[
                at + chans : at + 2 * chans
            ].astype(BF16)


def grad_strip(step, wide, halves, old, last):
    _, rows, outs = halves[0].shape
    depth, cols = wide.shape[3], wide.shape[1]
    shape = (depth, 3 * outs)
    half = (depth // 2, 3 * outs)
    if last:
        out_shape = (jax.ShapeDtypeStruct(half, F32), jax.ShapeDtypeStruct(half, BF16))
    else:
        out_shape = (jax.ShapeDtypeStruct(shape, F32),)
    args = [wide, *halves] + ([old] if old is not None else [])
    out = pl.pallas_call(
        functools.partial(grad_kernel, step, old is not None, last),
        out_shape=out_shape,
        in_specs=[VMEM_SPEC] * len(args),
        out_specs=tuple([VMEM_SPEC] * len(out_shape)),
        scratch_shapes=[pltpu.VMEM((cols + 2, rows, outs), BF16)],
        compiler_params=pltpu.CompilerParams(vmem_limit_bytes=5 * 2**20),
        cost_estimate=QUICK,
        name="grad_first",
    )(*args)
    return out if last else out[0]


def spread_tile(columns, wide_ref):
    rows, chans = wide_ref.shape[1], wide_ref.shape[2] // 3
    place = lax.broadcasted_iota(jnp.int32, (rows, chans), 0)
    for j, (mid, before, after) in enumerate(columns):
        wide = mid.astype(F32)
        ahead = jnp.where(place == 0, before.astype(F32), pltpu.roll(wide, 1, 0))
        behind = jnp.where(place == rows - 1, after.astype(F32), pltpu.roll(wide, rows - 1, 0))
        wide_ref[j, :, 0:chans] = ahead.astype(BF16)
        wide_ref[j, :, chans : 2 * chans] = mid
        wide_ref[j, :, 2 * chans :] = behind.astype(BF16)


def back_kernel(cot_ref, left_ref, right_ref, edge_ref, kernel_ref, out_ref, wide_ref):
    cols, rows, chans = cot_ref.shape
    start = edge_ref.shape[1] - 2 * cols

    def beside(k, j):
        low, high = start + j, start + cols + j
        return jnp.concatenate(
            [edge_ref[k, low : low + 1, :], edge_ref[k, high : high + 1, :]], axis=-1
        )

    def whole(ref):
        return ref[0:rows], ref[rows : rows + 1], ref[rows + 1 : rows + 2]

    columns = [(cot_ref[j], beside(0, j), beside(1, j)) for j in range(cols)]
    spread_tile([whole(left_ref)] + columns + [whole(right_ref)], wide_ref)
    total = None
    for tap_col in range(3):
        lhs = wide_ref[tap_col : tap_col + cols].reshape(cols * rows, 3 * chans)
        for tap_row in range(3):
            part = lax.dot_general(
                lhs[:, tap_row * chans : (tap_row + 1) * chans],
                kernel_ref[2 - tap_col, 2 - tap_row],
                (((1,), (1,)), ((), ())),
                preferred_element_type=F32,
            )
            total = part if total is None else total + part
    out_ref[...] = total.reshape(cols, rows, -1)


def back_tile(tile, left, right, edges, kernel):
    cols, rows, chans = tile.shape
    return pl.pallas_call(
        back_kernel,
        out_shape=jax.ShapeDtypeStruct((cols, rows, kernel.shape[2]), F32),
        in_specs=[VMEM_SPEC] * 5,
        out_specs=VMEM_SPEC,
        scratch_shapes=[pltpu.VMEM((cols + 2, rows, 3 * chans), BF16)],
        compiler_params=pltpu.CompilerParams(vmem_limit_bytes=4 * 2**20),
        cost_estimate=QUICK,
        name="back",
    )(tile, left, right, edges, kernel)


def second_kernel(
    chips, hid_ref, edge_ref, kernel_ref, cot_ref,
    out_ref, near_ref, far_ref, wide_ref, pad_ref, sum_ref,
):
    chans = hid_ref.shape[2]
    cols, rows, outs = cot_ref.shape
    width = wide_ref.shape[0]
    core = lax.axis_index("c")
    columns = [
        (hid_ref[j], edge_ref[0, j : j + 1, :], edge_ref[1, j : j + 1, :]) for j in range(cols + 2)
    ]
    spread_tile(columns, wide_ref)
    wide_ref[cols + 2 :] = jnp.zeros((width - cols - 2, rows, 3 * chans), BF16)
    pieces = [wide_ref[tap : tap + cols] for tap in range(3)]
    lhs = jnp.concatenate(pieces, axis=-1).reshape(cols * rows, 9 * chans)
    total = jnp.dot(lhs, kernel_ref[...], preferred_element_type=F32)
    out_ref[...] = total.reshape(cols, rows, outs).astype(BF16)

    pad_ref[0:2] = jnp.zeros((2, rows, outs), BF16)
    pad_ref[2 : 2 + cols] = cot_ref[...]
    pad_ref[2 + cols :] = jnp.zeros((width - cols, rows, outs), BF16)
    rhs = jnp.concatenate(
        [pad_ref[2 - tap : 2 - tap + width].reshape(width * rows, outs) for tap in range(3)],
        axis=-1,
    )
    sum_ref[...] = lax.dot_general(
        wide_ref[...].reshape(width * rows, 3 * chans),
        rhs,
        (((0,), (0,)), ((), ())),
        preferred_element_type=F32,
    )
    size = sum_ref.shape[0] // (2 * chips)
    for half, ref in ((core, near_ref), (1 - core, far_ref)):
        for chip in range(chips):
            at = pl.multiple_of((half * chips + chip) * size, size)
            for tap in range(3):
                ref[chip, tap * size : (tap + 1) * size, :] = sum_ref[
                    pl.ds(at, size), tap * outs : (tap + 1) * outs
                ].astype(ref.dtype)


def second_tile(tile, edges, kernel, cotangent, chips):
    chans = tile.shape[2]
    cols, rows, outs = cotangent.shape
    width = cols + 8
    cut = (chips, 9 * chans // (2 * chips), outs)
    return pl.pallas_call(
        functools.partial(second_kernel, chips),
        out_shape=(
            jax.ShapeDtypeStruct((cols, rows, outs), BF16),
            jax.ShapeDtypeStruct(cut, F32),
            jax.ShapeDtypeStruct(cut, BF16),
        ),
        in_specs=[VMEM_SPEC] * 4,
        out_specs=(VMEM_SPEC,) * 3,
        scratch_shapes=[
            pltpu.VMEM((width, rows, 3 * chans), BF16),
            pltpu.VMEM((width + 2, rows, outs), BF16),
            pltpu.VMEM((3 * chans, 3 * outs), F32),
        ],
        compiler_params=pltpu.CompilerParams(vmem_limit_bytes=9 * 2**20),
        cost_estimate=QUICK,
        name="second",
    )(tile, edges, kernel.reshape(9 * chans, outs), cotangent)


def point_kernel(own_ref, a0_ref, a1_ref, b0_ref, b1_ref, back_ref, da_ref, db_ref, hidden_ref):
    cols = own_ref.shape[0]
    half = da_ref.shape[0]
    strip = 2 * lax.axis_index("y") + lax.axis_index("c")
    strips = 2 * lax.axis_size("y")

    def column(j, i, refs, delta_ref, keep):
        pre = own_ref[j] + refs[0][i].astype(F32) + refs[1][i].astype(F32)
        sigma = jax.nn.sigmoid(pre)
        hidden = pre * sigma
        if keep is not None:
            hidden = jnp.where(keep, hidden, 0.0)
        hidden_ref[j] = hidden.astype(BF16)
        if keep is None:
            slope = sigma * (1.0 + pre * (1.0 - sigma))
            at = j - 1 if delta_ref is da_ref else j - 1 - half
            delta_ref[at] = (back_ref[j - 1] * slope).astype(BF16)

    left, right = (a0_ref, a1_ref), (b0_ref, b1_ref)
    column(0, 0, left, None, strip > 0)
    column(cols - 1, half, right, None, strip < strips - 1)

    def each(i, _):
        column(i, i, left, da_ref, None)
        column(half + i, i - 1, right, db_ref, None)

    lax.fori_loop(1, half + 1, each, None)


def point(own, left, right, back):
    strip, rows, outs = back.shape
    cut = jax.ShapeDtypeStruct((strip // 2, rows, outs), BF16)
    return pl.pallas_call(
        point_kernel,
        out_shape=(cut, cut, jax.ShapeDtypeStruct(own.shape, BF16)),
        in_specs=[VMEM_SPEC] * 6,
        out_specs=(VMEM_SPEC,) * 3,
        compiler_params=pltpu.CompilerParams(vmem_limit_bytes=2 * 2**20),
        cost_estimate=QUICK,
        name="point",
    )(own, *left, *right, back)


def fold_kernel(near_ref, got_ref, keep_ref, *send_refs):
    chips = near_ref.shape[0]
    here = lax.axis_index("y")
    keep_ref[...] = near_ref[here] + got_ref[here].astype(F32)
    for step, ref in zip(STEPS[1:], send_refs):
        to = lax.rem(here + step, chips)
        ref[...] = (near_ref[to] + got_ref[to].astype(F32)).astype(BF16)


def fold(near, got):
    shape = near.shape[1:]
    return pl.pallas_call(
        fold_kernel,
        out_shape=(jax.ShapeDtypeStruct(shape, F32),) + (jax.ShapeDtypeStruct(shape, BF16),) * 3,
        in_specs=[VMEM_SPEC] * 2,
        out_specs=(VMEM_SPEC,) * 4,
        compiler_params=pltpu.CompilerParams(vmem_limit_bytes=2 * 2**20),
        cost_estimate=QUICK,
        name="fold",
    )(near, got)


def row_halo(ends):
    count = lax.axis_size(SKY)
    up = [(i, i + 1) for i in range(count - 1)]
    down = [(j, i) for i, j in up]
    return jnp.stack([lax.ppermute(ends[0], SKY, up), lax.ppermute(ends[1], SKY, down)])


def join_kernel(own_ref, far_ref, keep_ref, a_ref, b_ref, c_ref, out_ref):
    pieces, total, outs = out_ref.shape
    chans = own_ref.shape[0] // 3
    size = chans // pieces
    for tap_col in range(3):
        for tap_row in range(3):
            rows = slice(tap_row * chans, (tap_row + 1) * chans)
            lanes = slice(tap_col * outs, (tap_col + 1) * outs)
            value = own_ref[rows, lanes] + far_ref[rows, lanes].astype(F32)
            at = (3 * tap_col + tap_row) * size
            out_ref[:, at : at + size, :] = value.reshape(pieces, size, outs).astype(BF16)
    second = keep_ref[...]
    for ref in (a_ref, b_ref, c_ref):
        second = second + ref[...].astype(F32)
    sx = lax.axis_size("x")
    sz = pieces // sx
    third = second.shape[0] // 3
    size_x = third // sx
    extra = total - 9 * size
    for x in range(sx):
        value = jnp.concatenate(
            [second[tap * third + x * size_x : tap * third + (x + 1) * size_x] for tap in range(3)],
            axis=0,
        )
        for z in range(sz):
            out_ref[z * sx + x, 9 * size :, :] = value[z * extra : (z + 1) * extra].astype(BF16)


def join(own, far, keep, got, pieces):
    outs = keep.shape[1]
    rows = 9 * (own.shape[0] // 3 // pieces) + keep.shape[0] // pieces
    return pl.pallas_call(
        join_kernel,
        out_shape=jax.ShapeDtypeStruct((pieces, rows, outs), BF16),
        in_specs=[VMEM_SPEC] * 6,
        out_specs=VMEM_SPEC,
        compiler_params=pltpu.CompilerParams(vmem_limit_bytes=4 * 2**20),
        cost_estimate=QUICK,
        name="join",
    )(own, far, keep, *got)


STEPS = (0, 1, 3, 2)


def order_kernel(extra, a_ref, b_ref, c_ref, d_ref, out_ref):
    rows = a_ref.shape[0] - extra
    sz = lax.axis_size("z")
    me = lax.axis_index("z")
    values = [ref[...].astype(F32) for ref in (a_ref, b_ref, c_ref, d_ref)]
    rest = []
    for z in range(len(STEPS)):
        value = values[0]
        for step, other in zip(STEPS[1:], values[1:]):
            value = jnp.where(lax.rem(me + sz - step, sz) == z, other, value)
        out_ref[z * rows : (z + 1) * rows, :] = value[:rows].astype(BF16)
        rest.append(value[rows:])
    out_ref[len(STEPS) * rows :, :] = jnp.concatenate(rest, axis=0).astype(BF16)


def order_pieces(parts, extra):
    rows, outs = parts[0].shape
    return pl.pallas_call(
        functools.partial(order_kernel, extra),
        out_shape=jax.ShapeDtypeStruct((4 * rows, outs), BF16),
        in_specs=[VMEM_SPEC] * 4,
        out_specs=VMEM_SPEC,
        compiler_params=pltpu.CompilerParams(vmem_limit_bytes=4 * 2**20),
        cost_estimate=QUICK,
        name="order_pieces",
    )(*parts)


def first_kernel(sz, a_ref, b_ref, c_ref, d_ref, out_ref):
    sx = lax.axis_size("x")
    size = out_ref.shape[2] // (sx * sz)
    me = lax.axis_index("x")
    for step, ref in zip(STEPS, (a_ref, b_ref, c_ref, d_ref)):
        x = lax.rem(me + sx - step, sx)
        value = ref[...].astype(F32)
        for z in range(sz):
            at = pl.multiple_of((z * sx + x) * size, size)
            for tap in range(9):
                rows = (z * 9 + tap) * size
                out_ref[tap // 3, tap % 3, pl.ds(at, size), :] = value[rows : rows + size]


def lay_first(parts, sz, chans):
    outs = parts[0].shape[1]
    return pl.pallas_call(
        functools.partial(first_kernel, sz),
        out_shape=jax.ShapeDtypeStruct((3, 3, chans, outs), F32),
        in_specs=[VMEM_SPEC] * 4,
        out_specs=VMEM_SPEC,
        compiler_params=pltpu.CompilerParams(vmem_limit_bytes=4 * 2**20),
        cost_estimate=QUICK,
        name="lay_first",
    )(*parts)


def lay_second_kernel(near_ref, far_ref, out_ref):
    sy, sx, rows, _ = near_ref.shape
    size = rows // 3
    third = out_ref.shape[0] // 3
    core, y, x = lax.axis_index("c"), lax.axis_index("y"), lax.axis_index("x")
    for half, ref in ((core, near_ref), (1 - core, far_ref)):
        for i in range(sy):
            for j in range(sx):
                place = (half * sy + lax.rem(y + sy - STEPS[i], sy)) * sx
                place = place + lax.rem(x + sx - STEPS[j], sx)
                value = ref[i, j].astype(F32)
                for tap in range(3):
                    at = pl.multiple_of(tap * third + place * size, 8)
                    out_ref[pl.ds(at, size), :] = value[tap * size : (tap + 1) * size]


def lay_second(near, far):
    sy, sx, rows, outs = near.shape
    return pl.pallas_call(
        lay_second_kernel,
        out_shape=jax.ShapeDtypeStruct((2 * sy * sx * rows, outs), F32),
        in_specs=[VMEM_SPEC] * 2,
        out_specs=VMEM_SPEC,
        compiler_params=pltpu.CompilerParams(vmem_limit_bytes=4 * 2**20),
        cost_estimate=QUICK,
        name="lay_second",
    )(near, far)


def gather_steps(piece, axis):
    return [piece] + [shift(piece, axis, step) for step in STEPS[1:]]


def body(sky_cube, weight_first, weight_second, cotangent):
    cols, rows, chans = sky_cube.shape
    strip, _, outs = cotangent.shape
    chips = lax.axis_size("y")

    ends = [
        jnp.concatenate(
            [sky_cube[:, r], cotangent[:, r, : outs // 2], cotangent[:, r, outs // 2 :]], axis=0
        )
        for r in (rows - 1, 0)
    ]
    edges = row_halo(ends)
    far_cube = shift(sky_cube, "c", 1)
    far_weight = shift(weight_first, "c", 1)
    far_edges = shift(edges, "c", 1)
    wide = spread(sky_cube, far_cube, edges, far_edges, chips)
    kernel = jnp.concatenate([weight_first, far_weight], axis=2).reshape(18 * chans, outs)

    def side(col):
        beside = [
            jnp.concatenate(
                [edges[k, at + col : at + col + 1] for at in (cols, cols + strip)], axis=1
            )
            for k in range(2)
        ]
        return jnp.concatenate([cotangent[col]] + beside, axis=0)

    count = lax.axis_size(FREQ)
    up = [(i, i + 1) for i in range(count - 1)]
    down = [(j, i) for i, j in up]
    left = lax.ppermute(side(strip - 1), FREQ, up)
    right = lax.ppermute(side(0), FREQ, down)

    on, off = 1, chips - 1
    cut = strip // 2 + 1
    far_a, far_b = conv_parts(((2, 0), (2, cut)), wide, kernel, cut, BF16)
    hold, _ = lax.optimization_barrier((wide, far_a))
    near_b, near_a = conv_parts(((on, cut), (off, 0)), hold, kernel, cut, BF16)
    got_a, got_b = shift(far_a, "y", on), shift(far_b, "y", off)
    got_a, left, right = lax.optimization_barrier((got_a, left, right))
    both_a, both_b = conv_parts(((on, 0), (off, cut)), wide, kernel, cut, BF16, (got_a, got_b))
    own = conv_parts(((0, 0),), wide, kernel, strip + 2, F32)[0]
    from_a = shift(both_a, "y", on), shift(near_a, "y", off)
    from_b = shift(near_b, "y", on), shift(both_b, "y", off)

    back = back_tile(cotangent, left, right, edges, weight_second)
    delta_a, delta_b, hidden = point(own, from_a, from_b, back)

    on_a, off_b = shift(delta_a, "y", on), shift(delta_b, "y", off)
    on_b, off_a = shift(delta_b, "y", on), shift(delta_a, "y", off)
    on_a, off_b, edges = lax.optimization_barrier(
        (on_a, off_b, row_halo([hidden[:, rows - 1], hidden[:, 0]]))
    )
    fwd_a, fwd_b = shift(on_a, "y", on), shift(off_b, "y", off)
    total = grad_strip(0, wide, (delta_a, delta_b), None, False)
    features, near, far = second_tile(hidden, edges, weight_second, cotangent, chips)
    far, on_b, off_a = lax.optimization_barrier((far, on_b, off_a))
    keep, *sends = fold(near, shift(far, "c", 1))
    got = [shift(send, "y", step) for step, send in zip(STEPS[1:], sends)]
    total = grad_strip(off, wide, (on_a, on_b), total, False)
    total = grad_strip(on, wide, (off_a, off_b), total, False)
    first_own, first_far = grad_strip(2, wide, (fwd_a, fwd_b), total, True)

    sx, sz = lax.axis_size("x"), lax.axis_size("z")
    joined = join(first_own, shift(first_far, "c", 1), keep, got, sx * sz)
    extra = keep.shape[0] // (sx * sz)
    summed = lax.all_to_all(joined, SKY, 0, 0, tiled=True)
    summed = jnp.sum(summed.astype(F32), axis=0).astype(BF16)
    parts = gather_steps(order_pieces(gather_steps(summed, "z"), extra), "x")
    main = parts[0].shape[0] - sz * extra
    grad_first = lay_first(parts, sz, chans)
    share = jnp.stack([part[main:] for part in parts])
    share = jnp.stack(gather_steps(share, "y"))
    grad_second = lay_second(share, shift(share, "c", 1)).reshape(3, 3, outs, outs)
    return features, grad_first, grad_second


def solution(mesh):
    sizes = (mesh.devices.shape[0] // 2, 2, 4, mesh.devices.shape[1] // 4)
    fine = Mesh(mesh.devices.reshape(sizes), FREQ + SKY)
    return jax.shard_map(
        body,
        mesh=fine,
        in_specs=(P(None, SKY, FREQ), P(None, None, FREQ, None), P(), P(FREQ, SKY, None)),
        out_specs=(P(FREQ, SKY, None), P(None, None, FREQ, None), P()),
        check_vma=False,
    )
```

```python
import functools

import jax
import jax.numpy as jnp
from jax import lax
from jax.experimental import pallas as pl
from jax.experimental.pallas import tpu as pltpu
from jax.sharding import Mesh, PartitionSpec as P

FREQ = ("y", "c")
SKY = ("z", "x")
F32 = jnp.float32
BF16 = jnp.bfloat16
QUICK = pl.CostEstimate(flops=1, bytes_accessed=1, transcendentals=0)


def shift(x, axis, step):
    count = lax.axis_size(axis)
    return lax.ppermute(x, axis, [(i, (i + step) % count) for i in range(count)])


def spread_kernel(own_ref, far_ref, own_halo_ref, far_halo_ref, out_ref):
    chips, width, rows, depth = out_ref.shape
    cols, _, chans = own_ref.shape
    strip = cols // (2 * chips)
    core = lax.axis_index("c")
    step = 8
    row = lax.broadcasted_iota(jnp.int32, (step, rows, chans), 1)

    def block(i, base, chip):
        for side, (cube_ref, halo_ref) in enumerate(
            ((own_ref, own_halo_ref), (far_ref, far_halo_ref))
        ):
            at = pl.multiple_of(base + i * step, step)
            mid = cube_ref[pl.ds(at, step)]
            wide = mid.astype(F32).reshape(step * rows, chans)
            ahead = pltpu.roll(wide, 1, 0).reshape(step, rows, chans)
            behind = pltpu.roll(wide, step * rows - 1, 0).reshape(step, rows, chans)
            before = halo_ref[0, pl.ds(at, step), :].astype(F32)[:, None, :]
            after = halo_ref[1, pl.ds(at, step), :].astype(F32)[:, None, :]
            ahead = jnp.where(row == 0, before, ahead)
            behind = jnp.where(row == rows - 1, after, behind)
            to = pl.ds(2 + i * step, step)
            for tap, value in enumerate((ahead.astype(BF16), mid, behind.astype(BF16))):
                lane = (2 * tap + side) * chans
                out_ref[chip, to, :, lane : lane + chans] = value

    def edge(at, chip, slot):
        for side, (cube_ref, halo_ref) in enumerate(
            ((own_ref, own_halo_ref), (far_ref, far_halo_ref))
        ):
            first = pl.multiple_of((at // step) * step, step)
            mid = cube_ref[at]
            wide = mid.astype(F32)
            line = lax.broadcasted_iota(jnp.int32, (step, chans), 0) == at - first
            pick = lambda k: jnp.sum(
                jnp.where(line, halo_ref[k, pl.ds(first, step), :].astype(F32), 0.0),
                axis=0,
                keepdims=True,
            )
            place = lax.broadcasted_iota(jnp.int32, (rows, chans), 0)
            ahead = jnp.where(place == 0, pick(0), pltpu.roll(wide, 1, 0))
            behind = jnp.where(place == rows - 1, pick(1), pltpu.roll(wide, rows - 1, 0))
            for tap, value in enumerate((ahead.astype(BF16), mid, behind.astype(BF16))):
                lane = (2 * tap + side) * chans
                out_ref[chip, slot, :, lane : lane + chans] = value

    blank = jnp.zeros((rows, depth), BF16)
    for chip in range(chips):
        base = (2 * chip + core) * strip
        lax.fori_loop(0, strip // step, lambda i, _: block(i, base, chip), None)
        for slot in (0, 1):
            edge(jnp.maximum(base - 2 + slot, 0), chip, slot)
            edge(jnp.minimum(base + strip + slot, cols - 1), chip, strip + 2 + slot)
        for slot in range(strip + 4, width):
            out_ref[chip, slot] = blank

    @pl.when(core == 0)
    def _():
        out_ref[0, 0] = blank
        out_ref[0, 1] = blank

    @pl.when(core == 1)
    def _():
        out_ref[chips - 1, strip + 2] = blank
        out_ref[chips - 1, strip + 3] = blank


VMEM_SPEC = pl.BlockSpec(memory_space=pltpu.VMEM)


def spread(own, far, own_halo, far_halo, chips):
    cols, rows, chans = own.shape
    return pl.pallas_call(
        spread_kernel,
        out_shape=jax.ShapeDtypeStruct((chips, cols // (2 * chips) + 8, rows, 6 * chans), BF16),
        in_specs=[VMEM_SPEC] * 4,
        out_specs=VMEM_SPEC,
        compiler_params=pltpu.CompilerParams(vmem_limit_bytes=2 * 2**20),
        cost_estimate=QUICK,
        name="spread",
    )(own, far, own_halo, far_halo)


def chip_at(step):
    return lax.rem(lax.axis_index("y") + step, lax.axis_size("y"))


def conv_kernel(parts, adds, wide_ref, kernel_ref, *refs):
    rows = wide_ref.shape[2]
    for (step, first), add_ref, out_ref in zip(parts, refs[:adds] or [None] * len(parts), refs[adds:]):
        count, _, outs = out_ref.shape
        chip = chip_at(step)
        pieces = [wide_ref[chip, first + tap : first + tap + count] for tap in range(3)]
        lhs = jnp.concatenate(pieces, axis=-1).reshape(count * rows, -1)
        total = jnp.dot(lhs, kernel_ref[...], preferred_element_type=F32)
        total = total.reshape(count, rows, outs)
        if add_ref is not None:
            total = total + add_ref[...].astype(F32)
        out_ref[...] = total.astype(out_ref.dtype)


def conv_parts(parts, wide, kernel, count, dtype, adds=()):
    rows, outs = wide.shape[2], kernel.shape[1]
    return pl.pallas_call(
        functools.partial(conv_kernel, parts, len(adds)),
        out_shape=(jax.ShapeDtypeStruct((count, rows, outs), dtype),) * len(parts),
        in_specs=[VMEM_SPEC] * (2 + len(adds)),
        out_specs=(VMEM_SPEC,) * len(parts),
        compiler_params=pltpu.CompilerParams(vmem_limit_bytes=4 * 2**20),
        cost_estimate=QUICK,
        name="conv_first",
    )(wide, kernel, *adds)


def grad_kernel(step, has_old, last, wide_ref, a_ref, b_ref, *refs):
    old_ref = refs[0] if has_old else None
    outs_refs, pad_ref = refs[1 if has_old else 0 : -1], refs[-1]
    half, rows, outs = a_ref.shape
    strip = 2 * half
    cols, depth = wide_ref.shape[1], wide_ref.shape[3]
    pad_ref[0:3] = jnp.zeros((3, rows, outs), BF16)
    pad_ref[3 : 3 + half] = a_ref[...]
    pad_ref[3 + half : 3 + strip] = b_ref[...]
    pad_ref[3 + strip :] = jnp.zeros((cols - strip - 1, rows, outs), BF16)
    lhs = wide_ref[chip_at(step)].reshape(cols * rows, depth)
    rhs = jnp.concatenate(
        [pad_ref[2 - tap : 2 - tap + cols].reshape(cols * rows, outs) for tap in range(3)], axis=-1
    )
    total = lax.dot_general(lhs, rhs, (((0,), (0,)), ((), ())), preferred_element_type=F32)
    if has_old:
        total = total + old_ref[...]
    if not last:
        outs_refs[0][...] = total
    else:
        chans = depth // 6
        for tap in range(3):
            at = 2 * tap * chans
            outs_refs[0][tap * chans : (tap + 1) * chans] = total[at : at + chans]
            outs_refs[1][tap * chans : (tap + 1) * chans] = total[
                at + chans : at + 2 * chans
            ].astype(BF16)


def grad_strip(step, wide, halves, old, last):
    _, rows, outs = halves[0].shape
    depth, cols = wide.shape[3], wide.shape[1]
    shape = (depth, 3 * outs)
    half = (depth // 2, 3 * outs)
    if last:
        out_shape = (jax.ShapeDtypeStruct(half, F32), jax.ShapeDtypeStruct(half, BF16))
    else:
        out_shape = (jax.ShapeDtypeStruct(shape, F32),)
    args = [wide, *halves] + ([old] if old is not None else [])
    out = pl.pallas_call(
        functools.partial(grad_kernel, step, old is not None, last),
        out_shape=out_shape,
        in_specs=[VMEM_SPEC] * len(args),
        out_specs=tuple([VMEM_SPEC] * len(out_shape)),
        scratch_shapes=[pltpu.VMEM((cols + 2, rows, outs), BF16)],
        compiler_params=pltpu.CompilerParams(vmem_limit_bytes=5 * 2**20),
        cost_estimate=QUICK,
        name="grad_first",
    )(*args)
    return out if last else out[0]


def spread_tile(columns, wide_ref):
    rows, chans = wide_ref.shape[1], wide_ref.shape[2] // 3
    place = lax.broadcasted_iota(jnp.int32, (rows, chans), 0)
    for j, (mid, before, after) in enumerate(columns):
        wide = mid.astype(F32)
        ahead = jnp.where(place == 0, before.astype(F32), pltpu.roll(wide, 1, 0))
        behind = jnp.where(place == rows - 1, after.astype(F32), pltpu.roll(wide, rows - 1, 0))
        wide_ref[j, :, 0:chans] = ahead.astype(BF16)
        wide_ref[j, :, chans : 2 * chans] = mid
        wide_ref[j, :, 2 * chans :] = behind.astype(BF16)


def back_kernel(cot_ref, left_ref, right_ref, edge_ref, kernel_ref, out_ref, wide_ref):
    cols, rows, chans = cot_ref.shape
    start = edge_ref.shape[1] - 2 * cols

    def beside(k, j):
        low, high = start + j, start + cols + j
        return jnp.concatenate(
            [edge_ref[k, low : low + 1, :], edge_ref[k, high : high + 1, :]], axis=-1
        )

    def whole(ref):
        return ref[0:rows], ref[rows : rows + 1], ref[rows + 1 : rows + 2]

    columns = [(cot_ref[j], beside(0, j), beside(1, j)) for j in range(cols)]
    spread_tile([whole(left_ref)] + columns + [whole(right_ref)], wide_ref)
    total = None
    for tap_col in range(3):
        lhs = wide_ref[tap_col : tap_col + cols].reshape(cols * rows, 3 * chans)
        for tap_row in range(3):
            part = lax.dot_general(
                lhs[:, tap_row * chans : (tap_row + 1) * chans],
                kernel_ref[2 - tap_col, 2 - tap_row],
                (((1,), (1,)), ((), ())),
                preferred_element_type=F32,
            )
            total = part if total is None else total + part
    out_ref[...] = total.reshape(cols, rows, -1)


def back_tile(tile, left, right, edges, kernel):
    cols, rows, chans = tile.shape
    return pl.pallas_call(
        back_kernel,
        out_shape=jax.ShapeDtypeStruct((cols, rows, kernel.shape[2]), F32),
        in_specs=[VMEM_SPEC] * 5,
        out_specs=VMEM_SPEC,
        scratch_shapes=[pltpu.VMEM((cols + 2, rows, 3 * chans), BF16)],
        compiler_params=pltpu.CompilerParams(vmem_limit_bytes=4 * 2**20),
        cost_estimate=QUICK,
        name="back",
    )(tile, left, right, edges, kernel)


def second_kernel(
    chips, hid_ref, edge_ref, kernel_ref, cot_ref,
    out_ref, near_ref, far_ref, wide_ref, pad_ref, sum_ref,
):
    chans = hid_ref.shape[2]
    cols, rows, outs = cot_ref.shape
    width = wide_ref.shape[0]
    core = lax.axis_index("c")
    columns = [
        (hid_ref[j], edge_ref[0, j : j + 1, :], edge_ref[1, j : j + 1, :]) for j in range(cols + 2)
    ]
    spread_tile(columns, wide_ref)
    wide_ref[cols + 2 :] = jnp.zeros((width - cols - 2, rows, 3 * chans), BF16)
    pieces = [wide_ref[tap : tap + cols] for tap in range(3)]
    lhs = jnp.concatenate(pieces, axis=-1).reshape(cols * rows, 9 * chans)
    total = jnp.dot(lhs, kernel_ref[...], preferred_element_type=F32)
    out_ref[...] = total.reshape(cols, rows, outs).astype(BF16)

    pad_ref[0:2] = jnp.zeros((2, rows, outs), BF16)
    pad_ref[2 : 2 + cols] = cot_ref[...]
    pad_ref[2 + cols :] = jnp.zeros((width - cols, rows, outs), BF16)
    rhs = jnp.concatenate(
        [pad_ref[2 - tap : 2 - tap + width].reshape(width * rows, outs) for tap in range(3)],
        axis=-1,
    )
    sum_ref[...] = lax.dot_general(
        wide_ref[...].reshape(width * rows, 3 * chans),
        rhs,
        (((0,), (0,)), ((), ())),
        preferred_element_type=F32,
    )
    size = sum_ref.shape[0] // (2 * chips)
    for half, ref in ((core, near_ref), (1 - core, far_ref)):
        for chip in range(chips):
            at = pl.multiple_of((half * chips + chip) * size, size)
            for tap in range(3):
                ref[chip, tap * size : (tap + 1) * size, :] = sum_ref[
                    pl.ds(at, size), tap * outs : (tap + 1) * outs
                ].astype(ref.dtype)


def second_tile(tile, edges, kernel, cotangent, chips):
    chans = tile.shape[2]
    cols, rows, outs = cotangent.shape
    width = cols + 8
    cut = (chips, 9 * chans // (2 * chips), outs)
    return pl.pallas_call(
        functools.partial(second_kernel, chips),
        out_shape=(
            jax.ShapeDtypeStruct((cols, rows, outs), BF16),
            jax.ShapeDtypeStruct(cut, F32),
            jax.ShapeDtypeStruct(cut, BF16),
        ),
        in_specs=[VMEM_SPEC] * 4,
        out_specs=(VMEM_SPEC,) * 3,
        scratch_shapes=[
            pltpu.VMEM((width, rows, 3 * chans), BF16),
            pltpu.VMEM((width + 2, rows, outs), BF16),
            pltpu.VMEM((3 * chans, 3 * outs), F32),
        ],
        compiler_params=pltpu.CompilerParams(vmem_limit_bytes=9 * 2**20),
        cost_estimate=QUICK,
        name="second",
    )(tile, edges, kernel.reshape(9 * chans, outs), cotangent)


def point_kernel(own_ref, a0_ref, a1_ref, b0_ref, b1_ref, back_ref, da_ref, db_ref, hidden_ref):
    cols = own_ref.shape[0]
    half = da_ref.shape[0]
    strip = 2 * lax.axis_index("y") + lax.axis_index("c")
    strips = 2 * lax.axis_size("y")

    def column(j, i, refs, delta_ref, keep):
        pre = own_ref[j] + refs[0][i].astype(F32) + refs[1][i].astype(F32)
        sigma = jax.nn.sigmoid(pre)
        hidden = pre * sigma
        if keep is not None:
            hidden = jnp.where(keep, hidden, 0.0)
        hidden_ref[j] = hidden.astype(BF16)
        if keep is None:
            slope = sigma * (1.0 + pre * (1.0 - sigma))
            at = j - 1 if delta_ref is da_ref else j - 1 - half
            delta_ref[at] = (back_ref[j - 1] * slope).astype(BF16)

    left, right = (a0_ref, a1_ref), (b0_ref, b1_ref)
    column(0, 0, left, None, strip > 0)
    column(cols - 1, half, right, None, strip < strips - 1)

    def each(i, _):
        column(i, i, left, da_ref, None)
        column(half + i, i - 1, right, db_ref, None)

    lax.fori_loop(1, half + 1, each, None)


def point(own, left, right, back):
    strip, rows, outs = back.shape
    cut = jax.ShapeDtypeStruct((strip // 2, rows, outs), BF16)
    return pl.pallas_call(
        point_kernel,
        out_shape=(cut, cut, jax.ShapeDtypeStruct(own.shape, BF16)),
        in_specs=[VMEM_SPEC] * 6,
        out_specs=(VMEM_SPEC,) * 3,
        compiler_params=pltpu.CompilerParams(vmem_limit_bytes=2 * 2**20),
        cost_estimate=QUICK,
        name="point",
    )(own, *left, *right, back)


def fold_kernel(near_ref, got_ref, keep_ref, *send_refs):
    chips = near_ref.shape[0]
    here = lax.axis_index("y")
    keep_ref[...] = near_ref[here] + got_ref[here].astype(F32)
    for step, ref in zip(STEPS[1:], send_refs):
        to = lax.rem(here + step, chips)
        ref[...] = (near_ref[to] + got_ref[to].astype(F32)).astype(BF16)


def fold(near, got):
    shape = near.shape[1:]
    return pl.pallas_call(
        fold_kernel,
        out_shape=(jax.ShapeDtypeStruct(shape, F32),) + (jax.ShapeDtypeStruct(shape, BF16),) * 3,
        in_specs=[VMEM_SPEC] * 2,
        out_specs=(VMEM_SPEC,) * 4,
        compiler_params=pltpu.CompilerParams(vmem_limit_bytes=2 * 2**20),
        cost_estimate=QUICK,
        name="fold",
    )(near, got)


def row_halo(ends):
    count = lax.axis_size(SKY)
    up = [(i, i + 1) for i in range(count - 1)]
    down = [(j, i) for i, j in up]
    return jnp.stack([lax.ppermute(ends[0], SKY, up), lax.ppermute(ends[1], SKY, down)])


def join_kernel(own_ref, far_ref, keep_ref, a_ref, b_ref, c_ref, out_ref):
    pieces, total, outs = out_ref.shape
    chans = own_ref.shape[0] // 3
    size = chans // pieces
    for tap_col in range(3):
        for tap_row in range(3):
            rows = slice(tap_row * chans, (tap_row + 1) * chans)
            lanes = slice(tap_col * outs, (tap_col + 1) * outs)
            value = own_ref[rows, lanes] + far_ref[rows, lanes].astype(F32)
            at = (3 * tap_col + tap_row) * size
            out_ref[:, at : at + size, :] = value.reshape(pieces, size, outs).astype(BF16)
    second = keep_ref[...]
    for ref in (a_ref, b_ref, c_ref):
        second = second + ref[...].astype(F32)
    sx = lax.axis_size("x")
    sz = pieces // sx
    third = second.shape[0] // 3
    size_x = third // sx
    extra = total - 9 * size
    for x in range(sx):
        value = jnp.concatenate(
            [second[tap * third + x * size_x : tap * third + (x + 1) * size_x] for tap in range(3)],
            axis=0,
        )
        for z in range(sz):
            out_ref[z * sx + x, 9 * size :, :] = value[z * extra : (z + 1) * extra].astype(BF16)


def join(own, far, keep, got, pieces):
    outs = keep.shape[1]
    rows = 9 * (own.shape[0] // 3 // pieces) + keep.shape[0] // pieces
    return pl.pallas_call(
        join_kernel,
        out_shape=jax.ShapeDtypeStruct((pieces, rows, outs), BF16),
        in_specs=[VMEM_SPEC] * 6,
        out_specs=VMEM_SPEC,
        compiler_params=pltpu.CompilerParams(vmem_limit_bytes=4 * 2**20),
        cost_estimate=QUICK,
        name="join",
    )(own, far, keep, *got)


STEPS = (0, 1, 3, 2)


def order_kernel(extra, a_ref, b_ref, c_ref, d_ref, out_ref):
    rows = a_ref.shape[0] - extra
    sz = lax.axis_size("z")
    me = lax.axis_index("z")
    values = [ref[...].astype(F32) for ref in (a_ref, b_ref, c_ref, d_ref)]
    rest = []
    for z in range(len(STEPS)):
        value = values[0]
        for step, other in zip(STEPS[1:], values[1:]):
            value = jnp.where(lax.rem(me + sz - step, sz) == z, other, value)
        out_ref[z * rows : (z + 1) * rows, :] = value[:rows].astype(BF16)
        rest.append(value[rows:])
    out_ref[len(STEPS) * rows :, :] = jnp.concatenate(rest, axis=0).astype(BF16)


def order_pieces(parts, extra):
    rows, outs = parts[0].shape
    return pl.pallas_call(
        functools.partial(order_kernel, extra),
        out_shape=jax.ShapeDtypeStruct((4 * rows, outs), BF16),
        in_specs=[VMEM_SPEC] * 4,
        out_specs=VMEM_SPEC,
        compiler_params=pltpu.CompilerParams(vmem_limit_bytes=4 * 2**20),
        cost_estimate=QUICK,
        name="order_pieces",
    )(*parts)


def first_kernel(sz, a_ref, b_ref, c_ref, d_ref, out_ref):
    sx = lax.axis_size("x")
    size = out_ref.shape[2] // (sx * sz)
    me = lax.axis_index("x")
    for step, ref in zip(STEPS, (a_ref, b_ref, c_ref, d_ref)):
        x = lax.rem(me + sx - step, sx)
        value = ref[...].astype(F32)
        for z in range(sz):
            at = pl.multiple_of((z * sx + x) * size, size)
            for tap in range(9):
                rows = (z * 9 + tap) * size
                out_ref[tap // 3, tap % 3, pl.ds(at, size), :] = value[rows : rows + size]


def lay_first(parts, sz, chans):
    outs = parts[0].shape[1]
    return pl.pallas_call(
        functools.partial(first_kernel, sz),
        out_shape=jax.ShapeDtypeStruct((3, 3, chans, outs), F32),
        in_specs=[VMEM_SPEC] * 4,
        out_specs=VMEM_SPEC,
        compiler_params=pltpu.CompilerParams(vmem_limit_bytes=4 * 2**20),
        cost_estimate=QUICK,
        name="lay_first",
    )(*parts)


def lay_second_kernel(near_ref, far_ref, out_ref):
    sy, sx, rows, _ = near_ref.shape
    size = rows // 3
    third = out_ref.shape[0] // 3
    core, y, x = lax.axis_index("c"), lax.axis_index("y"), lax.axis_index("x")
    for half, ref in ((core, near_ref), (1 - core, far_ref)):
        for i in range(sy):
            for j in range(sx):
                place = (half * sy + lax.rem(y + sy - STEPS[i], sy)) * sx
                place = place + lax.rem(x + sx - STEPS[j], sx)
                value = ref[i, j].astype(F32)
                for tap in range(3):
                    at = pl.multiple_of(tap * third + place * size, 8)
                    out_ref[pl.ds(at, size), :] = value[tap * size : (tap + 1) * size]


def lay_second(near, far):
    sy, sx, rows, outs = near.shape
    return pl.pallas_call(
        lay_second_kernel,
        out_shape=jax.ShapeDtypeStruct((2 * sy * sx * rows, outs), F32),
        in_specs=[VMEM_SPEC] * 2,
        out_specs=VMEM_SPEC,
        compiler_params=pltpu.CompilerParams(vmem_limit_bytes=4 * 2**20),
        cost_estimate=QUICK,
        name="lay_second",
    )(near, far)


def gather_steps(piece, axis):
    return [piece] + [shift(piece, axis, step) for step in STEPS[1:]]


def body(sky_cube, weight_first, weight_second, cotangent):
    cols, rows, chans = sky_cube.shape
    strip, _, outs = cotangent.shape
    chips = lax.axis_size("y")

    ends = [
        jnp.concatenate(
            [sky_cube[:, r], cotangent[:, r, : outs // 2], cotangent[:, r, outs // 2 :]], axis=0
        )
        for r in (rows - 1, 0)
    ]
    edges = row_halo(ends)
    far_cube = shift(sky_cube, "c", 1)
    far_weight = shift(weight_first, "c", 1)
    far_edges = shift(edges, "c", 1)
    wide = spread(sky_cube, far_cube, edges, far_edges, chips)
    kernel = jnp.concatenate([weight_first, far_weight], axis=2).reshape(18 * chans, outs)

    def side(col):
        beside = [
            jnp.concatenate(
                [edges[k, at + col : at + col + 1] for at in (cols, cols + strip)], axis=1
            )
            for k in range(2)
        ]
        return jnp.concatenate([cotangent[col]] + beside, axis=0)

    count = lax.axis_size(FREQ)
    up = [(i, i + 1) for i in range(count - 1)]
    down = [(j, i) for i, j in up]
    left = lax.ppermute(side(strip - 1), FREQ, up)
    right = lax.ppermute(side(0), FREQ, down)

    on, off = 1, chips - 1
    cut = strip // 2 + 1
    far_a, far_b = conv_parts(((2, 0), (2, cut)), wide, kernel, cut, BF16)
    hold, _ = lax.optimization_barrier((wide, far_a))
    near_b, near_a = conv_parts(((on, cut), (off, 0)), hold, kernel, cut, BF16)
    got_a, got_b = shift(far_a, "y", on), shift(far_b, "y", off)
    got_a, left, right = lax.optimization_barrier((got_a, left, right))
    both_a, both_b = conv_parts(((on, 0), (off, cut)), wide, kernel, cut, BF16, (got_a, got_b))
    own = conv_parts(((0, 0),), wide, kernel, strip + 2, F32)[0]
    from_a = shift(both_a, "y", on), shift(near_a, "y", off)
    from_b = shift(near_b, "y", on), shift(both_b, "y", off)

    back = back_tile(cotangent, left, right, edges, weight_second)
    delta_a, delta_b, hidden = point(own, from_a, from_b, back)

    on_a, off_b = shift(delta_a, "y", on), shift(delta_b, "y", off)
    edges = row_halo([hidden[:, rows - 1], hidden[:, 0]])
    on_a, off_b, edges, late_a, late_b = lax.optimization_barrier(
        (on_a, off_b, edges, delta_a, delta_b)
    )
    on_b, off_a = shift(late_b, "y", on), shift(late_a, "y", off)
    fwd_a, fwd_b = shift(on_a, "y", on), shift(off_b, "y", off)
    total = grad_strip(0, wide, (delta_a, delta_b), None, False)
    features, near, far = second_tile(hidden, edges, weight_second, cotangent, chips)
    far, on_b, off_a = lax.optimization_barrier((far, on_b, off_a))
    keep, *sends = fold(near, shift(far, "c", 1))
    got = [shift(send, "y", step) for step, send in zip(STEPS[1:], sends)]
    total = grad_strip(off, wide, (on_a, on_b), total, False)
    total = grad_strip(on, wide, (off_a, off_b), total, False)
    first_own, first_far = grad_strip(2, wide, (fwd_a, fwd_b), total, True)

    sx, sz = lax.axis_size("x"), lax.axis_size("z")
    joined = join(first_own, shift(first_far, "c", 1), keep, got, sx * sz)
    extra = keep.shape[0] // (sx * sz)
    summed = lax.all_to_all(joined, SKY, 0, 0, tiled=True)
    summed = jnp.sum(summed.astype(F32), axis=0).astype(BF16)
    parts = gather_steps(order_pieces(gather_steps(summed, "z"), extra), "x")
    main = parts[0].shape[0] - sz * extra
    grad_first = lay_first(parts, sz, chans)
    share = jnp.stack([part[main:] for part in parts])
    share = jnp.stack(gather_steps(share, "y"))
    grad_second = lay_second(share, shift(share, "c", 1)).reshape(3, 3, outs, outs)
    return features, grad_first, grad_second


def solution(mesh):
    sizes = (mesh.devices.shape[0] // 2, 2, 4, mesh.devices.shape[1] // 4)
    fine = Mesh(mesh.devices.reshape(sizes), FREQ + SKY)
    return jax.shard_map(
        body,
        mesh=fine,
        in_specs=(P(None, SKY, FREQ), P(None, None, FREQ, None), P(), P(FREQ, SKY, None)),
        out_specs=(P(FREQ, SKY, None), P(None, None, FREQ, None), P()),
        check_vma=False,
    )
```

```python
import functools

import jax
import jax.numpy as jnp
from jax import lax
from jax.experimental import pallas as pl
from jax.experimental.pallas import tpu as pltpu
from jax.sharding import Mesh, PartitionSpec as P

FREQ = ("y", "c")
SKY = ("z", "x")
F32 = jnp.float32
BF16 = jnp.bfloat16
QUICK = pl.CostEstimate(flops=1, bytes_accessed=1, transcendentals=0)


def shift(x, axis, step):
    count = lax.axis_size(axis)
    return lax.ppermute(x, axis, [(i, (i + step) % count) for i in range(count)])


def spread_kernel(own_ref, far_ref, own_halo_ref, far_halo_ref, out_ref):
    chips, width, rows, depth = out_ref.shape
    cols, _, chans = own_ref.shape
    strip = cols // (2 * chips)
    core = lax.axis_index("c")
    step = 8
    row = lax.broadcasted_iota(jnp.int32, (step, rows, chans), 1)

    def block(i, base, chip):
        for side, (cube_ref, halo_ref) in enumerate(
            ((own_ref, own_halo_ref), (far_ref, far_halo_ref))
        ):
            at = pl.multiple_of(base + i * step, step)
            mid = cube_ref[pl.ds(at, step)]
            wide = mid.astype(F32).reshape(step * rows, chans)
            ahead = pltpu.roll(wide, 1, 0).reshape(step, rows, chans)
            behind = pltpu.roll(wide, step * rows - 1, 0).reshape(step, rows, chans)
            before = halo_ref[0, pl.ds(at, step), :].astype(F32)[:, None, :]
            after = halo_ref[1, pl.ds(at, step), :].astype(F32)[:, None, :]
            ahead = jnp.where(row == 0, before, ahead)
            behind = jnp.where(row == rows - 1, after, behind)
            to = pl.ds(2 + i * step, step)
            for tap, value in enumerate((ahead.astype(BF16), mid, behind.astype(BF16))):
                lane = (2 * tap + side) * chans
                out_ref[chip, to, :, lane : lane + chans] = value

    def edge(at, chip, slot):
        for side, (cube_ref, halo_ref) in enumerate(
            ((own_ref, own_halo_ref), (far_ref, far_halo_ref))
        ):
            first = pl.multiple_of((at // step) * step, step)
            mid = cube_ref[at]
            wide = mid.astype(F32)
            line = lax.broadcasted_iota(jnp.int32, (step, chans), 0) == at - first
            pick = lambda k: jnp.sum(
                jnp.where(line, halo_ref[k, pl.ds(first, step), :].astype(F32), 0.0),
                axis=0,
                keepdims=True,
            )
            place = lax.broadcasted_iota(jnp.int32, (rows, chans), 0)
            ahead = jnp.where(place == 0, pick(0), pltpu.roll(wide, 1, 0))
            behind = jnp.where(place == rows - 1, pick(1), pltpu.roll(wide, rows - 1, 0))
            for tap, value in enumerate((ahead.astype(BF16), mid, behind.astype(BF16))):
                lane = (2 * tap + side) * chans
                out_ref[chip, slot, :, lane : lane + chans] = value

    blank = jnp.zeros((rows, depth), BF16)
    for chip in range(chips):
        base = (2 * chip + core) * strip
        lax.fori_loop(0, strip // step, lambda i, _: block(i, base, chip), None)
        for slot in (0, 1):
            edge(jnp.maximum(base - 2 + slot, 0), chip, slot)
            edge(jnp.minimum(base + strip + slot, cols - 1), chip, strip + 2 + slot)
        for slot in range(strip + 4, width):
            out_ref[chip, slot] = blank

    @pl.when(core == 0)
    def _():
        out_ref[0, 0] = blank
        out_ref[0, 1] = blank

    @pl.when(core == 1)
    def _():
        out_ref[chips - 1, strip + 2] = blank
        out_ref[chips - 1, strip + 3] = blank


VMEM_SPEC = pl.BlockSpec(memory_space=pltpu.VMEM)


def spread(own, far, own_halo, far_halo, chips):
    cols, rows, chans = own.shape
    return pl.pallas_call(
        spread_kernel,
        out_shape=jax.ShapeDtypeStruct((chips, cols // (2 * chips) + 8, rows, 6 * chans), BF16),
        in_specs=[VMEM_SPEC] * 4,
        out_specs=VMEM_SPEC,
        compiler_params=pltpu.CompilerParams(vmem_limit_bytes=2 * 2**20),
        cost_estimate=QUICK,
        name="spread",
    )(own, far, own_halo, far_halo)


def chip_at(step):
    return lax.rem(lax.axis_index("y") + step, lax.axis_size("y"))


def conv_kernel(parts, adds, wide_ref, kernel_ref, *refs):
    rows = wide_ref.shape[2]
    for (step, first), add_ref, out_ref in zip(parts, refs[:adds] or [None] * len(parts), refs[adds:]):
        count, _, outs = out_ref.shape
        chip = chip_at(step)
        pieces = [wide_ref[chip, first + tap : first + tap + count] for tap in range(3)]
        lhs = jnp.concatenate(pieces, axis=-1).reshape(count * rows, -1)
        total = jnp.dot(lhs, kernel_ref[...], preferred_element_type=F32)
        total = total.reshape(count, rows, outs)
        if add_ref is not None:
            total = total + add_ref[...].astype(F32)
        out_ref[...] = total.astype(out_ref.dtype)


def conv_parts(parts, wide, kernel, count, dtype, adds=()):
    rows, outs = wide.shape[2], kernel.shape[1]
    return pl.pallas_call(
        functools.partial(conv_kernel, parts, len(adds)),
        out_shape=(jax.ShapeDtypeStruct((count, rows, outs), dtype),) * len(parts),
        in_specs=[VMEM_SPEC] * (2 + len(adds)),
        out_specs=(VMEM_SPEC,) * len(parts),
        compiler_params=pltpu.CompilerParams(vmem_limit_bytes=4 * 2**20),
        cost_estimate=QUICK,
        name="conv_first",
    )(wide, kernel, *adds)


def grad_kernel(step, has_old, last, wide_ref, a_ref, b_ref, *refs):
    old_ref = refs[0] if has_old else None
    outs_refs, pad_ref = refs[1 if has_old else 0 : -1], refs[-1]
    half, rows, outs = a_ref.shape
    strip = 2 * half
    cols, depth = wide_ref.shape[1], wide_ref.shape[3]
    pad_ref[0:3] = jnp.zeros((3, rows, outs), BF16)
    pad_ref[3 : 3 + half] = a_ref[...]
    pad_ref[3 + half : 3 + strip] = b_ref[...]
    pad_ref[3 + strip :] = jnp.zeros((cols - strip - 1, rows, outs), BF16)
    lhs = wide_ref[chip_at(step)].reshape(cols * rows, depth)
    rhs = jnp.concatenate(
        [pad_ref[2 - tap : 2 - tap + cols].reshape(cols * rows, outs) for tap in range(3)], axis=-1
    )
    total = lax.dot_general(lhs, rhs, (((0,), (0,)), ((), ())), preferred_element_type=F32)
    if has_old:
        total = total + old_ref[...]
    if not last:
        outs_refs[0][...] = total
    else:
        chans = depth // 6
        for tap in range(3):
            at = 2 * tap * chans
            outs_refs[0][tap * chans : (tap + 1) * chans] = total[at : at + chans]
            outs_refs[1][tap * chans : (tap + 1) * chans] = total[
                at + chans : at + 2 * chans
            ].astype(BF16)


def grad_strip(step, wide, halves, old, last):
    _, rows, outs = halves[0].shape
    depth, cols = wide.shape[3], wide.shape[1]
    shape = (depth, 3 * outs)
    half = (depth // 2, 3 * outs)
    if last:
        out_shape = (jax.ShapeDtypeStruct(half, F32), jax.ShapeDtypeStruct(half, BF16))
    else:
        out_shape = (jax.ShapeDtypeStruct(shape, F32),)
    args = [wide, *halves] + ([old] if old is not None else [])
    out = pl.pallas_call(
        functools.partial(grad_kernel, step, old is not None, last),
        out_shape=out_shape,
        in_specs=[VMEM_SPEC] * len(args),
        out_specs=tuple([VMEM_SPEC] * len(out_shape)),
        scratch_shapes=[pltpu.VMEM((cols + 2, rows, outs), BF16)],
        compiler_params=pltpu.CompilerParams(vmem_limit_bytes=5 * 2**20),
        cost_estimate=QUICK,
        name="grad_first",
    )(*args)
    return out if last else out[0]


def spread_tile(columns, wide_ref):
    rows, chans = wide_ref.shape[1], wide_ref.shape[2] // 3
    place = lax.broadcasted_iota(jnp.int32, (rows, chans), 0)
    for j, (mid, before, after) in enumerate(columns):
        wide = mid.astype(F32)
        ahead = jnp.where(place == 0, before.astype(F32), pltpu.roll(wide, 1, 0))
        behind = jnp.where(place == rows - 1, after.astype(F32), pltpu.roll(wide, rows - 1, 0))
        wide_ref[j, :, 0:chans] = ahead.astype(BF16)
        wide_ref[j, :, chans : 2 * chans] = mid
        wide_ref[j, :, 2 * chans :] = behind.astype(BF16)


def back_kernel(cot_ref, left_ref, right_ref, edge_ref, kernel_ref, out_ref, wide_ref):
    cols, rows, chans = cot_ref.shape
    start = edge_ref.shape[1] - 2 * cols

    def beside(k, j):
        low, high = start + j, start + cols + j
        return jnp.concatenate(
            [edge_ref[k, low : low + 1, :], edge_ref[k, high : high + 1, :]], axis=-1
        )

    def whole(ref):
        return ref[0:rows], ref[rows : rows + 1], ref[rows + 1 : rows + 2]

    columns = [(cot_ref[j], beside(0, j), beside(1, j)) for j in range(cols)]
    spread_tile([whole(left_ref)] + columns + [whole(right_ref)], wide_ref)
    total = None
    for tap_col in range(3):
        lhs = wide_ref[tap_col : tap_col + cols].reshape(cols * rows, 3 * chans)
        for tap_row in range(3):
            part = lax.dot_general(
                lhs[:, tap_row * chans : (tap_row + 1) * chans],
                kernel_ref[2 - tap_col, 2 - tap_row],
                (((1,), (1,)), ((), ())),
                preferred_element_type=F32,
            )
            total = part if total is None else total + part
    out_ref[...] = total.reshape(cols, rows, -1)


def back_tile(tile, left, right, edges, kernel):
    cols, rows, chans = tile.shape
    return pl.pallas_call(
        back_kernel,
        out_shape=jax.ShapeDtypeStruct((cols, rows, kernel.shape[2]), F32),
        in_specs=[VMEM_SPEC] * 5,
        out_specs=VMEM_SPEC,
        scratch_shapes=[pltpu.VMEM((cols + 2, rows, 3 * chans), BF16)],
        compiler_params=pltpu.CompilerParams(vmem_limit_bytes=4 * 2**20),
        cost_estimate=QUICK,
        name="back",
    )(tile, left, right, edges, kernel)


def second_kernel(chips, hid_ref, edge_ref, cot_ref, wide_ref, near_ref, far_ref, pad_ref, sum_ref):
    chans = hid_ref.shape[2]
    cols, rows, outs = cot_ref.shape
    width = wide_ref.shape[0]
    core = lax.axis_index("c")
    columns = [
        (hid_ref[j], edge_ref[0, j : j + 1, :], edge_ref[1, j : j + 1, :]) for j in range(cols + 2)
    ]
    spread_tile(columns, wide_ref)
    wide_ref[cols + 2 :] = jnp.zeros((width - cols - 2, rows, 3 * chans), BF16)

    pad_ref[0:2] = jnp.zeros((2, rows, outs), BF16)
    pad_ref[2 : 2 + cols] = cot_ref[...]
    pad_ref[2 + cols :] = jnp.zeros((width - cols, rows, outs), BF16)
    rhs = jnp.concatenate(
        [pad_ref[2 - tap : 2 - tap + width].reshape(width * rows, outs) for tap in range(3)],
        axis=-1,
    )
    sum_ref[...] = lax.dot_general(
        wide_ref[...].reshape(width * rows, 3 * chans),
        rhs,
        (((0,), (0,)), ((), ())),
        preferred_element_type=F32,
    )
    size = sum_ref.shape[0] // (2 * chips)
    for half, ref in ((core, near_ref), (1 - core, far_ref)):
        for chip in range(chips):
            at = pl.multiple_of((half * chips + chip) * size, size)
            for tap in range(3):
                ref[chip, tap * size : (tap + 1) * size, :] = sum_ref[
                    pl.ds(at, size), tap * outs : (tap + 1) * outs
                ].astype(ref.dtype)


def second_tile(tile, edges, cotangent, chips):
    chans = tile.shape[2]
    cols, rows, outs = cotangent.shape
    width = cols + 8
    cut = (chips, 9 * chans // (2 * chips), outs)
    return pl.pallas_call(
        functools.partial(second_kernel, chips),
        out_shape=(
            jax.ShapeDtypeStruct((width, rows, 3 * chans), BF16),
            jax.ShapeDtypeStruct(cut, F32),
            jax.ShapeDtypeStruct(cut, BF16),
        ),
        in_specs=[VMEM_SPEC] * 3,
        out_specs=(VMEM_SPEC,) * 3,
        scratch_shapes=[
            pltpu.VMEM((width + 2, rows, outs), BF16),
            pltpu.VMEM((3 * chans, 3 * outs), F32),
        ],
        compiler_params=pltpu.CompilerParams(vmem_limit_bytes=9 * 2**20),
        cost_estimate=QUICK,
        name="second",
    )(tile, edges, cotangent)


def features_kernel(wide_ref, kernel_ref, out_ref):
    cols, rows, outs = out_ref.shape
    pieces = [wide_ref[tap : tap + cols] for tap in range(3)]
    lhs = jnp.concatenate(pieces, axis=-1).reshape(cols * rows, -1)
    total = jnp.dot(lhs, kernel_ref[...], preferred_element_type=F32)
    out_ref[...] = total.reshape(cols, rows, outs).astype(BF16)


def features_tile(wide, kernel, cols):
    rows, outs = wide.shape[1], kernel.shape[3]
    return pl.pallas_call(
        features_kernel,
        out_shape=jax.ShapeDtypeStruct((cols, rows, outs), BF16),
        in_specs=[VMEM_SPEC] * 2,
        out_specs=VMEM_SPEC,
        compiler_params=pltpu.CompilerParams(vmem_limit_bytes=4 * 2**20),
        cost_estimate=QUICK,
        name="features",
    )(wide, kernel.reshape(-1, outs))


def point_kernel(
    own_ref, a0_ref, a1_ref, b0_ref, b1_ref, back_ref,
    da_ref, db_ref, hidden_ref, last_ref, first_ref,
):
    cols, rows, _ = own_ref.shape
    half = da_ref.shape[0]
    strip = 2 * lax.axis_index("y") + lax.axis_index("c")
    strips = 2 * lax.axis_size("y")

    def column(j, i, refs, delta_ref, keep):
        pre = own_ref[j] + refs[0][i].astype(F32) + refs[1][i].astype(F32)
        sigma = jax.nn.sigmoid(pre)
        hidden = pre * sigma
        if keep is not None:
            hidden = jnp.where(keep, hidden, 0.0)
        hidden = hidden.astype(BF16)
        hidden_ref[j] = hidden
        last_ref[j : j + 1, :] = hidden[rows - 1 :]
        first_ref[j : j + 1, :] = hidden[:1]
        if keep is None:
            slope = sigma * (1.0 + pre * (1.0 - sigma))
            at = j - 1 if delta_ref is da_ref else j - 1 - half
            delta_ref[at] = (back_ref[j - 1] * slope).astype(BF16)

    left, right = (a0_ref, a1_ref), (b0_ref, b1_ref)
    column(0, 0, left, None, strip > 0)
    column(cols - 1, half, right, None, strip < strips - 1)

    for i in range(1, half + 1):
        column(i, i, left, da_ref, None)
        column(half + i, i - 1, right, db_ref, None)


def point(own, left, right, back):
    strip, rows, outs = back.shape
    cut = jax.ShapeDtypeStruct((strip // 2, rows, outs), BF16)
    edge = jax.ShapeDtypeStruct((strip + 2, outs), BF16)
    return pl.pallas_call(
        point_kernel,
        out_shape=(cut, cut, jax.ShapeDtypeStruct(own.shape, BF16), edge, edge),
        in_specs=[VMEM_SPEC] * 6,
        out_specs=(VMEM_SPEC,) * 5,
        compiler_params=pltpu.CompilerParams(vmem_limit_bytes=2 * 2**20),
        cost_estimate=QUICK,
        name="point",
    )(own, *left, *right, back)


def fold_kernel(near_ref, got_ref, keep_ref, *send_refs):
    chips = near_ref.shape[0]
    here = lax.axis_index("y")
    keep_ref[...] = near_ref[here] + got_ref[here].astype(F32)
    for step, ref in zip(STEPS[1:], send_refs):
        to = lax.rem(here + step, chips)
        ref[...] = (near_ref[to] + got_ref[to].astype(F32)).astype(BF16)


def fold(near, got):
    shape = near.shape[1:]
    return pl.pallas_call(
        fold_kernel,
        out_shape=(jax.ShapeDtypeStruct(shape, F32),) + (jax.ShapeDtypeStruct(shape, BF16),) * 3,
        in_specs=[VMEM_SPEC] * 2,
        out_specs=(VMEM_SPEC,) * 4,
        compiler_params=pltpu.CompilerParams(vmem_limit_bytes=2 * 2**20),
        cost_estimate=QUICK,
        name="fold",
    )(near, got)


def row_halo(ends):
    count = lax.axis_size(SKY)
    up = [(i, i + 1) for i in range(count - 1)]
    down = [(j, i) for i, j in up]
    return jnp.stack([lax.ppermute(ends[0], SKY, up), lax.ppermute(ends[1], SKY, down)])


def join_kernel(own_ref, far_ref, keep_ref, a_ref, b_ref, c_ref, out_ref):
    pieces, total, outs = out_ref.shape
    chans = own_ref.shape[0] // 3
    size = chans // pieces
    for tap_col in range(3):
        for tap_row in range(3):
            rows = slice(tap_row * chans, (tap_row + 1) * chans)
            lanes = slice(tap_col * outs, (tap_col + 1) * outs)
            value = own_ref[rows, lanes] + far_ref[rows, lanes].astype(F32)
            at = (3 * tap_col + tap_row) * size
            out_ref[:, at : at + size, :] = value.reshape(pieces, size, outs).astype(BF16)
    second = keep_ref[...]
    for ref in (a_ref, b_ref, c_ref):
        second = second + ref[...].astype(F32)
    sx = lax.axis_size("x")
    sz = pieces // sx
    third = second.shape[0] // 3
    size_x = third // sx
    extra = total - 9 * size
    for x in range(sx):
        value = jnp.concatenate(
            [second[tap * third + x * size_x : tap * third + (x + 1) * size_x] for tap in range(3)],
            axis=0,
        )
        for z in range(sz):
            out_ref[z * sx + x, 9 * size :, :] = value[z * extra : (z + 1) * extra].astype(BF16)


def join(own, far, keep, got, pieces):
    outs = keep.shape[1]
    rows = 9 * (own.shape[0] // 3 // pieces) + keep.shape[0] // pieces
    return pl.pallas_call(
        join_kernel,
        out_shape=jax.ShapeDtypeStruct((pieces, rows, outs), BF16),
        in_specs=[VMEM_SPEC] * 6,
        out_specs=VMEM_SPEC,
        compiler_params=pltpu.CompilerParams(vmem_limit_bytes=4 * 2**20),
        cost_estimate=QUICK,
        name="join",
    )(own, far, keep, *got)


STEPS = (0, 1, 3, 2)


def order_kernel(extra, a_ref, b_ref, c_ref, d_ref, out_ref):
    rows = a_ref.shape[0] - extra
    sz = lax.axis_size("z")
    me = lax.axis_index("z")
    values = [ref[...].astype(F32) for ref in (a_ref, b_ref, c_ref, d_ref)]
    rest = []
    for z in range(len(STEPS)):
        value = values[0]
        for step, other in zip(STEPS[1:], values[1:]):
            value = jnp.where(lax.rem(me + sz - step, sz) == z, other, value)
        out_ref[z * rows : (z + 1) * rows, :] = value[:rows].astype(BF16)
        rest.append(value[rows:])
    out_ref[len(STEPS) * rows :, :] = jnp.concatenate(rest, axis=0).astype(BF16)


def order_pieces(parts, extra):
    rows, outs = parts[0].shape
    return pl.pallas_call(
        functools.partial(order_kernel, extra),
        out_shape=jax.ShapeDtypeStruct((4 * rows, outs), BF16),
        in_specs=[VMEM_SPEC] * 4,
        out_specs=VMEM_SPEC,
        compiler_params=pltpu.CompilerParams(vmem_limit_bytes=4 * 2**20),
        cost_estimate=QUICK,
        name="order_pieces",
    )(*parts)


def first_kernel(sz, a_ref, b_ref, c_ref, d_ref, out_ref):
    sx = lax.axis_size("x")
    size = out_ref.shape[2] // (sx * sz)
    me = lax.axis_index("x")
    for step, ref in zip(STEPS, (a_ref, b_ref, c_ref, d_ref)):
        x = lax.rem(me + sx - step, sx)
        value = ref[...].astype(F32)
        for z in range(sz):
            at = pl.multiple_of((z * sx + x) * size, size)
            for tap in range(9):
                rows = (z * 9 + tap) * size
                out_ref[tap // 3, tap % 3, pl.ds(at, size), :] = value[rows : rows + size]


def lay_first(parts, sz, chans):
    outs = parts[0].shape[1]
    return pl.pallas_call(
        functools.partial(first_kernel, sz),
        out_shape=jax.ShapeDtypeStruct((3, 3, chans, outs), F32),
        in_specs=[VMEM_SPEC] * 4,
        out_specs=VMEM_SPEC,
        compiler_params=pltpu.CompilerParams(vmem_limit_bytes=4 * 2**20),
        cost_estimate=QUICK,
        name="lay_first",
    )(*parts)


def lay_second_kernel(near_ref, far_ref, out_ref):
    sy, sx, rows, _ = near_ref.shape
    size = rows // 3
    third = out_ref.shape[0] // 3
    core, y, x = lax.axis_index("c"), lax.axis_index("y"), lax.axis_index("x")
    for half, ref in ((core, near_ref), (1 - core, far_ref)):
        for i in range(sy):
            for j in range(sx):
                place = (half * sy + lax.rem(y + sy - STEPS[i], sy)) * sx
                place = place + lax.rem(x + sx - STEPS[j], sx)
                value = ref[i, j].astype(F32)
                for tap in range(3):
                    at = pl.multiple_of(tap * third + place * size, 8)
                    out_ref[pl.ds(at, size), :] = value[tap * size : (tap + 1) * size]


def lay_second(near, far):
    sy, sx, rows, outs = near.shape
    return pl.pallas_call(
        lay_second_kernel,
        out_shape=jax.ShapeDtypeStruct((2 * sy * sx * rows, outs), F32),
        in_specs=[VMEM_SPEC] * 2,
        out_specs=VMEM_SPEC,
        compiler_params=pltpu.CompilerParams(vmem_limit_bytes=4 * 2**20),
        cost_estimate=QUICK,
        name="lay_second",
    )(near, far)


def gather_steps(piece, axis):
    return [piece] + [shift(piece, axis, step) for step in STEPS[1:]]


def body(sky_cube, weight_first, weight_second, cotangent):
    cols, rows, chans = sky_cube.shape
    strip, _, outs = cotangent.shape
    chips = lax.axis_size("y")

    ends = [
        jnp.concatenate(
            [sky_cube[:, r], cotangent[:, r, : outs // 2], cotangent[:, r, outs // 2 :]], axis=0
        )
        for r in (rows - 1, 0)
    ]
    edges = row_halo(ends)
    far_cube = shift(sky_cube, "c", 1)
    far_weight = shift(weight_first, "c", 1)
    far_edges = shift(edges, "c", 1)
    wide = spread(sky_cube, far_cube, edges, far_edges, chips)
    kernel = jnp.concatenate([weight_first, far_weight], axis=2).reshape(18 * chans, outs)

    def side(col):
        beside = [
            jnp.concatenate(
                [edges[k, at + col : at + col + 1] for at in (cols, cols + strip)], axis=1
            )
            for k in range(2)
        ]
        return jnp.concatenate([cotangent[col]] + beside, axis=0)

    count = lax.axis_size(FREQ)
    up = [(i, i + 1) for i in range(count - 1)]
    down = [(j, i) for i, j in up]
    left = lax.ppermute(side(strip - 1), FREQ, up)
    right = lax.ppermute(side(0), FREQ, down)

    on, off = 1, chips - 1
    cut = strip // 2 + 1
    far_a, far_b = conv_parts(((2, 0), (2, cut)), wide, kernel, cut, BF16)
    hold, _ = lax.optimization_barrier((wide, far_a))
    near_b, near_a = conv_parts(((on, cut), (off, 0)), hold, kernel, cut, BF16)
    got_a, got_b = shift(far_a, "y", on), shift(far_b, "y", off)
    got_a, left, right = lax.optimization_barrier((got_a, left, right))
    both_a, both_b = conv_parts(((on, 0), (off, cut)), wide, kernel, cut, BF16, (got_a, got_b))
    own = conv_parts(((0, 0),), wide, kernel, strip + 2, F32)[0]
    from_a = shift(both_a, "y", on), shift(near_a, "y", off)
    from_b = shift(near_b, "y", on), shift(both_b, "y", off)

    back = back_tile(cotangent, left, right, edges, weight_second)
    delta_a, delta_b, hidden, *ends = point(own, from_a, from_b, back)

    on_a, off_b = shift(delta_a, "y", on), shift(delta_b, "y", off)
    edges = row_halo(ends)
    total = grad_strip(0, wide, (delta_a, delta_b), None, False)
    on_a, off_b, edges, late_a, late_b, total = lax.optimization_barrier(
        (on_a, off_b, edges, delta_a, delta_b, total)
    )
    on_b, off_a = shift(late_b, "y", on), shift(late_a, "y", off)
    fwd_a, fwd_b = shift(on_a, "y", on), shift(off_b, "y", off)
    wide_hidden, near, far = second_tile(hidden, edges, cotangent, chips)
    far, on_b, off_a = lax.optimization_barrier((far, on_b, off_a))
    keep, *sends = fold(near, shift(far, "c", 1))
    got = [shift(send, "y", step) for step, send in zip(STEPS[1:], sends)]
    total = grad_strip(off, wide, (on_a, on_b), total, False)
    total = grad_strip(on, wide, (off_a, off_b), total, False)
    first_own, first_far = grad_strip(2, wide, (fwd_a, fwd_b), total, True)

    sx, sz = lax.axis_size("x"), lax.axis_size("z")
    joined = join(first_own, shift(first_far, "c", 1), keep, got, sx * sz)
    extra = keep.shape[0] // (sx * sz)
    summed = lax.all_to_all(joined, SKY, 0, 0, tiled=True)
    summed = jnp.sum(summed.astype(F32), axis=0).astype(BF16)
    parts = gather_steps(order_pieces(gather_steps(summed, "z"), extra), "x")
    main = parts[0].shape[0] - sz * extra
    grad_first = lay_first(parts, sz, chans)
    features = features_tile(wide_hidden, weight_second, strip)
    share = jnp.stack([part[main:] for part in parts])
    share, features = lax.optimization_barrier((share, features))
    share = jnp.stack(gather_steps(share, "y"))
    grad_second = lay_second(share, shift(share, "c", 1)).reshape(3, 3, outs, outs)
    return features, grad_first, grad_second


def solution(mesh):
    sizes = (mesh.devices.shape[0] // 2, 2, 4, mesh.devices.shape[1] // 4)
    fine = Mesh(mesh.devices.reshape(sizes), FREQ + SKY)
    return jax.shard_map(
        body,
        mesh=fine,
        in_specs=(P(None, SKY, FREQ), P(None, None, FREQ, None), P(), P(FREQ, SKY, None)),
        out_specs=(P(FREQ, SKY, None), P(None, None, FREQ, None), P()),
        check_vma=False,
    )
```

```python
import functools

import jax
import jax.numpy as jnp
from jax import lax
from jax.experimental import pallas as pl
from jax.experimental.pallas import tpu as pltpu
from jax.sharding import Mesh, PartitionSpec as P

FREQ = ("y", "c")
SKY = ("z", "x")
F32 = jnp.float32
BF16 = jnp.bfloat16
QUICK = pl.CostEstimate(flops=1, bytes_accessed=1, transcendentals=0)


def shift(x, axis, step):
    count = lax.axis_size(axis)
    return lax.ppermute(x, axis, [(i, (i + step) % count) for i in range(count)])


def spread_kernel(own_ref, far_ref, own_halo_ref, far_halo_ref, out_ref):
    chips, width, rows, depth = out_ref.shape
    cols, _, chans = own_ref.shape
    strip = cols // (2 * chips)
    core = lax.axis_index("c")
    step = 8
    row = lax.broadcasted_iota(jnp.int32, (step, rows, chans), 1)

    def block(i, base, chip):
        for side, (cube_ref, halo_ref) in enumerate(
            ((own_ref, own_halo_ref), (far_ref, far_halo_ref))
        ):
            at = pl.multiple_of(base + i * step, step)
            mid = cube_ref[pl.ds(at, step)]
            wide = mid.astype(F32).reshape(step * rows, chans)
            ahead = pltpu.roll(wide, 1, 0).reshape(step, rows, chans)
            behind = pltpu.roll(wide, step * rows - 1, 0).reshape(step, rows, chans)
            before = halo_ref[0, pl.ds(at, step), :].astype(F32)[:, None, :]
            after = halo_ref[1, pl.ds(at, step), :].astype(F32)[:, None, :]
            ahead = jnp.where(row == 0, before, ahead)
            behind = jnp.where(row == rows - 1, after, behind)
            to = pl.ds(2 + i * step, step)
            for tap, value in enumerate((ahead.astype(BF16), mid, behind.astype(BF16))):
                lane = (2 * tap + side) * chans
                out_ref[chip, to, :, lane : lane + chans] = value

    def edge(at, chip, slot):
        for side, (cube_ref, halo_ref) in enumerate(
            ((own_ref, own_halo_ref), (far_ref, far_halo_ref))
        ):
            first = pl.multiple_of((at // step) * step, step)
            mid = cube_ref[at]
            wide = mid.astype(F32)
            line = lax.broadcasted_iota(jnp.int32, (step, chans), 0) == at - first
            pick = lambda k: jnp.sum(
                jnp.where(line, halo_ref[k, pl.ds(first, step), :].astype(F32), 0.0),
                axis=0,
                keepdims=True,
            )
            place = lax.broadcasted_iota(jnp.int32, (rows, chans), 0)
            ahead = jnp.where(place == 0, pick(0), pltpu.roll(wide, 1, 0))
            behind = jnp.where(place == rows - 1, pick(1), pltpu.roll(wide, rows - 1, 0))
            for tap, value in enumerate((ahead.astype(BF16), mid, behind.astype(BF16))):
                lane = (2 * tap + side) * chans
                out_ref[chip, slot, :, lane : lane + chans] = value

    blank = jnp.zeros((rows, depth), BF16)
    for chip in range(chips):
        base = (2 * chip + core) * strip
        lax.fori_loop(0, strip // step, lambda i, _: block(i, base, chip), None)
        for slot in (0, 1):
            edge(jnp.maximum(base - 2 + slot, 0), chip, slot)
            edge(jnp.minimum(base + strip + slot, cols - 1), chip, strip + 2 + slot)
        for slot in range(strip + 4, width):
            out_ref[chip, slot] = blank

    @pl.when(core == 0)
    def _():
        out_ref[0, 0] = blank
        out_ref[0, 1] = blank

    @pl.when(core == 1)
    def _():
        out_ref[chips - 1, strip + 2] = blank
        out_ref[chips - 1, strip + 3] = blank


VMEM_SPEC = pl.BlockSpec(memory_space=pltpu.VMEM)


def spread(own, far, own_halo, far_halo, chips):
    cols, rows, chans = own.shape
    return pl.pallas_call(
        spread_kernel,
        out_shape=jax.ShapeDtypeStruct((chips, cols // (2 * chips) + 8, rows, 6 * chans), BF16),
        in_specs=[VMEM_SPEC] * 4,
        out_specs=VMEM_SPEC,
        compiler_params=pltpu.CompilerParams(vmem_limit_bytes=2 * 2**20),
        cost_estimate=QUICK,
        name="spread",
    )(own, far, own_halo, far_halo)


def chip_at(step):
    return lax.rem(lax.axis_index("y") + step, lax.axis_size("y"))


def conv_kernel(parts, adds, wide_ref, kernel_ref, *refs):
    rows = wide_ref.shape[2]
    for (step, first), add_ref, out_ref in zip(parts, refs[:adds] or [None] * len(parts), refs[adds:]):
        count, _, outs = out_ref.shape
        chip = chip_at(step)
        pieces = [wide_ref[chip, first + tap : first + tap + count] for tap in range(3)]
        lhs = jnp.concatenate(pieces, axis=-1).reshape(count * rows, -1)
        total = jnp.dot(lhs, kernel_ref[...], preferred_element_type=F32)
        total = total.reshape(count, rows, outs)
        if add_ref is not None:
            total = total + add_ref[...].astype(F32)
        out_ref[...] = total.astype(out_ref.dtype)


def conv_parts(parts, wide, kernel, count, dtype, adds=()):
    rows, outs = wide.shape[2], kernel.shape[1]
    return pl.pallas_call(
        functools.partial(conv_kernel, parts, len(adds)),
        out_shape=(jax.ShapeDtypeStruct((count, rows, outs), dtype),) * len(parts),
        in_specs=[VMEM_SPEC] * (2 + len(adds)),
        out_specs=(VMEM_SPEC,) * len(parts),
        compiler_params=pltpu.CompilerParams(vmem_limit_bytes=4 * 2**20),
        cost_estimate=QUICK,
        name="conv_first",
    )(wide, kernel, *adds)


def grad_kernel(step, has_old, last, wide_ref, a_ref, b_ref, *refs):
    old_ref = refs[0] if has_old else None
    outs_refs, pad_ref = refs[1 if has_old else 0 : -1], refs[-1]
    half, rows, outs = a_ref.shape
    strip = 2 * half
    cols, depth = wide_ref.shape[1], wide_ref.shape[3]
    pad_ref[0:3] = jnp.zeros((3, rows, outs), BF16)
    pad_ref[3 : 3 + half] = a_ref[...]
    pad_ref[3 + half : 3 + strip] = b_ref[...]
    pad_ref[3 + strip :] = jnp.zeros((cols - strip - 1, rows, outs), BF16)
    lhs = wide_ref[chip_at(step)].reshape(cols * rows, depth)
    rhs = jnp.concatenate(
        [pad_ref[2 - tap : 2 - tap + cols].reshape(cols * rows, outs) for tap in range(3)], axis=-1
    )
    total = lax.dot_general(lhs, rhs, (((0,), (0,)), ((), ())), preferred_element_type=F32)
    if has_old:
        total = total + old_ref[...]
    if not last:
        outs_refs[0][...] = total
    else:
        chans = depth // 6
        for tap in range(3):
            at = 2 * tap * chans
            outs_refs[0][tap * chans : (tap + 1) * chans] = total[at : at + chans]
            outs_refs[1][tap * chans : (tap + 1) * chans] = total[
                at + chans : at + 2 * chans
            ].astype(BF16)


def grad_strip(step, wide, halves, old, last):
    _, rows, outs = halves[0].shape
    depth, cols = wide.shape[3], wide.shape[1]
    shape = (depth, 3 * outs)
    half = (depth // 2, 3 * outs)
    if last:
        out_shape = (jax.ShapeDtypeStruct(half, F32), jax.ShapeDtypeStruct(half, BF16))
    else:
        out_shape = (jax.ShapeDtypeStruct(shape, F32),)
    args = [wide, *halves] + ([old] if old is not None else [])
    out = pl.pallas_call(
        functools.partial(grad_kernel, step, old is not None, last),
        out_shape=out_shape,
        in_specs=[VMEM_SPEC] * len(args),
        out_specs=tuple([VMEM_SPEC] * len(out_shape)),
        scratch_shapes=[pltpu.VMEM((cols + 2, rows, outs), BF16)],
        compiler_params=pltpu.CompilerParams(vmem_limit_bytes=5 * 2**20),
        cost_estimate=QUICK,
        name="grad_first",
    )(*args)
    return out if last else out[0]


def spread_tile(columns, wide_ref):
    rows, chans = wide_ref.shape[1], wide_ref.shape[2] // 3
    place = lax.broadcasted_iota(jnp.int32, (rows, chans), 0)
    for j, (mid, before, after) in enumerate(columns):
        wide = mid.astype(F32)
        ahead = jnp.where(place == 0, before.astype(F32), pltpu.roll(wide, 1, 0))
        behind = jnp.where(place == rows - 1, after.astype(F32), pltpu.roll(wide, rows - 1, 0))
        wide_ref[j, :, 0:chans] = ahead.astype(BF16)
        wide_ref[j, :, chans : 2 * chans] = mid
        wide_ref[j, :, 2 * chans :] = behind.astype(BF16)


def back_kernel(cot_ref, left_ref, right_ref, edge_ref, kernel_ref, out_ref, wide_ref):
    cols, rows, chans = cot_ref.shape
    start = edge_ref.shape[1] - 2 * cols

    def beside(k, j):
        low, high = start + j, start + cols + j
        return jnp.concatenate(
            [edge_ref[k, low : low + 1, :], edge_ref[k, high : high + 1, :]], axis=-1
        )

    def whole(ref):
        return ref[0:rows], ref[rows : rows + 1], ref[rows + 1 : rows + 2]

    columns = [(cot_ref[j], beside(0, j), beside(1, j)) for j in range(cols)]
    spread_tile([whole(left_ref)] + columns + [whole(right_ref)], wide_ref)
    total = None
    for tap_col in range(3):
        lhs = wide_ref[tap_col : tap_col + cols].reshape(cols * rows, 3 * chans)
        for tap_row in range(3):
            part = lax.dot_general(
                lhs[:, tap_row * chans : (tap_row + 1) * chans],
                kernel_ref[2 - tap_col, 2 - tap_row],
                (((1,), (1,)), ((), ())),
                preferred_element_type=F32,
            )
            total = part if total is None else total + part
    out_ref[...] = total.reshape(cols, rows, -1)


def back_tile(tile, left, right, edges, kernel):
    cols, rows, chans = tile.shape
    return pl.pallas_call(
        back_kernel,
        out_shape=jax.ShapeDtypeStruct((cols, rows, kernel.shape[2]), F32),
        in_specs=[VMEM_SPEC] * 5,
        out_specs=VMEM_SPEC,
        scratch_shapes=[pltpu.VMEM((cols + 2, rows, 3 * chans), BF16)],
        compiler_params=pltpu.CompilerParams(vmem_limit_bytes=4 * 2**20),
        cost_estimate=QUICK,
        name="back",
    )(tile, left, right, edges, kernel)


def second_kernel(
    chips, hid_ref, before_ref, after_ref, cot_ref, wide_ref, near_ref, far_ref, pad_ref, sum_ref
):
    chans = hid_ref.shape[2]
    cols, rows, outs = cot_ref.shape
    width = wide_ref.shape[0]
    core = lax.axis_index("c")
    columns = [
        (hid_ref[j], before_ref[j : j + 1, :], after_ref[j : j + 1, :]) for j in range(cols + 2)
    ]
    spread_tile(columns, wide_ref)
    wide_ref[cols + 2 :] = jnp.zeros((width - cols - 2, rows, 3 * chans), BF16)

    pad_ref[0:2] = jnp.zeros((2, rows, outs), BF16)
    pad_ref[2 : 2 + cols] = cot_ref[...]
    pad_ref[2 + cols :] = jnp.zeros((width - cols, rows, outs), BF16)
    rhs = jnp.concatenate(
        [pad_ref[2 - tap : 2 - tap + width].reshape(width * rows, outs) for tap in range(3)],
        axis=-1,
    )
    sum_ref[...] = lax.dot_general(
        wide_ref[...].reshape(width * rows, 3 * chans),
        rhs,
        (((0,), (0,)), ((), ())),
        preferred_element_type=F32,
    )
    size = sum_ref.shape[0] // (2 * chips)
    for half, ref in ((core, near_ref), (1 - core, far_ref)):
        for chip in range(chips):
            at = pl.multiple_of((half * chips + chip) * size, size)
            for tap in range(3):
                ref[chip, tap * size : (tap + 1) * size, :] = sum_ref[
                    pl.ds(at, size), tap * outs : (tap + 1) * outs
                ].astype(ref.dtype)


def second_tile(tile, edges, cotangent, chips):
    chans = tile.shape[2]
    cols, rows, outs = cotangent.shape
    width = cols + 8
    cut = (chips, 9 * chans // (2 * chips), outs)
    return pl.pallas_call(
        functools.partial(second_kernel, chips),
        out_shape=(
            jax.ShapeDtypeStruct((width, rows, 3 * chans), BF16),
            jax.ShapeDtypeStruct(cut, F32),
            jax.ShapeDtypeStruct(cut, BF16),
        ),
        in_specs=[VMEM_SPEC] * 4,
        out_specs=(VMEM_SPEC,) * 3,
        scratch_shapes=[
            pltpu.VMEM((width + 2, rows, outs), BF16),
            pltpu.VMEM((3 * chans, 3 * outs), F32),
        ],
        compiler_params=pltpu.CompilerParams(vmem_limit_bytes=9 * 2**20),
        cost_estimate=QUICK,
        name="second",
    )(tile, *edges, cotangent)


def features_kernel(wide_ref, kernel_ref, out_ref):
    cols, rows, outs = out_ref.shape
    pieces = [wide_ref[tap : tap + cols] for tap in range(3)]
    lhs = jnp.concatenate(pieces, axis=-1).reshape(cols * rows, -1)
    total = jnp.dot(lhs, kernel_ref[...], preferred_element_type=F32)
    out_ref[...] = total.reshape(cols, rows, outs).astype(BF16)


def features_tile(wide, kernel, cols):
    rows, outs = wide.shape[1], kernel.shape[3]
    return pl.pallas_call(
        features_kernel,
        out_shape=jax.ShapeDtypeStruct((cols, rows, outs), BF16),
        in_specs=[VMEM_SPEC] * 2,
        out_specs=VMEM_SPEC,
        compiler_params=pltpu.CompilerParams(vmem_limit_bytes=4 * 2**20),
        cost_estimate=QUICK,
        name="features",
    )(wide, kernel.reshape(-1, outs))


def point_kernel(
    own_ref, a0_ref, a1_ref, b0_ref, b1_ref, back_ref,
    da_ref, db_ref, hidden_ref, last_ref, first_ref,
):
    cols, rows, _ = own_ref.shape
    half = da_ref.shape[0]
    strip = 2 * lax.axis_index("y") + lax.axis_index("c")
    strips = 2 * lax.axis_size("y")

    def column(j, i, refs, delta_ref, keep):
        pre = own_ref[j] + refs[0][i].astype(F32) + refs[1][i].astype(F32)
        sigma = jax.nn.sigmoid(pre)
        hidden = pre * sigma
        if keep is not None:
            hidden = jnp.where(keep, hidden, 0.0)
        hidden = hidden.astype(BF16)
        hidden_ref[j] = hidden
        last_ref[j : j + 1, :] = hidden[rows - 1 :]
        first_ref[j : j + 1, :] = hidden[:1]
        if keep is None:
            slope = sigma * (1.0 + pre * (1.0 - sigma))
            at = j - 1 if delta_ref is da_ref else j - 1 - half
            delta_ref[at] = (back_ref[j - 1] * slope).astype(BF16)

    left, right = (a0_ref, a1_ref), (b0_ref, b1_ref)
    column(0, 0, left, None, strip > 0)
    column(cols - 1, half, right, None, strip < strips - 1)

    for i in range(1, half + 1):
        column(i, i, left, da_ref, None)
        column(half + i, i - 1, right, db_ref, None)


def point(own, left, right, back):
    strip, rows, outs = back.shape
    cut = jax.ShapeDtypeStruct((strip // 2, rows, outs), BF16)
    edge = jax.ShapeDtypeStruct((strip + 2, outs), BF16)
    return pl.pallas_call(
        point_kernel,
        out_shape=(cut, cut, jax.ShapeDtypeStruct(own.shape, BF16), edge, edge),
        in_specs=[VMEM_SPEC] * 6,
        out_specs=(VMEM_SPEC,) * 5,
        compiler_params=pltpu.CompilerParams(vmem_limit_bytes=2 * 2**20),
        cost_estimate=QUICK,
        name="point",
    )(own, *left, *right, back)


def fold_kernel(near_ref, got_ref, keep_ref, *send_refs):
    chips = near_ref.shape[0]
    here = lax.axis_index("y")
    keep_ref[...] = near_ref[here] + got_ref[here].astype(F32)
    for step, ref in zip(STEPS[1:], send_refs):
        to = lax.rem(here + step, chips)
        ref[...] = (near_ref[to] + got_ref[to].astype(F32)).astype(BF16)


def fold(near, got):
    shape = near.shape[1:]
    return pl.pallas_call(
        fold_kernel,
        out_shape=(jax.ShapeDtypeStruct(shape, F32),) + (jax.ShapeDtypeStruct(shape, BF16),) * 3,
        in_specs=[VMEM_SPEC] * 2,
        out_specs=(VMEM_SPEC,) * 4,
        compiler_params=pltpu.CompilerParams(vmem_limit_bytes=2 * 2**20),
        cost_estimate=QUICK,
        name="fold",
    )(near, got)


def row_halo(ends):
    count = lax.axis_size(SKY)
    up = [(i, i + 1) for i in range(count - 1)]
    down = [(j, i) for i, j in up]
    return lax.ppermute(ends[0], SKY, up), lax.ppermute(ends[1], SKY, down)


def join_kernel(own_ref, far_ref, keep_ref, a_ref, b_ref, c_ref, out_ref):
    pieces, total, outs = out_ref.shape
    chans = own_ref.shape[0] // 3
    size = chans // pieces
    for tap_col in range(3):
        for tap_row in range(3):
            rows = slice(tap_row * chans, (tap_row + 1) * chans)
            lanes = slice(tap_col * outs, (tap_col + 1) * outs)
            value = own_ref[rows, lanes] + far_ref[rows, lanes].astype(F32)
            at = (3 * tap_col + tap_row) * size
            out_ref[:, at : at + size, :] = value.reshape(pieces, size, outs).astype(BF16)
    second = keep_ref[...]
    for ref in (a_ref, b_ref, c_ref):
        second = second + ref[...].astype(F32)
    sx = lax.axis_size("x")
    sz = pieces // sx
    third = second.shape[0] // 3
    size_x = third // sx
    extra = total - 9 * size
    for x in range(sx):
        value = jnp.concatenate(
            [second[tap * third + x * size_x : tap * third + (x + 1) * size_x] for tap in range(3)],
            axis=0,
        )
        for z in range(sz):
            out_ref[z * sx + x, 9 * size :, :] = value[z * extra : (z + 1) * extra].astype(BF16)


def join(own, far, keep, got, pieces):
    outs = keep.shape[1]
    rows = 9 * (own.shape[0] // 3 // pieces) + keep.shape[0] // pieces
    return pl.pallas_call(
        join_kernel,
        out_shape=jax.ShapeDtypeStruct((pieces, rows, outs), BF16),
        in_specs=[VMEM_SPEC] * 6,
        out_specs=VMEM_SPEC,
        compiler_params=pltpu.CompilerParams(vmem_limit_bytes=4 * 2**20),
        cost_estimate=QUICK,
        name="join",
    )(own, far, keep, *got)


STEPS = (0, 1, 3, 2)


def order_kernel(extra, a_ref, b_ref, c_ref, d_ref, out_ref):
    rows = a_ref.shape[0] - extra
    sz = lax.axis_size("z")
    me = lax.axis_index("z")
    values = [ref[...].astype(F32) for ref in (a_ref, b_ref, c_ref, d_ref)]
    rest = []
    for z in range(len(STEPS)):
        value = values[0]
        for step, other in zip(STEPS[1:], values[1:]):
            value = jnp.where(lax.rem(me + sz - step, sz) == z, other, value)
        out_ref[z * rows : (z + 1) * rows, :] = value[:rows].astype(BF16)
        rest.append(value[rows:])
    out_ref[len(STEPS) * rows :, :] = jnp.concatenate(rest, axis=0).astype(BF16)


def order_pieces(parts, extra):
    rows, outs = parts[0].shape
    return pl.pallas_call(
        functools.partial(order_kernel, extra),
        out_shape=jax.ShapeDtypeStruct((4 * rows, outs), BF16),
        in_specs=[VMEM_SPEC] * 4,
        out_specs=VMEM_SPEC,
        compiler_params=pltpu.CompilerParams(vmem_limit_bytes=4 * 2**20),
        cost_estimate=QUICK,
        name="order_pieces",
    )(*parts)


def first_kernel(sz, a_ref, b_ref, c_ref, d_ref, out_ref):
    sx = lax.axis_size("x")
    size = out_ref.shape[2] // (sx * sz)
    me = lax.axis_index("x")
    for step, ref in zip(STEPS, (a_ref, b_ref, c_ref, d_ref)):
        x = lax.rem(me + sx - step, sx)
        value = ref[...].astype(F32)
        for z in range(sz):
            at = pl.multiple_of((z * sx + x) * size, size)
            for tap in range(9):
                rows = (z * 9 + tap) * size
                out_ref[tap // 3, tap % 3, pl.ds(at, size), :] = value[rows : rows + size]


def lay_first(parts, sz, chans):
    outs = parts[0].shape[1]
    return pl.pallas_call(
        functools.partial(first_kernel, sz),
        out_shape=jax.ShapeDtypeStruct((3, 3, chans, outs), F32),
        in_specs=[VMEM_SPEC] * 4,
        out_specs=VMEM_SPEC,
        compiler_params=pltpu.CompilerParams(vmem_limit_bytes=4 * 2**20),
        cost_estimate=QUICK,
        name="lay_first",
    )(*parts)


def sum_kernel(in_ref, out_ref):
    total = in_ref[0].astype(F32)
    for i in range(1, in_ref.shape[0]):
        total = total + in_ref[i].astype(F32)
    out_ref[...] = total.astype(BF16)


def sum_pieces(pieces):
    return pl.pallas_call(
        sum_kernel,
        out_shape=jax.ShapeDtypeStruct(pieces.shape[1:], BF16),
        in_specs=[VMEM_SPEC],
        out_specs=VMEM_SPEC,
        compiler_params=pltpu.CompilerParams(vmem_limit_bytes=4 * 2**20),
        cost_estimate=QUICK,
        name="sum_pieces",
    )(pieces)


def pick_kernel(first, a_ref, b_ref, c_ref, d_ref, out_ref):
    for i, ref in enumerate((a_ref, b_ref, c_ref, d_ref)):
        out_ref[i] = ref[first:, :]


def pick_rows(parts, first):
    rows, outs = parts[0].shape
    return pl.pallas_call(
        functools.partial(pick_kernel, first),
        out_shape=jax.ShapeDtypeStruct((len(parts), rows - first, outs), BF16),
        in_specs=[VMEM_SPEC] * 4,
        out_specs=VMEM_SPEC,
        compiler_params=pltpu.CompilerParams(vmem_limit_bytes=2 * 2**20),
        cost_estimate=QUICK,
        name="pick_rows",
    )(*parts)


def lay_second_kernel(other, in_ref, *refs):
    out_ref, half_ref, sems = refs[-3:]
    sy, sx, rows, _ = in_ref.shape
    size = rows // 3
    third = half_ref.shape[0] // 3
    core, y, x = lax.axis_index("c"), lax.axis_index("y"), lax.axis_index("x")
    half = 1 - core if other else core
    for i in range(sy):
        for j in range(sx):
            place = lax.rem(y + sy - STEPS[i], sy) * sx + lax.rem(x + sx - STEPS[j], sx)
            value = in_ref[i, j].astype(F32)
            for tap in range(3):
                at = pl.multiple_of(tap * third + place * size, 8)
                half_ref[pl.ds(at, size), :] = value[tap * size : (tap + 1) * size]
    copies = []
    for tap in range(3):
        to = pl.multiple_of((2 * tap + half) * third, 8)
        copies.append(
            pltpu.make_async_copy(
                half_ref.at[tap * third : (tap + 1) * third],
                out_ref.at[pl.ds(to, third)],
                sems.at[tap],
            )
        )
    for copy in copies:
        copy.start()
    for copy in copies:
        copy.wait()


def lay_second(half, whole=None):
    sy, sx, rows, outs = half.shape
    size = sy * sx * rows
    anywhere = pl.BlockSpec(memory_space=pl.ANY)
    given = [] if whole is None else [whole]
    return pl.pallas_call(
        functools.partial(lay_second_kernel, whole is not None),
        out_shape=jax.ShapeDtypeStruct((2 * size, outs), F32),
        in_specs=[VMEM_SPEC] + [anywhere] * len(given),
        out_specs=anywhere,
        scratch_shapes=[pltpu.VMEM((size, outs), F32), pltpu.SemaphoreType.DMA((3,))],
        compiler_params=pltpu.CompilerParams(vmem_limit_bytes=4 * 2**20),
        cost_estimate=QUICK,
        input_output_aliases={1: 0} if given else {},
        name="lay_second",
    )(half, *given)


def gather_steps(piece, axis):
    return [piece] + [shift(piece, axis, step) for step in STEPS[1:]]


def body(sky_cube, weight_first, weight_second, cotangent):
    cols, rows, chans = sky_cube.shape
    strip, _, outs = cotangent.shape
    chips = lax.axis_size("y")

    ends = [
        jnp.concatenate(
            [sky_cube[:, r], cotangent[:, r, : outs // 2], cotangent[:, r, outs // 2 :]], axis=0
        )
        for r in (rows - 1, 0)
    ]
    edges = jnp.stack(row_halo(ends))
    far_cube = shift(sky_cube, "c", 1)
    far_weight = shift(weight_first, "c", 1)
    far_edges = shift(edges, "c", 1)
    wide = spread(sky_cube, far_cube, edges, far_edges, chips)
    kernel = jnp.concatenate([weight_first, far_weight], axis=2).reshape(18 * chans, outs)

    def side(col):
        beside = [
            jnp.concatenate(
                [edges[k, at + col : at + col + 1] for at in (cols, cols + strip)], axis=1
            )
            for k in range(2)
        ]
        return jnp.concatenate([cotangent[col]] + beside, axis=0)

    count = lax.axis_size(FREQ)
    up = [(i, i + 1) for i in range(count - 1)]
    down = [(j, i) for i, j in up]
    left = lax.ppermute(side(strip - 1), FREQ, up)
    right = lax.ppermute(side(0), FREQ, down)

    on, off = 1, chips - 1
    cut = strip // 2 + 1
    far_a, far_b = conv_parts(((2, 0), (2, cut)), wide, kernel, cut, BF16)
    hold, _ = lax.optimization_barrier((wide, far_a))
    near_b, near_a = conv_parts(((on, cut), (off, 0)), hold, kernel, cut, BF16)
    got_a, got_b = shift(far_a, "y", on), shift(far_b, "y", off)
    got_a, left, right = lax.optimization_barrier((got_a, left, right))
    both_a, both_b = conv_parts(((on, 0), (off, cut)), wide, kernel, cut, BF16, (got_a, got_b))
    own = conv_parts(((0, 0),), wide, kernel, strip + 2, F32)[0]
    from_a = shift(both_a, "y", on), shift(near_a, "y", off)
    from_b = shift(near_b, "y", on), shift(both_b, "y", off)

    back = back_tile(cotangent, left, right, edges, weight_second)
    delta_a, delta_b, hidden, *ends = point(own, from_a, from_b, back)

    on_a, off_b = shift(delta_a, "y", on), shift(delta_b, "y", off)
    edges = row_halo(ends)
    total = grad_strip(0, wide, (delta_a, delta_b), None, False)
    on_a, off_b, edges, late_a, late_b, total = lax.optimization_barrier(
        (on_a, off_b, edges, delta_a, delta_b, total)
    )
    on_b, off_a = shift(late_b, "y", on), shift(late_a, "y", off)
    fwd_a, fwd_b = shift(on_a, "y", on), shift(off_b, "y", off)
    wide_hidden, near, far = second_tile(hidden, edges, cotangent, chips)
    far, on_b, off_a = lax.optimization_barrier((far, on_b, off_a))
    keep, *sends = fold(near, shift(far, "c", 1))
    got = [shift(send, "y", step) for step, send in zip(STEPS[1:], sends)]
    total = grad_strip(off, wide, (on_a, on_b), total, False)
    total = grad_strip(on, wide, (off_a, off_b), total, False)
    first_own, first_far = grad_strip(2, wide, (fwd_a, fwd_b), total, True)

    sx, sz = lax.axis_size("x"), lax.axis_size("z")
    joined = join(first_own, shift(first_far, "c", 1), keep, got, sx * sz)
    extra = keep.shape[0] // (sx * sz)
    summed = lax.all_to_all(joined, SKY, 0, 0, tiled=True)
    summed = sum_pieces(summed)
    parts = gather_steps(order_pieces(gather_steps(summed, "z"), extra), "x")
    main = parts[0].shape[0] - sz * extra
    grad_first = lay_first(parts, sz, chans)
    features = features_tile(wide_hidden, weight_second, strip)
    share = pick_rows(parts, main)
    share, features = lax.optimization_barrier((share, features))
    share = jnp.stack(gather_steps(share, "y"))
    grad_second = lay_second(shift(share, "c", 1), lay_second(share))
    grad_second = grad_second.reshape(3, 3, outs, outs)
    return features, grad_first, grad_second


def solution(mesh):
    sizes = (mesh.devices.shape[0] // 2, 2, 4, mesh.devices.shape[1] // 4)
    fine = Mesh(mesh.devices.reshape(sizes), FREQ + SKY)
    return jax.shard_map(
        body,
        mesh=fine,
        in_specs=(P(None, SKY, FREQ), P(None, None, FREQ, None), P(), P(FREQ, SKY, None)),
        out_specs=(P(FREQ, SKY, None), P(None, None, FREQ, None), P()),
        check_vma=False,
    )
```

```python
import functools

import jax
import jax.numpy as jnp
from jax import lax
from jax.experimental import pallas as pl
from jax.experimental.pallas import tpu as pltpu
from jax.sharding import Mesh, PartitionSpec as P

FREQ = ("y", "c")
SKY = ("z", "x")
F32 = jnp.float32
BF16 = jnp.bfloat16
QUICK = pl.CostEstimate(flops=1, bytes_accessed=1, transcendentals=0)


def shift(x, axis, step):
    count = lax.axis_size(axis)
    return lax.ppermute(x, axis, [(i, (i + step) % count) for i in range(count)])


def spread_kernel(own_ref, far_ref, own_halo_ref, far_halo_ref, out_ref):
    chips, width, rows, depth = out_ref.shape
    cols, _, chans = own_ref.shape
    strip = cols // (2 * chips)
    core = lax.axis_index("c")
    step = 8
    row = lax.broadcasted_iota(jnp.int32, (step, rows, chans), 1)

    def block(i, base, chip):
        for side, (cube_ref, halo_ref) in enumerate(
            ((own_ref, own_halo_ref), (far_ref, far_halo_ref))
        ):
            at = pl.multiple_of(base + i * step, step)
            mid = cube_ref[pl.ds(at, step)]
            wide = mid.astype(F32).reshape(step * rows, chans)
            ahead = pltpu.roll(wide, 1, 0).reshape(step, rows, chans)
            behind = pltpu.roll(wide, step * rows - 1, 0).reshape(step, rows, chans)
            before = halo_ref[0, pl.ds(at, step), :].astype(F32)[:, None, :]
            after = halo_ref[1, pl.ds(at, step), :].astype(F32)[:, None, :]
            ahead = jnp.where(row == 0, before, ahead)
            behind = jnp.where(row == rows - 1, after, behind)
            to = pl.ds(2 + i * step, step)
            for tap, value in enumerate((ahead.astype(BF16), mid, behind.astype(BF16))):
                lane = (2 * tap + side) * chans
                out_ref[chip, to, :, lane : lane + chans] = value

    def edge(at, chip, slot):
        for side, (cube_ref, halo_ref) in enumerate(
            ((own_ref, own_halo_ref), (far_ref, far_halo_ref))
        ):
            first = pl.multiple_of((at // step) * step, step)
            mid = cube_ref[at]
            wide = mid.astype(F32)
            line = lax.broadcasted_iota(jnp.int32, (step, chans), 0) == at - first
            pick = lambda k: jnp.sum(
                jnp.where(line, halo_ref[k, pl.ds(first, step), :].astype(F32), 0.0),
                axis=0,
                keepdims=True,
            )
            place = lax.broadcasted_iota(jnp.int32, (rows, chans), 0)
            ahead = jnp.where(place == 0, pick(0), pltpu.roll(wide, 1, 0))
            behind = jnp.where(place == rows - 1, pick(1), pltpu.roll(wide, rows - 1, 0))
            for tap, value in enumerate((ahead.astype(BF16), mid, behind.astype(BF16))):
                lane = (2 * tap + side) * chans
                out_ref[chip, slot, :, lane : lane + chans] = value

    blank = jnp.zeros((rows, depth), BF16)
    for chip in range(chips):
        base = (2 * chip + core) * strip
        lax.fori_loop(0, strip // step, lambda i, _: block(i, base, chip), None)
        for slot in (0, 1):
            edge(jnp.maximum(base - 2 + slot, 0), chip, slot)
            edge(jnp.minimum(base + strip + slot, cols - 1), chip, strip + 2 + slot)
        for slot in range(strip + 4, width):
            out_ref[chip, slot] = blank

    @pl.when(core == 0)
    def _():
        out_ref[0, 0] = blank
        out_ref[0, 1] = blank

    @pl.when(core == 1)
    def _():
        out_ref[chips - 1, strip + 2] = blank
        out_ref[chips - 1, strip + 3] = blank


VMEM_SPEC = pl.BlockSpec(memory_space=pltpu.VMEM)


def spread(own, far, own_halo, far_halo, chips):
    cols, rows, chans = own.shape
    return pl.pallas_call(
        spread_kernel,
        out_shape=jax.ShapeDtypeStruct((chips, cols // (2 * chips) + 8, rows, 6 * chans), BF16),
        in_specs=[VMEM_SPEC] * 4,
        out_specs=VMEM_SPEC,
        compiler_params=pltpu.CompilerParams(vmem_limit_bytes=2 * 2**20),
        cost_estimate=QUICK,
        name="spread",
    )(own, far, own_halo, far_halo)


def chip_at(step):
    return lax.rem(lax.axis_index("y") + step, lax.axis_size("y"))


def conv_kernel(parts, adds, wide_ref, kernel_ref, *refs):
    rows = wide_ref.shape[2]
    for (step, first), add_ref, out_ref in zip(parts, refs[:adds] or [None] * len(parts), refs[adds:]):
        count, _, outs = out_ref.shape
        chip = chip_at(step)
        pieces = [wide_ref[chip, first + tap : first + tap + count] for tap in range(3)]
        lhs = jnp.concatenate(pieces, axis=-1).reshape(count * rows, -1)
        total = jnp.dot(lhs, kernel_ref[...], preferred_element_type=F32)
        total = total.reshape(count, rows, outs)
        if add_ref is not None:
            total = total + add_ref[...].astype(F32)
        out_ref[...] = total.astype(out_ref.dtype)


def conv_parts(parts, wide, kernel, count, dtype, adds=()):
    rows, outs = wide.shape[2], kernel.shape[1]
    return pl.pallas_call(
        functools.partial(conv_kernel, parts, len(adds)),
        out_shape=(jax.ShapeDtypeStruct((count, rows, outs), dtype),) * len(parts),
        in_specs=[VMEM_SPEC] * (2 + len(adds)),
        out_specs=(VMEM_SPEC,) * len(parts),
        compiler_params=pltpu.CompilerParams(vmem_limit_bytes=4 * 2**20),
        cost_estimate=QUICK,
        name="conv_first",
    )(wide, kernel, *adds)


def grad_kernel(step, pieces, has_old, last, wide_ref, *refs):
    piece_refs, refs = refs[:pieces], refs[pieces:]
    old_ref = refs[0] if has_old else None
    outs_refs, pad_ref = refs[1 if has_old else 0 : -1], refs[-1]
    count, rows, outs = piece_refs[0].shape
    strip = pieces * count
    cols, depth = wide_ref.shape[1], wide_ref.shape[3]
    pad_ref[0:3] = jnp.zeros((3, rows, outs), BF16)
    for i, ref in enumerate(piece_refs):
        pad_ref[3 + i * count : 3 + (i + 1) * count] = ref[...]
    pad_ref[3 + strip :] = jnp.zeros((cols - strip - 1, rows, outs), BF16)
    lhs = wide_ref[chip_at(step)].reshape(cols * rows, depth)
    rhs = jnp.concatenate(
        [pad_ref[2 - tap : 2 - tap + cols].reshape(cols * rows, outs) for tap in range(3)], axis=-1
    )
    total = lax.dot_general(lhs, rhs, (((0,), (0,)), ((), ())), preferred_element_type=F32)
    if has_old:
        total = total + old_ref[...]
    if not last:
        outs_refs[0][...] = total
    else:
        chans = depth // 6
        for tap in range(3):
            at = 2 * tap * chans
            outs_refs[0][tap * chans : (tap + 1) * chans] = total[at : at + chans]
            outs_refs[1][tap * chans : (tap + 1) * chans] = total[
                at + chans : at + 2 * chans
            ].astype(BF16)


def grad_strip(step, wide, pieces, old, last):
    _, rows, outs = pieces[0].shape
    depth, cols = wide.shape[3], wide.shape[1]
    shape = (depth, 3 * outs)
    half = (depth // 2, 3 * outs)
    if last:
        out_shape = (jax.ShapeDtypeStruct(half, F32), jax.ShapeDtypeStruct(half, BF16))
    else:
        out_shape = (jax.ShapeDtypeStruct(shape, F32),)
    args = [wide, *pieces] + ([old] if old is not None else [])
    out = pl.pallas_call(
        functools.partial(grad_kernel, step, len(pieces), old is not None, last),
        out_shape=out_shape,
        in_specs=[VMEM_SPEC] * len(args),
        out_specs=tuple([VMEM_SPEC] * len(out_shape)),
        scratch_shapes=[pltpu.VMEM((cols + 2, rows, outs), BF16)],
        compiler_params=pltpu.CompilerParams(vmem_limit_bytes=5 * 2**20),
        cost_estimate=QUICK,
        name="grad_first",
    )(*args)
    return out if last else out[0]


def spread_tile(columns, wide_ref):
    rows, chans = wide_ref.shape[1], wide_ref.shape[2] // 3
    place = lax.broadcasted_iota(jnp.int32, (rows, chans), 0)
    for j, (mid, before, after) in enumerate(columns):
        wide = mid.astype(F32)
        ahead = jnp.where(place == 0, before.astype(F32), pltpu.roll(wide, 1, 0))
        behind = jnp.where(place == rows - 1, after.astype(F32), pltpu.roll(wide, rows - 1, 0))
        wide_ref[j, :, 0:chans] = ahead.astype(BF16)
        wide_ref[j, :, chans : 2 * chans] = mid
        wide_ref[j, :, 2 * chans :] = behind.astype(BF16)


def back_kernel(cot_ref, left_ref, right_ref, edge_ref, kernel_ref, out_ref, wide_ref):
    cols, rows, chans = cot_ref.shape
    start = edge_ref.shape[1] - 2 * cols

    def beside(k, j):
        low, high = start + j, start + cols + j
        return jnp.concatenate(
            [edge_ref[k, low : low + 1, :], edge_ref[k, high : high + 1, :]], axis=-1
        )

    def whole(ref):
        return ref[0:rows], ref[rows : rows + 1], ref[rows + 1 : rows + 2]

    columns = [(cot_ref[j], beside(0, j), beside(1, j)) for j in range(cols)]
    spread_tile([whole(left_ref)] + columns + [whole(right_ref)], wide_ref)
    total = None
    for tap_col in range(3):
        lhs = wide_ref[tap_col : tap_col + cols].reshape(cols * rows, 3 * chans)
        for tap_row in range(3):
            part = lax.dot_general(
                lhs[:, tap_row * chans : (tap_row + 1) * chans],
                kernel_ref[2 - tap_col, 2 - tap_row],
                (((1,), (1,)), ((), ())),
                preferred_element_type=F32,
            )
            total = part if total is None else total + part
    out_ref[...] = total.reshape(cols, rows, -1)


def back_tile(tile, left, right, edges, kernel):
    cols, rows, chans = tile.shape
    return pl.pallas_call(
        back_kernel,
        out_shape=jax.ShapeDtypeStruct((cols, rows, kernel.shape[2]), F32),
        in_specs=[VMEM_SPEC] * 5,
        out_specs=VMEM_SPEC,
        scratch_shapes=[pltpu.VMEM((cols + 2, rows, 3 * chans), BF16)],
        compiler_params=pltpu.CompilerParams(vmem_limit_bytes=4 * 2**20),
        cost_estimate=QUICK,
        name="back",
    )(tile, left, right, edges, kernel)


def second_kernel(
    chips, hid_ref, before_ref, after_ref, cot_ref, wide_ref, near_ref, far_ref, pad_ref, sum_ref
):
    chans = hid_ref.shape[2]
    cols, rows, outs = cot_ref.shape
    width = wide_ref.shape[0]
    core = lax.axis_index("c")
    columns = [
        (hid_ref[j], before_ref[j : j + 1, :], after_ref[j : j + 1, :]) for j in range(cols + 2)
    ]
    spread_tile(columns, wide_ref)
    wide_ref[cols + 2 :] = jnp.zeros((width - cols - 2, rows, 3 * chans), BF16)

    pad_ref[0:2] = jnp.zeros((2, rows, outs), BF16)
    pad_ref[2 : 2 + cols] = cot_ref[...]
    pad_ref[2 + cols :] = jnp.zeros((width - cols, rows, outs), BF16)
    rhs = jnp.concatenate(
        [pad_ref[2 - tap : 2 - tap + width].reshape(width * rows, outs) for tap in range(3)],
        axis=-1,
    )
    sum_ref[...] = lax.dot_general(
        wide_ref[...].reshape(width * rows, 3 * chans),
        rhs,
        (((0,), (0,)), ((), ())),
        preferred_element_type=F32,
    )
    size = sum_ref.shape[0] // (2 * chips)
    for half, ref in ((core, near_ref), (1 - core, far_ref)):
        for chip in range(chips):
            at = pl.multiple_of((half * chips + chip) * size, size)
            for tap in range(3):
                ref[chip, tap * size : (tap + 1) * size, :] = sum_ref[
                    pl.ds(at, size), tap * outs : (tap + 1) * outs
                ].astype(ref.dtype)


def second_tile(tile, edges, cotangent, chips):
    chans = tile.shape[2]
    cols, rows, outs = cotangent.shape
    width = cols + 8
    cut = (chips, 9 * chans // (2 * chips), outs)
    return pl.pallas_call(
        functools.partial(second_kernel, chips),
        out_shape=(
            jax.ShapeDtypeStruct((width, rows, 3 * chans), BF16),
            jax.ShapeDtypeStruct(cut, F32),
            jax.ShapeDtypeStruct(cut, BF16),
        ),
        in_specs=[VMEM_SPEC] * 4,
        out_specs=(VMEM_SPEC,) * 3,
        scratch_shapes=[
            pltpu.VMEM((width + 2, rows, outs), BF16),
            pltpu.VMEM((3 * chans, 3 * outs), F32),
        ],
        compiler_params=pltpu.CompilerParams(vmem_limit_bytes=9 * 2**20),
        cost_estimate=QUICK,
        name="second",
    )(tile, *edges, cotangent)


def features_kernel(wide_ref, kernel_ref, out_ref):
    cols, rows, outs = out_ref.shape
    pieces = [wide_ref[tap : tap + cols] for tap in range(3)]
    lhs = jnp.concatenate(pieces, axis=-1).reshape(cols * rows, -1)
    total = jnp.dot(lhs, kernel_ref[...], preferred_element_type=F32)
    out_ref[...] = total.reshape(cols, rows, outs).astype(BF16)


def features_tile(wide, kernel, cols):
    rows, outs = wide.shape[1], kernel.shape[3]
    return pl.pallas_call(
        features_kernel,
        out_shape=jax.ShapeDtypeStruct((cols, rows, outs), BF16),
        in_specs=[VMEM_SPEC] * 2,
        out_specs=VMEM_SPEC,
        compiler_params=pltpu.CompilerParams(vmem_limit_bytes=4 * 2**20),
        cost_estimate=QUICK,
        name="features",
    )(wide, kernel.reshape(-1, outs))


def point_kernel(
    own_ref, a0_ref, a1_ref, b0_ref, b1_ref, back_ref,
    delta_ref, hidden_ref, last_ref, first_ref,
):
    cols, rows, _ = own_ref.shape
    half = delta_ref.shape[0] // 2
    strip = 2 * lax.axis_index("y") + lax.axis_index("c")
    strips = 2 * lax.axis_size("y")

    def column(j, i, refs, keep):
        pre = own_ref[j] + refs[0][i].astype(F32) + refs[1][i].astype(F32)
        sigma = jax.nn.sigmoid(pre)
        hidden = pre * sigma
        if keep is not None:
            hidden = jnp.where(keep, hidden, 0.0)
        hidden = hidden.astype(BF16)
        hidden_ref[j] = hidden
        last_ref[j : j + 1, :] = hidden[rows - 1 :]
        first_ref[j : j + 1, :] = hidden[:1]
        if keep is None:
            slope = sigma * (1.0 + pre * (1.0 - sigma))
            delta_ref[j - 1] = (back_ref[j - 1] * slope).astype(BF16)

    left, right = (a0_ref, a1_ref), (b0_ref, b1_ref)
    column(0, 0, left, strip > 0)
    column(cols - 1, half, right, strip < strips - 1)

    for i in range(1, half + 1):
        column(i, i, left, None)
        column(half + i, i - 1, right, None)


def point(own, left, right, back):
    strip, rows, outs = back.shape
    delta = jax.ShapeDtypeStruct(back.shape, BF16)
    edge = jax.ShapeDtypeStruct((strip + 2, outs), BF16)
    return pl.pallas_call(
        point_kernel,
        out_shape=(delta, jax.ShapeDtypeStruct(own.shape, BF16), edge, edge),
        in_specs=[VMEM_SPEC] * 6,
        out_specs=(VMEM_SPEC,) * 4,
        compiler_params=pltpu.CompilerParams(vmem_limit_bytes=2 * 2**20),
        cost_estimate=QUICK,
        name="point",
    )(own, *left, *right, back)


def fold_kernel(near_ref, got_ref, keep_ref, *send_refs):
    chips = near_ref.shape[0]
    here = lax.axis_index("y")
    keep_ref[...] = near_ref[here] + got_ref[here].astype(F32)
    for step, ref in zip(STEPS[1:], send_refs):
        to = lax.rem(here + step, chips)
        ref[...] = (near_ref[to] + got_ref[to].astype(F32)).astype(BF16)


def fold(near, got):
    shape = near.shape[1:]
    return pl.pallas_call(
        fold_kernel,
        out_shape=(jax.ShapeDtypeStruct(shape, F32),) + (jax.ShapeDtypeStruct(shape, BF16),) * 3,
        in_specs=[VMEM_SPEC] * 2,
        out_specs=(VMEM_SPEC,) * 4,
        compiler_params=pltpu.CompilerParams(vmem_limit_bytes=2 * 2**20),
        cost_estimate=QUICK,
        name="fold",
    )(near, got)


def row_halo(ends):
    count = lax.axis_size(SKY)
    up = [(i, i + 1) for i in range(count - 1)]
    down = [(j, i) for i, j in up]
    return lax.ppermute(ends[0], SKY, up), lax.ppermute(ends[1], SKY, down)


def join_kernel(own_ref, far_ref, keep_ref, a_ref, b_ref, c_ref, out_ref):
    pieces, total, outs = out_ref.shape
    chans = own_ref.shape[0] // 3
    size = chans // pieces
    for tap_col in range(3):
        for tap_row in range(3):
            rows = slice(tap_row * chans, (tap_row + 1) * chans)
            lanes = slice(tap_col * outs, (tap_col + 1) * outs)
            value = own_ref[rows, lanes] + far_ref[rows, lanes].astype(F32)
            at = (3 * tap_col + tap_row) * size
            out_ref[:, at : at + size, :] = value.reshape(pieces, size, outs).astype(BF16)
    second = keep_ref[...]
    for ref in (a_ref, b_ref, c_ref):
        second = second + ref[...].astype(F32)
    sx = lax.axis_size("x")
    sz = pieces // sx
    third = second.shape[0] // 3
    size_x = third // sx
    extra = total - 9 * size
    for x in range(sx):
        value = jnp.concatenate(
            [second[tap * third + x * size_x : tap * third + (x + 1) * size_x] for tap in range(3)],
            axis=0,
        )
        for z in range(sz):
            out_ref[z * sx + x, 9 * size :, :] = value[z * extra : (z + 1) * extra].astype(BF16)


def join(own, far, keep, got, pieces):
    outs = keep.shape[1]
    rows = 9 * (own.shape[0] // 3 // pieces) + keep.shape[0] // pieces
    return pl.pallas_call(
        join_kernel,
        out_shape=jax.ShapeDtypeStruct((pieces, rows, outs), BF16),
        in_specs=[VMEM_SPEC] * 6,
        out_specs=VMEM_SPEC,
        compiler_params=pltpu.CompilerParams(vmem_limit_bytes=4 * 2**20),
        cost_estimate=QUICK,
        name="join",
    )(own, far, keep, *got)


STEPS = (0, 1, 3, 2)


def order_kernel(extra, a_ref, b_ref, c_ref, d_ref, out_ref):
    rows = a_ref.shape[0] - extra
    sz = lax.axis_size("z")
    me = lax.axis_index("z")
    values = [ref[...].astype(F32) for ref in (a_ref, b_ref, c_ref, d_ref)]
    rest = []
    for z in range(len(STEPS)):
        value = values[0]
        for step, other in zip(STEPS[1:], values[1:]):
            value = jnp.where(lax.rem(me + sz - step, sz) == z, other, value)
        out_ref[z * rows : (z + 1) * rows, :] = value[:rows].astype(BF16)
        rest.append(value[rows:])
    out_ref[len(STEPS) * rows :, :] = jnp.concatenate(rest, axis=0).astype(BF16)


def order_pieces(parts, extra):
    rows, outs = parts[0].shape
    return pl.pallas_call(
        functools.partial(order_kernel, extra),
        out_shape=jax.ShapeDtypeStruct((4 * rows, outs), BF16),
        in_specs=[VMEM_SPEC] * 4,
        out_specs=VMEM_SPEC,
        compiler_params=pltpu.CompilerParams(vmem_limit_bytes=4 * 2**20),
        cost_estimate=QUICK,
        name="order_pieces",
    )(*parts)


def first_kernel(sz, a_ref, b_ref, c_ref, d_ref, out_ref):
    sx = lax.axis_size("x")
    size = out_ref.shape[2] // (sx * sz)
    me = lax.axis_index("x")
    for step, ref in zip(STEPS, (a_ref, b_ref, c_ref, d_ref)):
        x = lax.rem(me + sx - step, sx)
        value = ref[...].astype(F32)
        for z in range(sz):
            at = pl.multiple_of((z * sx + x) * size, size)
            for tap in range(9):
                rows = (z * 9 + tap) * size
                out_ref[tap // 3, tap % 3, pl.ds(at, size), :] = value[rows : rows + size]


def lay_first(parts, sz, chans):
    outs = parts[0].shape[1]
    return pl.pallas_call(
        functools.partial(first_kernel, sz),
        out_shape=jax.ShapeDtypeStruct((3, 3, chans, outs), F32),
        in_specs=[VMEM_SPEC] * 4,
        out_specs=VMEM_SPEC,
        compiler_params=pltpu.CompilerParams(vmem_limit_bytes=4 * 2**20),
        cost_estimate=QUICK,
        name="lay_first",
    )(*parts)


def sum_kernel(in_ref, out_ref):
    total = in_ref[0].astype(F32)
    for i in range(1, in_ref.shape[0]):
        total = total + in_ref[i].astype(F32)
    out_ref[...] = total.astype(BF16)


def sum_pieces(pieces):
    return pl.pallas_call(
        sum_kernel,
        out_shape=jax.ShapeDtypeStruct(pieces.shape[1:], BF16),
        in_specs=[VMEM_SPEC],
        out_specs=VMEM_SPEC,
        compiler_params=pltpu.CompilerParams(vmem_limit_bytes=4 * 2**20),
        cost_estimate=QUICK,
        name="sum_pieces",
    )(pieces)


def pick_kernel(first, a_ref, b_ref, c_ref, d_ref, out_ref):
    for i, ref in enumerate((a_ref, b_ref, c_ref, d_ref)):
        out_ref[i] = ref[first:, :]


def pick_rows(parts, first):
    rows, outs = parts[0].shape
    return pl.pallas_call(
        functools.partial(pick_kernel, first),
        out_shape=jax.ShapeDtypeStruct((len(parts), rows - first, outs), BF16),
        in_specs=[VMEM_SPEC] * 4,
        out_specs=VMEM_SPEC,
        compiler_params=pltpu.CompilerParams(vmem_limit_bytes=2 * 2**20),
        cost_estimate=QUICK,
        name="pick_rows",
    )(*parts)


def lay_second_kernel(other, in_ref, *refs):
    out_ref, half_ref, sems = refs[-3:]
    sy, sx, rows, _ = in_ref.shape
    size = rows // 3
    third = half_ref.shape[0] // 3
    core, y, x = lax.axis_index("c"), lax.axis_index("y"), lax.axis_index("x")
    half = 1 - core if other else core
    for i in range(sy):
        for j in range(sx):
            place = lax.rem(y + sy - STEPS[i], sy) * sx + lax.rem(x + sx - STEPS[j], sx)
            value = in_ref[i, j].astype(F32)
            for tap in range(3):
                at = pl.multiple_of(tap * third + place * size, 8)
                half_ref[pl.ds(at, size), :] = value[tap * size : (tap + 1) * size]
    copies = []
    for tap in range(3):
        to = pl.multiple_of((2 * tap + half) * third, 8)
        copies.append(
            pltpu.make_async_copy(
                half_ref.at[tap * third : (tap + 1) * third],
                out_ref.at[pl.ds(to, third)],
                sems.at[tap],
            )
        )
    for copy in copies:
        copy.start()
    for copy in copies:
        copy.wait()


def lay_second(half, whole=None):
    sy, sx, rows, outs = half.shape
    size = sy * sx * rows
    anywhere = pl.BlockSpec(memory_space=pl.ANY)
    given = [] if whole is None else [whole]
    return pl.pallas_call(
        functools.partial(lay_second_kernel, whole is not None),
        out_shape=jax.ShapeDtypeStruct((2 * size, outs), F32),
        in_specs=[VMEM_SPEC] + [anywhere] * len(given),
        out_specs=anywhere,
        scratch_shapes=[pltpu.VMEM((size, outs), F32), pltpu.SemaphoreType.DMA((3,))],
        compiler_params=pltpu.CompilerParams(vmem_limit_bytes=4 * 2**20),
        cost_estimate=QUICK,
        input_output_aliases={1: 0} if given else {},
        name="lay_second",
    )(half, *given)


def gather_steps(piece, axis):
    return [piece] + [shift(piece, axis, step) for step in STEPS[1:]]


def body(sky_cube, weight_first, weight_second, cotangent):
    cols, rows, chans = sky_cube.shape
    strip, _, outs = cotangent.shape
    chips = lax.axis_size("y")

    ends = [
        jnp.concatenate(
            [sky_cube[:, r], cotangent[:, r, : outs // 2], cotangent[:, r, outs // 2 :]], axis=0
        )
        for r in (rows - 1, 0)
    ]
    edges = jnp.stack(row_halo(ends))
    far_cube = shift(sky_cube, "c", 1)
    far_weight = shift(weight_first, "c", 1)
    far_edges = shift(edges, "c", 1)
    wide = spread(sky_cube, far_cube, edges, far_edges, chips)
    kernel = jnp.concatenate([weight_first, far_weight], axis=2).reshape(18 * chans, outs)

    def side(col):
        beside = [
            jnp.concatenate(
                [edges[k, at + col : at + col + 1] for at in (cols, cols + strip)], axis=1
            )
            for k in range(2)
        ]
        return jnp.concatenate([cotangent[col]] + beside, axis=0)

    count = lax.axis_size(FREQ)
    up = [(i, i + 1) for i in range(count - 1)]
    down = [(j, i) for i, j in up]
    left = lax.ppermute(side(strip - 1), FREQ, up)
    right = lax.ppermute(side(0), FREQ, down)

    on, off = 1, chips - 1
    cut = strip // 2 + 1
    far_a, far_b = conv_parts(((2, 0), (2, cut)), wide, kernel, cut, BF16)
    hold, _ = lax.optimization_barrier((wide, far_a))
    near_b, near_a = conv_parts(((on, cut), (off, 0)), hold, kernel, cut, BF16)
    got_a, got_b = shift(far_a, "y", on), shift(far_b, "y", off)
    got_a, left, right = lax.optimization_barrier((got_a, left, right))
    both_a, both_b = conv_parts(((on, 0), (off, cut)), wide, kernel, cut, BF16, (got_a, got_b))
    own = conv_parts(((0, 0),), wide, kernel, strip + 2, F32)[0]
    from_a = shift(both_a, "y", on), shift(near_a, "y", off)
    from_b = shift(near_b, "y", on), shift(both_b, "y", off)

    back = back_tile(cotangent, left, right, edges, weight_second)
    delta, hidden, *ends = point(own, from_a, from_b, back)

    from_on, from_off = shift(delta, "y", on), shift(delta, "y", off)
    half = strip // 2
    fwd_a, fwd_b = shift(from_on[:half], "y", on), shift(from_off[half:], "y", off)
    edges = row_halo(ends)
    total = grad_strip(0, wide, (delta,), None, False)
    wide_hidden, near, far = second_tile(hidden, edges, cotangent, chips)
    keep, *sends = fold(near, shift(far, "c", 1))
    got = [shift(send, "y", step) for step, send in zip(STEPS[1:], sends)]
    total = grad_strip(off, wide, (from_on,), total, False)
    total = grad_strip(on, wide, (from_off,), total, False)
    first_own, first_far = grad_strip(2, wide, (fwd_a, fwd_b), total, True)

    sx, sz = lax.axis_size("x"), lax.axis_size("z")
    first_far, *got = lax.optimization_barrier((first_far, *got))
    joined = join(first_own, shift(first_far, "c", 1), keep, got, sx * sz)
    extra = keep.shape[0] // (sx * sz)
    summed = lax.all_to_all(joined, SKY, 0, 0, tiled=True)
    summed = sum_pieces(summed)
    parts = gather_steps(order_pieces(gather_steps(summed, "z"), extra), "x")
    main = parts[0].shape[0] - sz * extra
    grad_first = lay_first(parts, sz, chans)
    features = features_tile(wide_hidden, weight_second, strip)
    share = pick_rows(parts, main)
    share, features = lax.optimization_barrier((share, features))
    share, grad_first = lax.optimization_barrier(
        (jnp.stack(gather_steps(share, "y")), grad_first)
    )
    grad_second = lay_second(shift(share, "c", 1), lay_second(share))
    grad_second = grad_second.reshape(3, 3, outs, outs)
    return features, grad_first, grad_second


def solution(mesh):
    sizes = (mesh.devices.shape[0] // 2, 2, 4, mesh.devices.shape[1] // 4)
    fine = Mesh(mesh.devices.reshape(sizes), FREQ + SKY)
    return jax.shard_map(
        body,
        mesh=fine,
        in_specs=(P(None, SKY, FREQ), P(None, None, FREQ, None), P(), P(FREQ, SKY, None)),
        out_specs=(P(FREQ, SKY, None), P(None, None, FREQ, None), P()),
        check_vma=False,
    )
```

```python
import functools

import jax
import jax.numpy as jnp
from jax import lax
from jax.experimental import pallas as pl
from jax.experimental.pallas import tpu as pltpu
from jax.sharding import Mesh, PartitionSpec as P

FREQ = ("y", "c")
SKY = ("z", "x")
F32 = jnp.float32
BF16 = jnp.bfloat16
QUICK = pl.CostEstimate(flops=1, bytes_accessed=1, transcendentals=0)


def shift(x, axis, step):
    count = lax.axis_size(axis)
    return lax.ppermute(x, axis, [(i, (i + step) % count) for i in range(count)])


def spread_kernel(own_ref, far_ref, own_halo_ref, far_halo_ref, out_ref):
    chips, width, rows, depth = out_ref.shape
    cols, _, chans = own_ref.shape
    strip = cols // (2 * chips)
    core = lax.axis_index("c")
    step = 8
    row = lax.broadcasted_iota(jnp.int32, (step, rows, chans), 1)

    def block(i, base, chip):
        for side, (cube_ref, halo_ref) in enumerate(
            ((own_ref, own_halo_ref), (far_ref, far_halo_ref))
        ):
            at = pl.multiple_of(base + i * step, step)
            mid = cube_ref[pl.ds(at, step)]
            wide = mid.astype(F32).reshape(step * rows, chans)
            ahead = pltpu.roll(wide, 1, 0).reshape(step, rows, chans)
            behind = pltpu.roll(wide, step * rows - 1, 0).reshape(step, rows, chans)
            before = halo_ref[0, pl.ds(at, step), :].astype(F32)[:, None, :]
            after = halo_ref[1, pl.ds(at, step), :].astype(F32)[:, None, :]
            ahead = jnp.where(row == 0, before, ahead)
            behind = jnp.where(row == rows - 1, after, behind)
            to = pl.ds(2 + i * step, step)
            for tap, value in enumerate((ahead.astype(BF16), mid, behind.astype(BF16))):
                lane = (2 * tap + side) * chans
                out_ref[chip, to, :, lane : lane + chans] = value

    def edge(at, chip, slot):
        for side, (cube_ref, halo_ref) in enumerate(
            ((own_ref, own_halo_ref), (far_ref, far_halo_ref))
        ):
            first = pl.multiple_of((at // step) * step, step)
            mid = cube_ref[at]
            wide = mid.astype(F32)
            line = lax.broadcasted_iota(jnp.int32, (step, chans), 0) == at - first
            pick = lambda k: jnp.sum(
                jnp.where(line, halo_ref[k, pl.ds(first, step), :].astype(F32), 0.0),
                axis=0,
                keepdims=True,
            )
            place = lax.broadcasted_iota(jnp.int32, (rows, chans), 0)
            ahead = jnp.where(place == 0, pick(0), pltpu.roll(wide, 1, 0))
            behind = jnp.where(place == rows - 1, pick(1), pltpu.roll(wide, rows - 1, 0))
            for tap, value in enumerate((ahead.astype(BF16), mid, behind.astype(BF16))):
                lane = (2 * tap + side) * chans
                out_ref[chip, slot, :, lane : lane + chans] = value

    blank = jnp.zeros((rows, depth), BF16)
    for chip in range(chips):
        base = (2 * chip + core) * strip
        lax.fori_loop(0, strip // step, lambda i, _: block(i, base, chip), None)
        for slot in (0, 1):
            edge(jnp.maximum(base - 2 + slot, 0), chip, slot)
            edge(jnp.minimum(base + strip + slot, cols - 1), chip, strip + 2 + slot)
        for slot in range(strip + 4, width):
            out_ref[chip, slot] = blank

    @pl.when(core == 0)
    def _():
        out_ref[0, 0] = blank
        out_ref[0, 1] = blank

    @pl.when(core == 1)
    def _():
        out_ref[chips - 1, strip + 2] = blank
        out_ref[chips - 1, strip + 3] = blank


VMEM_SPEC = pl.BlockSpec(memory_space=pltpu.VMEM)


def spread(own, far, own_halo, far_halo, chips):
    cols, rows, chans = own.shape
    return pl.pallas_call(
        spread_kernel,
        out_shape=jax.ShapeDtypeStruct((chips, cols // (2 * chips) + 8, rows, 6 * chans), BF16),
        in_specs=[VMEM_SPEC] * 4,
        out_specs=VMEM_SPEC,
        compiler_params=pltpu.CompilerParams(vmem_limit_bytes=2 * 2**20),
        cost_estimate=QUICK,
        name="spread",
    )(own, far, own_halo, far_halo)


def chip_at(step):
    return lax.rem(lax.axis_index("y") + step, lax.axis_size("y"))


def conv_kernel(parts, adds, wide_ref, kernel_ref, *refs):
    rows = wide_ref.shape[2]
    for (step, first), add_ref, out_ref in zip(parts, refs[:adds] or [None] * len(parts), refs[adds:]):
        count, _, outs = out_ref.shape
        chip = chip_at(step)
        pieces = [wide_ref[chip, first + tap : first + tap + count] for tap in range(3)]
        lhs = jnp.concatenate(pieces, axis=-1).reshape(count * rows, -1)
        total = jnp.dot(lhs, kernel_ref[...], preferred_element_type=F32)
        total = total.reshape(count, rows, outs)
        if add_ref is not None:
            total = total + add_ref[...].astype(F32)
        out_ref[...] = total.astype(out_ref.dtype)


def conv_parts(parts, wide, kernel, count, dtype, adds=()):
    rows, outs = wide.shape[2], kernel.shape[1]
    return pl.pallas_call(
        functools.partial(conv_kernel, parts, len(adds)),
        out_shape=(jax.ShapeDtypeStruct((count, rows, outs), dtype),) * len(parts),
        in_specs=[VMEM_SPEC] * (2 + len(adds)),
        out_specs=(VMEM_SPEC,) * len(parts),
        compiler_params=pltpu.CompilerParams(vmem_limit_bytes=4 * 2**20),
        cost_estimate=QUICK,
        name="conv_first",
    )(wide, kernel, *adds)


def grad_kernel(step, pieces, has_old, last, wide_ref, *refs):
    piece_refs, refs = refs[:pieces], refs[pieces:]
    old_ref = refs[0] if has_old else None
    outs_refs, pad_ref = refs[1 if has_old else 0 : -1], refs[-1]
    count, rows, outs = piece_refs[0].shape
    strip = pieces * count
    cols, depth = wide_ref.shape[1], wide_ref.shape[3]
    pad_ref[0:3] = jnp.zeros((3, rows, outs), BF16)
    for i, ref in enumerate(piece_refs):
        pad_ref[3 + i * count : 3 + (i + 1) * count] = ref[...]
    pad_ref[3 + strip :] = jnp.zeros((cols - strip - 1, rows, outs), BF16)
    lhs = wide_ref[chip_at(step)].reshape(cols * rows, depth)
    rhs = jnp.concatenate(
        [pad_ref[2 - tap : 2 - tap + cols].reshape(cols * rows, outs) for tap in range(3)], axis=-1
    )
    total = lax.dot_general(lhs, rhs, (((0,), (0,)), ((), ())), preferred_element_type=F32)
    if has_old:
        total = total + old_ref[...]
    if not last:
        outs_refs[0][...] = total
    else:
        chans = depth // 6
        for tap in range(3):
            at = 2 * tap * chans
            outs_refs[0][tap * chans : (tap + 1) * chans] = total[at : at + chans]
            outs_refs[1][tap * chans : (tap + 1) * chans] = total[
                at + chans : at + 2 * chans
            ].astype(BF16)


def grad_strip(step, wide, pieces, old, last):
    _, rows, outs = pieces[0].shape
    depth, cols = wide.shape[3], wide.shape[1]
    shape = (depth, 3 * outs)
    half = (depth // 2, 3 * outs)
    if last:
        out_shape = (jax.ShapeDtypeStruct(half, F32), jax.ShapeDtypeStruct(half, BF16))
    else:
        out_shape = (jax.ShapeDtypeStruct(shape, F32),)
    args = [wide, *pieces] + ([old] if old is not None else [])
    out = pl.pallas_call(
        functools.partial(grad_kernel, step, len(pieces), old is not None, last),
        out_shape=out_shape,
        in_specs=[VMEM_SPEC] * len(args),
        out_specs=tuple([VMEM_SPEC] * len(out_shape)),
        scratch_shapes=[pltpu.VMEM((cols + 2, rows, outs), BF16)],
        compiler_params=pltpu.CompilerParams(vmem_limit_bytes=5 * 2**20),
        cost_estimate=QUICK,
        name="grad_first",
    )(*args)
    return out if last else out[0]


def spread_tile(columns, wide_ref):
    rows, chans = wide_ref.shape[1], wide_ref.shape[2] // 3
    place = lax.broadcasted_iota(jnp.int32, (rows, chans), 0)
    for j, (mid, before, after) in enumerate(columns):
        wide = mid.astype(F32)
        ahead = jnp.where(place == 0, before.astype(F32), pltpu.roll(wide, 1, 0))
        behind = jnp.where(place == rows - 1, after.astype(F32), pltpu.roll(wide, rows - 1, 0))
        wide_ref[j, :, 0:chans] = ahead.astype(BF16)
        wide_ref[j, :, chans : 2 * chans] = mid
        wide_ref[j, :, 2 * chans :] = behind.astype(BF16)


def back_kernel(cot_ref, left_ref, right_ref, edge_ref, kernel_ref, out_ref, wide_ref):
    cols, rows, chans = cot_ref.shape
    start = edge_ref.shape[1] - 2 * cols

    def beside(k, j):
        low, high = start + j, start + cols + j
        return jnp.concatenate(
            [edge_ref[k, low : low + 1, :], edge_ref[k, high : high + 1, :]], axis=-1
        )

    def whole(ref):
        return ref[0:rows], ref[rows : rows + 1], ref[rows + 1 : rows + 2]

    columns = [(cot_ref[j], beside(0, j), beside(1, j)) for j in range(cols)]
    spread_tile([whole(left_ref)] + columns + [whole(right_ref)], wide_ref)
    total = None
    for tap_col in range(3):
        lhs = wide_ref[tap_col : tap_col + cols].reshape(cols * rows, 3 * chans)
        for tap_row in range(3):
            part = lax.dot_general(
                lhs[:, tap_row * chans : (tap_row + 1) * chans],
                kernel_ref[2 - tap_col, 2 - tap_row],
                (((1,), (1,)), ((), ())),
                preferred_element_type=F32,
            )
            total = part if total is None else total + part
    out_ref[...] = total.reshape(cols, rows, -1)


def back_tile(tile, left, right, edges, kernel):
    cols, rows, chans = tile.shape
    return pl.pallas_call(
        back_kernel,
        out_shape=(
            jax.ShapeDtypeStruct((cols, rows, kernel.shape[2]), F32),
            jax.ShapeDtypeStruct((cols + 2, rows, 3 * chans), BF16),
        ),
        in_specs=[VMEM_SPEC] * 5,
        out_specs=(VMEM_SPEC,) * 2,
        compiler_params=pltpu.CompilerParams(vmem_limit_bytes=4 * 2**20),
        cost_estimate=QUICK,
        name="back",
    )(tile, left, right, edges, kernel)


def second_kernel(chips, hid_ref, wide_ref, near_ref, far_ref, sum_ref):
    chans = hid_ref.shape[2]
    cols, rows, outs = hid_ref.shape[0] - 2, hid_ref.shape[1], wide_ref.shape[2] // 3
    core = lax.axis_index("c")
    lhs = hid_ref[1 : cols + 1].reshape(cols * rows, chans)
    for tap_col in range(3):
        rhs = wide_ref[2 - tap_col : 2 - tap_col + cols].reshape(cols * rows, 3 * outs)
        part = lax.dot_general(lhs, rhs, (((0,), (0,)), ((), ())), preferred_element_type=F32)
        for tap_row in range(3):
            sum_ref[
                tap_row * chans : (tap_row + 1) * chans, tap_col * outs : (tap_col + 1) * outs
            ] = part[:, (2 - tap_row) * outs : (3 - tap_row) * outs]
    size = sum_ref.shape[0] // (2 * chips)
    for half, ref in ((core, near_ref), (1 - core, far_ref)):
        for chip in range(chips):
            at = pl.multiple_of((half * chips + chip) * size, size)
            for tap in range(3):
                ref[chip, tap * size : (tap + 1) * size, :] = sum_ref[
                    pl.ds(at, size), tap * outs : (tap + 1) * outs
                ].astype(ref.dtype)


def second_tile(tile, wide, chips):
    chans, outs = tile.shape[2], wide.shape[2] // 3
    cut = (chips, 9 * chans // (2 * chips), outs)
    return pl.pallas_call(
        functools.partial(second_kernel, chips),
        out_shape=(jax.ShapeDtypeStruct(cut, F32), jax.ShapeDtypeStruct(cut, BF16)),
        in_specs=[VMEM_SPEC] * 2,
        out_specs=(VMEM_SPEC,) * 2,
        scratch_shapes=[pltpu.VMEM((3 * chans, 3 * outs), F32)],
        compiler_params=pltpu.CompilerParams(vmem_limit_bytes=9 * 2**20),
        cost_estimate=QUICK,
        name="second",
    )(tile, wide)


def features_kernel(hid_ref, before_ref, after_ref, kernel_ref, out_ref, wide_ref):
    cols, rows, outs = out_ref.shape
    columns = [
        (hid_ref[j], before_ref[j : j + 1, :], after_ref[j : j + 1, :]) for j in range(cols + 2)
    ]
    spread_tile(columns, wide_ref)
    pieces = [wide_ref[tap : tap + cols] for tap in range(3)]
    lhs = jnp.concatenate(pieces, axis=-1).reshape(cols * rows, -1)
    total = jnp.dot(lhs, kernel_ref[...], preferred_element_type=F32)
    out_ref[...] = total.reshape(cols, rows, outs).astype(BF16)


def features_tile(tile, edges, kernel):
    cols, rows, chans = tile.shape
    outs = kernel.shape[3]
    return pl.pallas_call(
        features_kernel,
        out_shape=jax.ShapeDtypeStruct((cols - 2, rows, outs), BF16),
        in_specs=[VMEM_SPEC] * 4,
        out_specs=VMEM_SPEC,
        scratch_shapes=[pltpu.VMEM((cols, rows, 3 * chans), BF16)],
        compiler_params=pltpu.CompilerParams(vmem_limit_bytes=9 * 2**20),
        cost_estimate=QUICK,
        name="features",
    )(tile, *edges, kernel.reshape(-1, outs))


def point_kernel(
    own_ref, a0_ref, a1_ref, b0_ref, b1_ref, back_ref,
    delta_ref, hidden_ref, last_ref, first_ref,
):
    cols, rows, _ = own_ref.shape
    half = delta_ref.shape[0] // 2
    strip = 2 * lax.axis_index("y") + lax.axis_index("c")
    strips = 2 * lax.axis_size("y")

    def column(j, i, refs, keep):
        pre = own_ref[j] + refs[0][i].astype(F32) + refs[1][i].astype(F32)
        sigma = jax.nn.sigmoid(pre)
        hidden = pre * sigma
        if keep is not None:
            hidden = jnp.where(keep, hidden, 0.0)
        hidden = hidden.astype(BF16)
        hidden_ref[j] = hidden
        last_ref[j : j + 1, :] = hidden[rows - 1 :]
        first_ref[j : j + 1, :] = hidden[:1]
        if keep is None:
            slope = sigma * (1.0 + pre * (1.0 - sigma))
            delta_ref[j - 1] = (back_ref[j - 1] * slope).astype(BF16)

    left, right = (a0_ref, a1_ref), (b0_ref, b1_ref)
    column(0, 0, left, strip > 0)
    column(cols - 1, half, right, strip < strips - 1)

    for i in range(1, half + 1):
        column(i, i, left, None)
        column(half + i, i - 1, right, None)


def point(own, left, right, back):
    strip, rows, outs = back.shape
    delta = jax.ShapeDtypeStruct(back.shape, BF16)
    edge = jax.ShapeDtypeStruct((strip + 2, outs), BF16)
    return pl.pallas_call(
        point_kernel,
        out_shape=(delta, jax.ShapeDtypeStruct(own.shape, BF16), edge, edge),
        in_specs=[VMEM_SPEC] * 6,
        out_specs=(VMEM_SPEC,) * 4,
        compiler_params=pltpu.CompilerParams(vmem_limit_bytes=2 * 2**20),
        cost_estimate=QUICK,
        name="point",
    )(own, *left, *right, back)


def fold_kernel(near_ref, got_ref, keep_ref, *send_refs):
    chips = near_ref.shape[0]
    here = lax.axis_index("y")
    keep_ref[...] = near_ref[here] + got_ref[here].astype(F32)
    for step, ref in zip(STEPS[1:], send_refs):
        to = lax.rem(here + step, chips)
        ref[...] = (near_ref[to] + got_ref[to].astype(F32)).astype(BF16)


def fold(near, got):
    shape = near.shape[1:]
    return pl.pallas_call(
        fold_kernel,
        out_shape=(jax.ShapeDtypeStruct(shape, F32),) + (jax.ShapeDtypeStruct(shape, BF16),) * 3,
        in_specs=[VMEM_SPEC] * 2,
        out_specs=(VMEM_SPEC,) * 4,
        compiler_params=pltpu.CompilerParams(vmem_limit_bytes=2 * 2**20),
        cost_estimate=QUICK,
        name="fold",
    )(near, got)


def row_halo(ends):
    count = lax.axis_size(SKY)
    up = [(i, i + 1) for i in range(count - 1)]
    down = [(j, i) for i, j in up]
    return lax.ppermute(ends[0], SKY, up), lax.ppermute(ends[1], SKY, down)


def join_kernel(own_ref, far_ref, keep_ref, a_ref, b_ref, c_ref, out_ref):
    pieces, total, outs = out_ref.shape
    chans = own_ref.shape[0] // 3
    size = chans // pieces
    for tap_col in range(3):
        for tap_row in range(3):
            rows = slice(tap_row * chans, (tap_row + 1) * chans)
            lanes = slice(tap_col * outs, (tap_col + 1) * outs)
            value = own_ref[rows, lanes] + far_ref[rows, lanes].astype(F32)
            at = (3 * tap_col + tap_row) * size
            out_ref[:, at : at + size, :] = value.reshape(pieces, size, outs).astype(BF16)
    second = keep_ref[...]
    for ref in (a_ref, b_ref, c_ref):
        second = second + ref[...].astype(F32)
    sx = lax.axis_size("x")
    sz = pieces // sx
    third = second.shape[0] // 3
    size_x = third // sx
    extra = total - 9 * size
    for x in range(sx):
        value = jnp.concatenate(
            [second[tap * third + x * size_x : tap * third + (x + 1) * size_x] for tap in range(3)],
            axis=0,
        )
        for z in range(sz):
            out_ref[z * sx + x, 9 * size :, :] = value[z * extra : (z + 1) * extra].astype(BF16)


def join(own, far, keep, got, pieces):
    outs = keep.shape[1]
    rows = 9 * (own.shape[0] // 3 // pieces) + keep.shape[0] // pieces
    return pl.pallas_call(
        join_kernel,
        out_shape=jax.ShapeDtypeStruct((pieces, rows, outs), BF16),
        in_specs=[VMEM_SPEC] * 6,
        out_specs=VMEM_SPEC,
        compiler_params=pltpu.CompilerParams(vmem_limit_bytes=4 * 2**20),
        cost_estimate=QUICK,
        name="join",
    )(own, far, keep, *got)


STEPS = (0, 1, 3, 2)


def order_kernel(extra, a_ref, b_ref, c_ref, d_ref, out_ref):
    rows = a_ref.shape[0] - extra
    sz = lax.axis_size("z")
    me = lax.axis_index("z")
    values = [ref[...].astype(F32) for ref in (a_ref, b_ref, c_ref, d_ref)]
    rest = []
    for z in range(len(STEPS)):
        value = values[0]
        for step, other in zip(STEPS[1:], values[1:]):
            value = jnp.where(lax.rem(me + sz - step, sz) == z, other, value)
        out_ref[z * rows : (z + 1) * rows, :] = value[:rows].astype(BF16)
        rest.append(value[rows:])
    out_ref[len(STEPS) * rows :, :] = jnp.concatenate(rest, axis=0).astype(BF16)


def order_pieces(parts, extra):
    rows, outs = parts[0].shape
    return pl.pallas_call(
        functools.partial(order_kernel, extra),
        out_shape=jax.ShapeDtypeStruct((4 * rows, outs), BF16),
        in_specs=[VMEM_SPEC] * 4,
        out_specs=VMEM_SPEC,
        compiler_params=pltpu.CompilerParams(vmem_limit_bytes=4 * 2**20),
        cost_estimate=QUICK,
        name="order_pieces",
    )(*parts)


def first_kernel(sz, a_ref, b_ref, c_ref, d_ref, out_ref):
    sx = lax.axis_size("x")
    size = out_ref.shape[2] // (sx * sz)
    me = lax.axis_index("x")
    for step, ref in zip(STEPS, (a_ref, b_ref, c_ref, d_ref)):
        x = lax.rem(me + sx - step, sx)
        value = ref[...].astype(F32)
        for z in range(sz):
            at = pl.multiple_of((z * sx + x) * size, size)
            for tap in range(9):
                rows = (z * 9 + tap) * size
                out_ref[tap // 3, tap % 3, pl.ds(at, size), :] = value[rows : rows + size]


def lay_first(parts, sz, chans):
    outs = parts[0].shape[1]
    return pl.pallas_call(
        functools.partial(first_kernel, sz),
        out_shape=jax.ShapeDtypeStruct((3, 3, chans, outs), F32),
        in_specs=[VMEM_SPEC] * 4,
        out_specs=VMEM_SPEC,
        compiler_params=pltpu.CompilerParams(vmem_limit_bytes=4 * 2**20),
        cost_estimate=QUICK,
        name="lay_first",
    )(*parts)


def sum_kernel(in_ref, out_ref):
    total = in_ref[0].astype(F32)
    for i in range(1, in_ref.shape[0]):
        total = total + in_ref[i].astype(F32)
    out_ref[...] = total.astype(BF16)


def sum_pieces(pieces):
    return pl.pallas_call(
        sum_kernel,
        out_shape=jax.ShapeDtypeStruct(pieces.shape[1:], BF16),
        in_specs=[VMEM_SPEC],
        out_specs=VMEM_SPEC,
        compiler_params=pltpu.CompilerParams(vmem_limit_bytes=4 * 2**20),
        cost_estimate=QUICK,
        name="sum_pieces",
    )(pieces)


def pick_kernel(first, a_ref, b_ref, c_ref, d_ref, out_ref):
    for i, ref in enumerate((a_ref, b_ref, c_ref, d_ref)):
        out_ref[i] = ref[first:, :]


def pick_rows(parts, first):
    rows, outs = parts[0].shape
    return pl.pallas_call(
        functools.partial(pick_kernel, first),
        out_shape=jax.ShapeDtypeStruct((len(parts), rows - first, outs), BF16),
        in_specs=[VMEM_SPEC] * 4,
        out_specs=VMEM_SPEC,
        compiler_params=pltpu.CompilerParams(vmem_limit_bytes=2 * 2**20),
        cost_estimate=QUICK,
        name="pick_rows",
    )(*parts)


def lay_second_kernel(other, in_ref, *refs):
    out_ref, half_ref, sems = refs[-3:]
    sy, sx, rows, _ = in_ref.shape
    size = rows // 3
    third = half_ref.shape[0] // 3
    core, y, x = lax.axis_index("c"), lax.axis_index("y"), lax.axis_index("x")
    half = 1 - core if other else core
    for i in range(sy):
        for j in range(sx):
            place = lax.rem(y + sy - STEPS[i], sy) * sx + lax.rem(x + sx - STEPS[j], sx)
            value = in_ref[i, j].astype(F32)
            for tap in range(3):
                at = pl.multiple_of(tap * third + place * size, 8)
                half_ref[pl.ds(at, size), :] = value[tap * size : (tap + 1) * size]
    copies = []
    for tap in range(3):
        to = pl.multiple_of((2 * tap + half) * third, 8)
        copies.append(
            pltpu.make_async_copy(
                half_ref.at[tap * third : (tap + 1) * third],
                out_ref.at[pl.ds(to, third)],
                sems.at[tap],
            )
        )
    for copy in copies:
        copy.start()
    for copy in copies:
        copy.wait()


def lay_second(half, whole=None):
    sy, sx, rows, outs = half.shape
    size = sy * sx * rows
    anywhere = pl.BlockSpec(memory_space=pl.ANY)
    given = [] if whole is None else [whole]
    return pl.pallas_call(
        functools.partial(lay_second_kernel, whole is not None),
        out_shape=jax.ShapeDtypeStruct((2 * size, outs), F32),
        in_specs=[VMEM_SPEC] + [anywhere] * len(given),
        out_specs=anywhere,
        scratch_shapes=[pltpu.VMEM((size, outs), F32), pltpu.SemaphoreType.DMA((3,))],
        compiler_params=pltpu.CompilerParams(vmem_limit_bytes=4 * 2**20),
        cost_estimate=QUICK,
        input_output_aliases={1: 0} if given else {},
        name="lay_second",
    )(half, *given)


def gather_steps(piece, axis):
    return [piece] + [shift(piece, axis, step) for step in STEPS[1:]]


def body(sky_cube, weight_first, weight_second, cotangent):
    cols, rows, chans = sky_cube.shape
    strip, _, outs = cotangent.shape
    chips = lax.axis_size("y")

    ends = [
        jnp.concatenate(
            [sky_cube[:, r], cotangent[:, r, : outs // 2], cotangent[:, r, outs // 2 :]], axis=0
        )
        for r in (rows - 1, 0)
    ]
    edges = jnp.stack(row_halo(ends))
    far_cube = shift(sky_cube, "c", 1)
    far_weight = shift(weight_first, "c", 1)
    far_edges = shift(edges, "c", 1)
    wide = spread(sky_cube, far_cube, edges, far_edges, chips)
    kernel = jnp.concatenate([weight_first, far_weight], axis=2).reshape(18 * chans, outs)

    def side(col):
        beside = [
            jnp.concatenate(
                [edges[k, at + col : at + col + 1] for at in (cols, cols + strip)], axis=1
            )
            for k in range(2)
        ]
        return jnp.concatenate([cotangent[col]] + beside, axis=0)

    count = lax.axis_size(FREQ)
    up = [(i, i + 1) for i in range(count - 1)]
    down = [(j, i) for i, j in up]
    left = lax.ppermute(side(strip - 1), FREQ, up)
    right = lax.ppermute(side(0), FREQ, down)

    on, off = 1, chips - 1
    cut = strip // 2 + 1
    far_a, far_b = conv_parts(((2, 0), (2, cut)), wide, kernel, cut, BF16)
    hold, _ = lax.optimization_barrier((wide, far_a))
    near_b, near_a = conv_parts(((on, cut), (off, 0)), hold, kernel, cut, BF16)
    got_a, got_b = shift(far_a, "y", on), shift(far_b, "y", off)
    got_a, left, right = lax.optimization_barrier((got_a, left, right))
    both_a, both_b = conv_parts(((on, 0), (off, cut)), wide, kernel, cut, BF16, (got_a, got_b))
    own = conv_parts(((0, 0),), wide, kernel, strip + 2, F32)[0]
    from_a = shift(both_a, "y", on), shift(near_a, "y", off)
    from_b = shift(near_b, "y", on), shift(both_b, "y", off)

    back, wide_cotangent = back_tile(cotangent, left, right, edges, weight_second)
    delta, hidden, *ends = point(own, from_a, from_b, back)

    from_on, from_off = shift(delta, "y", on), shift(delta, "y", off)
    half = strip // 2
    total = grad_strip(0, wide, (delta,), None, False)
    from_on, from_off, total, *edges = lax.optimization_barrier(
        (from_on, from_off, total, *row_halo(ends))
    )
    fwd_a, fwd_b = shift(from_on[:half], "y", on), shift(from_off[half:], "y", off)
    near, far = second_tile(hidden, wide_cotangent, chips)
    features = features_tile(hidden, edges, weight_second)
    keep, *sends = fold(near, shift(far, "c", 1))
    got = [shift(send, "y", step) for step, send in zip(STEPS[1:], sends)]
    total = grad_strip(off, wide, (from_on,), total, False)
    total = grad_strip(on, wide, (from_off,), total, False)
    fwd_a, features = lax.optimization_barrier((fwd_a, features))
    first_own, first_far = grad_strip(2, wide, (fwd_a, fwd_b), total, True)

    sx, sz = lax.axis_size("x"), lax.axis_size("z")
    first_far, *got = lax.optimization_barrier((first_far, *got))
    joined = join(first_own, shift(first_far, "c", 1), keep, got, sx * sz)
    extra = keep.shape[0] // (sx * sz)
    summed = lax.all_to_all(joined, SKY, 0, 0, tiled=True)
    summed = sum_pieces(summed)
    parts = gather_steps(order_pieces(gather_steps(summed, "z"), extra), "x")
    main = parts[0].shape[0] - sz * extra
    grad_first = lay_first(parts, sz, chans)
    share = pick_rows(parts, main)
    share, grad_first = lax.optimization_barrier(
        (jnp.stack(gather_steps(share, "y")), grad_first)
    )
    grad_second = lay_second(shift(share, "c", 1), lay_second(share))
    grad_second = grad_second.reshape(3, 3, outs, outs)
    return features, grad_first, grad_second


def solution(mesh):
    sizes = (mesh.devices.shape[0] // 2, 2, 4, mesh.devices.shape[1] // 4)
    fine = Mesh(mesh.devices.reshape(sizes), FREQ + SKY)
    return jax.shard_map(
        body,
        mesh=fine,
        in_specs=(P(None, SKY, FREQ), P(None, None, FREQ, None), P(), P(FREQ, SKY, None)),
        out_specs=(P(FREQ, SKY, None), P(None, None, FREQ, None), P()),
        check_vma=False,
    )
```

```python
import functools

import jax
import jax.numpy as jnp
from jax import lax
from jax.experimental import pallas as pl
from jax.experimental.pallas import tpu as pltpu
from jax.sharding import Mesh, PartitionSpec as P

FREQ = ("y", "c")
SKY = ("z", "x")
F32 = jnp.float32
BF16 = jnp.bfloat16
QUICK = pl.CostEstimate(flops=1, bytes_accessed=1, transcendentals=0)


def shift(x, axis, step):
    count = lax.axis_size(axis)
    return lax.ppermute(x, axis, [(i, (i + step) % count) for i in range(count)])


def spread_kernel(own_ref, far_ref, own_halo_ref, far_halo_ref, out_ref):
    chips, width, rows, depth = out_ref.shape
    cols, _, chans = own_ref.shape
    strip = cols // (2 * chips)
    core = lax.axis_index("c")
    step = 8
    row = lax.broadcasted_iota(jnp.int32, (step, rows, chans), 1)

    def block(i, base, chip):
        for side, (cube_ref, halo_ref) in enumerate(
            ((own_ref, own_halo_ref), (far_ref, far_halo_ref))
        ):
            at = pl.multiple_of(base + i * step, step)
            mid = cube_ref[pl.ds(at, step)]
            wide = mid.astype(F32).reshape(step * rows, chans)
            ahead = pltpu.roll(wide, 1, 0).reshape(step, rows, chans)
            behind = pltpu.roll(wide, step * rows - 1, 0).reshape(step, rows, chans)
            before = halo_ref[0, pl.ds(at, step), :].astype(F32)[:, None, :]
            after = halo_ref[1, pl.ds(at, step), :].astype(F32)[:, None, :]
            ahead = jnp.where(row == 0, before, ahead)
            behind = jnp.where(row == rows - 1, after, behind)
            to = pl.ds(2 + i * step, step)
            for tap, value in enumerate((ahead.astype(BF16), mid, behind.astype(BF16))):
                lane = (2 * tap + side) * chans
                out_ref[chip, to, :, lane : lane + chans] = value

    def edge(at, chip, slot):
        for side, (cube_ref, halo_ref) in enumerate(
            ((own_ref, own_halo_ref), (far_ref, far_halo_ref))
        ):
            first = pl.multiple_of((at // step) * step, step)
            mid = cube_ref[at]
            wide = mid.astype(F32)
            line = lax.broadcasted_iota(jnp.int32, (step, chans), 0) == at - first
            pick = lambda k: jnp.sum(
                jnp.where(line, halo_ref[k, pl.ds(first, step), :].astype(F32), 0.0),
                axis=0,
                keepdims=True,
            )
            place = lax.broadcasted_iota(jnp.int32, (rows, chans), 0)
            ahead = jnp.where(place == 0, pick(0), pltpu.roll(wide, 1, 0))
            behind = jnp.where(place == rows - 1, pick(1), pltpu.roll(wide, rows - 1, 0))
            for tap, value in enumerate((ahead.astype(BF16), mid, behind.astype(BF16))):
                lane = (2 * tap + side) * chans
                out_ref[chip, slot, :, lane : lane + chans] = value

    blank = jnp.zeros((rows, depth), BF16)
    for chip in range(chips):
        base = (2 * chip + core) * strip
        lax.fori_loop(0, strip // step, lambda i, _: block(i, base, chip), None)
        for slot in (0, 1):
            edge(jnp.maximum(base - 2 + slot, 0), chip, slot)
            edge(jnp.minimum(base + strip + slot, cols - 1), chip, strip + 2 + slot)
        for slot in range(strip + 4, width):
            out_ref[chip, slot] = blank

    @pl.when(core == 0)
    def _():
        out_ref[0, 0] = blank
        out_ref[0, 1] = blank

    @pl.when(core == 1)
    def _():
        out_ref[chips - 1, strip + 2] = blank
        out_ref[chips - 1, strip + 3] = blank


VMEM_SPEC = pl.BlockSpec(memory_space=pltpu.VMEM)


def spread(own, far, own_halo, far_halo, chips):
    cols, rows, chans = own.shape
    return pl.pallas_call(
        spread_kernel,
        out_shape=jax.ShapeDtypeStruct((chips, cols // (2 * chips) + 8, rows, 6 * chans), BF16),
        in_specs=[VMEM_SPEC] * 4,
        out_specs=VMEM_SPEC,
        compiler_params=pltpu.CompilerParams(vmem_limit_bytes=2 * 2**20),
        cost_estimate=QUICK,
        name="spread",
    )(own, far, own_halo, far_halo)


def chip_at(step):
    return lax.rem(lax.axis_index("y") + step, lax.axis_size("y"))


def conv_kernel(parts, adds, wide_ref, kernel_ref, *refs):
    rows = wide_ref.shape[2]
    for (step, first), add_ref, out_ref in zip(parts, refs[:adds] or [None] * len(parts), refs[adds:]):
        count, _, outs = out_ref.shape
        chip = chip_at(step)
        pieces = [wide_ref[chip, first + tap : first + tap + count] for tap in range(3)]
        lhs = jnp.concatenate(pieces, axis=-1).reshape(count * rows, -1)
        total = jnp.dot(lhs, kernel_ref[...], preferred_element_type=F32)
        total = total.reshape(count, rows, outs)
        if add_ref is not None:
            total = total + add_ref[...].astype(F32)
        out_ref[...] = total.astype(out_ref.dtype)


def conv_parts(parts, wide, kernel, count, dtype, adds=()):
    rows, outs = wide.shape[2], kernel.shape[1]
    return pl.pallas_call(
        functools.partial(conv_kernel, parts, len(adds)),
        out_shape=(jax.ShapeDtypeStruct((count, rows, outs), dtype),) * len(parts),
        in_specs=[VMEM_SPEC] * (2 + len(adds)),
        out_specs=(VMEM_SPEC,) * len(parts),
        compiler_params=pltpu.CompilerParams(vmem_limit_bytes=4 * 2**20),
        cost_estimate=QUICK,
        name="conv_first",
    )(wide, kernel, *adds)


def grad_kernel(step, pieces, has_old, last, wide_ref, *refs):
    piece_refs, refs = refs[:pieces], refs[pieces:]
    old_ref = refs[0] if has_old else None
    outs_refs, pad_ref = refs[1 if has_old else 0 : -1], refs[-1]
    count, rows, outs = piece_refs[0].shape
    strip = pieces * count
    cols, depth = wide_ref.shape[1], wide_ref.shape[3]
    pad_ref[0:3] = jnp.zeros((3, rows, outs), BF16)
    for i, ref in enumerate(piece_refs):
        pad_ref[3 + i * count : 3 + (i + 1) * count] = ref[...]
    pad_ref[3 + strip :] = jnp.zeros((cols - strip - 1, rows, outs), BF16)
    lhs = wide_ref[chip_at(step)].reshape(cols * rows, depth)
    rhs = jnp.concatenate(
        [pad_ref[2 - tap : 2 - tap + cols].reshape(cols * rows, outs) for tap in range(3)], axis=-1
    )
    total = lax.dot_general(lhs, rhs, (((0,), (0,)), ((), ())), preferred_element_type=F32)
    if has_old:
        total = total + old_ref[...]
    if not last:
        outs_refs[0][...] = total
    else:
        chans = depth // 6
        for tap in range(3):
            at = 2 * tap * chans
            outs_refs[0][tap * chans : (tap + 1) * chans] = total[at : at + chans]
            outs_refs[1][tap * chans : (tap + 1) * chans] = total[
                at + chans : at + 2 * chans
            ].astype(BF16)


def grad_strip(step, wide, pieces, old, last):
    _, rows, outs = pieces[0].shape
    depth, cols = wide.shape[3], wide.shape[1]
    shape = (depth, 3 * outs)
    half = (depth // 2, 3 * outs)
    if last:
        out_shape = (jax.ShapeDtypeStruct(half, F32), jax.ShapeDtypeStruct(half, BF16))
    else:
        out_shape = (jax.ShapeDtypeStruct(shape, F32),)
    args = [wide, *pieces] + ([old] if old is not None else [])
    out = pl.pallas_call(
        functools.partial(grad_kernel, step, len(pieces), old is not None, last),
        out_shape=out_shape,
        in_specs=[VMEM_SPEC] * len(args),
        out_specs=tuple([VMEM_SPEC] * len(out_shape)),
        scratch_shapes=[pltpu.VMEM((cols + 2, rows, outs), BF16)],
        compiler_params=pltpu.CompilerParams(vmem_limit_bytes=5 * 2**20),
        cost_estimate=QUICK,
        name="grad_first",
    )(*args)
    return out if last else out[0]


def spread_tile(columns, wide_ref):
    rows, chans = wide_ref.shape[1], wide_ref.shape[2] // 3
    place = lax.broadcasted_iota(jnp.int32, (rows, chans), 0)
    for j, (mid, before, after) in enumerate(columns):
        wide = mid.astype(F32)
        ahead = jnp.where(place == 0, before.astype(F32), pltpu.roll(wide, 1, 0))
        behind = jnp.where(place == rows - 1, after.astype(F32), pltpu.roll(wide, rows - 1, 0))
        wide_ref[j, :, 0:chans] = ahead.astype(BF16)
        wide_ref[j, :, chans : 2 * chans] = mid
        wide_ref[j, :, 2 * chans :] = behind.astype(BF16)


def back_kernel(cot_ref, left_ref, right_ref, edge_ref, kernel_ref, out_ref, wide_ref):
    cols, rows, chans = cot_ref.shape
    start = edge_ref.shape[1] - 2 * cols

    def beside(k, j):
        low, high = start + j, start + cols + j
        return jnp.concatenate(
            [edge_ref[k, low : low + 1, :], edge_ref[k, high : high + 1, :]], axis=-1
        )

    def whole(ref):
        return ref[0:rows], ref[rows : rows + 1], ref[rows + 1 : rows + 2]

    columns = [(cot_ref[j], beside(0, j), beside(1, j)) for j in range(cols)]
    spread_tile([whole(left_ref)] + columns + [whole(right_ref)], wide_ref)
    total = None
    for tap_col in range(3):
        lhs = wide_ref[tap_col : tap_col + cols].reshape(cols * rows, 3 * chans)
        for tap_row in range(3):
            part = lax.dot_general(
                lhs[:, tap_row * chans : (tap_row + 1) * chans],
                kernel_ref[2 - tap_col, 2 - tap_row],
                (((1,), (1,)), ((), ())),
                preferred_element_type=F32,
            )
            total = part if total is None else total + part
    out_ref[...] = total.reshape(cols, rows, -1)


def back_tile(tile, left, right, edges, kernel):
    cols, rows, chans = tile.shape
    return pl.pallas_call(
        back_kernel,
        out_shape=(
            jax.ShapeDtypeStruct((cols, rows, kernel.shape[2]), F32),
            jax.ShapeDtypeStruct((cols + 2, rows, 3 * chans), BF16),
        ),
        in_specs=[VMEM_SPEC] * 5,
        out_specs=(VMEM_SPEC,) * 2,
        compiler_params=pltpu.CompilerParams(vmem_limit_bytes=4 * 2**20),
        cost_estimate=QUICK,
        name="back",
    )(tile, left, right, edges, kernel)


def second_kernel(chips, hid_ref, wide_ref, near_ref, far_ref, sum_ref):
    chans = hid_ref.shape[2]
    cols, rows, outs = hid_ref.shape[0] - 2, hid_ref.shape[1], wide_ref.shape[2] // 3
    core = lax.axis_index("c")
    lhs = hid_ref[1 : cols + 1].reshape(cols * rows, chans)
    for tap_col in range(3):
        rhs = wide_ref[2 - tap_col : 2 - tap_col + cols].reshape(cols * rows, 3 * outs)
        part = lax.dot_general(lhs, rhs, (((0,), (0,)), ((), ())), preferred_element_type=F32)
        for tap_row in range(3):
            sum_ref[
                tap_row * chans : (tap_row + 1) * chans, tap_col * outs : (tap_col + 1) * outs
            ] = part[:, (2 - tap_row) * outs : (3 - tap_row) * outs]
    size = sum_ref.shape[0] // (2 * chips)
    for half, ref in ((core, near_ref), (1 - core, far_ref)):
        for chip in range(chips):
            at = pl.multiple_of((half * chips + chip) * size, size)
            for tap in range(3):
                ref[chip, tap * size : (tap + 1) * size, :] = sum_ref[
                    pl.ds(at, size), tap * outs : (tap + 1) * outs
                ].astype(ref.dtype)


def second_tile(tile, wide, chips):
    chans, outs = tile.shape[2], wide.shape[2] // 3
    cut = (chips, 9 * chans // (2 * chips), outs)
    return pl.pallas_call(
        functools.partial(second_kernel, chips),
        out_shape=(jax.ShapeDtypeStruct(cut, F32), jax.ShapeDtypeStruct(cut, BF16)),
        in_specs=[VMEM_SPEC] * 2,
        out_specs=(VMEM_SPEC,) * 2,
        scratch_shapes=[pltpu.VMEM((3 * chans, 3 * outs), F32)],
        compiler_params=pltpu.CompilerParams(vmem_limit_bytes=9 * 2**20),
        cost_estimate=QUICK,
        name="second",
    )(tile, wide)


def features_kernel(hid_ref, before_ref, after_ref, kernel_ref, out_ref, wide_ref):
    cols, rows, outs = out_ref.shape
    columns = [
        (hid_ref[j], before_ref[j : j + 1, :], after_ref[j : j + 1, :]) for j in range(cols + 2)
    ]
    spread_tile(columns, wide_ref)
    pieces = [wide_ref[tap : tap + cols] for tap in range(3)]
    lhs = jnp.concatenate(pieces, axis=-1).reshape(cols * rows, -1)
    total = jnp.dot(lhs, kernel_ref[...], preferred_element_type=F32)
    out_ref[...] = total.reshape(cols, rows, outs).astype(BF16)


def features_tile(tile, edges, kernel):
    cols, rows, chans = tile.shape
    outs = kernel.shape[3]
    return pl.pallas_call(
        features_kernel,
        out_shape=jax.ShapeDtypeStruct((cols - 2, rows, outs), BF16),
        in_specs=[VMEM_SPEC] * 4,
        out_specs=VMEM_SPEC,
        scratch_shapes=[pltpu.VMEM((cols, rows, 3 * chans), BF16)],
        compiler_params=pltpu.CompilerParams(vmem_limit_bytes=9 * 2**20),
        cost_estimate=QUICK,
        name="features",
    )(tile, *edges, kernel.reshape(-1, outs))


def point_kernel(
    own_ref, a0_ref, a1_ref, b0_ref, b1_ref, back_ref,
    delta_ref, hidden_ref, last_ref, first_ref,
):
    cols, rows, _ = own_ref.shape
    half = delta_ref.shape[0] // 2
    strip = 2 * lax.axis_index("y") + lax.axis_index("c")
    strips = 2 * lax.axis_size("y")

    def column(j, i, refs, keep):
        pre = own_ref[j] + refs[0][i].astype(F32) + refs[1][i].astype(F32)
        sigma = jax.nn.sigmoid(pre)
        hidden = pre * sigma
        if keep is not None:
            hidden = jnp.where(keep, hidden, 0.0)
        hidden = hidden.astype(BF16)
        hidden_ref[j] = hidden
        last_ref[j : j + 1, :] = hidden[rows - 1 :]
        first_ref[j : j + 1, :] = hidden[:1]
        if keep is None:
            slope = sigma * (1.0 + pre * (1.0 - sigma))
            delta_ref[j - 1] = (back_ref[j - 1] * slope).astype(BF16)

    left, right = (a0_ref, a1_ref), (b0_ref, b1_ref)
    column(0, 0, left, strip > 0)
    column(cols - 1, half, right, strip < strips - 1)

    for i in range(1, half + 1):
        column(i, i, left, None)
        column(half + i, i - 1, right, None)


def point(own, left, right, back):
    strip, rows, outs = back.shape
    delta = jax.ShapeDtypeStruct(back.shape, BF16)
    edge = jax.ShapeDtypeStruct((strip + 2, outs), BF16)
    return pl.pallas_call(
        point_kernel,
        out_shape=(delta, jax.ShapeDtypeStruct(own.shape, BF16), edge, edge),
        in_specs=[VMEM_SPEC] * 6,
        out_specs=(VMEM_SPEC,) * 4,
        compiler_params=pltpu.CompilerParams(vmem_limit_bytes=2 * 2**20),
        cost_estimate=QUICK,
        name="point",
    )(own, *left, *right, back)


def fold_kernel(near_ref, got_ref, keep_ref, *send_refs):
    chips = near_ref.shape[0]
    here = lax.axis_index("y")
    keep_ref[...] = near_ref[here] + got_ref[here].astype(F32)
    for step, ref in zip(STEPS[1:], send_refs):
        to = lax.rem(here + step, chips)
        ref[...] = (near_ref[to] + got_ref[to].astype(F32)).astype(BF16)


def fold(near, got):
    shape = near.shape[1:]
    return pl.pallas_call(
        fold_kernel,
        out_shape=(jax.ShapeDtypeStruct(shape, F32),) + (jax.ShapeDtypeStruct(shape, BF16),) * 3,
        in_specs=[VMEM_SPEC] * 2,
        out_specs=(VMEM_SPEC,) * 4,
        compiler_params=pltpu.CompilerParams(vmem_limit_bytes=2 * 2**20),
        cost_estimate=QUICK,
        name="fold",
    )(near, got)


def row_halo(ends):
    count = lax.axis_size(SKY)
    up = [(i, i + 1) for i in range(count - 1)]
    down = [(j, i) for i, j in up]
    return lax.ppermute(ends[0], SKY, up), lax.ppermute(ends[1], SKY, down)


def join_kernel(own_ref, far_ref, keep_ref, a_ref, b_ref, c_ref, out_ref):
    pieces, total, outs = out_ref.shape
    chans = own_ref.shape[0] // 3
    size = chans // pieces
    for tap_col in range(3):
        for tap_row in range(3):
            rows = slice(tap_row * chans, (tap_row + 1) * chans)
            lanes = slice(tap_col * outs, (tap_col + 1) * outs)
            value = own_ref[rows, lanes] + far_ref[rows, lanes].astype(F32)
            at = (3 * tap_col + tap_row) * size
            out_ref[:, at : at + size, :] = value.reshape(pieces, size, outs).astype(BF16)
    second = keep_ref[...]
    for ref in (a_ref, b_ref, c_ref):
        second = second + ref[...].astype(F32)
    sx = lax.axis_size("x")
    sz = pieces // sx
    third = second.shape[0] // 3
    size_x = third // sx
    extra = total - 9 * size
    for x in range(sx):
        value = jnp.concatenate(
            [second[tap * third + x * size_x : tap * third + (x + 1) * size_x] for tap in range(3)],
            axis=0,
        )
        for z in range(sz):
            out_ref[z * sx + x, 9 * size :, :] = value[z * extra : (z + 1) * extra].astype(BF16)


def join(own, far, keep, got, pieces):
    outs = keep.shape[1]
    rows = 9 * (own.shape[0] // 3 // pieces) + keep.shape[0] // pieces
    return pl.pallas_call(
        join_kernel,
        out_shape=jax.ShapeDtypeStruct((pieces, rows, outs), BF16),
        in_specs=[VMEM_SPEC] * 6,
        out_specs=VMEM_SPEC,
        compiler_params=pltpu.CompilerParams(vmem_limit_bytes=4 * 2**20),
        cost_estimate=QUICK,
        name="join",
    )(own, far, keep, *got)


STEPS = (0, 1, 3, 2)


def order_kernel(extra, a_ref, b_ref, c_ref, d_ref, out_ref):
    rows = a_ref.shape[0] - extra
    sz = lax.axis_size("z")
    me = lax.axis_index("z")
    values = [ref[...].astype(F32) for ref in (a_ref, b_ref, c_ref, d_ref)]
    rest = []
    for z in range(len(STEPS)):
        value = values[0]
        for step, other in zip(STEPS[1:], values[1:]):
            value = jnp.where(lax.rem(me + sz - step, sz) == z, other, value)
        out_ref[z * rows : (z + 1) * rows, :] = value[:rows].astype(BF16)
        rest.append(value[rows:])
    out_ref[len(STEPS) * rows :, :] = jnp.concatenate(rest, axis=0).astype(BF16)


def order_pieces(parts, extra):
    rows, outs = parts[0].shape
    return pl.pallas_call(
        functools.partial(order_kernel, extra),
        out_shape=jax.ShapeDtypeStruct((4 * rows, outs), BF16),
        in_specs=[VMEM_SPEC] * 4,
        out_specs=VMEM_SPEC,
        compiler_params=pltpu.CompilerParams(vmem_limit_bytes=4 * 2**20),
        cost_estimate=QUICK,
        name="order_pieces",
    )(*parts)


def first_kernel(sz, a_ref, b_ref, c_ref, d_ref, out_ref):
    sx = lax.axis_size("x")
    size = out_ref.shape[2] // (sx * sz)
    me = lax.axis_index("x")
    for step, ref in zip(STEPS, (a_ref, b_ref, c_ref, d_ref)):
        x = lax.rem(me + sx - step, sx)
        value = ref[...].astype(F32)
        for z in range(sz):
            at = pl.multiple_of((z * sx + x) * size, size)
            for tap in range(9):
                rows = (z * 9 + tap) * size
                out_ref[tap // 3, tap % 3, pl.ds(at, size), :] = value[rows : rows + size]


def lay_first(parts, sz, chans):
    outs = parts[0].shape[1]
    return pl.pallas_call(
        functools.partial(first_kernel, sz),
        out_shape=jax.ShapeDtypeStruct((3, 3, chans, outs), F32),
        in_specs=[VMEM_SPEC] * 4,
        out_specs=VMEM_SPEC,
        compiler_params=pltpu.CompilerParams(vmem_limit_bytes=4 * 2**20),
        cost_estimate=QUICK,
        name="lay_first",
    )(*parts)


def sum_kernel(in_ref, out_ref):
    total = in_ref[0].astype(F32)
    for i in range(1, in_ref.shape[0]):
        total = total + in_ref[i].astype(F32)
    out_ref[...] = total.astype(BF16)


def sum_pieces(pieces):
    return pl.pallas_call(
        sum_kernel,
        out_shape=jax.ShapeDtypeStruct(pieces.shape[1:], BF16),
        in_specs=[VMEM_SPEC],
        out_specs=VMEM_SPEC,
        compiler_params=pltpu.CompilerParams(vmem_limit_bytes=4 * 2**20),
        cost_estimate=QUICK,
        name="sum_pieces",
    )(pieces)


def pick_kernel(first, a_ref, b_ref, c_ref, d_ref, out_ref):
    for i, ref in enumerate((a_ref, b_ref, c_ref, d_ref)):
        out_ref[i] = ref[first:, :]


def pick_rows(parts, first):
    rows, outs = parts[0].shape
    return pl.pallas_call(
        functools.partial(pick_kernel, first),
        out_shape=jax.ShapeDtypeStruct((len(parts), rows - first, outs), BF16),
        in_specs=[VMEM_SPEC] * 4,
        out_specs=VMEM_SPEC,
        compiler_params=pltpu.CompilerParams(vmem_limit_bytes=2 * 2**20),
        cost_estimate=QUICK,
        name="pick_rows",
    )(*parts)


def lay_second_kernel(other, in_ref, *refs):
    out_ref, half_ref, sems = refs[-3:]
    sy, sx, rows, _ = in_ref.shape
    size = rows // 3
    third = half_ref.shape[0] // 3
    core, y, x = lax.axis_index("c"), lax.axis_index("y"), lax.axis_index("x")
    half = 1 - core if other else core
    copies = []
    for tap in range(3):
        for i in range(sy):
            for j in range(sx):
                place = lax.rem(y + sy - STEPS[i], sy) * sx + lax.rem(x + sx - STEPS[j], sx)
                at = pl.multiple_of(tap * third + place * size, 8)
                value = in_ref[i, j, tap * size : (tap + 1) * size, :].astype(F32)
                half_ref[pl.ds(at, size), :] = value
        to = pl.multiple_of((2 * tap + half) * third, 8)
        copy = pltpu.make_async_copy(
            half_ref.at[tap * third : (tap + 1) * third],
            out_ref.at[pl.ds(to, third)],
            sems.at[tap],
        )
        copy.start()
        copies.append(copy)
    for copy in copies:
        copy.wait()


def lay_second(half, whole=None):
    sy, sx, rows, outs = half.shape
    size = sy * sx * rows
    anywhere = pl.BlockSpec(memory_space=pl.ANY)
    given = [] if whole is None else [whole]
    return pl.pallas_call(
        functools.partial(lay_second_kernel, whole is not None),
        out_shape=jax.ShapeDtypeStruct((2 * size, outs), F32),
        in_specs=[VMEM_SPEC] + [anywhere] * len(given),
        out_specs=anywhere,
        scratch_shapes=[pltpu.VMEM((size, outs), F32), pltpu.SemaphoreType.DMA((3,))],
        compiler_params=pltpu.CompilerParams(vmem_limit_bytes=4 * 2**20),
        cost_estimate=QUICK,
        input_output_aliases={1: 0} if given else {},
        name="lay_second",
    )(half, *given)


def gather_steps(piece, axis):
    return [piece] + [shift(piece, axis, step) for step in STEPS[1:]]


def body(sky_cube, weight_first, weight_second, cotangent):
    cols, rows, chans = sky_cube.shape
    strip, _, outs = cotangent.shape
    chips = lax.axis_size("y")

    ends = [
        jnp.concatenate(
            [sky_cube[:, r], cotangent[:, r, : outs // 2], cotangent[:, r, outs // 2 :]], axis=0
        )
        for r in (rows - 1, 0)
    ]
    edges = jnp.stack(row_halo(ends))
    far_cube = shift(sky_cube, "c", 1)
    far_weight = shift(weight_first, "c", 1)
    far_edges = shift(edges, "c", 1)
    wide = spread(sky_cube, far_cube, edges, far_edges, chips)
    kernel = jnp.concatenate([weight_first, far_weight], axis=2).reshape(18 * chans, outs)

    def side(col):
        beside = [
            jnp.concatenate(
                [edges[k, at + col : at + col + 1] for at in (cols, cols + strip)], axis=1
            )
            for k in range(2)
        ]
        return jnp.concatenate([cotangent[col]] + beside, axis=0)

    count = lax.axis_size(FREQ)
    up = [(i, i + 1) for i in range(count - 1)]
    down = [(j, i) for i, j in up]
    left = lax.ppermute(side(strip - 1), FREQ, up)
    right = lax.ppermute(side(0), FREQ, down)

    on, off = 1, chips - 1
    cut = strip // 2 + 1
    far_a, far_b = conv_parts(((2, 0), (2, cut)), wide, kernel, cut, BF16)
    hold, _ = lax.optimization_barrier((wide, far_a))
    near_b, near_a = conv_parts(((on, cut), (off, 0)), hold, kernel, cut, BF16)
    got_a, got_b = shift(far_a, "y", on), shift(far_b, "y", off)
    got_a, left, right = lax.optimization_barrier((got_a, left, right))
    both_a, both_b = conv_parts(((on, 0), (off, cut)), wide, kernel, cut, BF16, (got_a, got_b))
    own = conv_parts(((0, 0),), wide, kernel, strip + 2, F32)[0]
    from_a = shift(both_a, "y", on), shift(near_a, "y", off)
    from_b = shift(near_b, "y", on), shift(both_b, "y", off)

    back, wide_cotangent = back_tile(cotangent, left, right, edges, weight_second)
    delta, hidden, *ends = point(own, from_a, from_b, back)

    from_on, from_off = shift(delta, "y", on), shift(delta, "y", off)
    half = strip // 2
    total = grad_strip(0, wide, (delta,), None, False)
    from_on, from_off, total, *edges = lax.optimization_barrier(
        (from_on, from_off, total, *row_halo(ends))
    )
    fwd_a, fwd_b = shift(from_on[:half], "y", on), shift(from_off[half:], "y", off)
    near, far = second_tile(hidden, wide_cotangent, chips)
    features = features_tile(hidden, edges, weight_second)
    keep, *sends = fold(near, shift(far, "c", 1))
    got = [shift(send, "y", step) for step, send in zip(STEPS[1:], sends)]
    total = grad_strip(off, wide, (from_on,), total, False)
    total = grad_strip(on, wide, (from_off,), total, False)
    first_own, first_far = grad_strip(2, wide, (fwd_a, fwd_b), total, True)

    sx, sz = lax.axis_size("x"), lax.axis_size("z")
    first_far, *got = lax.optimization_barrier((first_far, *got))
    joined = join(first_own, shift(first_far, "c", 1), keep, got, sx * sz)
    extra = keep.shape[0] // (sx * sz)
    summed = lax.all_to_all(joined, SKY, 0, 0, tiled=True)
    summed = sum_pieces(summed)
    parts = gather_steps(order_pieces(gather_steps(summed, "z"), extra), "x")
    main = parts[0].shape[0] - sz * extra
    grad_first = lay_first(parts, sz, chans)
    share = pick_rows(parts, main)
    share, features = lax.optimization_barrier((share, features))
    share, grad_first = lax.optimization_barrier(
        (jnp.stack(gather_steps(share, "y")), grad_first)
    )
    grad_second = lay_second(shift(share, "c", 1), lay_second(share))
    grad_second = grad_second.reshape(3, 3, outs, outs)
    return features, grad_first, grad_second


def solution(mesh):
    sizes = (mesh.devices.shape[0] // 2, 2, 4, mesh.devices.shape[1] // 4)
    fine = Mesh(mesh.devices.reshape(sizes), FREQ + SKY)
    return jax.shard_map(
        body,
        mesh=fine,
        in_specs=(P(None, SKY, FREQ), P(None, None, FREQ, None), P(), P(FREQ, SKY, None)),
        out_specs=(P(FREQ, SKY, None), P(None, None, FREQ, None), P()),
        check_vma=False,
    )
```

```python
import functools

import jax
import jax.numpy as jnp
from jax import lax
from jax.experimental import pallas as pl
from jax.experimental.pallas import tpu as pltpu
from jax.sharding import Mesh, PartitionSpec as P

FREQ = ("y", "c")
SKY = ("z", "x")
F32 = jnp.float32
BF16 = jnp.bfloat16
QUICK = pl.CostEstimate(flops=1, bytes_accessed=1, transcendentals=0)


def shift(x, axis, step):
    count = lax.axis_size(axis)
    return lax.ppermute(x, axis, [(i, (i + step) % count) for i in range(count)])


def spread_kernel(own_ref, far_ref, own_halo_ref, far_halo_ref, out_ref):
    chips, width, rows, depth = out_ref.shape
    cols, _, chans = own_ref.shape
    strip = cols // (2 * chips)
    core = lax.axis_index("c")
    step = 8
    row = lax.broadcasted_iota(jnp.int32, (step, rows, chans), 1)

    def block(i, base, chip):
        for side, (cube_ref, halo_ref) in enumerate(
            ((own_ref, own_halo_ref), (far_ref, far_halo_ref))
        ):
            at = pl.multiple_of(base + i * step, step)
            mid = cube_ref[pl.ds(at, step)]
            wide = mid.astype(F32).reshape(step * rows, chans)
            ahead = pltpu.roll(wide, 1, 0).reshape(step, rows, chans)
            behind = pltpu.roll(wide, step * rows - 1, 0).reshape(step, rows, chans)
            before = halo_ref[0, pl.ds(at, step), :].astype(F32)[:, None, :]
            after = halo_ref[1, pl.ds(at, step), :].astype(F32)[:, None, :]
            ahead = jnp.where(row == 0, before, ahead)
            behind = jnp.where(row == rows - 1, after, behind)
            to = pl.ds(2 + i * step, step)
            for tap, value in enumerate((ahead.astype(BF16), mid, behind.astype(BF16))):
                lane = (2 * tap + side) * chans
                out_ref[chip, to, :, lane : lane + chans] = value

    def edge(at, chip, slot):
        for side, (cube_ref, halo_ref) in enumerate(
            ((own_ref, own_halo_ref), (far_ref, far_halo_ref))
        ):
            first = pl.multiple_of((at // step) * step, step)
            mid = cube_ref[at]
            wide = mid.astype(F32)
            line = lax.broadcasted_iota(jnp.int32, (step, chans), 0) == at - first
            pick = lambda k: jnp.sum(
                jnp.where(line, halo_ref[k, pl.ds(first, step), :].astype(F32), 0.0),
                axis=0,
                keepdims=True,
            )
            place = lax.broadcasted_iota(jnp.int32, (rows, chans), 0)
            ahead = jnp.where(place == 0, pick(0), pltpu.roll(wide, 1, 0))
            behind = jnp.where(place == rows - 1, pick(1), pltpu.roll(wide, rows - 1, 0))
            for tap, value in enumerate((ahead.astype(BF16), mid, behind.astype(BF16))):
                lane = (2 * tap + side) * chans
                out_ref[chip, slot, :, lane : lane + chans] = value

    blank = jnp.zeros((rows, depth), BF16)
    for chip in range(chips):
        base = (2 * chip + core) * strip
        lax.fori_loop(0, strip // step, lambda i, _: block(i, base, chip), None)
        for slot in (0, 1):
            edge(jnp.maximum(base - 2 + slot, 0), chip, slot)
            edge(jnp.minimum(base + strip + slot, cols - 1), chip, strip + 2 + slot)
        for slot in range(strip + 4, width):
            out_ref[chip, slot] = blank

    @pl.when(core == 0)
    def _():
        out_ref[0, 0] = blank
        out_ref[0, 1] = blank

    @pl.when(core == 1)
    def _():
        out_ref[chips - 1, strip + 2] = blank
        out_ref[chips - 1, strip + 3] = blank


VMEM_SPEC = pl.BlockSpec(memory_space=pltpu.VMEM)


def spread(own, far, own_halo, far_halo, chips):
    cols, rows, chans = own.shape
    return pl.pallas_call(
        spread_kernel,
        out_shape=jax.ShapeDtypeStruct((chips, cols // (2 * chips) + 8, rows, 6 * chans), BF16),
        in_specs=[VMEM_SPEC] * 4,
        out_specs=VMEM_SPEC,
        compiler_params=pltpu.CompilerParams(vmem_limit_bytes=2 * 2**20),
        cost_estimate=QUICK,
        name="spread",
    )(own, far, own_halo, far_halo)


def chip_at(step):
    return lax.rem(lax.axis_index("y") + step, lax.axis_size("y"))


def conv_kernel(parts, adds, wide_ref, kernel_ref, *refs):
    rows = wide_ref.shape[2]
    for (step, first), add_ref, out_ref in zip(parts, refs[:adds] or [None] * len(parts), refs[adds:]):
        count, _, outs = out_ref.shape
        chip = chip_at(step)
        pieces = [wide_ref[chip, first + tap : first + tap + count] for tap in range(3)]
        lhs = jnp.concatenate(pieces, axis=-1).reshape(count * rows, -1)
        total = jnp.dot(lhs, kernel_ref[...], preferred_element_type=F32)
        total = total.reshape(count, rows, outs)
        if add_ref is not None:
            total = total + add_ref[...].astype(F32)
        out_ref[...] = total.astype(out_ref.dtype)


def conv_parts(parts, wide, kernel, count, dtype, adds=()):
    rows, outs = wide.shape[2], kernel.shape[1]
    return pl.pallas_call(
        functools.partial(conv_kernel, parts, len(adds)),
        out_shape=(jax.ShapeDtypeStruct((count, rows, outs), dtype),) * len(parts),
        in_specs=[VMEM_SPEC] * (2 + len(adds)),
        out_specs=(VMEM_SPEC,) * len(parts),
        compiler_params=pltpu.CompilerParams(vmem_limit_bytes=4 * 2**20),
        cost_estimate=QUICK,
        name="conv_first",
    )(wide, kernel, *adds)


def grad_kernel(step, pieces, has_old, last, wide_ref, *refs):
    piece_refs, refs = refs[:pieces], refs[pieces:]
    old_ref = refs[0] if has_old else None
    outs_refs, pad_ref = refs[1 if has_old else 0 : -1], refs[-1]
    count, rows, outs = piece_refs[0].shape
    strip = pieces * count
    cols, depth = wide_ref.shape[1], wide_ref.shape[3]
    pad_ref[0:3] = jnp.zeros((3, rows, outs), BF16)
    for i, ref in enumerate(piece_refs):
        pad_ref[3 + i * count : 3 + (i + 1) * count] = ref[...]
    pad_ref[3 + strip :] = jnp.zeros((cols - strip - 1, rows, outs), BF16)
    lhs = wide_ref[chip_at(step)].reshape(cols * rows, depth)
    rhs = jnp.concatenate(
        [pad_ref[2 - tap : 2 - tap + cols].reshape(cols * rows, outs) for tap in range(3)], axis=-1
    )
    total = lax.dot_general(lhs, rhs, (((0,), (0,)), ((), ())), preferred_element_type=F32)
    if has_old:
        total = total + old_ref[...]
    if not last:
        outs_refs[0][...] = total
    else:
        chans = depth // 6
        for tap in range(3):
            at = 2 * tap * chans
            outs_refs[0][tap * chans : (tap + 1) * chans] = total[at : at + chans]
            outs_refs[1][tap * chans : (tap + 1) * chans] = total[
                at + chans : at + 2 * chans
            ].astype(BF16)


def grad_strip(step, wide, pieces, old, last):
    _, rows, outs = pieces[0].shape
    depth, cols = wide.shape[3], wide.shape[1]
    shape = (depth, 3 * outs)
    half = (depth // 2, 3 * outs)
    if last:
        out_shape = (jax.ShapeDtypeStruct(half, F32), jax.ShapeDtypeStruct(half, BF16))
    else:
        out_shape = (jax.ShapeDtypeStruct(shape, F32),)
    args = [wide, *pieces] + ([old] if old is not None else [])
    out = pl.pallas_call(
        functools.partial(grad_kernel, step, len(pieces), old is not None, last),
        out_shape=out_shape,
        in_specs=[VMEM_SPEC] * len(args),
        out_specs=tuple([VMEM_SPEC] * len(out_shape)),
        scratch_shapes=[pltpu.VMEM((cols + 2, rows, outs), BF16)],
        compiler_params=pltpu.CompilerParams(vmem_limit_bytes=5 * 2**20),
        cost_estimate=QUICK,
        name="grad_first",
    )(*args)
    return out if last else out[0]


def spread_tile(columns, wide_ref):
    rows, chans = wide_ref.shape[1], wide_ref.shape[2] // 3
    place = lax.broadcasted_iota(jnp.int32, (rows, chans), 0)
    for j, (mid, before, after) in enumerate(columns):
        wide = mid.astype(F32)
        ahead = jnp.where(place == 0, before.astype(F32), pltpu.roll(wide, 1, 0))
        behind = jnp.where(place == rows - 1, after.astype(F32), pltpu.roll(wide, rows - 1, 0))
        wide_ref[j, :, 0:chans] = ahead.astype(BF16)
        wide_ref[j, :, chans : 2 * chans] = mid
        wide_ref[j, :, 2 * chans :] = behind.astype(BF16)


def back_kernel(cot_ref, left_ref, right_ref, edge_ref, kernel_ref, out_ref, wide_ref):
    cols, rows, chans = cot_ref.shape
    start = edge_ref.shape[1] - 2 * cols

    def beside(k, j):
        low, high = start + j, start + cols + j
        return jnp.concatenate(
            [edge_ref[k, low : low + 1, :], edge_ref[k, high : high + 1, :]], axis=-1
        )

    def whole(ref):
        return ref[0:rows], ref[rows : rows + 1], ref[rows + 1 : rows + 2]

    columns = [(cot_ref[j], beside(0, j), beside(1, j)) for j in range(cols)]
    spread_tile([whole(left_ref)] + columns + [whole(right_ref)], wide_ref)
    total = None
    for tap_col in range(3):
        lhs = wide_ref[tap_col : tap_col + cols].reshape(cols * rows, 3 * chans)
        for tap_row in range(3):
            part = lax.dot_general(
                lhs[:, tap_row * chans : (tap_row + 1) * chans],
                kernel_ref[2 - tap_col, 2 - tap_row],
                (((1,), (1,)), ((), ())),
                preferred_element_type=F32,
            )
            total = part if total is None else total + part
    out_ref[...] = total.reshape(cols, rows, -1)


def back_tile(tile, left, right, edges, kernel):
    cols, rows, chans = tile.shape
    return pl.pallas_call(
        back_kernel,
        out_shape=(
            jax.ShapeDtypeStruct((cols, rows, kernel.shape[2]), F32),
            jax.ShapeDtypeStruct((cols + 2, rows, 3 * chans), BF16),
        ),
        in_specs=[VMEM_SPEC] * 5,
        out_specs=(VMEM_SPEC,) * 2,
        compiler_params=pltpu.CompilerParams(vmem_limit_bytes=4 * 2**20),
        cost_estimate=QUICK,
        name="back",
    )(tile, left, right, edges, kernel)


def second_kernel(chips, hid_ref, wide_ref, near_ref, far_ref, sum_ref):
    chans = hid_ref.shape[2]
    cols, rows, outs = hid_ref.shape[0] - 2, hid_ref.shape[1], wide_ref.shape[2] // 3
    core = lax.axis_index("c")
    lhs = hid_ref[1 : cols + 1].reshape(cols * rows, chans)
    for tap_col in range(3):
        rhs = wide_ref[2 - tap_col : 2 - tap_col + cols].reshape(cols * rows, 3 * outs)
        part = lax.dot_general(lhs, rhs, (((0,), (0,)), ((), ())), preferred_element_type=F32)
        for tap_row in range(3):
            sum_ref[
                tap_row * chans : (tap_row + 1) * chans, tap_col * outs : (tap_col + 1) * outs
            ] = part[:, (2 - tap_row) * outs : (3 - tap_row) * outs]
    size = sum_ref.shape[0] // (2 * chips)
    for half, ref in ((core, near_ref), (1 - core, far_ref)):
        for chip in range(chips):
            at = pl.multiple_of((half * chips + chip) * size, size)
            for tap in range(3):
                ref[chip, tap * size : (tap + 1) * size, :] = sum_ref[
                    pl.ds(at, size), tap * outs : (tap + 1) * outs
                ].astype(ref.dtype)


def second_tile(tile, wide, chips):
    chans, outs = tile.shape[2], wide.shape[2] // 3
    cut = (chips, 9 * chans // (2 * chips), outs)
    return pl.pallas_call(
        functools.partial(second_kernel, chips),
        out_shape=(jax.ShapeDtypeStruct(cut, F32), jax.ShapeDtypeStruct(cut, BF16)),
        in_specs=[VMEM_SPEC] * 2,
        out_specs=(VMEM_SPEC,) * 2,
        scratch_shapes=[pltpu.VMEM((3 * chans, 3 * outs), F32)],
        compiler_params=pltpu.CompilerParams(vmem_limit_bytes=9 * 2**20),
        cost_estimate=QUICK,
        name="second",
    )(tile, wide)


def features_kernel(hid_ref, before_ref, after_ref, kernel_ref, out_ref, wide_ref):
    cols, rows, outs = out_ref.shape
    columns = [
        (hid_ref[j], before_ref[j : j + 1, :], after_ref[j : j + 1, :]) for j in range(cols + 2)
    ]
    spread_tile(columns, wide_ref)
    pieces = [wide_ref[tap : tap + cols] for tap in range(3)]
    lhs = jnp.concatenate(pieces, axis=-1).reshape(cols * rows, -1)
    total = jnp.dot(lhs, kernel_ref[...], preferred_element_type=F32)
    out_ref[...] = total.reshape(cols, rows, outs).astype(BF16)


def features_tile(tile, edges, kernel):
    cols, rows, chans = tile.shape
    outs = kernel.shape[3]
    return pl.pallas_call(
        features_kernel,
        out_shape=jax.ShapeDtypeStruct((cols - 2, rows, outs), BF16),
        in_specs=[VMEM_SPEC] * 4,
        out_specs=VMEM_SPEC,
        scratch_shapes=[pltpu.VMEM((cols, rows, 3 * chans), BF16)],
        compiler_params=pltpu.CompilerParams(vmem_limit_bytes=9 * 2**20),
        cost_estimate=QUICK,
        name="features",
    )(tile, *edges, kernel.reshape(-1, outs))


def point_kernel(
    own_ref, a0_ref, a1_ref, b0_ref, b1_ref, back_ref,
    delta_ref, hidden_ref, last_ref, first_ref,
):
    cols, rows, _ = own_ref.shape
    half = delta_ref.shape[0] // 2
    strip = 2 * lax.axis_index("y") + lax.axis_index("c")
    strips = 2 * lax.axis_size("y")

    def column(j, i, refs, keep):
        pre = own_ref[j] + refs[0][i].astype(F32) + refs[1][i].astype(F32)
        sigma = jax.nn.sigmoid(pre)
        hidden = pre * sigma
        if keep is not None:
            hidden = jnp.where(keep, hidden, 0.0)
        hidden = hidden.astype(BF16)
        hidden_ref[j] = hidden
        last_ref[j : j + 1, :] = hidden[rows - 1 :]
        first_ref[j : j + 1, :] = hidden[:1]
        if keep is None:
            slope = sigma * (1.0 + pre * (1.0 - sigma))
            delta_ref[j - 1] = (back_ref[j - 1] * slope).astype(BF16)

    left, right = (a0_ref, a1_ref), (b0_ref, b1_ref)
    column(0, 0, left, strip > 0)
    column(cols - 1, half, right, strip < strips - 1)

    for i in range(1, half + 1):
        column(i, i, left, None)
        column(half + i, i - 1, right, None)


def point(own, left, right, back):
    strip, rows, outs = back.shape
    delta = jax.ShapeDtypeStruct(back.shape, BF16)
    edge = jax.ShapeDtypeStruct((strip + 2, outs), BF16)
    return pl.pallas_call(
        point_kernel,
        out_shape=(delta, jax.ShapeDtypeStruct(own.shape, BF16), edge, edge),
        in_specs=[VMEM_SPEC] * 6,
        out_specs=(VMEM_SPEC,) * 4,
        compiler_params=pltpu.CompilerParams(vmem_limit_bytes=2 * 2**20),
        cost_estimate=QUICK,
        name="point",
    )(own, *left, *right, back)


def fold_kernel(near_ref, got_ref, keep_ref, *send_refs):
    chips = near_ref.shape[0]
    here = lax.axis_index("y")
    keep_ref[...] = near_ref[here] + got_ref[here].astype(F32)
    for step, ref in zip(STEPS[1:], send_refs):
        to = lax.rem(here + step, chips)
        ref[...] = (near_ref[to] + got_ref[to].astype(F32)).astype(BF16)


def fold(near, got):
    shape = near.shape[1:]
    return pl.pallas_call(
        fold_kernel,
        out_shape=(jax.ShapeDtypeStruct(shape, F32),) + (jax.ShapeDtypeStruct(shape, BF16),) * 3,
        in_specs=[VMEM_SPEC] * 2,
        out_specs=(VMEM_SPEC,) * 4,
        compiler_params=pltpu.CompilerParams(vmem_limit_bytes=2 * 2**20),
        cost_estimate=QUICK,
        name="fold",
    )(near, got)


def row_halo(ends):
    count = lax.axis_size(SKY)
    up = [(i, i + 1) for i in range(count - 1)]
    down = [(j, i) for i, j in up]
    return lax.ppermute(ends[0], SKY, up), lax.ppermute(ends[1], SKY, down)


def join_kernel(own_ref, far_ref, keep_ref, a_ref, b_ref, c_ref, out_ref):
    pieces, total, outs = out_ref.shape
    chans = own_ref.shape[0] // 3
    size = chans // pieces
    for tap_col in range(3):
        for tap_row in range(3):
            rows = slice(tap_row * chans, (tap_row + 1) * chans)
            lanes = slice(tap_col * outs, (tap_col + 1) * outs)
            value = own_ref[rows, lanes] + far_ref[rows, lanes].astype(F32)
            at = (3 * tap_col + tap_row) * size
            out_ref[:, at : at + size, :] = value.reshape(pieces, size, outs).astype(BF16)
    second = keep_ref[...]
    for ref in (a_ref, b_ref, c_ref):
        second = second + ref[...].astype(F32)
    sx = lax.axis_size("x")
    sz = pieces // sx
    third = second.shape[0] // 3
    size_x = third // sx
    extra = total - 9 * size
    for x in range(sx):
        value = jnp.concatenate(
            [second[tap * third + x * size_x : tap * third + (x + 1) * size_x] for tap in range(3)],
            axis=0,
        )
        for z in range(sz):
            out_ref[z * sx + x, 9 * size :, :] = value[z * extra : (z + 1) * extra].astype(BF16)


def join(own, far, keep, got, pieces):
    outs = keep.shape[1]
    rows = 9 * (own.shape[0] // 3 // pieces) + keep.shape[0] // pieces
    return pl.pallas_call(
        join_kernel,
        out_shape=jax.ShapeDtypeStruct((pieces, rows, outs), BF16),
        in_specs=[VMEM_SPEC] * 6,
        out_specs=VMEM_SPEC,
        compiler_params=pltpu.CompilerParams(vmem_limit_bytes=4 * 2**20),
        cost_estimate=QUICK,
        name="join",
    )(own, far, keep, *got)


STEPS = (0, 1, 3, 2)


def order_kernel(extra, a_ref, b_ref, c_ref, d_ref, out_ref):
    rows = a_ref.shape[0] - extra
    sz = lax.axis_size("z")
    me = lax.axis_index("z")
    values = [ref[...].astype(F32) for ref in (a_ref, b_ref, c_ref, d_ref)]
    rest = []
    for z in range(len(STEPS)):
        value = values[0]
        for step, other in zip(STEPS[1:], values[1:]):
            value = jnp.where(lax.rem(me + sz - step, sz) == z, other, value)
        out_ref[z * rows : (z + 1) * rows, :] = value[:rows].astype(BF16)
        rest.append(value[rows:])
    out_ref[len(STEPS) * rows :, :] = jnp.concatenate(rest, axis=0).astype(BF16)


def order_pieces(parts, extra):
    rows, outs = parts[0].shape
    return pl.pallas_call(
        functools.partial(order_kernel, extra),
        out_shape=jax.ShapeDtypeStruct((4 * rows, outs), BF16),
        in_specs=[VMEM_SPEC] * 4,
        out_specs=VMEM_SPEC,
        compiler_params=pltpu.CompilerParams(vmem_limit_bytes=4 * 2**20),
        cost_estimate=QUICK,
        name="order_pieces",
    )(*parts)


def first_kernel(sz, a_ref, b_ref, c_ref, d_ref, out_ref):
    sx = lax.axis_size("x")
    size = out_ref.shape[2] // (sx * sz)
    me = lax.axis_index("x")
    for step, ref in zip(STEPS, (a_ref, b_ref, c_ref, d_ref)):
        x = lax.rem(me + sx - step, sx)
        value = ref[...].astype(F32)
        for z in range(sz):
            at = pl.multiple_of((z * sx + x) * size, size)
            for tap in range(9):
                rows = (z * 9 + tap) * size
                out_ref[tap // 3, tap % 3, pl.ds(at, size), :] = value[rows : rows + size]


def lay_first(parts, sz, chans):
    outs = parts[0].shape[1]
    return pl.pallas_call(
        functools.partial(first_kernel, sz),
        out_shape=jax.ShapeDtypeStruct((3, 3, chans, outs), F32),
        in_specs=[VMEM_SPEC] * 4,
        out_specs=VMEM_SPEC,
        compiler_params=pltpu.CompilerParams(vmem_limit_bytes=4 * 2**20),
        cost_estimate=QUICK,
        name="lay_first",
    )(*parts)


def sum_kernel(in_ref, out_ref):
    total = in_ref[0].astype(F32)
    for i in range(1, in_ref.shape[0]):
        total = total + in_ref[i].astype(F32)
    out_ref[...] = total.astype(BF16)


def sum_pieces(pieces):
    return pl.pallas_call(
        sum_kernel,
        out_shape=jax.ShapeDtypeStruct(pieces.shape[1:], BF16),
        in_specs=[VMEM_SPEC],
        out_specs=VMEM_SPEC,
        compiler_params=pltpu.CompilerParams(vmem_limit_bytes=4 * 2**20),
        cost_estimate=QUICK,
        name="sum_pieces",
    )(pieces)


def pick_kernel(first, a_ref, b_ref, c_ref, d_ref, out_ref):
    for i, ref in enumerate((a_ref, b_ref, c_ref, d_ref)):
        out_ref[i] = ref[first:, :]


def pick_rows(parts, first):
    rows, outs = parts[0].shape
    return pl.pallas_call(
        functools.partial(pick_kernel, first),
        out_shape=jax.ShapeDtypeStruct((len(parts), rows - first, outs), BF16),
        in_specs=[VMEM_SPEC] * 4,
        out_specs=VMEM_SPEC,
        compiler_params=pltpu.CompilerParams(vmem_limit_bytes=2 * 2**20),
        cost_estimate=QUICK,
        name="pick_rows",
    )(*parts)


def lay_second_kernel(other, in_ref, *refs):
    out_ref, half_ref, sems = refs[-3:]
    sy, sx, rows, _ = in_ref.shape
    size = rows // 3
    third = half_ref.shape[0] // 3
    core, y, x = lax.axis_index("c"), lax.axis_index("y"), lax.axis_index("x")
    half = 1 - core if other else core
    copies = []
    for tap in range(3):
        for i in range(sy):
            for j in range(sx):
                place = lax.rem(y + sy - STEPS[i], sy) * sx + lax.rem(x + sx - STEPS[j], sx)
                at = pl.multiple_of(tap * third + place * size, 8)
                value = in_ref[i, j, tap * size : (tap + 1) * size, :].astype(F32)
                half_ref[pl.ds(at, size), :] = value
        to = pl.multiple_of((2 * tap + half) * third, 8)
        copy = pltpu.make_async_copy(
            half_ref.at[tap * third : (tap + 1) * third],
            out_ref.at[pl.ds(to, third)],
            sems.at[tap],
        )
        copy.start()
        copies.append(copy)
    for copy in copies:
        copy.wait()


def lay_second(half, whole=None):
    sy, sx, rows, outs = half.shape
    size = sy * sx * rows
    anywhere = pl.BlockSpec(memory_space=pl.ANY)
    given = [] if whole is None else [whole]
    return pl.pallas_call(
        functools.partial(lay_second_kernel, whole is not None),
        out_shape=jax.ShapeDtypeStruct((2 * size, outs), F32),
        in_specs=[VMEM_SPEC] + [anywhere] * len(given),
        out_specs=anywhere,
        scratch_shapes=[pltpu.VMEM((size, outs), F32), pltpu.SemaphoreType.DMA((3,))],
        compiler_params=pltpu.CompilerParams(vmem_limit_bytes=4 * 2**20),
        cost_estimate=QUICK,
        input_output_aliases={1: 0} if given else {},
        name="lay_second",
    )(half, *given)


def gather_steps(piece, axis):
    return [piece] + [shift(piece, axis, step) for step in STEPS[1:]]


def body(sky_cube, weight_first, weight_second, cotangent):
    cols, rows, chans = sky_cube.shape
    strip, _, outs = cotangent.shape
    chips = lax.axis_size("y")

    ends = [
        jnp.concatenate(
            [sky_cube[:, r], cotangent[:, r, : outs // 2], cotangent[:, r, outs // 2 :]], axis=0
        )
        for r in (rows - 1, 0)
    ]
    edges = jnp.stack(row_halo(ends))
    far_cube = shift(sky_cube, "c", 1)
    far_weight = shift(weight_first, "c", 1)
    far_edges = shift(edges, "c", 1)
    wide = spread(sky_cube, far_cube, edges, far_edges, chips)
    kernel = jnp.concatenate([weight_first, far_weight], axis=2).reshape(18 * chans, outs)

    def side(col):
        beside = [
            jnp.concatenate(
                [edges[k, at + col : at + col + 1] for at in (cols, cols + strip)], axis=1
            )
            for k in range(2)
        ]
        return jnp.concatenate([cotangent[col]] + beside, axis=0)

    count = lax.axis_size(FREQ)
    up = [(i, i + 1) for i in range(count - 1)]
    down = [(j, i) for i, j in up]
    left = lax.ppermute(side(strip - 1), FREQ, up)
    right = lax.ppermute(side(0), FREQ, down)

    on, off = 1, chips - 1
    cut = strip // 2 + 1
    far_a, far_b = conv_parts(((2, 0), (2, cut)), wide, kernel, cut, BF16)
    hold, _ = lax.optimization_barrier((wide, far_a))
    near_b, near_a = conv_parts(((on, cut), (off, 0)), hold, kernel, cut, BF16)
    got_a, got_b = shift(far_a, "y", on), shift(far_b, "y", off)
    got_a, left, right = lax.optimization_barrier((got_a, left, right))
    both_a, both_b = conv_parts(((on, 0), (off, cut)), wide, kernel, cut, BF16, (got_a, got_b))
    own = conv_parts(((0, 0),), wide, kernel, strip + 2, F32)[0]
    from_a = shift(both_a, "y", on), shift(near_a, "y", off)
    from_b = shift(near_b, "y", on), shift(both_b, "y", off)

    back, wide_cotangent = back_tile(cotangent, left, right, edges, weight_second)
    delta, hidden, *ends = point(own, from_a, from_b, back)

    from_on, from_off = shift(delta, "y", on), shift(delta, "y", off)
    half = strip // 2
    total = grad_strip(0, wide, (delta,), None, False)
    from_on, from_off, total = lax.optimization_barrier((from_on, from_off, total))
    fwd_a, fwd_b = shift(from_on[:half], "y", on), shift(from_off[half:], "y", off)
    near, far = second_tile(hidden, wide_cotangent, chips)
    keep, *sends = fold(near, shift(far, "c", 1))
    got = [shift(send, "y", step) for step, send in zip(STEPS[1:], sends)]
    total = grad_strip(off, wide, (from_on,), total, False)
    total = grad_strip(on, wide, (from_off,), total, False)
    first_own, first_far = grad_strip(2, wide, (fwd_a, fwd_b), total, True)

    sx, sz = lax.axis_size("x"), lax.axis_size("z")
    first_far, *got = lax.optimization_barrier((first_far, *got))
    joined = join(first_own, shift(first_far, "c", 1), keep, got, sx * sz)
    extra = keep.shape[0] // (sx * sz)
    summed = lax.all_to_all(joined, SKY, 0, 0, tiled=True)
    summed = sum_pieces(summed)
    summed, *ends = lax.optimization_barrier((summed, *ends))
    edges = row_halo(ends)
    parts = gather_steps(order_pieces(gather_steps(summed, "z"), extra), "x")
    main = parts[0].shape[0] - sz * extra
    grad_first = lay_first(parts, sz, chans)
    share = pick_rows(parts, main)
    share, *edges = lax.optimization_barrier((share, *edges))
    features = features_tile(hidden, edges, weight_second)
    share, grad_first, features = lax.optimization_barrier(
        (jnp.stack(gather_steps(share, "y")), grad_first, features)
    )
    grad_second = lay_second(shift(share, "c", 1), lay_second(share))
    grad_second = grad_second.reshape(3, 3, outs, outs)
    return features, grad_first, grad_second


def solution(mesh):
    sizes = (mesh.devices.shape[0] // 2, 2, 4, mesh.devices.shape[1] // 4)
    fine = Mesh(mesh.devices.reshape(sizes), FREQ + SKY)
    return jax.shard_map(
        body,
        mesh=fine,
        in_specs=(P(None, SKY, FREQ), P(None, None, FREQ, None), P(), P(FREQ, SKY, None)),
        out_specs=(P(FREQ, SKY, None), P(None, None, FREQ, None), P()),
        check_vma=False,
    )
```

```python
import functools

import jax
import jax.numpy as jnp
from jax import lax
from jax.experimental import pallas as pl
from jax.experimental.pallas import tpu as pltpu
from jax.sharding import Mesh, PartitionSpec as P

FREQ = ("y", "c")
SKY = ("z", "x")
F32 = jnp.float32
BF16 = jnp.bfloat16
QUICK = pl.CostEstimate(flops=1, bytes_accessed=1, transcendentals=0)


def shift(x, axis, step):
    count = lax.axis_size(axis)
    return lax.ppermute(x, axis, [(i, (i + step) % count) for i in range(count)])


def spread_kernel(own_ref, far_ref, own_halo_ref, far_halo_ref, out_ref):
    chips, width, rows, depth = out_ref.shape
    cols, _, chans = own_ref.shape
    strip = cols // (2 * chips)
    core = lax.axis_index("c")
    step = 8
    row = lax.broadcasted_iota(jnp.int32, (step, rows, chans), 1)

    def block(i, base, chip):
        for side, (cube_ref, halo_ref) in enumerate(
            ((own_ref, own_halo_ref), (far_ref, far_halo_ref))
        ):
            at = pl.multiple_of(base + i * step, step)
            mid = cube_ref[pl.ds(at, step)]
            wide = mid.astype(F32).reshape(step * rows, chans)
            ahead = pltpu.roll(wide, 1, 0).reshape(step, rows, chans)
            behind = pltpu.roll(wide, step * rows - 1, 0).reshape(step, rows, chans)
            before = halo_ref[0, pl.ds(at, step), :].astype(F32)[:, None, :]
            after = halo_ref[1, pl.ds(at, step), :].astype(F32)[:, None, :]
            ahead = jnp.where(row == 0, before, ahead)
            behind = jnp.where(row == rows - 1, after, behind)
            to = pl.ds(2 + i * step, step)
            for tap, value in enumerate((ahead.astype(BF16), mid, behind.astype(BF16))):
                lane = (2 * tap + side) * chans
                out_ref[chip, to, :, lane : lane + chans] = value

    def edge(at, chip, slot):
        for side, (cube_ref, halo_ref) in enumerate(
            ((own_ref, own_halo_ref), (far_ref, far_halo_ref))
        ):
            first = pl.multiple_of((at // step) * step, step)
            mid = cube_ref[at]
            wide = mid.astype(F32)
            line = lax.broadcasted_iota(jnp.int32, (step, chans), 0) == at - first
            pick = lambda k: jnp.sum(
                jnp.where(line, halo_ref[k, pl.ds(first, step), :].astype(F32), 0.0),
                axis=0,
                keepdims=True,
            )
            place = lax.broadcasted_iota(jnp.int32, (rows, chans), 0)
            ahead = jnp.where(place == 0, pick(0), pltpu.roll(wide, 1, 0))
            behind = jnp.where(place == rows - 1, pick(1), pltpu.roll(wide, rows - 1, 0))
            for tap, value in enumerate((ahead.astype(BF16), mid, behind.astype(BF16))):
                lane = (2 * tap + side) * chans
                out_ref[chip, slot, :, lane : lane + chans] = value

    blank = jnp.zeros((rows, depth), BF16)
    for chip in range(chips):
        base = (2 * chip + core) * strip
        lax.fori_loop(0, strip // step, lambda i, _: block(i, base, chip), None)
        for slot in (0, 1):
            edge(jnp.maximum(base - 2 + slot, 0), chip, slot)
            edge(jnp.minimum(base + strip + slot, cols - 1), chip, strip + 2 + slot)
        for slot in range(strip + 4, width):
            out_ref[chip, slot] = blank

    @pl.when(core == 0)
    def _():
        out_ref[0, 0] = blank
        out_ref[0, 1] = blank

    @pl.when(core == 1)
    def _():
        out_ref[chips - 1, strip + 2] = blank
        out_ref[chips - 1, strip + 3] = blank


VMEM_SPEC = pl.BlockSpec(memory_space=pltpu.VMEM)


def spread(own, far, own_halo, far_halo, chips):
    cols, rows, chans = own.shape
    return pl.pallas_call(
        spread_kernel,
        out_shape=jax.ShapeDtypeStruct((chips, cols // (2 * chips) + 8, rows, 6 * chans), BF16),
        in_specs=[VMEM_SPEC] * 4,
        out_specs=VMEM_SPEC,
        compiler_params=pltpu.CompilerParams(vmem_limit_bytes=2 * 2**20),
        cost_estimate=QUICK,
        name="spread",
    )(own, far, own_halo, far_halo)


def chip_at(step):
    return lax.rem(lax.axis_index("y") + step, lax.axis_size("y"))


def conv_kernel(parts, adds, wide_ref, kernel_ref, *refs):
    rows = wide_ref.shape[2]
    for (step, first), add_ref, out_ref in zip(parts, refs[:adds] or [None] * len(parts), refs[adds:]):
        count, _, outs = out_ref.shape
        chip = chip_at(step)
        pieces = [wide_ref[chip, first + tap : first + tap + count] for tap in range(3)]
        lhs = jnp.concatenate(pieces, axis=-1).reshape(count * rows, -1)
        total = jnp.dot(lhs, kernel_ref[...], preferred_element_type=F32)
        total = total.reshape(count, rows, outs)
        if add_ref is not None:
            total = total + add_ref[...].astype(F32)
        out_ref[...] = total.astype(out_ref.dtype)


def conv_parts(parts, wide, kernel, count, dtype, adds=()):
    rows, outs = wide.shape[2], kernel.shape[1]
    return pl.pallas_call(
        functools.partial(conv_kernel, parts, len(adds)),
        out_shape=(jax.ShapeDtypeStruct((count, rows, outs), dtype),) * len(parts),
        in_specs=[VMEM_SPEC] * (2 + len(adds)),
        out_specs=(VMEM_SPEC,) * len(parts),
        compiler_params=pltpu.CompilerParams(vmem_limit_bytes=4 * 2**20),
        cost_estimate=QUICK,
        name="conv_first",
    )(wide, kernel, *adds)


def grad_kernel(step, pieces, has_old, last, wide_ref, *refs):
    piece_refs, refs = refs[:pieces], refs[pieces:]
    old_ref = refs[0] if has_old else None
    outs_refs, pad_ref = refs[1 if has_old else 0 : -1], refs[-1]
    count, rows, outs = piece_refs[0].shape
    strip = pieces * count
    cols, depth = wide_ref.shape[1], wide_ref.shape[3]
    pad_ref[0:3] = jnp.zeros((3, rows, outs), BF16)
    for i, ref in enumerate(piece_refs):
        pad_ref[3 + i * count : 3 + (i + 1) * count] = ref[...]
    pad_ref[3 + strip :] = jnp.zeros((cols - strip - 1, rows, outs), BF16)
    lhs = wide_ref[chip_at(step)].reshape(cols * rows, depth)
    rhs = jnp.concatenate(
        [pad_ref[2 - tap : 2 - tap + cols].reshape(cols * rows, outs) for tap in range(3)], axis=-1
    )
    total = lax.dot_general(lhs, rhs, (((0,), (0,)), ((), ())), preferred_element_type=F32)
    if has_old:
        total = total + old_ref[...]
    if not last:
        outs_refs[0][...] = total
    else:
        chans = depth // 6
        for tap in range(3):
            at = 2 * tap * chans
            outs_refs[0][tap * chans : (tap + 1) * chans] = total[at : at + chans]
            outs_refs[1][tap * chans : (tap + 1) * chans] = total[
                at + chans : at + 2 * chans
            ].astype(BF16)


def grad_strip(step, wide, pieces, old, last):
    _, rows, outs = pieces[0].shape
    depth, cols = wide.shape[3], wide.shape[1]
    shape = (depth, 3 * outs)
    half = (depth // 2, 3 * outs)
    if last:
        out_shape = (jax.ShapeDtypeStruct(half, F32), jax.ShapeDtypeStruct(half, BF16))
    else:
        out_shape = (jax.ShapeDtypeStruct(shape, F32),)
    args = [wide, *pieces] + ([old] if old is not None else [])
    out = pl.pallas_call(
        functools.partial(grad_kernel, step, len(pieces), old is not None, last),
        out_shape=out_shape,
        in_specs=[VMEM_SPEC] * len(args),
        out_specs=tuple([VMEM_SPEC] * len(out_shape)),
        scratch_shapes=[pltpu.VMEM((cols + 2, rows, outs), BF16)],
        compiler_params=pltpu.CompilerParams(vmem_limit_bytes=5 * 2**20),
        cost_estimate=QUICK,
        name="grad_first",
    )(*args)
    return out if last else out[0]


def spread_tile(columns, wide_ref):
    rows, chans = wide_ref.shape[1], wide_ref.shape[2] // 3
    place = lax.broadcasted_iota(jnp.int32, (rows, chans), 0)
    for j, (mid, before, after) in enumerate(columns):
        wide = mid.astype(F32)
        ahead = jnp.where(place == 0, before.astype(F32), pltpu.roll(wide, 1, 0))
        behind = jnp.where(place == rows - 1, after.astype(F32), pltpu.roll(wide, rows - 1, 0))
        wide_ref[j, :, 0:chans] = ahead.astype(BF16)
        wide_ref[j, :, chans : 2 * chans] = mid
        wide_ref[j, :, 2 * chans :] = behind.astype(BF16)


def back_kernel(cot_ref, left_ref, right_ref, edge_ref, kernel_ref, out_ref, wide_ref):
    cols, rows, chans = cot_ref.shape
    start = edge_ref.shape[1] - 2 * cols

    def beside(k, j):
        low, high = start + j, start + cols + j
        return jnp.concatenate(
            [edge_ref[k, low : low + 1, :], edge_ref[k, high : high + 1, :]], axis=-1
        )

    def whole(ref):
        return ref[0:rows], ref[rows : rows + 1], ref[rows + 1 : rows + 2]

    columns = [(cot_ref[j], beside(0, j), beside(1, j)) for j in range(cols)]
    spread_tile([whole(left_ref)] + columns + [whole(right_ref)], wide_ref)
    total = None
    for tap_col in range(3):
        lhs = wide_ref[tap_col : tap_col + cols].reshape(cols * rows, 3 * chans)
        for tap_row in range(3):
            part = lax.dot_general(
                lhs[:, tap_row * chans : (tap_row + 1) * chans],
                kernel_ref[2 - tap_col, 2 - tap_row],
                (((1,), (1,)), ((), ())),
                preferred_element_type=F32,
            )
            total = part if total is None else total + part
    out_ref[...] = total.reshape(cols, rows, -1)


def back_tile(tile, left, right, edges, kernel):
    cols, rows, chans = tile.shape
    return pl.pallas_call(
        back_kernel,
        out_shape=(
            jax.ShapeDtypeStruct((cols, rows, kernel.shape[2]), F32),
            jax.ShapeDtypeStruct((cols + 2, rows, 3 * chans), BF16),
        ),
        in_specs=[VMEM_SPEC] * 5,
        out_specs=(VMEM_SPEC,) * 2,
        compiler_params=pltpu.CompilerParams(vmem_limit_bytes=4 * 2**20),
        cost_estimate=QUICK,
        name="back",
    )(tile, left, right, edges, kernel)


def second_kernel(chips, hid_ref, wide_ref, near_ref, far_ref, sum_ref):
    chans = hid_ref.shape[2]
    cols, rows, outs = hid_ref.shape[0] - 2, hid_ref.shape[1], wide_ref.shape[2] // 3
    core = lax.axis_index("c")
    lhs = hid_ref[1 : cols + 1].reshape(cols * rows, chans)
    for tap_col in range(3):
        rhs = wide_ref[2 - tap_col : 2 - tap_col + cols].reshape(cols * rows, 3 * outs)
        part = lax.dot_general(lhs, rhs, (((0,), (0,)), ((), ())), preferred_element_type=F32)
        for tap_row in range(3):
            sum_ref[
                tap_row * chans : (tap_row + 1) * chans, tap_col * outs : (tap_col + 1) * outs
            ] = part[:, (2 - tap_row) * outs : (3 - tap_row) * outs]
    size = sum_ref.shape[0] // (2 * chips)
    for half, ref in ((core, near_ref), (1 - core, far_ref)):
        for chip in range(chips):
            at = pl.multiple_of((half * chips + chip) * size, size)
            for tap in range(3):
                ref[chip, tap * size : (tap + 1) * size, :] = sum_ref[
                    pl.ds(at, size), tap * outs : (tap + 1) * outs
                ].astype(ref.dtype)


def second_tile(tile, wide, chips):
    chans, outs = tile.shape[2], wide.shape[2] // 3
    cut = (chips, 9 * chans // (2 * chips), outs)
    return pl.pallas_call(
        functools.partial(second_kernel, chips),
        out_shape=(jax.ShapeDtypeStruct(cut, F32), jax.ShapeDtypeStruct(cut, BF16)),
        in_specs=[VMEM_SPEC] * 2,
        out_specs=(VMEM_SPEC,) * 2,
        scratch_shapes=[pltpu.VMEM((3 * chans, 3 * outs), F32)],
        compiler_params=pltpu.CompilerParams(vmem_limit_bytes=9 * 2**20),
        cost_estimate=QUICK,
        name="second",
    )(tile, wide)


def features_kernel(hid_ref, before_ref, after_ref, kernel_ref, out_ref, wide_ref):
    cols, rows, outs = out_ref.shape
    columns = [
        (hid_ref[j], before_ref[j : j + 1, :], after_ref[j : j + 1, :]) for j in range(cols + 2)
    ]
    spread_tile(columns, wide_ref)
    pieces = [wide_ref[tap : tap + cols] for tap in range(3)]
    lhs = jnp.concatenate(pieces, axis=-1).reshape(cols * rows, -1)
    total = jnp.dot(lhs, kernel_ref[...], preferred_element_type=F32)
    out_ref[...] = total.reshape(cols, rows, outs).astype(BF16)


def features_tile(tile, edges, kernel):
    cols, rows, chans = tile.shape
    outs = kernel.shape[3]
    return pl.pallas_call(
        features_kernel,
        out_shape=jax.ShapeDtypeStruct((cols - 2, rows, outs), BF16),
        in_specs=[VMEM_SPEC] * 4,
        out_specs=VMEM_SPEC,
        scratch_shapes=[pltpu.VMEM((cols, rows, 3 * chans), BF16)],
        compiler_params=pltpu.CompilerParams(vmem_limit_bytes=9 * 2**20),
        cost_estimate=QUICK,
        name="features",
    )(tile, *edges, kernel.reshape(-1, outs))


def point_kernel(
    own_ref, a0_ref, a1_ref, b0_ref, b1_ref, back_ref,
    delta_ref, hidden_ref, last_ref, first_ref,
):
    cols, rows, _ = own_ref.shape
    half = delta_ref.shape[0] // 2
    strip = 2 * lax.axis_index("y") + lax.axis_index("c")
    strips = 2 * lax.axis_size("y")

    def column(j, i, refs, keep):
        pre = own_ref[j] + refs[0][i].astype(F32) + refs[1][i].astype(F32)
        sigma = jax.nn.sigmoid(pre)
        hidden = pre * sigma
        if keep is not None:
            hidden = jnp.where(keep, hidden, 0.0)
        hidden = hidden.astype(BF16)
        hidden_ref[j] = hidden
        last_ref[j : j + 1, :] = hidden[rows - 1 :]
        first_ref[j : j + 1, :] = hidden[:1]
        if keep is None:
            slope = sigma * (1.0 + pre * (1.0 - sigma))
            delta_ref[j - 1] = (back_ref[j - 1] * slope).astype(BF16)

    left, right = (a0_ref, a1_ref), (b0_ref, b1_ref)
    column(0, 0, left, strip > 0)
    column(cols - 1, half, right, strip < strips - 1)

    for i in range(1, half + 1):
        column(i, i, left, None)
        column(half + i, i - 1, right, None)


def point(own, left, right, back):
    strip, rows, outs = back.shape
    delta = jax.ShapeDtypeStruct(back.shape, BF16)
    edge = jax.ShapeDtypeStruct((strip + 2, outs), BF16)
    return pl.pallas_call(
        point_kernel,
        out_shape=(delta, jax.ShapeDtypeStruct(own.shape, BF16), edge, edge),
        in_specs=[VMEM_SPEC] * 6,
        out_specs=(VMEM_SPEC,) * 4,
        compiler_params=pltpu.CompilerParams(vmem_limit_bytes=2 * 2**20),
        cost_estimate=QUICK,
        name="point",
    )(own, *left, *right, back)


def fold_kernel(near_ref, got_ref, keep_ref, *send_refs):
    chips = near_ref.shape[0]
    here = lax.axis_index("y")
    keep_ref[...] = near_ref[here] + got_ref[here].astype(F32)
    for step, ref in zip(STEPS[1:], send_refs):
        to = lax.rem(here + step, chips)
        ref[...] = (near_ref[to] + got_ref[to].astype(F32)).astype(BF16)


def fold(near, got):
    shape = near.shape[1:]
    return pl.pallas_call(
        fold_kernel,
        out_shape=(jax.ShapeDtypeStruct(shape, F32),) + (jax.ShapeDtypeStruct(shape, BF16),) * 3,
        in_specs=[VMEM_SPEC] * 2,
        out_specs=(VMEM_SPEC,) * 4,
        compiler_params=pltpu.CompilerParams(vmem_limit_bytes=2 * 2**20),
        cost_estimate=QUICK,
        name="fold",
    )(near, got)


def row_halo(ends):
    count = lax.axis_size(SKY)
    up = [(i, i + 1) for i in range(count - 1)]
    down = [(j, i) for i, j in up]
    return lax.ppermute(ends[0], SKY, up), lax.ppermute(ends[1], SKY, down)


def join_kernel(own_ref, far_ref, keep_ref, a_ref, b_ref, c_ref, out_ref):
    pieces, total, outs = out_ref.shape
    chans = own_ref.shape[0] // 3
    size = chans // pieces
    for tap_col in range(3):
        for tap_row in range(3):
            rows = slice(tap_row * chans, (tap_row + 1) * chans)
            lanes = slice(tap_col * outs, (tap_col + 1) * outs)
            value = own_ref[rows, lanes] + far_ref[rows, lanes].astype(F32)
            at = (3 * tap_col + tap_row) * size
            out_ref[:, at : at + size, :] = value.reshape(pieces, size, outs).astype(BF16)
    second = keep_ref[...]
    for ref in (a_ref, b_ref, c_ref):
        second = second + ref[...].astype(F32)
    sx = lax.axis_size("x")
    sz = pieces // sx
    third = second.shape[0] // 3
    size_x = third // sx
    extra = total - 9 * size
    for x in range(sx):
        value = jnp.concatenate(
            [second[tap * third + x * size_x : tap * third + (x + 1) * size_x] for tap in range(3)],
            axis=0,
        )
        for z in range(sz):
            out_ref[z * sx + x, 9 * size :, :] = value[z * extra : (z + 1) * extra].astype(BF16)


def join(own, far, keep, got, pieces):
    outs = keep.shape[1]
    rows = 9 * (own.shape[0] // 3 // pieces) + keep.shape[0] // pieces
    return pl.pallas_call(
        join_kernel,
        out_shape=jax.ShapeDtypeStruct((pieces, rows, outs), BF16),
        in_specs=[VMEM_SPEC] * 6,
        out_specs=VMEM_SPEC,
        compiler_params=pltpu.CompilerParams(vmem_limit_bytes=4 * 2**20),
        cost_estimate=QUICK,
        name="join",
    )(own, far, keep, *got)


STEPS = (0, 1, 3, 2)


def order_kernel(extra, a_ref, b_ref, c_ref, d_ref, out_ref):
    rows = a_ref.shape[0] - extra
    sz = lax.axis_size("z")
    me = lax.axis_index("z")
    values = [ref[...].astype(F32) for ref in (a_ref, b_ref, c_ref, d_ref)]
    rest = []
    for z in range(len(STEPS)):
        value = values[0]
        for step, other in zip(STEPS[1:], values[1:]):
            value = jnp.where(lax.rem(me + sz - step, sz) == z, other, value)
        out_ref[z * rows : (z + 1) * rows, :] = value[:rows].astype(BF16)
        rest.append(value[rows:])
    out_ref[len(STEPS) * rows :, :] = jnp.concatenate(rest, axis=0).astype(BF16)


def order_pieces(parts, extra):
    rows, outs = parts[0].shape
    return pl.pallas_call(
        functools.partial(order_kernel, extra),
        out_shape=jax.ShapeDtypeStruct((4 * rows, outs), BF16),
        in_specs=[VMEM_SPEC] * 4,
        out_specs=VMEM_SPEC,
        compiler_params=pltpu.CompilerParams(vmem_limit_bytes=4 * 2**20),
        cost_estimate=QUICK,
        name="order_pieces",
    )(*parts)


def first_kernel(sz, a_ref, b_ref, c_ref, d_ref, out_ref):
    sx = lax.axis_size("x")
    size = out_ref.shape[2] // (sx * sz)
    me = lax.axis_index("x")
    for step, ref in zip(STEPS, (a_ref, b_ref, c_ref, d_ref)):
        x = lax.rem(me + sx - step, sx)
        value = ref[...].astype(F32)
        for z in range(sz):
            at = pl.multiple_of((z * sx + x) * size, size)
            for tap in range(9):
                rows = (z * 9 + tap) * size
                out_ref[tap // 3, tap % 3, pl.ds(at, size), :] = value[rows : rows + size]


def lay_first(parts, sz, chans):
    outs = parts[0].shape[1]
    return pl.pallas_call(
        functools.partial(first_kernel, sz),
        out_shape=jax.ShapeDtypeStruct((3, 3, chans, outs), F32),
        in_specs=[VMEM_SPEC] * 4,
        out_specs=VMEM_SPEC,
        compiler_params=pltpu.CompilerParams(vmem_limit_bytes=4 * 2**20),
        cost_estimate=QUICK,
        name="lay_first",
    )(*parts)


def sum_kernel(in_ref, out_ref):
    total = in_ref[0].astype(F32)
    for i in range(1, in_ref.shape[0]):
        total = total + in_ref[i].astype(F32)
    out_ref[...] = total.astype(BF16)


def sum_pieces(pieces):
    return pl.pallas_call(
        sum_kernel,
        out_shape=jax.ShapeDtypeStruct(pieces.shape[1:], BF16),
        in_specs=[VMEM_SPEC],
        out_specs=VMEM_SPEC,
        compiler_params=pltpu.CompilerParams(vmem_limit_bytes=4 * 2**20),
        cost_estimate=QUICK,
        name="sum_pieces",
    )(pieces)


def pick_kernel(first, a_ref, b_ref, c_ref, d_ref, out_ref):
    for i, ref in enumerate((a_ref, b_ref, c_ref, d_ref)):
        out_ref[i] = ref[first:, :]


def pick_rows(parts, first):
    rows, outs = parts[0].shape
    return pl.pallas_call(
        functools.partial(pick_kernel, first),
        out_shape=jax.ShapeDtypeStruct((len(parts), rows - first, outs), BF16),
        in_specs=[VMEM_SPEC] * 4,
        out_specs=VMEM_SPEC,
        compiler_params=pltpu.CompilerParams(vmem_limit_bytes=2 * 2**20),
        cost_estimate=QUICK,
        name="pick_rows",
    )(*parts)


def lay_second_kernel(other, in_ref, *refs):
    out_ref, half_ref, sems = refs[-3:]
    sy, sx, rows, _ = in_ref.shape
    size = rows // 3
    third = half_ref.shape[0] // 3
    core, y, x = lax.axis_index("c"), lax.axis_index("y"), lax.axis_index("x")
    half = 1 - core if other else core
    copies = []
    for tap in range(3):
        for i in range(sy):
            for j in range(sx):
                place = lax.rem(y + sy - STEPS[i], sy) * sx + lax.rem(x + sx - STEPS[j], sx)
                at = pl.multiple_of(tap * third + place * size, 8)
                value = in_ref[i, j, tap * size : (tap + 1) * size, :].astype(F32)
                half_ref[pl.ds(at, size), :] = value
        to = pl.multiple_of((2 * tap + half) * third, 8)
        copy = pltpu.make_async_copy(
            half_ref.at[tap * third : (tap + 1) * third],
            out_ref.at[pl.ds(to, third)],
            sems.at[tap],
        )
        copy.start()
        copies.append(copy)
    for copy in copies:
        copy.wait()


def lay_second(half, whole=None):
    sy, sx, rows, outs = half.shape
    size = sy * sx * rows
    anywhere = pl.BlockSpec(memory_space=pl.ANY)
    given = [] if whole is None else [whole]
    return pl.pallas_call(
        functools.partial(lay_second_kernel, whole is not None),
        out_shape=jax.ShapeDtypeStruct((2 * size, outs), F32),
        in_specs=[VMEM_SPEC] + [anywhere] * len(given),
        out_specs=anywhere,
        scratch_shapes=[pltpu.VMEM((size, outs), F32), pltpu.SemaphoreType.DMA((3,))],
        compiler_params=pltpu.CompilerParams(vmem_limit_bytes=4 * 2**20),
        cost_estimate=QUICK,
        input_output_aliases={1: 0} if given else {},
        name="lay_second",
    )(half, *given)


def gather_steps(piece, axis):
    return [piece] + [shift(piece, axis, step) for step in STEPS[1:]]


def body(sky_cube, weight_first, weight_second, cotangent):
    cols, rows, chans = sky_cube.shape
    strip, _, outs = cotangent.shape
    chips = lax.axis_size("y")

    ends = [
        jnp.concatenate(
            [sky_cube[:, r], cotangent[:, r, : outs // 2], cotangent[:, r, outs // 2 :]], axis=0
        )
        for r in (rows - 1, 0)
    ]
    edges = jnp.stack(row_halo(ends))
    far_cube = shift(sky_cube, "c", 1)
    far_weight = shift(weight_first, "c", 1)
    far_edges = shift(edges, "c", 1)
    wide = spread(sky_cube, far_cube, edges, far_edges, chips)
    kernel = jnp.concatenate([weight_first, far_weight], axis=2).reshape(18 * chans, outs)

    def side(col):
        beside = [
            jnp.concatenate(
                [edges[k, at + col : at + col + 1] for at in (cols, cols + strip)], axis=1
            )
            for k in range(2)
        ]
        return jnp.concatenate([cotangent[col]] + beside, axis=0)

    count = lax.axis_size(FREQ)
    up = [(i, i + 1) for i in range(count - 1)]
    down = [(j, i) for i, j in up]
    left = lax.ppermute(side(strip - 1), FREQ, up)
    right = lax.ppermute(side(0), FREQ, down)

    on, off = 1, chips - 1
    cut = strip // 2 + 1
    far_a, far_b = conv_parts(((2, 0), (2, cut)), wide, kernel, cut, BF16)
    hold, _ = lax.optimization_barrier((wide, far_a))
    near_b, near_a = conv_parts(((on, cut), (off, 0)), hold, kernel, cut, BF16)
    got_a, got_b = shift(far_a, "y", on), shift(far_b, "y", off)
    got_a, left, right = lax.optimization_barrier((got_a, left, right))
    both_a, both_b = conv_parts(((on, 0), (off, cut)), wide, kernel, cut, BF16, (got_a, got_b))
    own = conv_parts(((0, 0),), wide, kernel, strip + 2, F32)[0]
    from_a = shift(both_a, "y", on), shift(near_a, "y", off)
    from_b = shift(near_b, "y", on), shift(both_b, "y", off)

    back, wide_cotangent = back_tile(cotangent, left, right, edges, weight_second)
    delta, hidden, *ends = point(own, from_a, from_b, back)

    from_on, from_off = shift(delta, "y", on), shift(delta, "y", off)
    half = strip // 2
    total = grad_strip(0, wide, (delta,), None, False)
    from_on, from_off, total = lax.optimization_barrier((from_on, from_off, total))
    fwd_a, fwd_b = shift(from_on[:half], "y", on), shift(from_off[half:], "y", off)
    near, far = second_tile(hidden, wide_cotangent, chips)
    keep, *sends = fold(near, shift(far, "c", 1))
    got = [shift(send, "y", step) for step, send in zip(STEPS[1:], sends)]
    total = grad_strip(off, wide, (from_on,), total, False)
    total = grad_strip(on, wide, (from_off,), total, False)
    first_own, first_far = grad_strip(2, wide, (fwd_a, fwd_b), total, True)

    sx, sz = lax.axis_size("x"), lax.axis_size("z")
    first_far, ends, *got = lax.optimization_barrier((first_far, ends, *got))
    far, *edges = lax.optimization_barrier((shift(first_far, "c", 1), *row_halo(ends)))
    joined = join(first_own, far, keep, got, sx * sz)
    extra = keep.shape[0] // (sx * sz)
    summed = lax.all_to_all(joined, SKY, 0, 0, tiled=True)
    summed = sum_pieces(summed)
    parts = gather_steps(order_pieces(gather_steps(summed, "z"), extra), "x")
    main = parts[0].shape[0] - sz * extra
    grad_first = lay_first(parts, sz, chans)
    share = pick_rows(parts, main)
    share, *edges = lax.optimization_barrier((share, *edges))
    features = features_tile(hidden, edges, weight_second)
    share, grad_first, features = lax.optimization_barrier(
        (jnp.stack(gather_steps(share, "y")), grad_first, features)
    )
    grad_second = lay_second(shift(share, "c", 1), lay_second(share))
    grad_second = grad_second.reshape(3, 3, outs, outs)
    return features, grad_first, grad_second


def solution(mesh):
    sizes = (mesh.devices.shape[0] // 2, 2, 4, mesh.devices.shape[1] // 4)
    fine = Mesh(mesh.devices.reshape(sizes), FREQ + SKY)
    return jax.shard_map(
        body,
        mesh=fine,
        in_specs=(P(None, SKY, FREQ), P(None, None, FREQ, None), P(), P(FREQ, SKY, None)),
        out_specs=(P(FREQ, SKY, None), P(None, None, FREQ, None), P()),
        check_vma=False,
    )
```

```python
import functools

import jax
import jax.numpy as jnp
from jax import lax
from jax.experimental import pallas as pl
from jax.experimental.pallas import tpu as pltpu
from jax.sharding import Mesh, PartitionSpec as P

FREQ = ("y", "c")
SKY = ("z", "x")
F32 = jnp.float32
BF16 = jnp.bfloat16
QUICK = pl.CostEstimate(flops=1, bytes_accessed=1, transcendentals=0)


def shift(x, axis, step):
    count = lax.axis_size(axis)
    return lax.ppermute(x, axis, [(i, (i + step) % count) for i in range(count)])


def spread_kernel(own_ref, far_ref, own_halo_ref, far_halo_ref, out_ref):
    chips, width, rows, depth = out_ref.shape
    cols, _, chans = own_ref.shape
    strip = cols // (2 * chips)
    core = lax.axis_index("c")
    step = 8
    row = lax.broadcasted_iota(jnp.int32, (step, rows, chans), 1)

    def block(i, base, chip):
        for side, (cube_ref, halo_ref) in enumerate(
            ((own_ref, own_halo_ref), (far_ref, far_halo_ref))
        ):
            at = pl.multiple_of(base + i * step, step)
            mid = cube_ref[pl.ds(at, step)]
            wide = mid.astype(F32).reshape(step * rows, chans)
            ahead = pltpu.roll(wide, 1, 0).reshape(step, rows, chans)
            behind = pltpu.roll(wide, step * rows - 1, 0).reshape(step, rows, chans)
            before = halo_ref[0, pl.ds(at, step), :].astype(F32)[:, None, :]
            after = halo_ref[1, pl.ds(at, step), :].astype(F32)[:, None, :]
            ahead = jnp.where(row == 0, before, ahead)
            behind = jnp.where(row == rows - 1, after, behind)
            to = pl.ds(2 + i * step, step)
            for tap, value in enumerate((ahead.astype(BF16), mid, behind.astype(BF16))):
                lane = (2 * tap + side) * chans
                out_ref[chip, to, :, lane : lane + chans] = value

    def edge(at, chip, slot):
        for side, (cube_ref, halo_ref) in enumerate(
            ((own_ref, own_halo_ref), (far_ref, far_halo_ref))
        ):
            first = pl.multiple_of((at // step) * step, step)
            mid = cube_ref[at]
            wide = mid.astype(F32)
            line = lax.broadcasted_iota(jnp.int32, (step, chans), 0) == at - first
            pick = lambda k: jnp.sum(
                jnp.where(line, halo_ref[k, pl.ds(first, step), :].astype(F32), 0.0),
                axis=0,
                keepdims=True,
            )
            place = lax.broadcasted_iota(jnp.int32, (rows, chans), 0)
            ahead = jnp.where(place == 0, pick(0), pltpu.roll(wide, 1, 0))
            behind = jnp.where(place == rows - 1, pick(1), pltpu.roll(wide, rows - 1, 0))
            for tap, value in enumerate((ahead.astype(BF16), mid, behind.astype(BF16))):
                lane = (2 * tap + side) * chans
                out_ref[chip, slot, :, lane : lane + chans] = value

    blank = jnp.zeros((rows, depth), BF16)
    for chip in range(chips):
        base = (2 * chip + core) * strip
        lax.fori_loop(0, strip // step, lambda i, _: block(i, base, chip), None)
        for slot in (0, 1):
            edge(jnp.maximum(base - 2 + slot, 0), chip, slot)
            edge(jnp.minimum(base + strip + slot, cols - 1), chip, strip + 2 + slot)
        for slot in range(strip + 4, width):
            out_ref[chip, slot] = blank

    @pl.when(core == 0)
    def _():
        out_ref[0, 0] = blank
        out_ref[0, 1] = blank

    @pl.when(core == 1)
    def _():
        out_ref[chips - 1, strip + 2] = blank
        out_ref[chips - 1, strip + 3] = blank


VMEM_SPEC = pl.BlockSpec(memory_space=pltpu.VMEM)


def spread(own, far, own_halo, far_halo, chips):
    cols, rows, chans = own.shape
    return pl.pallas_call(
        spread_kernel,
        out_shape=jax.ShapeDtypeStruct((chips, cols // (2 * chips) + 8, rows, 6 * chans), BF16),
        in_specs=[VMEM_SPEC] * 4,
        out_specs=VMEM_SPEC,
        compiler_params=pltpu.CompilerParams(vmem_limit_bytes=2 * 2**20),
        cost_estimate=QUICK,
        name="spread",
    )(own, far, own_halo, far_halo)


def chip_at(step):
    return lax.rem(lax.axis_index("y") + step, lax.axis_size("y"))


def conv_kernel(parts, adds, wide_ref, kernel_ref, *refs):
    rows = wide_ref.shape[2]
    for (step, first), add_ref, out_ref in zip(parts, refs[:adds] or [None] * len(parts), refs[adds:]):
        count, _, outs = out_ref.shape
        chip = chip_at(step)
        pieces = [wide_ref[chip, first + tap : first + tap + count] for tap in range(3)]
        lhs = jnp.concatenate(pieces, axis=-1).reshape(count * rows, -1)
        total = jnp.dot(lhs, kernel_ref[...], preferred_element_type=F32)
        total = total.reshape(count, rows, outs)
        if add_ref is not None:
            total = total + add_ref[...].astype(F32)
        out_ref[...] = total.astype(out_ref.dtype)


def conv_parts(parts, wide, kernel, count, dtype, adds=()):
    rows, outs = wide.shape[2], kernel.shape[1]
    return pl.pallas_call(
        functools.partial(conv_kernel, parts, len(adds)),
        out_shape=(jax.ShapeDtypeStruct((count, rows, outs), dtype),) * len(parts),
        in_specs=[VMEM_SPEC] * (2 + len(adds)),
        out_specs=(VMEM_SPEC,) * len(parts),
        compiler_params=pltpu.CompilerParams(vmem_limit_bytes=4 * 2**20),
        cost_estimate=QUICK,
        name="conv_first",
    )(wide, kernel, *adds)


def grad_kernel(step, pieces, has_old, last, wide_ref, *refs):
    piece_refs, refs = refs[:pieces], refs[pieces:]
    old_ref = refs[0] if has_old else None
    outs_refs, pad_ref = refs[1 if has_old else 0 : -1], refs[-1]
    count, rows, outs = piece_refs[0].shape
    strip = pieces * count
    cols, depth = wide_ref.shape[1], wide_ref.shape[3]
    pad_ref[0:3] = jnp.zeros((3, rows, outs), BF16)
    for i, ref in enumerate(piece_refs):
        pad_ref[3 + i * count : 3 + (i + 1) * count] = ref[...]
    pad_ref[3 + strip :] = jnp.zeros((cols - strip - 1, rows, outs), BF16)
    lhs = wide_ref[chip_at(step)].reshape(cols * rows, depth)
    rhs = jnp.concatenate(
        [pad_ref[2 - tap : 2 - tap + cols].reshape(cols * rows, outs) for tap in range(3)], axis=-1
    )
    total = lax.dot_general(lhs, rhs, (((0,), (0,)), ((), ())), preferred_element_type=F32)
    if has_old:
        total = total + old_ref[...]
    if not last:
        outs_refs[0][...] = total
    else:
        chans = depth // 6
        for tap in range(3):
            at = 2 * tap * chans
            outs_refs[0][tap * chans : (tap + 1) * chans] = total[at : at + chans]
            outs_refs[1][tap * chans : (tap + 1) * chans] = total[
                at + chans : at + 2 * chans
            ].astype(BF16)


def grad_strip(step, wide, pieces, old, last):
    _, rows, outs = pieces[0].shape
    depth, cols = wide.shape[3], wide.shape[1]
    shape = (depth, 3 * outs)
    half = (depth // 2, 3 * outs)
    if last:
        out_shape = (jax.ShapeDtypeStruct(half, F32), jax.ShapeDtypeStruct(half, BF16))
    else:
        out_shape = (jax.ShapeDtypeStruct(shape, F32),)
    args = [wide, *pieces] + ([old] if old is not None else [])
    out = pl.pallas_call(
        functools.partial(grad_kernel, step, len(pieces), old is not None, last),
        out_shape=out_shape,
        in_specs=[VMEM_SPEC] * len(args),
        out_specs=tuple([VMEM_SPEC] * len(out_shape)),
        scratch_shapes=[pltpu.VMEM((cols + 2, rows, outs), BF16)],
        compiler_params=pltpu.CompilerParams(vmem_limit_bytes=5 * 2**20),
        cost_estimate=QUICK,
        name="grad_first",
    )(*args)
    return out if last else out[0]


def spread_tile(columns, wide_ref):
    rows, chans = wide_ref.shape[1], wide_ref.shape[2] // 3
    place = lax.broadcasted_iota(jnp.int32, (rows, chans), 0)
    for j, (mid, before, after) in enumerate(columns):
        wide = mid.astype(F32)
        ahead = jnp.where(place == 0, before.astype(F32), pltpu.roll(wide, 1, 0))
        behind = jnp.where(place == rows - 1, after.astype(F32), pltpu.roll(wide, rows - 1, 0))
        wide_ref[j, :, 0:chans] = ahead.astype(BF16)
        wide_ref[j, :, chans : 2 * chans] = mid
        wide_ref[j, :, 2 * chans :] = behind.astype(BF16)


def back_kernel(cot_ref, left_ref, right_ref, edge_ref, kernel_ref, out_ref, wide_ref):
    cols, rows, chans = cot_ref.shape
    start = edge_ref.shape[1] - 2 * cols

    def beside(k, j):
        low, high = start + j, start + cols + j
        return jnp.concatenate(
            [edge_ref[k, low : low + 1, :], edge_ref[k, high : high + 1, :]], axis=-1
        )

    def whole(ref):
        return ref[0:rows], ref[rows : rows + 1], ref[rows + 1 : rows + 2]

    columns = [(cot_ref[j], beside(0, j), beside(1, j)) for j in range(cols)]
    spread_tile([whole(left_ref)] + columns + [whole(right_ref)], wide_ref)
    total = None
    for tap_col in range(3):
        lhs = wide_ref[tap_col : tap_col + cols].reshape(cols * rows, 3 * chans)
        for tap_row in range(3):
            part = lax.dot_general(
                lhs[:, tap_row * chans : (tap_row + 1) * chans],
                kernel_ref[2 - tap_col, 2 - tap_row],
                (((1,), (1,)), ((), ())),
                preferred_element_type=F32,
            )
            total = part if total is None else total + part
    out_ref[...] = total.reshape(cols, rows, -1)


def back_tile(tile, left, right, edges, kernel):
    cols, rows, chans = tile.shape
    return pl.pallas_call(
        back_kernel,
        out_shape=(
            jax.ShapeDtypeStruct((cols, rows, kernel.shape[2]), F32),
            jax.ShapeDtypeStruct((cols + 2, rows, 3 * chans), BF16),
        ),
        in_specs=[VMEM_SPEC] * 5,
        out_specs=(VMEM_SPEC,) * 2,
        compiler_params=pltpu.CompilerParams(vmem_limit_bytes=4 * 2**20),
        cost_estimate=QUICK,
        name="back",
    )(tile, left, right, edges, kernel)


def second_kernel(chips, hid_ref, wide_ref, near_ref, far_ref, sum_ref):
    chans = hid_ref.shape[2]
    cols, rows, outs = hid_ref.shape[0] - 2, hid_ref.shape[1], wide_ref.shape[2] // 3
    core = lax.axis_index("c")
    lhs = hid_ref[1 : cols + 1].reshape(cols * rows, chans)
    for tap_col in range(3):
        rhs = wide_ref[2 - tap_col : 2 - tap_col + cols].reshape(cols * rows, 3 * outs)
        part = lax.dot_general(lhs, rhs, (((0,), (0,)), ((), ())), preferred_element_type=F32)
        for tap_row in range(3):
            sum_ref[
                tap_row * chans : (tap_row + 1) * chans, tap_col * outs : (tap_col + 1) * outs
            ] = part[:, (2 - tap_row) * outs : (3 - tap_row) * outs]
    size = sum_ref.shape[0] // (2 * chips)
    for half, ref in ((core, near_ref), (1 - core, far_ref)):
        for chip in range(chips):
            at = pl.multiple_of((half * chips + chip) * size, size)
            for tap in range(3):
                ref[chip, tap * size : (tap + 1) * size, :] = sum_ref[
                    pl.ds(at, size), tap * outs : (tap + 1) * outs
                ].astype(ref.dtype)


def second_tile(tile, wide, chips):
    chans, outs = tile.shape[2], wide.shape[2] // 3
    cut = (chips, 9 * chans // (2 * chips), outs)
    return pl.pallas_call(
        functools.partial(second_kernel, chips),
        out_shape=(jax.ShapeDtypeStruct(cut, F32), jax.ShapeDtypeStruct(cut, BF16)),
        in_specs=[VMEM_SPEC] * 2,
        out_specs=(VMEM_SPEC,) * 2,
        scratch_shapes=[pltpu.VMEM((3 * chans, 3 * outs), F32)],
        compiler_params=pltpu.CompilerParams(vmem_limit_bytes=9 * 2**20),
        cost_estimate=QUICK,
        name="second",
    )(tile, wide)


def features_kernel(hid_ref, before_ref, after_ref, kernel_ref, out_ref, wide_ref):
    cols, rows, outs = out_ref.shape
    columns = [
        (hid_ref[j], before_ref[j : j + 1, :], after_ref[j : j + 1, :]) for j in range(cols + 2)
    ]
    spread_tile(columns, wide_ref)
    pieces = [wide_ref[tap : tap + cols] for tap in range(3)]
    lhs = jnp.concatenate(pieces, axis=-1).reshape(cols * rows, -1)
    total = jnp.dot(lhs, kernel_ref[...], preferred_element_type=F32)
    out_ref[...] = total.reshape(cols, rows, outs).astype(BF16)


def features_tile(tile, edges, kernel):
    cols, rows, chans = tile.shape
    outs = kernel.shape[3]
    return pl.pallas_call(
        features_kernel,
        out_shape=jax.ShapeDtypeStruct((cols - 2, rows, outs), BF16),
        in_specs=[VMEM_SPEC] * 4,
        out_specs=VMEM_SPEC,
        scratch_shapes=[pltpu.VMEM((cols, rows, 3 * chans), BF16)],
        compiler_params=pltpu.CompilerParams(vmem_limit_bytes=9 * 2**20),
        cost_estimate=QUICK,
        name="features",
    )(tile, *edges, kernel.reshape(-1, outs))


def point_kernel(
    own_ref, a0_ref, a1_ref, b0_ref, b1_ref, back_ref,
    delta_ref, hidden_ref, last_ref, first_ref,
):
    cols, rows, _ = own_ref.shape
    half = delta_ref.shape[0] // 2
    strip = 2 * lax.axis_index("y") + lax.axis_index("c")
    strips = 2 * lax.axis_size("y")

    def column(j, i, refs, keep):
        pre = own_ref[j] + refs[0][i].astype(F32) + refs[1][i].astype(F32)
        sigma = jax.nn.sigmoid(pre)
        hidden = pre * sigma
        if keep is not None:
            hidden = jnp.where(keep, hidden, 0.0)
        hidden = hidden.astype(BF16)
        hidden_ref[j] = hidden
        last_ref[j : j + 1, :] = hidden[rows - 1 :]
        first_ref[j : j + 1, :] = hidden[:1]
        if keep is None:
            slope = sigma * (1.0 + pre * (1.0 - sigma))
            delta_ref[j - 1] = (back_ref[j - 1] * slope).astype(BF16)

    left, right = (a0_ref, a1_ref), (b0_ref, b1_ref)
    column(0, 0, left, strip > 0)
    column(cols - 1, half, right, strip < strips - 1)

    for i in range(1, half + 1):
        column(i, i, left, None)
        column(half + i, i - 1, right, None)


def point(own, left, right, back):
    strip, rows, outs = back.shape
    delta = jax.ShapeDtypeStruct(back.shape, BF16)
    edge = jax.ShapeDtypeStruct((strip + 2, outs), BF16)
    return pl.pallas_call(
        point_kernel,
        out_shape=(delta, jax.ShapeDtypeStruct(own.shape, BF16), edge, edge),
        in_specs=[VMEM_SPEC] * 6,
        out_specs=(VMEM_SPEC,) * 4,
        compiler_params=pltpu.CompilerParams(vmem_limit_bytes=2 * 2**20),
        cost_estimate=QUICK,
        name="point",
    )(own, *left, *right, back)


def fold_kernel(near_ref, got_ref, keep_ref, *send_refs):
    chips = near_ref.shape[0]
    here = lax.axis_index("y")
    keep_ref[...] = near_ref[here] + got_ref[here].astype(F32)
    for step, ref in zip(STEPS[1:], send_refs):
        to = lax.rem(here + step, chips)
        ref[...] = (near_ref[to] + got_ref[to].astype(F32)).astype(BF16)


def fold(near, got):
    shape = near.shape[1:]
    return pl.pallas_call(
        fold_kernel,
        out_shape=(jax.ShapeDtypeStruct(shape, F32),) + (jax.ShapeDtypeStruct(shape, BF16),) * 3,
        in_specs=[VMEM_SPEC] * 2,
        out_specs=(VMEM_SPEC,) * 4,
        compiler_params=pltpu.CompilerParams(vmem_limit_bytes=2 * 2**20),
        cost_estimate=QUICK,
        name="fold",
    )(near, got)


def row_halo(ends):
    count = lax.axis_size(SKY)
    up = [(i, i + 1) for i in range(count - 1)]
    down = [(j, i) for i, j in up]
    return lax.ppermute(ends[0], SKY, up), lax.ppermute(ends[1], SKY, down)


def join_kernel(own_ref, far_ref, keep_ref, a_ref, b_ref, c_ref, out_ref):
    pieces, total, outs = out_ref.shape
    chans = own_ref.shape[0] // 3
    size = chans // pieces
    for tap_col in range(3):
        for tap_row in range(3):
            rows = slice(tap_row * chans, (tap_row + 1) * chans)
            lanes = slice(tap_col * outs, (tap_col + 1) * outs)
            value = own_ref[rows, lanes] + far_ref[rows, lanes].astype(F32)
            at = (3 * tap_col + tap_row) * size
            out_ref[:, at : at + size, :] = value.reshape(pieces, size, outs).astype(BF16)
    second = keep_ref[...]
    for ref in (a_ref, b_ref, c_ref):
        second = second + ref[...].astype(F32)
    sx = lax.axis_size("x")
    sz = pieces // sx
    third = second.shape[0] // 3
    size_x = third // sx
    extra = total - 9 * size
    for x in range(sx):
        value = jnp.concatenate(
            [second[tap * third + x * size_x : tap * third + (x + 1) * size_x] for tap in range(3)],
            axis=0,
        )
        for z in range(sz):
            out_ref[z * sx + x, 9 * size :, :] = value[z * extra : (z + 1) * extra].astype(BF16)


def join(own, far, keep, got, pieces):
    outs = keep.shape[1]
    rows = 9 * (own.shape[0] // 3 // pieces) + keep.shape[0] // pieces
    return pl.pallas_call(
        join_kernel,
        out_shape=jax.ShapeDtypeStruct((pieces, rows, outs), BF16),
        in_specs=[VMEM_SPEC] * 6,
        out_specs=VMEM_SPEC,
        compiler_params=pltpu.CompilerParams(vmem_limit_bytes=4 * 2**20),
        cost_estimate=QUICK,
        name="join",
    )(own, far, keep, *got)


STEPS = (0, 1, 3, 2)


def order_kernel(extra, a_ref, b_ref, c_ref, d_ref, out_ref):
    rows = a_ref.shape[0] - extra
    sz = lax.axis_size("z")
    me = lax.axis_index("z")
    values = [ref[...].astype(F32) for ref in (a_ref, b_ref, c_ref, d_ref)]
    rest = []
    for z in range(len(STEPS)):
        value = values[0]
        for step, other in zip(STEPS[1:], values[1:]):
            value = jnp.where(lax.rem(me + sz - step, sz) == z, other, value)
        out_ref[z * rows : (z + 1) * rows, :] = value[:rows].astype(BF16)
        rest.append(value[rows:])
    out_ref[len(STEPS) * rows :, :] = jnp.concatenate(rest, axis=0).astype(BF16)


def order_pieces(parts, extra):
    rows, outs = parts[0].shape
    return pl.pallas_call(
        functools.partial(order_kernel, extra),
        out_shape=jax.ShapeDtypeStruct((4 * rows, outs), BF16),
        in_specs=[VMEM_SPEC] * 4,
        out_specs=VMEM_SPEC,
        compiler_params=pltpu.CompilerParams(vmem_limit_bytes=4 * 2**20),
        cost_estimate=QUICK,
        name="order_pieces",
    )(*parts)


def first_kernel(sz, a_ref, b_ref, c_ref, d_ref, out_ref):
    sx = lax.axis_size("x")
    size = out_ref.shape[2] // (sx * sz)
    me = lax.axis_index("x")
    for step, ref in zip(STEPS, (a_ref, b_ref, c_ref, d_ref)):
        x = lax.rem(me + sx - step, sx)
        value = ref[...].astype(F32)
        for z in range(sz):
            at = pl.multiple_of((z * sx + x) * size, size)
            for tap in range(9):
                rows = (z * 9 + tap) * size
                out_ref[tap // 3, tap % 3, pl.ds(at, size), :] = value[rows : rows + size]


def lay_first(parts, sz, chans):
    outs = parts[0].shape[1]
    return pl.pallas_call(
        functools.partial(first_kernel, sz),
        out_shape=jax.ShapeDtypeStruct((3, 3, chans, outs), F32),
        in_specs=[VMEM_SPEC] * 4,
        out_specs=VMEM_SPEC,
        compiler_params=pltpu.CompilerParams(vmem_limit_bytes=4 * 2**20),
        cost_estimate=QUICK,
        name="lay_first",
    )(*parts)


def sum_kernel(in_ref, out_ref):
    total = in_ref[0].astype(F32)
    for i in range(1, in_ref.shape[0]):
        total = total + in_ref[i].astype(F32)
    out_ref[...] = total.astype(BF16)


def sum_pieces(pieces):
    return pl.pallas_call(
        sum_kernel,
        out_shape=jax.ShapeDtypeStruct(pieces.shape[1:], BF16),
        in_specs=[VMEM_SPEC],
        out_specs=VMEM_SPEC,
        compiler_params=pltpu.CompilerParams(vmem_limit_bytes=4 * 2**20),
        cost_estimate=QUICK,
        name="sum_pieces",
    )(pieces)


def pick_kernel(first, a_ref, b_ref, c_ref, d_ref, out_ref):
    for i, ref in enumerate((a_ref, b_ref, c_ref, d_ref)):
        out_ref[i] = ref[first:, :]


def pick_rows(parts, first):
    rows, outs = parts[0].shape
    return pl.pallas_call(
        functools.partial(pick_kernel, first),
        out_shape=jax.ShapeDtypeStruct((len(parts), rows - first, outs), BF16),
        in_specs=[VMEM_SPEC] * 4,
        out_specs=VMEM_SPEC,
        compiler_params=pltpu.CompilerParams(vmem_limit_bytes=2 * 2**20),
        cost_estimate=QUICK,
        name="pick_rows",
    )(*parts)


def lay_second_kernel(other, in_ref, *refs):
    out_ref, half_ref, sems = refs[-3:]
    sy, sx, rows, _ = in_ref.shape
    size = rows // 3
    third = half_ref.shape[0] // 3
    core, y, x = lax.axis_index("c"), lax.axis_index("y"), lax.axis_index("x")
    half = 1 - core if other else core
    copies = []
    for tap in range(3):
        for i in range(sy):
            for j in range(sx):
                place = lax.rem(y + sy - STEPS[i], sy) * sx + lax.rem(x + sx - STEPS[j], sx)
                at = pl.multiple_of(tap * third + place * size, 8)
                value = in_ref[i, j, tap * size : (tap + 1) * size, :].astype(F32)
                half_ref[pl.ds(at, size), :] = value
        to = pl.multiple_of((2 * tap + half) * third, 8)
        copy = pltpu.make_async_copy(
            half_ref.at[tap * third : (tap + 1) * third],
            out_ref.at[pl.ds(to, third)],
            sems.at[tap],
        )
        copy.start()
        copies.append(copy)
    for copy in copies:
        copy.wait()


def lay_second(half, whole=None):
    sy, sx, rows, outs = half.shape
    size = sy * sx * rows
    anywhere = pl.BlockSpec(memory_space=pl.ANY)
    given = [] if whole is None else [whole]
    return pl.pallas_call(
        functools.partial(lay_second_kernel, whole is not None),
        out_shape=jax.ShapeDtypeStruct((2 * size, outs), F32),
        in_specs=[VMEM_SPEC] + [anywhere] * len(given),
        out_specs=anywhere,
        scratch_shapes=[pltpu.VMEM((size, outs), F32), pltpu.SemaphoreType.DMA((3,))],
        compiler_params=pltpu.CompilerParams(vmem_limit_bytes=4 * 2**20),
        cost_estimate=QUICK,
        input_output_aliases={1: 0} if given else {},
        name="lay_second",
    )(half, *given)


def gather_steps(piece, axis):
    return [piece] + [shift(piece, axis, step) for step in STEPS[1:]]


def body(sky_cube, weight_first, weight_second, cotangent):
    cols, rows, chans = sky_cube.shape
    strip, _, outs = cotangent.shape
    chips = lax.axis_size("y")

    ends = [
        jnp.concatenate(
            [sky_cube[:, r], cotangent[:, r, : outs // 2], cotangent[:, r, outs // 2 :]], axis=0
        )
        for r in (rows - 1, 0)
    ]
    edges = jnp.stack(row_halo(ends))
    far_cube = shift(sky_cube, "c", 1)
    far_weight = shift(weight_first, "c", 1)
    far_edges = shift(edges, "c", 1)
    wide = spread(sky_cube, far_cube, edges, far_edges, chips)
    kernel = jnp.concatenate([weight_first, far_weight], axis=2).reshape(18 * chans, outs)

    def side(col):
        beside = [
            jnp.concatenate(
                [edges[k, at + col : at + col + 1] for at in (cols, cols + strip)], axis=1
            )
            for k in range(2)
        ]
        return jnp.concatenate([cotangent[col]] + beside, axis=0)

    count = lax.axis_size(FREQ)
    up = [(i, i + 1) for i in range(count - 1)]
    down = [(j, i) for i, j in up]
    left = lax.ppermute(side(strip - 1), FREQ, up)
    right = lax.ppermute(side(0), FREQ, down)

    on, off = 1, chips - 1
    cut = strip // 2 + 1
    far_a, far_b = conv_parts(((2, 0), (2, cut)), wide, kernel, cut, BF16)
    hold, _ = lax.optimization_barrier((wide, far_a))
    near_b, near_a = conv_parts(((on, cut), (off, 0)), hold, kernel, cut, BF16)
    got_a, got_b = shift(far_a, "y", on), shift(far_b, "y", off)
    got_a, left, right = lax.optimization_barrier((got_a, left, right))
    both_a, both_b = conv_parts(((on, 0), (off, cut)), wide, kernel, cut, BF16, (got_a, got_b))
    own = conv_parts(((0, 0),), wide, kernel, strip + 2, F32)[0]
    from_a = shift(both_a, "y", on), shift(near_a, "y", off)
    from_b = shift(near_b, "y", on), shift(both_b, "y", off)

    back, wide_cotangent = back_tile(cotangent, left, right, edges, weight_second)
    delta, hidden, *ends = point(own, from_a, from_b, back)

    from_on, from_off = shift(delta, "y", on), shift(delta, "y", off)
    half = strip // 2
    total = grad_strip(0, wide, (delta,), None, False)
    from_on, from_off, total = lax.optimization_barrier((from_on, from_off, total))
    fwd_a, fwd_b = shift(from_on[:half], "y", on), shift(from_off[half:], "y", off)
    near, far = second_tile(hidden, wide_cotangent, chips)
    keep, *sends = fold(near, shift(far, "c", 1))
    got = [shift(send, "y", step) for step, send in zip(STEPS[1:], sends)]
    total = grad_strip(off, wide, (from_on,), total, False)
    total = grad_strip(on, wide, (from_off,), total, False)
    first_own, first_far = grad_strip(2, wide, (fwd_a, fwd_b), total, True)

    sx, sz = lax.axis_size("x"), lax.axis_size("z")
    first_far, *got = lax.optimization_barrier((first_far, *got))
    joined = join(first_own, shift(first_far, "c", 1), keep, got, sx * sz)
    extra = keep.shape[0] // (sx * sz)
    summed = lax.all_to_all(joined, SKY, 0, 0, tiled=True)
    summed = sum_pieces(summed)
    summed, *ends = lax.optimization_barrier((summed, *ends))
    edges = row_halo(ends)
    *pieces, before, after = lax.optimization_barrier((*gather_steps(summed, "z"), *edges))
    features = features_tile(hidden, (before, after), weight_second)
    parts = gather_steps(order_pieces(pieces, extra), "x")
    main = parts[0].shape[0] - sz * extra
    grad_first = lay_first(parts, sz, chans)
    share = pick_rows(parts, main)
    share, features = lax.optimization_barrier((share, features))
    share, grad_first = lax.optimization_barrier(
        (jnp.stack(gather_steps(share, "y")), grad_first)
    )
    grad_second = lay_second(shift(share, "c", 1), lay_second(share))
    grad_second = grad_second.reshape(3, 3, outs, outs)
    return features, grad_first, grad_second


def solution(mesh):
    sizes = (mesh.devices.shape[0] // 2, 2, 4, mesh.devices.shape[1] // 4)
    fine = Mesh(mesh.devices.reshape(sizes), FREQ + SKY)
    return jax.shard_map(
        body,
        mesh=fine,
        in_specs=(P(None, SKY, FREQ), P(None, None, FREQ, None), P(), P(FREQ, SKY, None)),
        out_specs=(P(FREQ, SKY, None), P(None, None, FREQ, None), P()),
        check_vma=False,
    )
```

```python
import functools

import jax
import jax.numpy as jnp
from jax import lax
from jax.experimental import pallas as pl
from jax.experimental.pallas import tpu as pltpu
from jax.sharding import Mesh, PartitionSpec as P

FREQ = ("y", "c")
SKY = ("z", "x")
F32 = jnp.float32
BF16 = jnp.bfloat16
QUICK = pl.CostEstimate(flops=1, bytes_accessed=1, transcendentals=0)


def shift(x, axis, step):
    count = lax.axis_size(axis)
    return lax.ppermute(x, axis, [(i, (i + step) % count) for i in range(count)])


def spread_kernel(own_ref, far_ref, own_halo_ref, far_halo_ref, out_ref):
    chips, width, rows, depth = out_ref.shape
    cols, _, chans = own_ref.shape
    strip = cols // (2 * chips)
    core = lax.axis_index("c")
    step = 8
    row = lax.broadcasted_iota(jnp.int32, (step, rows, chans), 1)

    def block(i, base, chip):
        for side, (cube_ref, halo_ref) in enumerate(
            ((own_ref, own_halo_ref), (far_ref, far_halo_ref))
        ):
            at = pl.multiple_of(base + i * step, step)
            mid = cube_ref[pl.ds(at, step)]
            wide = mid.astype(F32).reshape(step * rows, chans)
            ahead = pltpu.roll(wide, 1, 0).reshape(step, rows, chans)
            behind = pltpu.roll(wide, step * rows - 1, 0).reshape(step, rows, chans)
            before = halo_ref[0, pl.ds(at, step), :].astype(F32)[:, None, :]
            after = halo_ref[1, pl.ds(at, step), :].astype(F32)[:, None, :]
            ahead = jnp.where(row == 0, before, ahead)
            behind = jnp.where(row == rows - 1, after, behind)
            to = pl.ds(2 + i * step, step)
            for tap, value in enumerate((ahead.astype(BF16), mid, behind.astype(BF16))):
                lane = (2 * tap + side) * chans
                out_ref[chip, to, :, lane : lane + chans] = value

    def edge(at, chip, slot):
        for side, (cube_ref, halo_ref) in enumerate(
            ((own_ref, own_halo_ref), (far_ref, far_halo_ref))
        ):
            first = pl.multiple_of((at // step) * step, step)
            mid = cube_ref[at]
            wide = mid.astype(F32)
            line = lax.broadcasted_iota(jnp.int32, (step, chans), 0) == at - first
            pick = lambda k: jnp.sum(
                jnp.where(line, halo_ref[k, pl.ds(first, step), :].astype(F32), 0.0),
                axis=0,
                keepdims=True,
            )
            place = lax.broadcasted_iota(jnp.int32, (rows, chans), 0)
            ahead = jnp.where(place == 0, pick(0), pltpu.roll(wide, 1, 0))
            behind = jnp.where(place == rows - 1, pick(1), pltpu.roll(wide, rows - 1, 0))
            for tap, value in enumerate((ahead.astype(BF16), mid, behind.astype(BF16))):
                lane = (2 * tap + side) * chans
                out_ref[chip, slot, :, lane : lane + chans] = value

    blank = jnp.zeros((rows, depth), BF16)
    for chip in range(chips):
        base = (2 * chip + core) * strip
        lax.fori_loop(0, strip // step, lambda i, _: block(i, base, chip), None)
        for slot in (0, 1):
            edge(jnp.maximum(base - 2 + slot, 0), chip, slot)
            edge(jnp.minimum(base + strip + slot, cols - 1), chip, strip + 2 + slot)
        for slot in range(strip + 4, width):
            out_ref[chip, slot] = blank

    @pl.when(core == 0)
    def _():
        out_ref[0, 0] = blank
        out_ref[0, 1] = blank

    @pl.when(core == 1)
    def _():
        out_ref[chips - 1, strip + 2] = blank
        out_ref[chips - 1, strip + 3] = blank


VMEM_SPEC = pl.BlockSpec(memory_space=pltpu.VMEM)


def spread(own, far, own_halo, far_halo, chips):
    cols, rows, chans = own.shape
    return pl.pallas_call(
        spread_kernel,
        out_shape=jax.ShapeDtypeStruct((chips, cols // (2 * chips) + 8, rows, 6 * chans), BF16),
        in_specs=[VMEM_SPEC] * 4,
        out_specs=VMEM_SPEC,
        compiler_params=pltpu.CompilerParams(vmem_limit_bytes=2 * 2**20),
        cost_estimate=QUICK,
        name="spread",
    )(own, far, own_halo, far_halo)


def chip_at(step):
    return lax.rem(lax.axis_index("y") + step, lax.axis_size("y"))


def conv_kernel(parts, adds, wide_ref, kernel_ref, *refs):
    rows = wide_ref.shape[2]
    for (step, first), add_ref, out_ref in zip(parts, refs[:adds] or [None] * len(parts), refs[adds:]):
        count, _, outs = out_ref.shape
        chip = chip_at(step)
        pieces = [wide_ref[chip, first + tap : first + tap + count] for tap in range(3)]
        lhs = jnp.concatenate(pieces, axis=-1).reshape(count * rows, -1)
        total = jnp.dot(lhs, kernel_ref[...], preferred_element_type=F32)
        total = total.reshape(count, rows, outs)
        if add_ref is not None:
            total = total + add_ref[...].astype(F32)
        out_ref[...] = total.astype(out_ref.dtype)


def conv_parts(parts, wide, kernel, count, dtype, adds=()):
    rows, outs = wide.shape[2], kernel.shape[1]
    return pl.pallas_call(
        functools.partial(conv_kernel, parts, len(adds)),
        out_shape=(jax.ShapeDtypeStruct((count, rows, outs), dtype),) * len(parts),
        in_specs=[VMEM_SPEC] * (2 + len(adds)),
        out_specs=(VMEM_SPEC,) * len(parts),
        compiler_params=pltpu.CompilerParams(vmem_limit_bytes=4 * 2**20),
        cost_estimate=QUICK,
        name="conv_first",
    )(wide, kernel, *adds)


def grad_kernel(step, pieces, has_old, last, wide_ref, *refs):
    piece_refs, refs = refs[:pieces], refs[pieces:]
    old_ref = refs[0] if has_old else None
    outs_refs, pad_ref = refs[1 if has_old else 0 : -1], refs[-1]
    count, rows, outs = piece_refs[0].shape
    strip = pieces * count
    cols, depth = wide_ref.shape[1], wide_ref.shape[3]
    pad_ref[0:3] = jnp.zeros((3, rows, outs), BF16)
    for i, ref in enumerate(piece_refs):
        pad_ref[3 + i * count : 3 + (i + 1) * count] = ref[...]
    pad_ref[3 + strip :] = jnp.zeros((cols - strip - 1, rows, outs), BF16)
    lhs = wide_ref[chip_at(step)].reshape(cols * rows, depth)
    rhs = jnp.concatenate(
        [pad_ref[2 - tap : 2 - tap + cols].reshape(cols * rows, outs) for tap in range(3)], axis=-1
    )
    total = lax.dot_general(lhs, rhs, (((0,), (0,)), ((), ())), preferred_element_type=F32)
    if has_old:
        total = total + old_ref[...]
    if not last:
        outs_refs[0][...] = total
    else:
        chans = depth // 6
        for tap in range(3):
            at = 2 * tap * chans
            outs_refs[0][tap * chans : (tap + 1) * chans] = total[at : at + chans]
            outs_refs[1][tap * chans : (tap + 1) * chans] = total[
                at + chans : at + 2 * chans
            ].astype(BF16)


def grad_strip(step, wide, pieces, old, last):
    _, rows, outs = pieces[0].shape
    depth, cols = wide.shape[3], wide.shape[1]
    shape = (depth, 3 * outs)
    half = (depth // 2, 3 * outs)
    if last:
        out_shape = (jax.ShapeDtypeStruct(half, F32), jax.ShapeDtypeStruct(half, BF16))
    else:
        out_shape = (jax.ShapeDtypeStruct(shape, F32),)
    args = [wide, *pieces] + ([old] if old is not None else [])
    out = pl.pallas_call(
        functools.partial(grad_kernel, step, len(pieces), old is not None, last),
        out_shape=out_shape,
        in_specs=[VMEM_SPEC] * len(args),
        out_specs=tuple([VMEM_SPEC] * len(out_shape)),
        scratch_shapes=[pltpu.VMEM((cols + 2, rows, outs), BF16)],
        compiler_params=pltpu.CompilerParams(vmem_limit_bytes=5 * 2**20),
        cost_estimate=QUICK,
        name="grad_first",
    )(*args)
    return out if last else out[0]


def spread_tile(columns, wide_ref):
    rows, chans = wide_ref.shape[1], wide_ref.shape[2] // 3
    place = lax.broadcasted_iota(jnp.int32, (rows, chans), 0)
    for j, (mid, before, after) in enumerate(columns):
        wide = mid.astype(F32)
        ahead = jnp.where(place == 0, before.astype(F32), pltpu.roll(wide, 1, 0))
        behind = jnp.where(place == rows - 1, after.astype(F32), pltpu.roll(wide, rows - 1, 0))
        wide_ref[j, :, 0:chans] = ahead.astype(BF16)
        wide_ref[j, :, chans : 2 * chans] = mid
        wide_ref[j, :, 2 * chans :] = behind.astype(BF16)


def back_kernel(cot_ref, left_ref, right_ref, edge_ref, kernel_ref, out_ref, wide_ref):
    cols, rows, chans = cot_ref.shape
    start = edge_ref.shape[1] - 2 * cols

    def beside(k, j):
        low, high = start + j, start + cols + j
        return jnp.concatenate(
            [edge_ref[k, low : low + 1, :], edge_ref[k, high : high + 1, :]], axis=-1
        )

    def whole(ref):
        return ref[0:rows], ref[rows : rows + 1], ref[rows + 1 : rows + 2]

    columns = [(cot_ref[j], beside(0, j), beside(1, j)) for j in range(cols)]
    spread_tile([whole(left_ref)] + columns + [whole(right_ref)], wide_ref)
    total = None
    for tap_col in range(3):
        lhs = wide_ref[tap_col : tap_col + cols].reshape(cols * rows, 3 * chans)
        for tap_row in range(3):
            part = lax.dot_general(
                lhs[:, tap_row * chans : (tap_row + 1) * chans],
                kernel_ref[2 - tap_col, 2 - tap_row],
                (((1,), (1,)), ((), ())),
                preferred_element_type=F32,
            )
            total = part if total is None else total + part
    out_ref[...] = total.reshape(cols, rows, -1)


def back_tile(tile, left, right, edges, kernel):
    cols, rows, chans = tile.shape
    return pl.pallas_call(
        back_kernel,
        out_shape=(
            jax.ShapeDtypeStruct((cols, rows, kernel.shape[2]), F32),
            jax.ShapeDtypeStruct((cols + 2, rows, 3 * chans), BF16),
        ),
        in_specs=[VMEM_SPEC] * 5,
        out_specs=(VMEM_SPEC,) * 2,
        compiler_params=pltpu.CompilerParams(vmem_limit_bytes=4 * 2**20),
        cost_estimate=QUICK,
        name="back",
    )(tile, left, right, edges, kernel)


def second_kernel(chips, hid_ref, wide_ref, near_ref, far_ref, sum_ref):
    chans = hid_ref.shape[2]
    cols, rows, outs = hid_ref.shape[0] - 2, hid_ref.shape[1], wide_ref.shape[2] // 3
    core = lax.axis_index("c")
    lhs = hid_ref[1 : cols + 1].reshape(cols * rows, chans)
    for tap_col in range(3):
        rhs = wide_ref[2 - tap_col : 2 - tap_col + cols].reshape(cols * rows, 3 * outs)
        part = lax.dot_general(lhs, rhs, (((0,), (0,)), ((), ())), preferred_element_type=F32)
        for tap_row in range(3):
            sum_ref[
                tap_row * chans : (tap_row + 1) * chans, tap_col * outs : (tap_col + 1) * outs
            ] = part[:, (2 - tap_row) * outs : (3 - tap_row) * outs]
    size = sum_ref.shape[0] // (2 * chips)
    for half, ref in ((core, near_ref), (1 - core, far_ref)):
        for chip in range(chips):
            at = pl.multiple_of((half * chips + chip) * size, size)
            for tap in range(3):
                ref[chip, tap * size : (tap + 1) * size, :] = sum_ref[
                    pl.ds(at, size), tap * outs : (tap + 1) * outs
                ].astype(ref.dtype)


def second_tile(tile, wide, chips):
    chans, outs = tile.shape[2], wide.shape[2] // 3
    cut = (chips, 9 * chans // (2 * chips), outs)
    return pl.pallas_call(
        functools.partial(second_kernel, chips),
        out_shape=(jax.ShapeDtypeStruct(cut, F32), jax.ShapeDtypeStruct(cut, BF16)),
        in_specs=[VMEM_SPEC] * 2,
        out_specs=(VMEM_SPEC,) * 2,
        scratch_shapes=[pltpu.VMEM((3 * chans, 3 * outs), F32)],
        compiler_params=pltpu.CompilerParams(vmem_limit_bytes=9 * 2**20),
        cost_estimate=QUICK,
        name="second",
    )(tile, wide)


def features_kernel(hid_ref, before_ref, after_ref, kernel_ref, out_ref, wide_ref):
    cols, rows, outs = out_ref.shape
    columns = [
        (hid_ref[j], before_ref[j : j + 1, :], after_ref[j : j + 1, :]) for j in range(cols + 2)
    ]
    spread_tile(columns, wide_ref)
    pieces = [wide_ref[tap : tap + cols] for tap in range(3)]
    lhs = jnp.concatenate(pieces, axis=-1).reshape(cols * rows, -1)
    total = jnp.dot(lhs, kernel_ref[...], preferred_element_type=F32)
    out_ref[...] = total.reshape(cols, rows, outs).astype(BF16)


def features_tile(tile, edges, kernel):
    cols, rows, chans = tile.shape
    outs = kernel.shape[3]
    return pl.pallas_call(
        features_kernel,
        out_shape=jax.ShapeDtypeStruct((cols - 2, rows, outs), BF16),
        in_specs=[VMEM_SPEC] * 4,
        out_specs=VMEM_SPEC,
        scratch_shapes=[pltpu.VMEM((cols, rows, 3 * chans), BF16)],
        compiler_params=pltpu.CompilerParams(vmem_limit_bytes=9 * 2**20),
        cost_estimate=QUICK,
        name="features",
    )(tile, *edges, kernel.reshape(-1, outs))


def point_kernel(
    own_ref, a0_ref, a1_ref, b0_ref, b1_ref, back_ref,
    delta_ref, hidden_ref, last_ref, first_ref,
):
    cols, rows, _ = own_ref.shape
    half = delta_ref.shape[0] // 2
    strip = 2 * lax.axis_index("y") + lax.axis_index("c")
    strips = 2 * lax.axis_size("y")

    def column(j, i, refs, keep):
        pre = own_ref[j] + refs[0][i].astype(F32) + refs[1][i].astype(F32)
        sigma = jax.nn.sigmoid(pre)
        hidden = pre * sigma
        if keep is not None:
            hidden = jnp.where(keep, hidden, 0.0)
        hidden = hidden.astype(BF16)
        hidden_ref[j] = hidden
        last_ref[j : j + 1, :] = hidden[rows - 1 :]
        first_ref[j : j + 1, :] = hidden[:1]
        if keep is None:
            slope = sigma * (1.0 + pre * (1.0 - sigma))
            delta_ref[j - 1] = (back_ref[j - 1] * slope).astype(BF16)

    left, right = (a0_ref, a1_ref), (b0_ref, b1_ref)
    column(0, 0, left, strip > 0)
    column(cols - 1, half, right, strip < strips - 1)

    for i in range(1, half + 1):
        column(i, i, left, None)
        column(half + i, i - 1, right, None)


def point(own, left, right, back):
    strip, rows, outs = back.shape
    delta = jax.ShapeDtypeStruct(back.shape, BF16)
    edge = jax.ShapeDtypeStruct((strip + 2, outs), BF16)
    return pl.pallas_call(
        point_kernel,
        out_shape=(delta, jax.ShapeDtypeStruct(own.shape, BF16), edge, edge),
        in_specs=[VMEM_SPEC] * 6,
        out_specs=(VMEM_SPEC,) * 4,
        compiler_params=pltpu.CompilerParams(vmem_limit_bytes=2 * 2**20),
        cost_estimate=QUICK,
        name="point",
    )(own, *left, *right, back)


def fold_kernel(near_ref, got_ref, keep_ref, *send_refs):
    chips = near_ref.shape[0]
    here = lax.axis_index("y")
    keep_ref[...] = near_ref[here] + got_ref[here].astype(F32)
    for step, ref in zip(STEPS[1:], send_refs):
        to = lax.rem(here + step, chips)
        ref[...] = (near_ref[to] + got_ref[to].astype(F32)).astype(BF16)


def fold(near, got):
    shape = near.shape[1:]
    return pl.pallas_call(
        fold_kernel,
        out_shape=(jax.ShapeDtypeStruct(shape, F32),) + (jax.ShapeDtypeStruct(shape, BF16),) * 3,
        in_specs=[VMEM_SPEC] * 2,
        out_specs=(VMEM_SPEC,) * 4,
        compiler_params=pltpu.CompilerParams(vmem_limit_bytes=2 * 2**20),
        cost_estimate=QUICK,
        name="fold",
    )(near, got)


def row_halo(ends):
    count = lax.axis_size(SKY)
    up = [(i, i + 1) for i in range(count - 1)]
    down = [(j, i) for i, j in up]
    return lax.ppermute(ends[0], SKY, up), lax.ppermute(ends[1], SKY, down)


def join_kernel(own_ref, far_ref, keep_ref, a_ref, b_ref, c_ref, out_ref):
    pieces, total, outs = out_ref.shape
    chans = own_ref.shape[0] // 3
    size = chans // pieces
    for tap_col in range(3):
        for tap_row in range(3):
            rows = slice(tap_row * chans, (tap_row + 1) * chans)
            lanes = slice(tap_col * outs, (tap_col + 1) * outs)
            value = own_ref[rows, lanes] + far_ref[rows, lanes].astype(F32)
            at = (3 * tap_col + tap_row) * size
            out_ref[:, at : at + size, :] = value.reshape(pieces, size, outs).astype(BF16)
    second = keep_ref[...]
    for ref in (a_ref, b_ref, c_ref):
        second = second + ref[...].astype(F32)
    sx = lax.axis_size("x")
    sz = pieces // sx
    third = second.shape[0] // 3
    size_x = third // sx
    extra = total - 9 * size
    for x in range(sx):
        value = jnp.concatenate(
            [second[tap * third + x * size_x : tap * third + (x + 1) * size_x] for tap in range(3)],
            axis=0,
        )
        for z in range(sz):
            out_ref[z * sx + x, 9 * size :, :] = value[z * extra : (z + 1) * extra].astype(BF16)


def join(own, far, keep, got, pieces):
    outs = keep.shape[1]
    rows = 9 * (own.shape[0] // 3 // pieces) + keep.shape[0] // pieces
    return pl.pallas_call(
        join_kernel,
        out_shape=jax.ShapeDtypeStruct((pieces, rows, outs), BF16),
        in_specs=[VMEM_SPEC] * 6,
        out_specs=VMEM_SPEC,
        compiler_params=pltpu.CompilerParams(vmem_limit_bytes=4 * 2**20),
        cost_estimate=QUICK,
        name="join",
    )(own, far, keep, *got)


STEPS = (0, 1, 3, 2)


def order_kernel(extra, a_ref, b_ref, c_ref, d_ref, out_ref):
    rows = a_ref.shape[0] - extra
    sz = lax.axis_size("z")
    me = lax.axis_index("z")
    values = [ref[...].astype(F32) for ref in (a_ref, b_ref, c_ref, d_ref)]
    rest = []
    for z in range(len(STEPS)):
        value = values[0]
        for step, other in zip(STEPS[1:], values[1:]):
            value = jnp.where(lax.rem(me + sz - step, sz) == z, other, value)
        out_ref[z * rows : (z + 1) * rows, :] = value[:rows].astype(BF16)
        rest.append(value[rows:])
    out_ref[len(STEPS) * rows :, :] = jnp.concatenate(rest, axis=0).astype(BF16)


def order_pieces(parts, extra):
    rows, outs = parts[0].shape
    return pl.pallas_call(
        functools.partial(order_kernel, extra),
        out_shape=jax.ShapeDtypeStruct((4 * rows, outs), BF16),
        in_specs=[VMEM_SPEC] * 4,
        out_specs=VMEM_SPEC,
        compiler_params=pltpu.CompilerParams(vmem_limit_bytes=4 * 2**20),
        cost_estimate=QUICK,
        name="order_pieces",
    )(*parts)


def first_kernel(sz, a_ref, b_ref, c_ref, d_ref, out_ref):
    sx = lax.axis_size("x")
    size = out_ref.shape[2] // (sx * sz)
    me = lax.axis_index("x")
    for step, ref in zip(STEPS, (a_ref, b_ref, c_ref, d_ref)):
        x = lax.rem(me + sx - step, sx)
        value = ref[...].astype(F32)
        for z in range(sz):
            at = pl.multiple_of((z * sx + x) * size, size)
            for tap in range(9):
                rows = (z * 9 + tap) * size
                out_ref[tap // 3, tap % 3, pl.ds(at, size), :] = value[rows : rows + size]


def lay_first(parts, sz, chans):
    outs = parts[0].shape[1]
    return pl.pallas_call(
        functools.partial(first_kernel, sz),
        out_shape=jax.ShapeDtypeStruct((3, 3, chans, outs), F32),
        in_specs=[VMEM_SPEC] * 4,
        out_specs=VMEM_SPEC,
        compiler_params=pltpu.CompilerParams(vmem_limit_bytes=4 * 2**20),
        cost_estimate=QUICK,
        name="lay_first",
    )(*parts)


def sum_kernel(in_ref, out_ref):
    total = in_ref[0].astype(F32)
    for i in range(1, in_ref.shape[0]):
        total = total + in_ref[i].astype(F32)
    out_ref[...] = total.astype(BF16)


def sum_pieces(pieces):
    return pl.pallas_call(
        sum_kernel,
        out_shape=jax.ShapeDtypeStruct(pieces.shape[1:], BF16),
        in_specs=[VMEM_SPEC],
        out_specs=VMEM_SPEC,
        compiler_params=pltpu.CompilerParams(vmem_limit_bytes=4 * 2**20),
        cost_estimate=QUICK,
        name="sum_pieces",
    )(pieces)


def pick_kernel(first, a_ref, b_ref, c_ref, d_ref, out_ref):
    for i, ref in enumerate((a_ref, b_ref, c_ref, d_ref)):
        out_ref[i] = ref[first:, :]


def pick_rows(parts, first):
    rows, outs = parts[0].shape
    return pl.pallas_call(
        functools.partial(pick_kernel, first),
        out_shape=jax.ShapeDtypeStruct((len(parts), rows - first, outs), BF16),
        in_specs=[VMEM_SPEC] * 4,
        out_specs=VMEM_SPEC,
        compiler_params=pltpu.CompilerParams(vmem_limit_bytes=2 * 2**20),
        cost_estimate=QUICK,
        name="pick_rows",
    )(*parts)


def lay_second_kernel(other, in_ref, *refs):
    out_ref, half_ref, sems = refs[-3:]
    sy, sx, rows, _ = in_ref.shape
    size = rows // 3
    third = half_ref.shape[0] // 3
    core, y, x = lax.axis_index("c"), lax.axis_index("y"), lax.axis_index("x")
    half = 1 - core if other else core
    copies = []
    for tap in range(3):
        for i in range(sy):
            for j in range(sx):
                place = lax.rem(y + sy - STEPS[i], sy) * sx + lax.rem(x + sx - STEPS[j], sx)
                at = pl.multiple_of(tap * third + place * size, 8)
                value = in_ref[i, j, tap * size : (tap + 1) * size, :].astype(F32)
                half_ref[pl.ds(at, size), :] = value
        to = pl.multiple_of((2 * tap + half) * third, 8)
        copy = pltpu.make_async_copy(
            half_ref.at[tap * third : (tap + 1) * third],
            out_ref.at[pl.ds(to, third)],
            sems.at[tap],
        )
        copy.start()
        copies.append(copy)
    for copy in copies:
        copy.wait()


def lay_second(half, whole=None):
    sy, sx, rows, outs = half.shape
    size = sy * sx * rows
    anywhere = pl.BlockSpec(memory_space=pl.ANY)
    given = [] if whole is None else [whole]
    return pl.pallas_call(
        functools.partial(lay_second_kernel, whole is not None),
        out_shape=jax.ShapeDtypeStruct((2 * size, outs), F32),
        in_specs=[VMEM_SPEC] + [anywhere] * len(given),
        out_specs=anywhere,
        scratch_shapes=[pltpu.VMEM((size, outs), F32), pltpu.SemaphoreType.DMA((3,))],
        compiler_params=pltpu.CompilerParams(vmem_limit_bytes=4 * 2**20),
        cost_estimate=QUICK,
        input_output_aliases={1: 0} if given else {},
        name="lay_second",
    )(half, *given)


def gather_steps(piece, axis):
    return [piece] + [shift(piece, axis, step) for step in STEPS[1:]]


def body(sky_cube, weight_first, weight_second, cotangent):
    cols, rows, chans = sky_cube.shape
    strip, _, outs = cotangent.shape
    chips = lax.axis_size("y")

    ends = [
        jnp.concatenate(
            [sky_cube[:, r], cotangent[:, r, : outs // 2], cotangent[:, r, outs // 2 :]], axis=0
        )
        for r in (rows - 1, 0)
    ]
    edges = jnp.stack(row_halo(ends))
    far_cube = shift(sky_cube, "c", 1)
    far_weight = shift(weight_first, "c", 1)
    far_edges = shift(edges, "c", 1)
    wide = spread(sky_cube, far_cube, edges, far_edges, chips)
    kernel = jnp.concatenate([weight_first, far_weight], axis=2).reshape(18 * chans, outs)

    def side(col):
        beside = [
            jnp.concatenate(
                [edges[k, at + col : at + col + 1] for at in (cols, cols + strip)], axis=1
            )
            for k in range(2)
        ]
        return jnp.concatenate([cotangent[col]] + beside, axis=0)

    count = lax.axis_size(FREQ)
    up = [(i, i + 1) for i in range(count - 1)]
    down = [(j, i) for i, j in up]
    left = lax.ppermute(side(strip - 1), FREQ, up)
    right = lax.ppermute(side(0), FREQ, down)

    on, off = 1, chips - 1
    cut = strip // 2 + 1
    far_a, far_b = conv_parts(((2, 0), (2, cut)), wide, kernel, cut, BF16)
    hold, _ = lax.optimization_barrier((wide, far_a))
    near_b, near_a = conv_parts(((on, cut), (off, 0)), hold, kernel, cut, BF16)
    got_a, got_b = shift(far_a, "y", on), shift(far_b, "y", off)
    got_a, left, right = lax.optimization_barrier((got_a, left, right))
    both_a, both_b = conv_parts(((on, 0), (off, cut)), wide, kernel, cut, BF16, (got_a, got_b))
    own = conv_parts(((0, 0),), wide, kernel, strip + 2, F32)[0]
    from_a = shift(both_a, "y", on), shift(near_a, "y", off)
    from_b = shift(near_b, "y", on), shift(both_b, "y", off)

    back, wide_cotangent = back_tile(cotangent, left, right, edges, weight_second)
    delta, hidden, *ends = point(own, from_a, from_b, back)

    from_on, from_off = shift(delta, "y", on), shift(delta, "y", off)
    half = strip // 2
    total = grad_strip(0, wide, (delta,), None, False)
    from_on, from_off, total = lax.optimization_barrier((from_on, from_off, total))
    fwd_a, fwd_b = shift(from_on[:half], "y", on), shift(from_off[half:], "y", off)
    near, far = second_tile(hidden, wide_cotangent, chips)
    keep, *sends = fold(near, shift(far, "c", 1))
    got = [shift(send, "y", step) for step, send in zip(STEPS[1:], sends)]
    total = grad_strip(off, wide, (from_on,), total, False)
    total = grad_strip(on, wide, (from_off,), total, False)
    first_own, first_far = grad_strip(2, wide, (fwd_a, fwd_b), total, True)

    sx, sz = lax.axis_size("x"), lax.axis_size("z")
    first_far, *got = lax.optimization_barrier((first_far, *got))
    joined = join(first_own, shift(first_far, "c", 1), keep, got, sx * sz)
    extra = keep.shape[0] // (sx * sz)
    summed = lax.all_to_all(joined, SKY, 0, 0, tiled=True)
    summed = sum_pieces(summed)
    parts = gather_steps(order_pieces(gather_steps(summed, "z"), extra), "x")
    main = parts[0].shape[0] - sz * extra
    grad_first = lay_first(parts, sz, chans)
    share = pick_rows(parts, main)
    share, *ends = lax.optimization_barrier((share, *ends))
    features = features_tile(hidden, row_halo(ends), weight_second)
    share, grad_first, features = lax.optimization_barrier(
        (jnp.stack(gather_steps(share, "y")), grad_first, features)
    )
    grad_second = lay_second(shift(share, "c", 1), lay_second(share))
    grad_second = grad_second.reshape(3, 3, outs, outs)
    return features, grad_first, grad_second


def solution(mesh):
    sizes = (mesh.devices.shape[0] // 2, 2, 4, mesh.devices.shape[1] // 4)
    fine = Mesh(mesh.devices.reshape(sizes), FREQ + SKY)
    return jax.shard_map(
        body,
        mesh=fine,
        in_specs=(P(None, SKY, FREQ), P(None, None, FREQ, None), P(), P(FREQ, SKY, None)),
        out_specs=(P(FREQ, SKY, None), P(None, None, FREQ, None), P()),
        check_vma=False,
    )
```
